32 devices in a mesh: dp: 8 (over z, x), ffn: 4 (over y, core).
Axes of the slice: x: 2, y: 2, z: 4, core: 2. Of those that a mesh axis runs over, the one named last changes fastest.
Arguments:
- tokens: bfloat16 [32768, 768], P(('dp', 'ffn')), may hold values from -6 to 6
- long_seq: int32 [32], P(('dp', 'ffn')), may hold values from 0 to 1, as said below
- cotangent: bfloat16 [32768, 768], P(('dp', 'ffn')), may hold values from -6 to 6
- query_weight: bfloat16 [768, 192], P(('dp', 'ffn')), may hold values from -0.4375 to 0.4375
- key_weight: bfloat16 [768, 192], P(('dp', 'ffn')), may hold values from -0.4375 to 0.4375
- value_weight: bfloat16 [768, 192], P(('dp', 'ffn')), may hold values from -0.4375 to 0.4375
- out_weight: bfloat16 [768, 768], P(('dp', 'ffn')), may hold values from -0.875 to 0.875
- query_bias: bfloat16 [768], P(('dp', 'ffn')), may hold values from -3 to 3
- value_bias: bfloat16 [768], P(('dp', 'ffn')), may hold values from -3 to 3
- out_bias: bfloat16 [768], P(('dp', 'ffn')), may hold values from -3 to 3
- attn_gain: bfloat16 [768], P(('dp', 'ffn')), may hold values from 0.5 to 1.5
- attn_shift: bfloat16 [768], P(('dp', 'ffn')), may hold values from -3 to 3
- ffn_in_weight: bfloat16 [4, 192, 768], P(None, None, 'ffn'), may hold values from -0.4375 to 0.4375
- ffn_in_bias: bfloat16 [4, 768], P(None, 'ffn'), may hold values from -3 to 3
- ffn_out_weight: bfloat16 [4, 768, 192], P(None, 'ffn'), may hold values from -0.21875 to 0.21875
- ffn_out_bias: bfloat16 [768], P(('dp', 'ffn')), may hold values from -3 to 3
- ffn_gain: bfloat16 [768], P(('dp', 'ffn')), may hold values from 0.5 to 1.5
- ffn_shift: bfloat16 [768], P(('dp', 'ffn')), may hold values from -3 to 3
Outputs:
- output: bfloat16 [32768, 768], P(('dp', 'ffn'))
- grad_tokens: bfloat16 [32768, 768], P(('dp', 'ffn'))
- query_weight_grad: float32 [768, 192], P(('dp', 'ffn'))
- key_weight_grad: float32 [768, 192], P(('dp', 'ffn'))
- value_weight_grad: float32 [768, 192], P(('dp', 'ffn'))
- out_weight_grad: float32 [768, 768], P(('dp', 'ffn'))
- query_bias_grad: float32 [768], P(('dp', 'ffn'))
- value_bias_grad: float32 [768], P(('dp', 'ffn'))
- out_bias_grad: float32 [768], P(('dp', 'ffn'))
- attn_gain_grad: float32 [768], P(('dp', 'ffn'))
- attn_shift_grad: float32 [768], P(('dp', 'ffn'))
- ffn_in_weight_grad: float32 [4, 192, 768], P(None, None, 'ffn')
- ffn_in_bias_grad: float32 [4, 768], P(None, 'ffn')
- ffn_out_weight_grad: float32 [4, 768, 192], P(None, 'ffn')
- ffn_out_bias_grad: float32 [768], P(('dp', 'ffn'))
- ffn_gain_grad: float32 [768], P(('dp', 'ffn'))
- ffn_shift_grad: float32 [768], P(('dp', 'ffn'))
The draws below stay inside these ranges and needn't reach their ends.
Inputs may be any that keep to these rules, and one draw needn't show every extreme that they name: `long_seq`: 1: the device's 1024 tokens form 1024 // 512 sequences of 512 tokens; 0: they form 1024 // 128 sequences of 128 tokens. Exactly (64) // 3 devices hold a 1.
All inputs are finite; a program needn't handle non-finite values.
Results may differ from the reference program's by a relative error of at most 0.017.
Values may be sent and summed in bfloat16 or wider, within the bound.
No kernel may reach another device: no remote copies, remote signals or barrier semaphores. Data moves between devices by JAX's collectives and lax.ppermute only.
A program may use at most 256 MiB of HBM per device.

```python
import jax
import jax.numpy as jnp
from jax import lax

D = 768
HEADS = 12
HEAD = 64
GROUPS = 4
TOK_DEV = 1024
LONG = 512
SHORT = 128
GW = 192
FG = 768
SHARDS = 32
TOKENS = 32768


def draw_long_seq(key, part):
    order = jax.random.permutation(key, SHARDS)
    return (order < 2 * SHARDS // 3).astype(jnp.int32)


def level_of(key, dims, pieces, least, largest):
    level, own = 1.0, jax.random.fold_in(key, 6)
    for dim, blocks in pieces:
        draws = jnp.exp(jax.random.uniform(jax.random.fold_in(own, dim), (blocks,), jnp.float32, least / len(pieces), largest / len(pieces)))
        level = level * jnp.repeat(draws, dims[dim] // blocks).reshape([-1 if axis == dim else 1 for axis in range(len(dims))])
    return level


def bell_draw(rng, dims, scale, reach, split=(), held_as=jnp.bfloat16):
    level = level_of(rng, dims, split, -0.22, 0.18) if split else 1.0
    entries = jax.random.normal(rng, dims, jnp.float32) * scale * level
    return jnp.minimum(jnp.maximum(entries, -reach), reach).astype(held_as)


def setup_inputs(seed: int = 0) -> dict:
    splits = jax.random.split(jax.random.key(seed), 19)
    tokens = bell_draw(splits[0], (TOKENS, D), 1.0, 6.0, ((0, 32),))
    long_seq = draw_long_seq(jax.random.fold_in(splits[18], 71), 0)
    cotangent = bell_draw(splits[2], (TOKENS, D), 1.0, 6.0, ((0, 32),))
    query_weight = bell_draw(splits[3], (D, GW), GW ** -0.5, 0.4375, ((0, 32),))
    key_weight = bell_draw(splits[4], (D, GW), GW ** -0.5, 0.4375, ((0, 32),))
    value_weight = bell_draw(splits[5], (D, GW), GW ** -0.5, 0.4375, ((0, 32),))
    out_weight = bell_draw(splits[6], (D, D), (D // 16) ** -0.5, 0.875, ((0, 32),))
    query_bias = bell_draw(splits[7], (D,), 0.5, 3.0, ((0, 32),))
    value_bias = bell_draw(splits[8], (D,), 0.5, 3.0, ((0, 32),))
    out_bias = bell_draw(splits[9], (D,), 0.5, 3.0, ((0, 32),))
    attn_gain = jnp.clip(1.0 + 0.1 * jax.random.normal(splits[10], (D,), jnp.float32), 0.5, 1.5).astype(jnp.bfloat16)
    attn_shift = bell_draw(splits[11], (D,), 0.5, 3.0, ((0, 32),))
    ffn_in_weight = bell_draw(splits[12], (GROUPS, GW, FG), GW ** -0.5, 0.4375, ((2, 4),))
    ffn_in_bias = bell_draw(splits[13], (GROUPS, FG), 0.5, 3.0, ((1, 4),))
    ffn_out_weight = bell_draw(splits[14], (GROUPS, FG, GW), FG ** -0.5, 0.21875, ((1, 4),))
    ffn_out_bias = bell_draw(splits[15], (D,), 0.5, 3.0, ((0, 32),))
    ffn_gain = jnp.clip(1.0 + 0.1 * jax.random.normal(splits[16], (D,), jnp.float32), 0.5, 1.5).astype(jnp.bfloat16)
    ffn_shift = bell_draw(splits[17], (D,), 0.5, 3.0, ((0, 32),))
    return {"tokens": tokens, "long_seq": long_seq, "cotangent": cotangent, "query_weight": query_weight, "key_weight": key_weight, "value_weight": value_weight, "out_weight": out_weight, "query_bias": query_bias, "value_bias": value_bias, "out_bias": out_bias, "attn_gain": attn_gain, "attn_shift": attn_shift, "ffn_in_weight": ffn_in_weight, "ffn_in_bias": ffn_in_bias, "ffn_out_weight": ffn_out_weight, "ffn_out_bias": ffn_out_bias, "ffn_gain": ffn_gain, "ffn_shift": ffn_shift}


@jax.custom_vjp
def low(v):
    return lax.optimization_barrier(v.astype(jnp.bfloat16)).astype(jnp.float32)

@jax.custom_vjp
def low_back(v):
    return v

def low_keep(v):
    return (low(v), None)

def low_pass(kept, grad):
    return (grad,)

def back_keep(v):
    return (v, None)

def back_low(kept, grad):
    return (low(grad),)
low.defvjp(low_keep, low_pass)
low_back.defvjp(back_keep, back_low)
eps = 1e-12
big_negative = -1000000000.0

def layer_norm(inputs, gain, shift):
    center = inputs - lax.optimization_barrier(jnp.mean(inputs, axis=-1, keepdims=True))
    spread = lax.optimization_barrier(jnp.mean(center * center, axis=-1, keepdims=True))
    return center * lax.rsqrt(spread + eps) * gain + shift

def grouped(inputs, weight):
    tok_count = inputs.shape[0]
    parts = inputs.reshape(tok_count, GROUPS, GW)
    return jnp.einsum('ngi,gio->ngo', parts, weight.reshape(GROUPS, GW, GW), precision=lax.Precision.HIGHEST).reshape(tok_count, D)

def attend_block(q_block, k_block, v_block, flag):
    position = jnp.arange(TOK_DEV)
    segment = jnp.where(flag == 1, position // LONG, position // SHORT)
    same_seq = segment[:, None] == segment[None, :]
    q_heads = q_block.reshape(TOK_DEV, HEADS, HEAD)
    k_heads = k_block.reshape(TOK_DEV, HEADS, HEAD)
    v_heads = v_block.reshape(TOK_DEV, HEADS, HEAD)
    raw_scores = jnp.einsum('qhd,khd->hqk', q_heads, k_heads, precision=lax.Precision.HIGHEST)
    scores = jnp.where(same_seq[None], low_back(raw_scores) * HEAD ** (-0.5), big_negative)
    probs = low(jax.nn.softmax(scores, axis=-1))
    context = jnp.einsum('hqk,khd->qhd', probs, v_heads, precision=lax.Precision.HIGHEST)
    return low(low_back(context.reshape(TOK_DEV, D)))

def block_forward(inputs, long_seq, w_query, w_key, w_value, w_out, b_query, b_value, b_out, gain_attn, shift_attn, w_first, b_first, w_second, bias_last, gain_last, shift_last):
    tok_count = inputs.shape[0]
    q_all = low(low_back(grouped(inputs, w_query)) + b_query)
    k_all = low(low_back(grouped(inputs, w_key)))
    v_all = low(low_back(grouped(inputs, w_value)) + b_value)
    shards = tok_count // TOK_DEV
    attend = jax.checkpoint(attend_block)
    context = lax.map(lambda item: attend(item[0], item[1], item[2], item[3]), (q_all.reshape(shards, TOK_DEV, D), k_all.reshape(shards, TOK_DEV, D), v_all.reshape(shards, TOK_DEV, D), long_seq))
    context = context.reshape(tok_count, D)
    attn_sum = inputs + low_back(jnp.dot(context, w_out, precision=lax.Precision.HIGHEST)) + b_out
    normed = layer_norm(attn_sum, gain_attn, shift_attn)
    normed_low = low(normed)
    pre_act = low_back(jnp.einsum('ngi,gic->ngc', normed_low.reshape(tok_count, GROUPS, GW), w_first, precision=lax.Precision.HIGHEST)) + b_first
    activ = low(jax.nn.gelu(pre_act, approximate=False))
    ffn_out = low_back(jnp.einsum('ngc,gco->ngo', activ, w_second, precision=lax.Precision.HIGHEST).reshape(tok_count, D))
    ffn_sum = normed + ffn_out + bias_last
    return layer_norm(ffn_sum, gain_last, shift_last)

def reference(tokens, long_seq, cotangent, query_weight, key_weight, value_weight, out_weight, query_bias, value_bias, out_bias, attn_gain, attn_shift, ffn_in_weight, ffn_in_bias, ffn_out_weight, ffn_out_bias, ffn_gain, ffn_shift):
    params = [item.astype(jnp.float32) for item in (query_weight, key_weight, value_weight, out_weight, query_bias, value_bias, out_bias, attn_gain, attn_shift, ffn_in_weight, ffn_in_bias, ffn_out_weight, ffn_out_bias, ffn_gain, ffn_shift)]

    def forward(inputs, w_query, w_key, w_value, w_out, b_query, b_value, b_out, gain_attn, shift_attn, w_first, b_first, w_second, bias_last, gain_last, shift_last):
        return block_forward(inputs, long_seq, w_query, w_key, w_value, w_out, b_query, b_value, b_out, gain_attn, shift_attn, w_first, b_first, w_second, bias_last, gain_last, shift_last)
    result, back = jax.vjp(forward, tokens.astype(jnp.float32), *params)
    grads = back(cotangent.astype(jnp.float32))
    return (result.astype(jnp.bfloat16), grads[0].astype(jnp.bfloat16), grads[1], grads[2], grads[3], grads[4], grads[5], grads[6], grads[7], grads[8], grads[9], grads[10], grads[11], grads[12], grads[13], grads[14], grads[15])
```

```python
import functools

import jax
import jax.numpy as jnp
from jax import lax
from jax.experimental import pallas as pl
from jax.experimental.pallas import tpu as pltpu
from jax.sharding import PartitionSpec as P

F32 = jnp.float32
BF = jnp.bfloat16
HEADS = 12
LONG = 512
SHORT = 128
EPS = 1e-12
AXES = ("dp", "ffn")
PAD = 16

TAIL_P = 0.3
TAIL = (
    7.2369888953694e-06,
    0.1194865245949597,
    0.12192867168298993,
    0.09465089133364463,
    0.14261228132875567,
    -0.07661778627208168,
    0.22875753326362114,
    -0.1692133381644571,
    0.03838801421466209,
)


def dg(a, b, ca, cb):
    return lax.dot_general(a, b, (((ca,), (cb,)), ((), ())), preferred_element_type=F32)


def lane_sum(v):
    out = v[:, :128]
    for c in range(128, v.shape[1], 128):
        out = out + v[:, c : c + 128]
    return out


def params(limit=56):
    return pltpu.CompilerParams(vmem_limit_bytes=limit << 20)


def attn_fwd_kernel(flag_ref, x_ref, w_ref, q_ref, k_ref, v_ref, e_ref, c_ref, inv_ref, *, gw, hd, qc):
    w = w_ref[...]
    p = dg(w[:, : 3 * gw], x_ref[...], 0, 0)
    bq = w[:, 3 * gw : 3 * gw + 1].astype(F32)
    bv = w[:, 3 * gw + 1 : 3 * gw + 2].astype(F32)
    q_ref[...] = (p[:gw] + bq).astype(BF)
    k_ref[...] = p[gw : 2 * gw].astype(BF)
    v_ref[...] = (p[2 * gw :] + bv).astype(BF)
    nh = gw // hd
    inv_ref[...] = jnp.zeros_like(inv_ref)

    def run(span, step):
        ones = jnp.ones((16, span), BF)
        for h in range(nh):
            r = slice(h * hd, (h + 1) * hd)
            for s0 in range(0, LONG, span):
                ks = slice(s0, s0 + span)
                k = k_ref[r, ks]
                vx = jnp.concatenate([v_ref[r, ks], ones], 0)
                for c0 in range(s0, s0 + span, step):
                    cs = slice(c0, c0 + step)
                    q = q_ref[r, cs] * jnp.asarray(hd**-0.5, BF)
                    s = dg(k, q, 0, 0)
                    m = jnp.max(s, axis=0, keepdims=True)
                    e = jnp.exp(s - m).astype(BF)
                    e_ref[h, 0, ks, cs] = e
                    o = dg(vx, e, 1, 0)
                    inv = 1.0 / o[hd : hd + 1]
                    c_ref[r, cs] = (o[:hd] * inv).astype(BF)
                    inv_ref[h : h + 1, cs] = inv

    @pl.when(flag_ref[0] == 1)
    def _():
        run(LONG, qc)

    @pl.when(flag_ref[0] != 1)
    def _():
        run(SHORT, SHORT)


def attn_fwd(flag, xt, w, g, gw, hd, qc=256):
    width, toks = xt.shape
    blocks = toks // LONG
    nh = gw // hd
    own = lambda: pl.BlockSpec((gw, LONG), lambda j, f: (0, j))
    return pl.pallas_call(
        functools.partial(attn_fwd_kernel, gw=gw, hd=hd, qc=qc),
        out_shape=[jax.ShapeDtypeStruct((gw, toks), BF)] * 3
        + [
            jax.ShapeDtypeStruct((nh, blocks, LONG, LONG), BF),
            jax.ShapeDtypeStruct((gw, toks), BF),
            jax.ShapeDtypeStruct((8, toks), F32),
        ],
        grid_spec=pltpu.PrefetchScalarGridSpec(
            num_scalar_prefetch=1,
            grid=(blocks,),
            in_specs=[
                pl.BlockSpec((gw, LONG), lambda j, f: (g, j)),
                pl.BlockSpec((gw, w.shape[1]), lambda j, f: (g, 0)),
            ],
            out_specs=[
                own(),
                own(),
                own(),
                pl.BlockSpec((nh, 1, LONG, LONG), lambda j, f: (0, j, 0, 0)),
                own(),
                pl.BlockSpec((8, LONG), lambda j, f: (0, j)),
            ],
        ),
        compiler_params=params(48),
        cost_estimate=pl.CostEstimate(flops=int(2e9), bytes_accessed=int(2e7), transcendentals=int(2e6)),
        name="attention_forward",
    )(flag, xt, w)


def attn_bwd_kernel(
    flag_ref, q_ref, k_ref, v_ref, e_ref, c_ref, inv_ref, dc_ref, x_ref, w_ref, dy_ref, vg_ref,
    g_ref, dw_ref, acc, dq, bacc, *, gw, hd, kc,
):
    nh = gw // hd
    j = pl.program_id(0)

    def run(span, step):
        for h in range(nh):
            r = slice(h * hd, (h + 1) * hd)
            dc = dc_ref[r, :].astype(F32)
            total = jnp.sum(dc * c_ref[r, :].astype(F32), axis=0, keepdims=True)
            inv = inv_ref[h : h + 1, :]
            dci = (dc * inv).astype(BF)
            ti = total * inv
            qs = q_ref[r, :] * jnp.asarray(hd**-0.5, BF)
            for s0 in range(0, LONG, span):
                ts = slice(s0, s0 + span)
                dcs = dci[:, ts]
                tis = ti[:, ts]
                qss = qs[:, ts]
                a = None
                for c0 in range(s0, s0 + span, step):
                    cs = slice(c0, c0 + step)
                    e = e_ref[h, 0, cs, ts]
                    dp = dg(v_ref[r, cs], dcs, 0, 0)
                    ds = (e.astype(F32) * (dp - tis)).astype(BF)
                    dq[2 * gw + h * hd : 2 * gw + (h + 1) * hd, cs] = dg(dcs, e, 1, 1)
                    dq[gw + h * hd : gw + (h + 1) * hd, cs] = dg(qss, ds, 1, 1)
                    t = dg(k_ref[r, cs], ds, 1, 0)
                    a = t if a is None else a + t
                dq[r, ts] = a * (hd**-0.5)

    @pl.when(flag_ref[0] == 1)
    def _():
        run(LONG, kc)

    @pl.when(flag_ref[0] != 1)
    def _():
        run(SHORT, SHORT)

    d = dq[...]
    dl = d.astype(BF)
    w = w_ref[...]
    g_ref[...] = (dy_ref[...] + dg(w[:, : 3 * gw], dl, 1, 0)).astype(BF)
    dw = dg(x_ref[...], dl, 1, 1)
    bq = lane_sum(d[:gw])
    bv = lane_sum(d[2 * gw :])

    @pl.when(j == 0)
    def _():
        acc[...] = dw
        bacc[0] = bq
        bacc[1] = bv

    @pl.when(j > 0)
    def _():
        acc[...] += dw
        bacc[0] += bq
        bacc[1] += bv

    @pl.when(j == pl.num_programs(0) - 1)
    def _():
        dw_ref[:, : 3 * gw] = acc[...].astype(BF)
        rest = dw_ref.shape[1] - 3 * gw
        bqc = jnp.sum(bacc[0], axis=1, keepdims=True)
        bvc = jnp.sum(bacc[1], axis=1, keepdims=True)
        lane = lax.broadcasted_iota(jnp.int32, (gw, rest), 1)
        t = jnp.where(lane == 0, bqc, jnp.where(lane == 1, bvc, vg_ref[:, :rest]))
        dw_ref[:, 3 * gw :] = t.astype(BF)


def attn_bwd(flag, saved, dct, xt, w, dyt, vg, g, gw, hd, kc=256):
    q, k, v, e, c, inv = saved
    width, toks = xt.shape
    blocks = toks // LONG
    nh = gw // hd
    cols = w.shape[1]
    own = lambda: pl.BlockSpec((gw, LONG), lambda j, f: (0, j))
    part = lambda: pl.BlockSpec((gw, LONG), lambda j, f: (g, j))
    return pl.pallas_call(
        functools.partial(attn_bwd_kernel, gw=gw, hd=hd, kc=kc),
        out_shape=[jax.ShapeDtypeStruct((gw, toks), BF), jax.ShapeDtypeStruct((gw, cols), BF)],
        grid_spec=pltpu.PrefetchScalarGridSpec(
            num_scalar_prefetch=1,
            grid=(blocks,),
            in_specs=[
                own(),
                own(),
                own(),
                pl.BlockSpec((nh, 1, LONG, LONG), lambda j, f: (0, j, 0, 0)),
                own(),
                pl.BlockSpec((8, LONG), lambda j, f: (0, j)),
                part(),
                part(),
                pl.BlockSpec((gw, cols), lambda j, f: (g, 0)),
                part(),
                pl.BlockSpec((gw, 128), lambda j, f: (g, 0)),
            ],
            out_specs=[own(), pl.BlockSpec((gw, cols), lambda j, f: (0, 0))],
            scratch_shapes=[
                pltpu.VMEM((gw, 3 * gw), F32),
                pltpu.VMEM((3 * gw, LONG), F32),
                pltpu.VMEM((2, gw, 128), F32),
            ],
        ),
        compiler_params=params(48),
        cost_estimate=pl.CostEstimate(flops=int(2e9), bytes_accessed=int(2e7), transcendentals=0),
        name="attention_backward",
    )(flag, q, k, v, e, c, inv, dct, xt, w, dyt, vg)


def ffn_kernel(
    me_ref, x_ref, c0_ref, c1_ref, c2_ref, c3_ref, vec_ref, wo_ref, wf_ref, cot_ref,
    out_ref, dy1_ref, dct_ref, keep_ref, send_ref, dwo_ref, vg_ref,
    ctx, n1, h1x, act, slope, y2, dyl, accw, acco, accv, *, gw, shards, vbase,
):
    j = pl.program_id(0)
    last = pl.num_programs(0) - 1
    groups = 4
    toks = x_ref.shape[1]
    width = groups * gw
    me = me_ref[0]
    inv_width = 1.0 / width

    def col(i):
        return vec_ref[:, vbase + i : vbase + i + 1].astype(F32)

    b_out, gain1, shift1, bias2, gain2, shift2 = [col(i) for i in range(2, 8)]

    def mean(v):
        return jnp.sum(v, axis=0, keepdims=True) * inv_width

    @pl.when(j == 0)
    def _():
        accw[...] = jnp.zeros_like(accw)
        acco[...] = jnp.zeros_like(acco)
        accv[...] = jnp.zeros_like(accv)

    for g, ref in enumerate((c0_ref, c1_ref, c2_ref, c3_ref)):
        ctx[g * gw : (g + 1) * gw, :] = ref[...]
    y1 = x_ref[...].astype(F32) + dg(wo_ref[...], ctx[...], 0, 0) + b_out
    center = y1 - mean(y1)
    rs1 = lax.rsqrt(mean(center * center) + EPS)
    norm1 = center * rs1
    n1[...] = norm1
    h1 = norm1 * gain1 + shift1
    y2[...] = (h1 + bias2).reshape(groups, gw, toks)
    h1x[:, :gw, :] = h1.astype(BF).reshape(groups, gw, toks)
    h1x[:, gw:, :] = jnp.ones((groups, PAD, toks), BF)

    def forward(i, carry):
        g = i // shards
        f = i % shards
        u = dg(wf_ref[f, g, :, :gw], h1x[g], 0, 0)
        a = jnp.abs(u)
        t = 1.0 / (1.0 + TAIL_P * a)
        ex = jnp.exp(u * u * -0.5)
        poly = TAIL[-1] * t + TAIL[-2]
        for c in TAIL[-3::-1]:
            poly = poly * t + c
        tail = poly * ex
        phi = jnp.where(u >= 0, 1.0 - tail, tail)
        low = (u * phi).astype(BF)
        act[g, f] = low
        slope[g, f] = phi + u * ex * 0.3989422804014327
        y2[g] += dg(wf_ref[f, g, :gw, gw : 2 * gw], low, 0, 0)
        return carry

    lax.fori_loop(0, groups * shards, forward, 0)

    yy = y2[...].reshape(width, toks)
    center = yy - mean(yy)
    rs2 = lax.rsqrt(mean(center * center) + EPS)
    norm2 = center * rs2
    out_ref[...] = (norm2 * gain2 + shift2).astype(BF)
    cot = cot_ref[...].astype(F32)
    e2 = cot * gain2
    dy2 = (e2 - mean(e2) - norm2 * mean(e2 * norm2)) * rs2
    accv[4] += lane_sum(cot * norm2)
    accv[5] += lane_sum(cot)
    accv[3] += lane_sum(dy2)
    y2[...] = dy2.reshape(groups, gw, toks)
    dyl[...] = dy2.astype(BF).reshape(groups, gw, toks)

    def backward(i, carry):
        g = i // shards
        s = i % shards
        f = s ^ me
        dact = dg(wf_ref[f, g, :gw, gw : 2 * gw], dyl[g], 1, 0)
        du = (dact * slope[g, f]).astype(BF)
        y2[g] += dg(wf_ref[f, g, :gw, :gw], du, 1, 0)
        accw[s, g, :, :gw] += dg(h1x[g], du, 1, 1)
        accw[s, g, :gw, gw : 2 * gw] += dg(act[g, f], dyl[g], 1, 1)
        return carry

    lax.fori_loop(0, groups * shards, backward, 0)

    dh1 = y2[...].reshape(width, toks)
    norm1 = n1[...]
    e1 = dh1 * gain1
    dy1 = (e1 - mean(e1) - norm1 * mean(e1 * norm1)) * rs1
    accv[1] += lane_sum(dh1 * norm1)
    accv[2] += lane_sum(dh1)
    accv[0] += lane_sum(dy1)
    dy1_ref[...] = dy1
    low1 = dy1.astype(BF)
    dct_ref[...] = dg(wo_ref[...], low1, 1, 0).astype(BF)
    acco[...] += dg(ctx[...], low1, 1, 1)

    @pl.when(j == last)
    def _():
        half = shards // 2
        for s in range(shards):
            (send_ref if s % 2 else keep_ref)[s // 2] = accw[s].astype(BF)
        dwo_ref[...] = acco[...].astype(BF)
        lane = lax.broadcasted_iota(jnp.int32, (width, 128), 1)
        t = jnp.zeros((width, 128), F32)
        for i in range(6):
            t = jnp.where(lane == i + 2, jnp.sum(accv[i], axis=1, keepdims=True), t)
        vg_ref[...] = t


def ffn_layer(me, xt, ctxs, w, wo, wf, cott, gw):
    width, toks = xt.shape
    blk = min(LONG, toks)
    shards = wf.shape[0]
    groups = wf.shape[1]
    vec_block = (3 * gw) // 128
    col_blk = lambda: pl.BlockSpec((width, blk), lambda j, m: (0, j))
    ctx_blk = lambda: pl.BlockSpec((gw, blk), lambda j, m: (0, j))
    whole = lambda shape: pl.BlockSpec(shape, lambda j, m: (0,) * len(shape), pipeline_mode=pl.Buffered(1))
    half = (shards // 2,) + wf.shape[1:]
    return pl.pallas_call(
        functools.partial(ffn_kernel, gw=gw, shards=shards, vbase=3 * gw - 128 * vec_block),
        out_shape=[
            jax.ShapeDtypeStruct((width, toks), BF),
            jax.ShapeDtypeStruct((width, toks), F32),
            jax.ShapeDtypeStruct((width, toks), BF),
            jax.ShapeDtypeStruct(half, BF),
            jax.ShapeDtypeStruct(half, BF),
            jax.ShapeDtypeStruct((width, width), BF),
            jax.ShapeDtypeStruct((width, 128), F32),
        ],
        grid_spec=pltpu.PrefetchScalarGridSpec(
            num_scalar_prefetch=1,
            grid=(toks // blk,),
            in_specs=[
                col_blk(),
                ctx_blk(),
                ctx_blk(),
                ctx_blk(),
                ctx_blk(),
                pl.BlockSpec((width, 128), lambda j, m: (0, vec_block)),
                whole((width, width)),
                whole(wf.shape),
                col_blk(),
            ],
            out_specs=[
                col_blk(),
                col_blk(),
                col_blk(),
                whole(half),
                whole(half),
                whole((width, width)),
                whole((width, 128)),
            ],
            scratch_shapes=[
                pltpu.VMEM((width, blk), BF),
                pltpu.VMEM((width, blk), F32),
                pltpu.VMEM((groups, gw + PAD, blk), BF),
                pltpu.VMEM((groups, shards, gw, blk), BF),
                pltpu.VMEM((groups, shards, gw, blk), F32),
                pltpu.VMEM((groups, gw, blk), F32),
                pltpu.VMEM((groups, gw, blk), BF),
                pltpu.VMEM(wf.shape, F32),
                pltpu.VMEM((width, width), F32),
                pltpu.VMEM((6, width, 128), F32),
            ],
        ),
        compiler_params=params(60),
        cost_estimate=pl.CostEstimate(flops=int(1.6e10), bytes_accessed=int(2e7), transcendentals=int(6e6)),
        name="token_local",
    )(me, xt, *ctxs, w, wo, wf, cott)


def swap(a, bit, count):
    return lax.ppermute(a, AXES, [(i, i ^ (1 << bit)) for i in range(count)])


def gather_bits(a, bits, index, count):
    cur = a[None]
    for b in sorted(bits, reverse=True):
        got = swap(cur, b, count)
        high = ((index >> b) & 1) == 1
        cur = jnp.stack([jnp.where(high, got, cur), jnp.where(high, cur, got)], axis=1)
        cur = cur.reshape((cur.shape[0] * 2,) + a.shape)
    return cur


def reduce_bits(a, bits, index, count):
    cur = a
    order = sorted(bits)
    for b in order:
        pair = cur.reshape((cur.shape[0] // 2, 2) + cur.shape[1:])
        mine = (index >> b) & 1
        send = lax.dynamic_index_in_dim(pair, 1 - mine, 1, keepdims=False)
        keep = lax.dynamic_index_in_dim(pair, mine, 1, keepdims=False)
        got = swap(send, b, count)
        cur = keep.astype(F32) + got.astype(F32)
        if b != order[-1]:
            cur = cur.astype(BF)
    return cur[0]


def log2(n):
    return n.bit_length() - 1


def body(
    dp, ffn, tokens, long_seq, cotangent, query_weight, key_weight, value_weight, out_weight,
    query_bias, value_bias, out_bias, attn_gain, attn_shift, ffn_in_weight, ffn_in_bias,
    ffn_out_weight, ffn_out_bias, ffn_gain, ffn_shift,
):
    count = dp * ffn
    index = lax.axis_index("dp") * ffn + lax.axis_index("ffn")
    ffn_bits = list(range(log2(ffn)))
    dp_bits = list(range(log2(ffn), log2(count)))
    all_bits = ffn_bits + dp_bits
    width = tokens.shape[1]
    groups = ffn_in_weight.shape[0]
    gw = width // groups
    hd = width // HEADS
    rows = query_weight.shape[0]

    vectors = [query_bias, value_bias, out_bias, attn_gain, attn_shift, ffn_out_bias, ffn_gain, ffn_shift]
    pack = jnp.concatenate([query_weight, key_weight, value_weight] + [v[:, None] for v in vectors], axis=1)
    cols = -(-pack.shape[1] // 128) * 128
    pack = jnp.pad(pack, ((0, 0), (0, cols - pack.shape[1])))
    w = gather_bits(pack, all_bits, index, count).reshape(width, cols)

    first = jnp.concatenate([ffn_in_weight, ffn_in_bias[:, None, :], jnp.zeros((groups, PAD - 1, gw), BF)], axis=1)
    second = jnp.pad(ffn_out_weight, ((0, 0), (0, PAD), (0, 0)))
    wf = gather_bits(jnp.concatenate([first, second], axis=2), ffn_bits, index, count)
    wo = gather_bits(out_weight, all_bits, index, count).reshape(width, width)

    xt = tokens.T
    cott = cotangent.T
    saved = [attn_fwd(long_seq, xt, w, g, gw, hd) for g in range(groups)]
    me = (index & (ffn - 1)).astype(jnp.int32)[None]
    outt, dyt, dct, keep, send, dwo, vg = ffn_layer(me, xt, [s[4] for s in saved], w, wo, wf, cott, gw)

    got = swap(send, 0, count)
    pair = keep.astype(F32) + got.astype(F32)
    mine = pair[0].astype(BF)
    for b in ffn_bits[1:]:
        got = swap(pair[1].astype(BF), b, count)
        mine = (pair[0] + got.astype(F32)).astype(BF)
    flat = mine.reshape(dp, -1, mine.shape[-1])
    part = reduce_bits(flat, dp_bits, index, count).astype(BF)
    ffn_sum = gather_bits(part, dp_bits, index, count).reshape(mine.shape).astype(F32)

    dwo_sum = reduce_bits(dwo.reshape(count, rows, width), all_bits, index, count)

    grads = [attn_bwd(long_seq, saved[g], dct, xt, w, dyt, vg, g, gw, hd) for g in range(groups)]
    gradt = jnp.concatenate([item[0] for item in grads], axis=0)
    dw = jnp.concatenate([item[1] for item in grads], axis=0)
    dw_sum = reduce_bits(dw.reshape(count, rows, cols), all_bits, index, count)
    vec = lambda i: dw_sum[:, 3 * gw + i]
    return (
        outt.T,
        gradt.T,
        dw_sum[:, :gw],
        dw_sum[:, gw : 2 * gw],
        dw_sum[:, 2 * gw : 3 * gw],
        dwo_sum,
        vec(0),
        vec(1),
        vec(2),
        vec(3),
        vec(4),
        ffn_sum[:, :gw, :gw],
        ffn_sum[:, gw, :gw],
        ffn_sum[:, :gw, gw:],
        vec(5),
        vec(6),
        vec(7),
    )


def solution(mesh):
    both = P(AXES)
    rows = P(AXES, None)
    return jax.shard_map(
        functools.partial(body, mesh.shape["dp"], mesh.shape["ffn"]),
        mesh=mesh,
        in_specs=(
            rows, both, rows, rows, rows, rows, rows, both, both, both, both, both,
            P(None, None, "ffn"), P(None, "ffn"), P(None, "ffn", None), both, both, both,
        ),
        out_specs=(
            rows, rows, rows, rows, rows, rows, both, both, both, both, both,
            P(None, None, "ffn"), P(None, "ffn"), P(None, "ffn", None), both, both, both,
        ),
        check_vma=False,
    )
```

```python
import functools

import jax
import jax.numpy as jnp
from jax import lax
from jax.experimental import pallas as pl
from jax.experimental.pallas import tpu as pltpu
from jax.sharding import PartitionSpec as P

F32 = jnp.float32
BF = jnp.bfloat16
HEADS = 12
LONG = 512
SHORT = 128
EPS = 1e-12
AXES = ("dp", "ffn")
PAD = 16

ROOT_HALF = 0.7071067811865476
INV_ROOT_2PI = 0.3989422804014327
HALF_LOG2E = -0.7213475204444817
SPLITS = ((0, 1), (1, 2), (3, 1))


def dg(a, b, ca, cb):
    return lax.dot_general(a, b, (((ca,), (cb,)), ((), ())), preferred_element_type=F32)


def lane_sum(v):
    out = v[:, :128]
    for c in range(128, v.shape[1], 128):
        out = out + v[:, c : c + 128]
    return out


def params():
    return pltpu.CompilerParams(vmem_limit_bytes=63 << 20)


def cost(us):
    return pl.CostEstimate(flops=int(us * 1e9), bytes_accessed=int(us * 3e6), transcendentals=0)


def attn_fwd_kernel(flag_ref, x_ref, w_ref, step_ref, last_ref, q_ref, k_ref, v_ref, e_ref, c_ref, inv_ref, *, gw, hd, qc):
    w = w_ref[...]
    p = dg(w[:, : 3 * gw], x_ref[...], 0, 0)
    bq = w[:, 3 * gw : 3 * gw + 1].astype(F32)
    bv = w[:, 3 * gw + 1 : 3 * gw + 2].astype(F32)
    q_ref[...] = (p[:gw] + bq).astype(BF)
    k_ref[...] = p[gw : 2 * gw].astype(BF)
    v_ref[...] = (p[2 * gw :] + bv).astype(BF)
    nh = gw // hd
    inv_ref[...] = jnp.zeros_like(inv_ref)

    def run(span, step):
        ones = jnp.ones((16, span), BF)
        for h in range(nh):
            r = slice(h * hd, (h + 1) * hd)
            for s0 in range(0, LONG, span):
                ks = slice(s0, s0 + span)
                k = k_ref[r, ks]
                vx = jnp.concatenate([v_ref[r, ks], ones], 0)
                for c0 in range(s0, s0 + span, step):
                    cs = slice(c0, c0 + step)
                    q = q_ref[r, cs] * jnp.asarray(hd**-0.5, BF)
                    s = dg(k, q, 0, 0)
                    m = jnp.max(s, axis=0, keepdims=True)
                    e = jnp.exp(s - m).astype(BF)
                    e_ref[h, 0, ks, cs] = e
                    o = dg(vx, e, 1, 0)
                    inv = 1.0 / o[hd : hd + 1]
                    c_ref[r, cs] = (o[:hd] * inv).astype(BF)
                    inv_ref[h : h + 1, cs] = inv

    @pl.when(flag_ref[0] == 1)
    def _():
        run(LONG, qc)

    @pl.when(flag_ref[0] != 1)
    def _():
        run(SHORT, SHORT)


def attn_fwd(flag, xt, w, step, last, g0, ng, gw, hd, qc=256):
    toks = xt.shape[1]
    blocks = toks // LONG
    nh = gw // hd
    own = lambda: pl.BlockSpec((gw, LONG), lambda g, j, f: (g, j))
    return pl.pallas_call(
        functools.partial(attn_fwd_kernel, gw=gw, hd=hd, qc=qc),
        out_shape=[jax.ShapeDtypeStruct((ng * gw, toks), BF)] * 3
        + [
            jax.ShapeDtypeStruct((ng * nh, blocks, LONG, LONG), BF),
            jax.ShapeDtypeStruct((ng * gw, toks), BF),
            jax.ShapeDtypeStruct((ng * 8, toks), F32),
        ],
        grid_spec=pltpu.PrefetchScalarGridSpec(
            num_scalar_prefetch=1,
            grid=(ng, blocks),
            in_specs=[
                pl.BlockSpec((gw, LONG), lambda g, j, f: (g0 + g, j)),
                pl.BlockSpec((gw, w.shape[1]), lambda g, j, f: (g0 + g, 0)),
                pl.BlockSpec(memory_space=pl.ANY),
                pl.BlockSpec(memory_space=pl.ANY),
            ],
            out_specs=[
                own(),
                own(),
                own(),
                pl.BlockSpec((nh, 1, LONG, LONG), lambda g, j, f: (g, j, 0, 0)),
                own(),
                pl.BlockSpec((8, LONG), lambda g, j, f: (g, j)),
            ],
        ),
        compiler_params=params(),
        cost_estimate=cost(7 * ng),
        name="attention_forward",
    )(flag, xt, w, step, last)


def attn_bwd_kernel(
    flag_ref, q_ref, k_ref, v_ref, e_ref, c_ref, inv_ref, dc_ref, x_ref, w_ref, dy_ref, vg_ref,
    step_ref, last_ref, g_ref, dw_ref, acc, dq, bacc, *, gw, hd, kc,
):
    nh = gw // hd
    j = pl.program_id(1)

    def run(span, step):
        for h in range(nh):
            r = slice(h * hd, (h + 1) * hd)
            dc = dc_ref[r, :].astype(F32)
            total = jnp.sum(dc * c_ref[r, :].astype(F32), axis=0, keepdims=True)
            inv = inv_ref[h : h + 1, :]
            dci = (dc * inv).astype(BF)
            ti = total * inv
            qs = q_ref[r, :] * jnp.asarray(hd**-0.5, BF)
            for s0 in range(0, LONG, span):
                ts = slice(s0, s0 + span)
                dcs = dci[:, ts]
                tis = ti[:, ts]
                qss = qs[:, ts]
                a = None
                for c0 in range(s0, s0 + span, step):
                    cs = slice(c0, c0 + step)
                    e = e_ref[h, 0, cs, ts]
                    dp = dg(v_ref[r, cs], dcs, 0, 0)
                    ds = (e.astype(F32) * (dp - tis)).astype(BF)
                    dq[2 * gw + h * hd : 2 * gw + (h + 1) * hd, cs] = dg(dcs, e, 1, 1)
                    dq[gw + h * hd : gw + (h + 1) * hd, cs] = dg(qss, ds, 1, 1)
                    t = dg(k_ref[r, cs], ds, 1, 0)
                    a = t if a is None else a + t
                dq[r, ts] = a * (hd**-0.5)

    @pl.when(flag_ref[0] == 1)
    def _():
        run(LONG, kc)

    @pl.when(flag_ref[0] != 1)
    def _():
        run(SHORT, SHORT)

    d = dq[...]
    dl = d.astype(BF)
    w = w_ref[...]
    g_ref[...] = (dy_ref[...] + dg(w[:, : 3 * gw], dl, 1, 0)).astype(BF)
    dw = dg(x_ref[...], dl, 1, 1)
    bq = lane_sum(d[:gw])
    bv = lane_sum(d[2 * gw :])

    @pl.when(j == 0)
    def _():
        acc[...] = dw
        bacc[0] = bq
        bacc[1] = bv

    @pl.when(j > 0)
    def _():
        acc[...] += dw
        bacc[0] += bq
        bacc[1] += bv

    @pl.when(j == pl.num_programs(1) - 1)
    def _():
        dw_ref[:, : 3 * gw] = acc[...].astype(BF)
        rest = dw_ref.shape[1] - 3 * gw
        bqc = jnp.sum(bacc[0], axis=1, keepdims=True)
        bvc = jnp.sum(bacc[1], axis=1, keepdims=True)
        lane = lax.broadcasted_iota(jnp.int32, (gw, rest), 1)
        t = jnp.where(lane == 0, bqc, jnp.where(lane == 1, bvc, vg_ref[:, :rest]))
        dw_ref[:, 3 * gw :] = t.astype(BF)


def attn_bwd(flag, saved, dct, xt, w, dyt, vg, step, last, g0, ng, gw, hd, kc=256):
    q, k, v, e, c, inv = saved
    toks = xt.shape[1]
    blocks = toks // LONG
    nh = gw // hd
    cols = w.shape[1]
    own = lambda: pl.BlockSpec((gw, LONG), lambda g, j, f: (g, j))
    part = lambda: pl.BlockSpec((gw, LONG), lambda g, j, f: (g0 + g, j))
    return pl.pallas_call(
        functools.partial(attn_bwd_kernel, gw=gw, hd=hd, kc=kc),
        out_shape=[jax.ShapeDtypeStruct((ng * gw, toks), BF), jax.ShapeDtypeStruct((ng * gw, cols), BF)],
        grid_spec=pltpu.PrefetchScalarGridSpec(
            num_scalar_prefetch=1,
            grid=(ng, blocks),
            in_specs=[
                own(),
                own(),
                own(),
                pl.BlockSpec((nh, 1, LONG, LONG), lambda g, j, f: (g, j, 0, 0)),
                own(),
                pl.BlockSpec((8, LONG), lambda g, j, f: (g, j)),
                part(),
                part(),
                pl.BlockSpec((gw, cols), lambda g, j, f: (g0 + g, 0)),
                part(),
                pl.BlockSpec((gw, 128), lambda g, j, f: (g0 + g, 0)),
                pl.BlockSpec(memory_space=pl.ANY),
                pl.BlockSpec(memory_space=pl.ANY),
            ],
            out_specs=[own(), pl.BlockSpec((gw, cols), lambda g, j, f: (g, 0))],
            scratch_shapes=[
                pltpu.VMEM((gw, 3 * gw), F32),
                pltpu.VMEM((3 * gw, LONG), F32),
                pltpu.VMEM((2, gw, 128), F32),
            ],
        ),
        compiler_params=params(),
        cost_estimate=cost(7 * ng),
        name="attention_backward",
    )(flag, q, k, v, e, c, inv, dct, xt, w, dyt, vg, step, last)


def fill_context(ctx, refs):
    row = 0
    for ref in refs:
        ctx[row : row + ref.shape[0], :] = ref[...]
        row += ref.shape[0]


def ffn_kernel(me_ref, x_ref, *refs, parts, gw, shards, vbase):
    ctx_refs = refs[:parts]
    vec_ref, wo_ref, wf_ref, cot_ref = refs[parts : parts + 4]
    out_ref, n1_ref, rs_ref, dh_ref, keep_ref, send_ref, vg_ref = refs[parts + 4 : parts + 11]
    ctx, h1x, act, slope, y2, dyl, accw, accv = refs[parts + 11 :]
    j = pl.program_id(0)
    last = pl.num_programs(0) - 1
    groups = h1x.shape[0]
    toks = x_ref.shape[1]
    width = groups * gw
    me = me_ref[0]
    inv_width = 1.0 / width

    def col(i):
        return vec_ref[:, vbase + i : vbase + i + 1].astype(F32)

    def mean(v):
        return jnp.sum(v, axis=0, keepdims=True) * inv_width

    @pl.when(j == 0)
    def _():
        accw[...] = jnp.zeros_like(accw)
        accv[...] = jnp.zeros_like(accv)

    fill_context(ctx, ctx_refs)
    y1 = x_ref[...].astype(F32) + dg(wo_ref[...], ctx[...], 0, 0) + col(2)
    center = y1 - mean(y1)
    rs1 = lax.rsqrt(mean(center * center) + EPS)
    rs_ref[...] = jnp.broadcast_to(rs1, rs_ref.shape)
    norm1 = center * rs1
    n1_ref[...] = norm1
    h1 = norm1 * col(3) + col(4)
    y2[...] = (h1 + col(5)).reshape(groups, gw, toks)
    h1x[:, :gw, :] = h1.astype(BF).reshape(groups, gw, toks)
    h1x[:, gw:, :] = jnp.ones((groups, PAD, toks), BF)

    def forward(i, carry):
        g = i // shards
        f = i % shards
        u = dg(wf_ref[f, g, :, :gw], h1x[g], 0, 0)
        phi = lax.erf(u * ROOT_HALF) * 0.5 + 0.5
        low = (u * phi).astype(BF)
        act[g, f] = low
        slope[g, f] = phi + u * INV_ROOT_2PI * jnp.exp2(u * u * HALF_LOG2E)
        y2[g] += dg(wf_ref[f, g, :gw, gw : 2 * gw], low, 0, 0)
        return carry

    lax.fori_loop(0, groups * shards, forward, 0)

    yy = y2[...].reshape(width, toks)
    center = yy - mean(yy)
    rs2 = lax.rsqrt(mean(center * center) + EPS)
    norm2 = center * rs2
    out_ref[...] = (norm2 * col(6) + col(7)).astype(BF)
    cot = cot_ref[...].astype(F32)
    e2 = cot * col(6)
    dy2 = (e2 - mean(e2) - norm2 * mean(e2 * norm2)) * rs2
    accv[0] += lane_sum(dy2)
    accv[1] += lane_sum(cot * norm2)
    accv[2] += lane_sum(cot)
    y2[...] = dy2.reshape(groups, gw, toks)
    dyl[...] = dy2.astype(BF).reshape(groups, gw, toks)

    def backward(i, carry):
        g = i // shards
        s = i % shards
        f = s ^ me
        dact = dg(wf_ref[f, g, :gw, gw : 2 * gw], dyl[g], 1, 0)
        du = (dact * slope[g, f]).astype(BF)
        y2[g] += dg(wf_ref[f, g, :gw, :gw], du, 1, 0)
        accw[s, g, :, :gw] += dg(h1x[g], du, 1, 1)
        accw[s, g, :gw, gw : 2 * gw] += dg(act[g, f], dyl[g], 1, 1)
        return carry

    lax.fori_loop(0, groups * shards, backward, 0)
    dh_ref[...] = y2[...].reshape(width, toks)

    @pl.when(j == last)
    def _():
        for s in range(shards):
            (send_ref if s % 2 else keep_ref)[s // 2] = accw[s].astype(BF)
        vg_ref[...] = spread(accv, 5)


def spread(sums, first):
    count, width, lanes = sums.shape
    lane = lax.broadcasted_iota(jnp.int32, (width, lanes), 1)
    t = jnp.zeros((width, lanes), F32)
    for i in range(count):
        t = jnp.where(lane == i + first, jnp.sum(sums[i], axis=1, keepdims=True), t)
    return t


def norm_kernel(*refs, parts, vbase):
    ctx_refs = refs[:parts]
    n1_ref, rs_ref, dh_ref, vec_ref, wo_ref, vga_ref = refs[parts : parts + 6]
    dy1_ref, dct_ref, dwo_ref, vg_ref = refs[parts + 6 : parts + 10]
    ctx, acco, accv = refs[parts + 10 :]
    j = pl.program_id(0)
    last = pl.num_programs(0) - 1
    inv_width = 1.0 / n1_ref.shape[0]

    def mean(v):
        return jnp.sum(v, axis=0, keepdims=True) * inv_width

    fill_context(ctx, ctx_refs)
    norm1 = n1_ref[...]
    dh1 = dh_ref[...]
    e1 = dh1 * vec_ref[:, vbase + 3 : vbase + 4].astype(F32)
    dy1 = (e1 - mean(e1) - norm1 * mean(e1 * norm1)) * rs_ref[0:1, :]
    dy1_ref[...] = dy1
    low1 = dy1.astype(BF)
    dct_ref[...] = dg(wo_ref[...], low1, 1, 0).astype(BF)
    sums = (lane_sum(dy1), lane_sum(dh1 * norm1), lane_sum(dh1))
    dwo = dg(ctx[...], low1, 1, 1)

    @pl.when(j == 0)
    def _():
        acco[...] = dwo
        for i in range(3):
            accv[i] = sums[i]

    @pl.when(j > 0)
    def _():
        acco[...] += dwo
        for i in range(3):
            accv[i] += sums[i]

    @pl.when(j == last)
    def _():
        dwo_ref[...] = acco[...].astype(BF)
        vg_ref[...] = vga_ref[...] + spread(accv, 2)


def whole(shape):
    return pl.BlockSpec(shape, lambda j, *m: (0,) * len(shape), pipeline_mode=pl.Buffered(1))


def ffn_layer(me, xt, ctxs, w, wo, wf, cott, gw):
    width, toks = xt.shape
    blk = min(LONG, toks)
    shards, groups = wf.shape[:2]
    vec_block = (3 * gw) // 128
    col_blk = lambda rows: pl.BlockSpec((rows, blk), lambda j, m: (0, j))
    half = (shards // 2,) + wf.shape[1:]
    return pl.pallas_call(
        functools.partial(ffn_kernel, parts=len(ctxs), gw=gw, shards=shards, vbase=3 * gw - 128 * vec_block),
        out_shape=[
            jax.ShapeDtypeStruct((width, toks), BF),
            jax.ShapeDtypeStruct((width, toks), F32),
            jax.ShapeDtypeStruct((8, toks), F32),
            jax.ShapeDtypeStruct((width, toks), F32),
            jax.ShapeDtypeStruct(half, BF),
            jax.ShapeDtypeStruct(half, BF),
            jax.ShapeDtypeStruct((width, 128), F32),
        ],
        grid_spec=pltpu.PrefetchScalarGridSpec(
            num_scalar_prefetch=1,
            grid=(toks // blk,),
            in_specs=[col_blk(width)]
            + [col_blk(c.shape[0]) for c in ctxs]
            + [
                pl.BlockSpec((width, 128), lambda j, m: (0, vec_block)),
                whole((width, width)),
                whole(wf.shape),
                col_blk(width),
            ],
            out_specs=[
                col_blk(width),
                col_blk(width),
                col_blk(8),
                col_blk(width),
                whole(half),
                whole(half),
                whole((width, 128)),
            ],
            scratch_shapes=[
                pltpu.VMEM((width, blk), BF),
                pltpu.VMEM((groups, gw + PAD, blk), BF),
                pltpu.VMEM((groups, shards, gw, blk), BF),
                pltpu.VMEM((groups, shards, gw, blk), F32),
                pltpu.VMEM((groups, gw, blk), F32),
                pltpu.VMEM((groups, gw, blk), BF),
                pltpu.VMEM(wf.shape, F32),
                pltpu.VMEM((3, width, 128), F32),
            ],
        ),
        compiler_params=params(),
        cost_estimate=cost(40),
        name="feed_forward",
    )(me, xt, *ctxs, w, wo, wf, cott)


def norm_layer(ctxs, n1, rs1, dh1, w, wo, vga, gw):
    width, toks = n1.shape
    blk = min(LONG, toks)
    vec_block = (3 * gw) // 128
    col_blk = lambda rows: pl.BlockSpec((rows, blk), lambda j: (0, j))
    return pl.pallas_call(
        functools.partial(norm_kernel, parts=len(ctxs), vbase=3 * gw - 128 * vec_block),
        out_shape=[
            jax.ShapeDtypeStruct((width, toks), F32),
            jax.ShapeDtypeStruct((width, toks), BF),
            jax.ShapeDtypeStruct((width, width), BF),
            jax.ShapeDtypeStruct((width, 128), F32),
        ],
        grid=(toks // blk,),
        in_specs=[col_blk(c.shape[0]) for c in ctxs]
        + [
            col_blk(width),
            col_blk(8),
            col_blk(width),
            pl.BlockSpec((width, 128), lambda j: (0, vec_block)),
            whole((width, width)),
            whole((width, 128)),
        ],
        out_specs=[col_blk(width), col_blk(width), whole((width, width)), whole((width, 128))],
        scratch_shapes=[
            pltpu.VMEM((width, blk), BF),
            pltpu.VMEM((width, width), F32),
            pltpu.VMEM((3, width, 128), F32),
        ],
        compiler_params=params(),
        cost_estimate=cost(7),
        name="norm_backward",
    )(*ctxs, n1, rs1, dh1, w, wo, vga)


def swap(a, bit, count):
    return lax.ppermute(a, AXES, [(i, i ^ (1 << bit)) for i in range(count)])


def gather_bit(cur, b, index, count):
    return merge(cur, swap(cur, b, count), b, index)


def merge(cur, got, b, index):
    high = ((index >> b) & 1) == 1
    new = jnp.stack([jnp.where(high, got, cur), jnp.where(high, cur, got)], axis=1)
    return new.reshape((cur.shape[0] * 2,) + cur.shape[1:])


def halves(cur, b, index):
    pair = cur.reshape((cur.shape[0] // 2, 2) + cur.shape[1:])
    mine = (index >> b) & 1
    keep = lax.dynamic_index_in_dim(pair, mine, 1, keepdims=False)
    return keep, lax.dynamic_index_in_dim(pair, 1 - mine, 1, keepdims=False)


def reduce_bit(cur, b, index, count):
    keep, send = halves(cur, b, index)
    return keep.astype(F32) + swap(send, b, count).astype(F32)


def log2(n):
    return n.bit_length() - 1


def body(
    dp, ffn, tokens, long_seq, cotangent, query_weight, key_weight, value_weight, out_weight,
    query_bias, value_bias, out_bias, attn_gain, attn_shift, ffn_in_weight, ffn_in_bias,
    ffn_out_weight, ffn_out_bias, ffn_gain, ffn_shift,
):
    count = dp * ffn
    index = lax.axis_index("dp") * ffn + lax.axis_index("ffn")
    ffn_bits = list(range(log2(ffn)))
    dp_bits = list(range(log2(ffn), log2(count)))
    all_bits = ffn_bits + dp_bits
    width = tokens.shape[1]
    groups = ffn_in_weight.shape[0]
    gw = width // groups
    hd = width // HEADS
    rows = query_weight.shape[0]

    vectors = [query_bias, value_bias, out_bias, attn_gain, attn_shift, ffn_out_bias, ffn_gain, ffn_shift]
    used = 3 * gw + len(vectors)
    cols = -(-used // 128) * 128
    columns = jnp.pad(jnp.stack(vectors), ((0, cols - used), (0, 0))).T
    w = jnp.concatenate([query_weight, key_weight, value_weight, columns], axis=1)[None]
    wo = out_weight[None]
    top = ffn_bits[-1]
    for b in reversed(dp_bits):
        w = gather_bit(w, b, index, count)
        wo = gather_bit(wo, b, index, count)
    w = gather_bit(w, top, index, count)
    first = jnp.concatenate([ffn_in_weight, ffn_in_bias[:, None, :], jnp.zeros((groups, PAD - 1, gw), BF)], axis=1)
    second = jnp.pad(ffn_out_weight, ((0, 0), (0, PAD), (0, 0)))
    wf = jnp.concatenate([first, second], axis=2)[None]
    w, wo, wf = lax.optimization_barrier((w, wo, wf))
    got_wo = swap(wo, top, count)
    got_wf = swap(wf, top, count)
    for b in reversed(ffn_bits[:-1]):
        w = gather_bit(w, b, index, count)
    w = w.reshape(width, cols)

    xt = tokens.T
    cott = cotangent.T
    saved = []
    step = last = xt
    for i, (g0, ng) in enumerate(SPLITS):
        out = list(attn_fwd(long_seq, xt, w, step, last, g0, ng, gw, hd))
        if i == 0:
            got_wo, out[4] = lax.optimization_barrier((got_wo, out[4]))
            step = wo = merge(wo, got_wo, top, index)
        if i == 1:
            got_wf, out[4] = lax.optimization_barrier((got_wf, out[4]))
            step = wf = merge(wf, got_wf, top, index)
        last = out[5]
        saved.append(out)
    for b in reversed(ffn_bits[:-1]):
        wo = gather_bit(wo, b, index, count)
        wf = gather_bit(wf, b, index, count)
    wo = wo.reshape(width, width)
    ctxs = [s[4] for s in saved]
    me = (index & (ffn - 1)).astype(jnp.int32)[None]
    outt, n1, rs1, dh1, keep, send, vga = ffn_layer(me, xt, ctxs, w, wo, wf, cott, gw)
    dyt, dct, dwo, vg = norm_layer(ctxs, n1, rs1, dh1, w, wo, vga, gw)

    pair = keep.astype(F32) + swap(send, 0, count).astype(F32)
    steps = []
    for b in ffn_bits[1:]:
        half = pair.shape[0] // 2
        send = pair[half:].astype(BF)
        steps.append(send)
        pair = pair[:half] + swap(send, b, count).astype(F32)
    mine = pair[0].astype(BF)
    keep_o, send_o = halves(dwo.reshape(count, rows, width), 0, index)
    got_o = swap(send_o, 0, count)

    grads = []
    step, last = steps[0], dct
    for i, (g0, ng) in enumerate(SPLITS):
        out = list(attn_bwd(long_seq, saved[i], dct, xt, w, dyt, vg, step, last, g0, ng, gw, hd))
        if i == 0:
            got_o, out[0] = lax.optimization_barrier((got_o, out[0]))
            step = dwo_sum = (keep_o.astype(F32) + got_o.astype(F32)).astype(BF)
        if i == 1:
            mine, dwo_sum, out[0] = lax.optimization_barrier((mine, dwo_sum, out[0]))
            step = mine
        last = out[1]
        grads.append(out)
    gradt = jnp.concatenate([item[0] for item in grads], axis=0)
    dw = jnp.concatenate([item[1] for item in grads], axis=0)

    ffn_sum = mine.reshape(dp, -1, mine.shape[-1])
    for b in dp_bits:
        ffn_sum = reduce_bit(ffn_sum, b, index, count).astype(BF)
    for b in reversed(dp_bits):
        ffn_sum = gather_bit(ffn_sum, b, index, count)
    ffn_sum = ffn_sum.reshape(mine.shape).astype(F32)

    for b in all_bits[1:]:
        dwo_sum = reduce_bit(dwo_sum, b, index, count)
        if b != all_bits[-1]:
            dwo_sum = dwo_sum.astype(BF)
    dwo_sum = dwo_sum[0]
    dw_sum = dw.reshape(count, rows, cols)
    for b in all_bits:
        dw_sum = reduce_bit(dw_sum, b, index, count)
        if b != all_bits[-1]:
            dw_sum = dw_sum.astype(BF)
    dw_sum = dw_sum[0]
    vec = lambda i: dw_sum[:, 3 * gw + i]
    return (
        outt.T,
        gradt.T,
        dw_sum[:, :gw],
        dw_sum[:, gw : 2 * gw],
        dw_sum[:, 2 * gw : 3 * gw],
        dwo_sum,
        vec(0),
        vec(1),
        vec(2),
        vec(3),
        vec(4),
        ffn_sum[:, :gw, :gw],
        ffn_sum[:, gw, :gw],
        ffn_sum[:, :gw, gw:],
        vec(5),
        vec(6),
        vec(7),
    )


def solution(mesh):
    both = P(AXES)
    rows = P(AXES, None)
    return jax.shard_map(
        functools.partial(body, mesh.shape["dp"], mesh.shape["ffn"]),
        mesh=mesh,
        in_specs=(
            rows, both, rows, rows, rows, rows, rows, both, both, both, both, both,
            P(None, None, "ffn"), P(None, "ffn"), P(None, "ffn", None), both, both, both,
        ),
        out_specs=(
            rows, rows, rows, rows, rows, rows, both, both, both, both, both,
            P(None, None, "ffn"), P(None, "ffn"), P(None, "ffn", None), both, both, both,
        ),
        check_vma=False,
    )
```

```python
import functools

import jax
import jax.numpy as jnp
from jax import lax
from jax.experimental import pallas as pl
from jax.experimental.pallas import tpu as pltpu
from jax.sharding import PartitionSpec as P

F32 = jnp.float32
BF = jnp.bfloat16
HEADS = 12
LONG = 512
SHORT = 128
EPS = 1e-12
AXES = ("dp", "ffn")
PAD = 16

ROOT_HALF = 0.7071067811865476
INV_ROOT_2PI = 0.3989422804014327
HALF_LOG2E = -0.7213475204444817
SPLITS = ((0, 1), (1, 2), (3, 1))


def dg(a, b, ca, cb):
    return lax.dot_general(a, b, (((ca,), (cb,)), ((), ())), preferred_element_type=F32)


def lane_sum(v):
    out = v[:, :128]
    for c in range(128, v.shape[1], 128):
        out = out + v[:, c : c + 128]
    return out


def params():
    return pltpu.CompilerParams(vmem_limit_bytes=63 << 20)


def cost(us):
    return pl.CostEstimate(flops=int(us * 1e9), bytes_accessed=int(us * 3e6), transcendentals=0)


def attn_fwd_kernel(flag_ref, x_ref, w_ref, step_ref, last_ref, q_ref, k_ref, v_ref, e_ref, c_ref, inv_ref, *, gw, hd, qc):
    w = w_ref[...]
    p = dg(w[:, : 3 * gw], x_ref[...], 0, 0)
    bq = w[:, 3 * gw : 3 * gw + 1].astype(F32)
    bv = w[:, 3 * gw + 1 : 3 * gw + 2].astype(F32)
    q_ref[...] = (p[:gw] + bq).astype(BF)
    k_ref[...] = p[gw : 2 * gw].astype(BF)
    v_ref[...] = (p[2 * gw :] + bv).astype(BF)
    nh = gw // hd
    inv_ref[...] = jnp.zeros_like(inv_ref)

    def run(span, step):
        ones = jnp.ones((16, span), BF)
        for h in range(nh):
            r = slice(h * hd, (h + 1) * hd)
            for s0 in range(0, LONG, span):
                ks = slice(s0, s0 + span)
                k = k_ref[r, ks]
                vx = jnp.concatenate([v_ref[r, ks], ones], 0)
                for c0 in range(s0, s0 + span, step):
                    cs = slice(c0, c0 + step)
                    q = q_ref[r, cs] * jnp.asarray(hd**-0.5, BF)
                    s = dg(k, q, 0, 0)
                    m = jnp.max(s, axis=0, keepdims=True)
                    e = jnp.exp(s - m).astype(BF)
                    e_ref[h, 0, ks, cs] = e
                    o = dg(vx, e, 1, 0)
                    inv = 1.0 / o[hd : hd + 1]
                    c_ref[r, cs] = (o[:hd] * inv).astype(BF)
                    inv_ref[h : h + 1, cs] = inv

    @pl.when(flag_ref[0] == 1)
    def _():
        run(LONG, qc)

    @pl.when(flag_ref[0] != 1)
    def _():
        run(SHORT, SHORT)


def attn_fwd(flag, xt, w, step, last, g0, ng, gw, hd, qc=256):
    toks = xt.shape[1]
    blocks = toks // LONG
    nh = gw // hd
    own = lambda: pl.BlockSpec((gw, LONG), lambda g, j, f: (g, j))
    return pl.pallas_call(
        functools.partial(attn_fwd_kernel, gw=gw, hd=hd, qc=qc),
        out_shape=[jax.ShapeDtypeStruct((ng * gw, toks), BF)] * 3
        + [
            jax.ShapeDtypeStruct((ng * nh, blocks, LONG, LONG), BF),
            jax.ShapeDtypeStruct((ng * gw, toks), BF),
            jax.ShapeDtypeStruct((ng * 8, toks), F32),
        ],
        grid_spec=pltpu.PrefetchScalarGridSpec(
            num_scalar_prefetch=1,
            grid=(ng, blocks),
            in_specs=[
                pl.BlockSpec((gw, LONG), lambda g, j, f: (g0 + g, j)),
                pl.BlockSpec((gw, w.shape[1]), lambda g, j, f: (g0 + g, 0)),
                pl.BlockSpec(memory_space=pl.ANY),
                pl.BlockSpec(memory_space=pl.ANY),
            ],
            out_specs=[
                own(),
                own(),
                own(),
                pl.BlockSpec((nh, 1, LONG, LONG), lambda g, j, f: (g, j, 0, 0)),
                own(),
                pl.BlockSpec((8, LONG), lambda g, j, f: (g, j)),
            ],
        ),
        compiler_params=params(),
        cost_estimate=cost(7 * ng),
        name="attention_forward",
    )(flag, xt, w, step, last)


def attn_bwd_kernel(
    flag_ref, q_ref, k_ref, v_ref, e_ref, c_ref, inv_ref, dc_ref, x_ref, w_ref, dy_ref, vg_ref,
    step_ref, last_ref, g_ref, dw_ref, acc, dq, bacc, *, gw, hd, kc,
):
    nh = gw // hd
    j = pl.program_id(1)

    def run(span, step):
        for h in range(nh):
            r = slice(h * hd, (h + 1) * hd)
            dc = dc_ref[r, :].astype(F32)
            total = jnp.sum(dc * c_ref[r, :].astype(F32), axis=0, keepdims=True)
            inv = inv_ref[h : h + 1, :]
            dci = (dc * inv).astype(BF)
            ti = total * inv
            qs = q_ref[r, :] * jnp.asarray(hd**-0.5, BF)
            for s0 in range(0, LONG, span):
                ts = slice(s0, s0 + span)
                dcs = dci[:, ts]
                tis = ti[:, ts]
                qss = qs[:, ts]
                a = None
                for c0 in range(s0, s0 + span, step):
                    cs = slice(c0, c0 + step)
                    e = e_ref[h, 0, cs, ts]
                    dp = dg(v_ref[r, cs], dcs, 0, 0)
                    ds = (e.astype(F32) * (dp - tis)).astype(BF)
                    dq[2 * gw + h * hd : 2 * gw + (h + 1) * hd, cs] = dg(dcs, e, 1, 1)
                    dq[gw + h * hd : gw + (h + 1) * hd, cs] = dg(qss, ds, 1, 1)
                    t = dg(k_ref[r, cs], ds, 1, 0)
                    a = t if a is None else a + t
                dq[r, ts] = a * (hd**-0.5)

    @pl.when(flag_ref[0] == 1)
    def _():
        run(LONG, kc)

    @pl.when(flag_ref[0] != 1)
    def _():
        run(SHORT, SHORT)

    d = dq[...]
    dl = d.astype(BF)
    w = w_ref[...]
    g_ref[...] = (dy_ref[...] + dg(w[:, : 3 * gw], dl, 1, 0)).astype(BF)
    dw = dg(x_ref[...], dl, 1, 1)
    bq = lane_sum(d[:gw])
    bv = lane_sum(d[2 * gw :])

    @pl.when(j == 0)
    def _():
        acc[...] = dw
        bacc[0] = bq
        bacc[1] = bv

    @pl.when(j > 0)
    def _():
        acc[...] += dw
        bacc[0] += bq
        bacc[1] += bv

    @pl.when(j == pl.num_programs(1) - 1)
    def _():
        dw_ref[:, : 3 * gw] = acc[...].astype(BF)
        rest = dw_ref.shape[1] - 3 * gw
        bqc = jnp.sum(bacc[0], axis=1, keepdims=True)
        bvc = jnp.sum(bacc[1], axis=1, keepdims=True)
        lane = lax.broadcasted_iota(jnp.int32, (gw, rest), 1)
        t = jnp.where(lane == 0, bqc, jnp.where(lane == 1, bvc, vg_ref[:, :rest]))
        dw_ref[:, 3 * gw :] = t.astype(BF)


def attn_bwd(flag, saved, dct, xt, w, dyt, vg, step, last, g0, ng, gw, hd, kc=256):
    q, k, v, e, c, inv = saved
    toks = xt.shape[1]
    blocks = toks // LONG
    nh = gw // hd
    cols = w.shape[1]
    own = lambda: pl.BlockSpec((gw, LONG), lambda g, j, f: (g, j))
    part = lambda: pl.BlockSpec((gw, LONG), lambda g, j, f: (g0 + g, j))
    return pl.pallas_call(
        functools.partial(attn_bwd_kernel, gw=gw, hd=hd, kc=kc),
        out_shape=[jax.ShapeDtypeStruct((ng * gw, toks), BF), jax.ShapeDtypeStruct((ng * gw, cols), BF)],
        grid_spec=pltpu.PrefetchScalarGridSpec(
            num_scalar_prefetch=1,
            grid=(ng, blocks),
            in_specs=[
                own(),
                own(),
                own(),
                pl.BlockSpec((nh, 1, LONG, LONG), lambda g, j, f: (g, j, 0, 0)),
                own(),
                pl.BlockSpec((8, LONG), lambda g, j, f: (g, j)),
                part(),
                part(),
                pl.BlockSpec((gw, cols), lambda g, j, f: (g0 + g, 0)),
                part(),
                pl.BlockSpec((gw, 128), lambda g, j, f: (g0 + g, 0)),
                pl.BlockSpec(memory_space=pl.ANY),
                pl.BlockSpec(memory_space=pl.ANY),
            ],
            out_specs=[own(), pl.BlockSpec((gw, cols), lambda g, j, f: (g, 0))],
            scratch_shapes=[
                pltpu.VMEM((gw, 3 * gw), F32),
                pltpu.VMEM((3 * gw, LONG), F32),
                pltpu.VMEM((2, gw, 128), F32),
            ],
        ),
        compiler_params=params(),
        cost_estimate=cost(7 * ng),
        name="attention_backward",
    )(flag, q, k, v, e, c, inv, dct, xt, w, dyt, vg, step, last)


def fill_context(ctx, refs):
    row = 0
    for ref in refs:
        ctx[row : row + ref.shape[0], :] = ref[...]
        row += ref.shape[0]


def ffn_kernel(x_ref, *refs, parts, shards, gw, vbase):
    ctx_refs = refs[:parts]
    vec_ref, wo_ref = refs[parts : parts + 2]
    wf_refs = refs[parts + 2 : parts + 2 + shards]
    cot_ref = refs[parts + 2 + shards]
    rest = refs[parts + 3 + shards :]
    out_ref, n1_ref, rs_ref, dh_ref = rest[:4]
    grad_refs = rest[4 : 4 + shards]
    vg_ref = rest[4 + shards]
    ctx, wf, h1x, h1t, act, slope, y2, dyl, dyt, acc1, acc2, accb, accv = rest[5 + shards :]
    j = pl.program_id(0)
    last = pl.num_programs(0) - 1
    groups = h1x.shape[0]
    toks = x_ref.shape[1]
    width = groups * gw
    inv_width = 1.0 / width

    def col(i):
        return vec_ref[:, vbase + i : vbase + i + 1].astype(F32)

    def mean(v):
        return jnp.sum(v, axis=0, keepdims=True) * inv_width

    @pl.when(j == 0)
    def _():
        for s in range(shards):
            wf[s] = wf_refs[s][...]
        acc1[...] = jnp.zeros_like(acc1)
        acc2[...] = jnp.zeros_like(acc2)
        accb[...] = jnp.zeros_like(accb)
        accv[...] = jnp.zeros_like(accv)

    fill_context(ctx, ctx_refs)
    y1 = x_ref[...].astype(F32) + dg(wo_ref[...], ctx[...], 0, 0) + col(2)
    center = y1 - mean(y1)
    rs1 = lax.rsqrt(mean(center * center) + EPS)
    rs_ref[...] = jnp.broadcast_to(rs1, rs_ref.shape)
    norm1 = center * rs1
    n1_ref[...] = norm1
    h1 = norm1 * col(3) + col(4)
    y2[...] = (h1 + col(5)).reshape(groups, gw, toks)
    h1x[:, :gw, :] = h1.astype(BF).reshape(groups, gw, toks)
    h1x[:, gw:, :] = jnp.ones((groups, PAD, toks), BF)
    for g in range(groups):
        h1t[g] = h1x[g, :gw, :].T

    def forward(i, carry):
        g = i // shards
        s = i % shards
        u = dg(wf[s, g, :, :gw], h1x[g], 0, 0)
        phi = lax.erf(u * ROOT_HALF) * 0.5 + 0.5
        low = (u * phi).astype(BF)
        act[g, s] = low
        slope[g, s] = phi + u * INV_ROOT_2PI * jnp.exp2(u * u * HALF_LOG2E)
        y2[g] += dg(wf[s, g, :gw, gw : 2 * gw], low, 0, 0)
        return carry

    lax.fori_loop(0, groups * shards, forward, 0, unroll=2)

    yy = y2[...].reshape(width, toks)
    center = yy - mean(yy)
    rs2 = lax.rsqrt(mean(center * center) + EPS)
    norm2 = center * rs2
    out_ref[...] = (norm2 * col(6) + col(7)).astype(BF)
    cot = cot_ref[...].astype(F32)
    e2 = cot * col(6)
    dy2 = (e2 - mean(e2) - norm2 * mean(e2 * norm2)) * rs2
    accv[0] += lane_sum(dy2)
    accv[1] += lane_sum(cot * norm2)
    accv[2] += lane_sum(cot)
    y2[...] = dy2.reshape(groups, gw, toks)
    dyl[...] = dy2.astype(BF).reshape(groups, gw, toks)
    for g in range(groups):
        dyt[g] = dyl[g].T

    def backward(i, carry):
        g = i // shards
        s = i % shards
        dact = dg(wf[s, g, :gw, gw : 2 * gw], dyl[g], 1, 0)
        du = dact * slope[g, s]
        low = du.astype(BF)
        acc2[s, g] += dg(act[g, s], dyt[g], 1, 0)
        y2[g] += dg(wf[s, g, :gw, :gw], low, 1, 0)
        acc1[s, g] += dg(low, h1t[g], 1, 0)
        accb[s, g] += lane_sum(du)
        return carry

    lax.fori_loop(0, groups * shards, backward, 0, unroll=2)
    dh_ref[...] = y2[...].reshape(width, toks)

    @pl.when(j == last)
    def _():
        for s in range(shards):

            def write(g, carry, s=s):
                grad_refs[s][g, :gw, :gw] = acc1[s, g].T.astype(BF)
                grad_refs[s][g, :gw, gw : 2 * gw] = acc2[s, g].astype(BF)
                row = jnp.sum(accb[s, g].T, axis=0, keepdims=True)
                tail = jnp.concatenate([row, jnp.zeros_like(row)], axis=1)
                grad_refs[s][g, gw:, :] = jnp.broadcast_to(tail, (PAD, 2 * gw)).astype(BF)
                return carry

            lax.fori_loop(0, groups, write, 0)
        vg_ref[...] = spread(accv, 5)


def spread(sums, first):
    count, width, lanes = sums.shape
    lane = lax.broadcasted_iota(jnp.int32, (width, lanes), 1)
    t = jnp.zeros((width, lanes), F32)
    for i in range(count):
        t = jnp.where(lane == i + first, jnp.sum(sums[i], axis=1, keepdims=True), t)
    return t


def norm_kernel(*refs, parts, vbase):
    ctx_refs = refs[:parts]
    n1_ref, rs_ref, dh_ref, vec_ref, wo_ref, vga_ref = refs[parts : parts + 6]
    dy1_ref, dct_ref, dwo_ref, vg_ref = refs[parts + 6 : parts + 10]
    ctx, acco, accv = refs[parts + 10 :]
    j = pl.program_id(0)
    last = pl.num_programs(0) - 1
    inv_width = 1.0 / n1_ref.shape[0]

    def mean(v):
        return jnp.sum(v, axis=0, keepdims=True) * inv_width

    fill_context(ctx, ctx_refs)
    norm1 = n1_ref[...]
    dh1 = dh_ref[...]
    e1 = dh1 * vec_ref[:, vbase + 3 : vbase + 4].astype(F32)
    dy1 = (e1 - mean(e1) - norm1 * mean(e1 * norm1)) * rs_ref[0:1, :]
    dy1_ref[...] = dy1
    low1 = dy1.astype(BF)
    dct_ref[...] = dg(wo_ref[...], low1, 1, 0).astype(BF)
    sums = (lane_sum(dy1), lane_sum(dh1 * norm1), lane_sum(dh1))
    dwo = dg(ctx[...], low1, 1, 1)

    @pl.when(j == 0)
    def _():
        acco[...] = dwo
        for i in range(3):
            accv[i] = sums[i]

    @pl.when(j > 0)
    def _():
        acco[...] += dwo
        for i in range(3):
            accv[i] += sums[i]

    @pl.when(j == last)
    def _():
        dwo_ref[...] = acco[...].astype(BF)
        vg_ref[...] = vga_ref[...] + spread(accv, 2)


def whole(shape):
    return pl.BlockSpec(shape, lambda j, *m: (0,) * len(shape), pipeline_mode=pl.Buffered(1))


def ffn_layer(xt, ctxs, w, wo, wfs, cott, gw):
    width, toks = xt.shape
    blk = min(LONG, toks)
    shards = len(wfs)
    groups = wfs[0].shape[0]
    vec_block = (3 * gw) // 128
    col_blk = lambda rows: pl.BlockSpec((rows, blk), lambda j: (0, j))
    return pl.pallas_call(
        functools.partial(ffn_kernel, parts=len(ctxs), shards=shards, gw=gw, vbase=3 * gw - 128 * vec_block),
        out_shape=[
            jax.ShapeDtypeStruct((width, toks), BF),
            jax.ShapeDtypeStruct((width, toks), F32),
            jax.ShapeDtypeStruct((8, toks), F32),
            jax.ShapeDtypeStruct((width, toks), F32),
        ]
        + [jax.ShapeDtypeStruct(wfs[0].shape, BF)] * shards
        + [jax.ShapeDtypeStruct((width, 128), F32)],
        grid=(toks // blk,),
        in_specs=[col_blk(width)]
        + [col_blk(c.shape[0]) for c in ctxs]
        + [pl.BlockSpec((width, 128), lambda j: (0, vec_block)), whole((width, width))]
        + [whole(wfs[0].shape) for _ in wfs]
        + [col_blk(width)],
        out_specs=[col_blk(width), col_blk(width), col_blk(8), col_blk(width)]
        + [whole(wfs[0].shape) for _ in wfs]
        + [whole((width, 128))],
        scratch_shapes=[
            pltpu.VMEM((width, blk), BF),
            pltpu.VMEM((shards,) + wfs[0].shape, BF),
            pltpu.VMEM((groups, gw + PAD, blk), BF),
            pltpu.VMEM((groups, blk, gw), BF),
            pltpu.VMEM((groups, shards, gw, blk), BF),
            pltpu.VMEM((groups, shards, gw, blk), F32),
            pltpu.VMEM((groups, gw, blk), F32),
            pltpu.VMEM((groups, gw, blk), BF),
            pltpu.VMEM((groups, blk, gw), BF),
            pltpu.VMEM((shards, groups, gw, gw), F32),
            pltpu.VMEM((shards, groups, gw, gw), F32),
            pltpu.VMEM((shards, groups, gw, 128), F32),
            pltpu.VMEM((3, width, 128), F32),
        ],
        compiler_params=params(),
        cost_estimate=cost(40),
        name="feed_forward",
    )(xt, *ctxs, w, wo, *wfs, cott)


def norm_layer(ctxs, n1, rs1, dh1, w, wo, vga, gw):
    width, toks = n1.shape
    blk = min(LONG, toks)
    vec_block = (3 * gw) // 128
    col_blk = lambda rows: pl.BlockSpec((rows, blk), lambda j: (0, j))
    return pl.pallas_call(
        functools.partial(norm_kernel, parts=len(ctxs), vbase=3 * gw - 128 * vec_block),
        out_shape=[
            jax.ShapeDtypeStruct((width, toks), F32),
            jax.ShapeDtypeStruct((width, toks), BF),
            jax.ShapeDtypeStruct((width, width), BF),
            jax.ShapeDtypeStruct((width, 128), F32),
        ],
        grid=(toks // blk,),
        in_specs=[col_blk(c.shape[0]) for c in ctxs]
        + [
            col_blk(width),
            col_blk(8),
            col_blk(width),
            pl.BlockSpec((width, 128), lambda j: (0, vec_block)),
            whole((width, width)),
            whole((width, 128)),
        ],
        out_specs=[col_blk(width), col_blk(width), whole((width, width)), whole((width, 128))],
        scratch_shapes=[
            pltpu.VMEM((width, blk), BF),
            pltpu.VMEM((width, width), F32),
            pltpu.VMEM((3, width, 128), F32),
        ],
        compiler_params=params(),
        cost_estimate=cost(7),
        name="norm_backward",
    )(*ctxs, n1, rs1, dh1, w, wo, vga)


def swap(a, bit, count):
    return lax.ppermute(a, AXES, [(i, i ^ (1 << bit)) for i in range(count)])


def gather_bit(cur, b, index, count):
    return merge(cur, swap(cur, b, count), b, index)


def merge(cur, got, b, index):
    place = lax.broadcasted_iota(jnp.int32, (1, 2) + (1,) * (cur.ndim - 1), 1)
    new = jnp.where(place == ((index >> b) & 1), cur[:, None], got[:, None])
    return new.reshape((cur.shape[0] * 2,) + cur.shape[1:])


def halves(cur, b, index):
    pair = cur.reshape((cur.shape[0] // 2, 2) + cur.shape[1:])
    mine = (index >> b) & 1
    keep = lax.dynamic_index_in_dim(pair, mine, 1, keepdims=False)
    return keep, lax.dynamic_index_in_dim(pair, 1 - mine, 1, keepdims=False)


def reduce_bit(cur, b, index, count):
    keep, send = halves(cur, b, index)
    return keep.astype(F32) + swap(send, b, count).astype(F32)


def log2(n):
    return n.bit_length() - 1


def body(
    dp, ffn, tokens, long_seq, cotangent, query_weight, key_weight, value_weight, out_weight,
    query_bias, value_bias, out_bias, attn_gain, attn_shift, ffn_in_weight, ffn_in_bias,
    ffn_out_weight, ffn_out_bias, ffn_gain, ffn_shift,
):
    count = dp * ffn
    index = lax.axis_index("dp") * ffn + lax.axis_index("ffn")
    ffn_bits = list(range(log2(ffn)))
    dp_bits = list(range(log2(ffn), log2(count)))
    all_bits = ffn_bits + dp_bits
    width = tokens.shape[1]
    groups = ffn_in_weight.shape[0]
    gw = width // groups
    hd = width // HEADS
    rows = query_weight.shape[0]

    vectors = [query_bias, value_bias, out_bias, attn_gain, attn_shift, ffn_out_bias, ffn_gain, ffn_shift]
    used = 3 * gw + len(vectors)
    cols = -(-used // 128) * 128
    columns = jnp.pad(jnp.stack(vectors), ((0, cols - used), (0, 0))).T
    w = jnp.concatenate([query_weight, key_weight, value_weight, columns], axis=1)[None]
    wo = out_weight[None]
    top = ffn_bits[-1]
    first = jnp.concatenate([ffn_in_weight, ffn_in_bias[:, None, :], jnp.zeros((groups, PAD - 1, gw), BF)], axis=1)
    second = jnp.pad(ffn_out_weight, ((0, 0), (0, PAD), (0, 0)))
    wf = jnp.concatenate([first, second], axis=2)
    xt = tokens.T
    cott = cotangent.T
    for n, b in enumerate(reversed(dp_bits)):
        w = gather_bit(w, b, index, count)
        wo = gather_bit(wo, b, index, count)
        if n == 0:
            w, xt = lax.optimization_barrier((w, xt))
        if n == 1:
            w, cott = lax.optimization_barrier((w, cott))
    w = gather_bit(w, top, index, count)
    w, wo = lax.optimization_barrier((w, wo))
    got_wo = swap(wo, top, count)
    for b in reversed(ffn_bits[:-1]):
        w = gather_bit(w, b, index, count)
    w, wf = lax.optimization_barrier((w, wf))
    w = w.reshape(width, cols)
    got_wf = swap(wf, top, count)
    slots = {0: wf}
    for b in ffn_bits[:-1]:
        slots[1 << b] = swap(wf, b, count)

    saved = []
    step = last = xt
    for i, (g0, ng) in enumerate(SPLITS):
        out = list(attn_fwd(long_seq, xt, w, step, last, g0, ng, gw, hd))
        if i == 0:
            got_wo, out[4] = lax.optimization_barrier((got_wo, out[4]))
            step = wo = merge(wo, got_wo, top, index)
        if i == 1:
            got_wf, out[4] = lax.optimization_barrier((got_wf, out[4]))
            step = got_wf
        last = out[5]
        saved.append(out)
    slots[1 << top] = got_wf
    for b in reversed(ffn_bits[:-1]):
        wo = gather_bit(wo, b, index, count)
        slots[(1 << top) + (1 << b)] = swap(got_wf, b, count)
    wo = wo.reshape(width, width)
    ctxs = [s[4] for s in saved]
    wfs = [slots[s] for s in range(ffn)]
    outs = ffn_layer(xt, ctxs, w, wo, wfs, cott, gw)
    outt, n1, rs1, dh1 = outs[:4]
    gf = outs[4 : 4 + ffn]
    dyt, dct, dwo, vg = norm_layer(ctxs, n1, rs1, dh1, w, wo, outs[4 + ffn], gw)

    got1 = swap(gf[1], 0, count)
    got3 = swap(gf[3], 0, count)
    send = (gf[2].astype(F32) + got3.astype(F32)).astype(BF)
    got2 = swap(send, top, count)
    keep_o, send_o = halves(dwo.reshape(count, rows, width), 0, index)
    got_o = swap(send_o, 0, count)

    grads = []
    step, last = send, dct
    for i, (g0, ng) in enumerate(SPLITS):
        out = list(attn_bwd(long_seq, saved[i], dct, xt, w, dyt, vg, step, last, g0, ng, gw, hd))
        if i == 0:
            got_o, out[0] = lax.optimization_barrier((got_o, out[0]))
            step = dwo_sum = (keep_o.astype(F32) + got_o.astype(F32)).astype(BF)
        if i == 1:
            got2, dwo_sum, out[0] = lax.optimization_barrier((got2, dwo_sum, out[0]))
            mine = (gf[0].astype(F32) + got1.astype(F32) + got2.astype(F32)).astype(BF)
            keep_f, step = halves(mine.reshape(dp, -1, mine.shape[-1]), dp_bits[0], index)
            got_f = swap(step, dp_bits[0], count)
            keep_o, send_o = halves(dwo_sum, top, index)
            got_o = swap(send_o, top, count)
        if i == 2:
            got_f, got_o, out[1] = lax.optimization_barrier((got_f, got_o, out[1]))
        last = out[1]
        grads.append(out)
    dw = jnp.concatenate([item[1] for item in grads], axis=0)
    dw_sum = reduce_bit(dw.reshape(count, rows, cols), 0, index, count).astype(BF)
    dw_sum, outt, gradts = lax.optimization_barrier((dw_sum, outt, [item[0] for item in grads]))
    gradt = jnp.concatenate(gradts, axis=0)
    ffn_sum = (keep_f.astype(F32) + got_f.astype(F32)).astype(BF)
    for b in dp_bits[1:]:
        ffn_sum = reduce_bit(ffn_sum, b, index, count).astype(BF)
    for b in reversed(dp_bits):
        ffn_sum = gather_bit(ffn_sum, b, index, count)
    ffn_sum = ffn_sum.reshape(mine.shape).astype(F32)

    dw_sum = reduce_bit(dw_sum, top, index, count).astype(BF)
    dwo_sum = (keep_o.astype(F32) + got_o.astype(F32)).astype(BF)
    both = jnp.concatenate([dw_sum, dwo_sum], axis=2)
    for b in dp_bits:
        both = reduce_bit(both, b, index, count)
        if b != dp_bits[-1]:
            both = both.astype(BF)
    dw_sum = both[0, :, :cols]
    dwo_sum = both[0, :, cols:]
    vec = lambda i: dw_sum[:, 3 * gw + i]
    return (
        outt.T,
        gradt.T,
        dw_sum[:, :gw],
        dw_sum[:, gw : 2 * gw],
        dw_sum[:, 2 * gw : 3 * gw],
        dwo_sum,
        vec(0),
        vec(1),
        vec(2),
        vec(3),
        vec(4),
        ffn_sum[:, :gw, :gw],
        ffn_sum[:, gw, :gw],
        ffn_sum[:, :gw, gw:],
        vec(5),
        vec(6),
        vec(7),
    )


def solution(mesh):
    both = P(AXES)
    rows = P(AXES, None)
    return jax.shard_map(
        functools.partial(body, mesh.shape["dp"], mesh.shape["ffn"]),
        mesh=mesh,
        in_specs=(
            rows, both, rows, rows, rows, rows, rows, both, both, both, both, both,
            P(None, None, "ffn"), P(None, "ffn"), P(None, "ffn", None), both, both, both,
        ),
        out_specs=(
            rows, rows, rows, rows, rows, rows, both, both, both, both, both,
            P(None, None, "ffn"), P(None, "ffn"), P(None, "ffn", None), both, both, both,
        ),
        check_vma=False,
    )
```

```python
import functools

import jax
import jax.numpy as jnp
from jax import lax
from jax.experimental import pallas as pl
from jax.experimental.pallas import tpu as pltpu
from jax.sharding import PartitionSpec as P

F32 = jnp.float32
BF = jnp.bfloat16
HEADS = 12
LONG = 512
SHORT = 128
EPS = 1e-12
AXES = ("dp", "ffn")
PAD = 16

ROOT_HALF = 0.7071067811865476
INV_ROOT_2PI = 0.3989422804014327
HALF_LOG2E = -0.7213475204444817
SPLITS = ((0, 1), (1, 2), (3, 1))


def dg(a, b, ca, cb):
    return lax.dot_general(a, b, (((ca,), (cb,)), ((), ())), preferred_element_type=F32)


def lane_sum(v):
    out = v[:, :128]
    for c in range(128, v.shape[1], 128):
        out = out + v[:, c : c + 128]
    return out


def params():
    return pltpu.CompilerParams(vmem_limit_bytes=63 << 20)


def cost(us):
    return pl.CostEstimate(flops=int(us * 1e9), bytes_accessed=int(us * 3e6), transcendentals=0)


def attn_fwd_kernel(flag_ref, x_ref, w_ref, step_ref, last_ref, q_ref, k_ref, v_ref, e_ref, c_ref, inv_ref, *, gw, hd, qc):
    w = w_ref[...]
    p = dg(w[:, : 3 * gw], x_ref[...], 0, 0)
    bq = w[:, 3 * gw : 3 * gw + 1].astype(F32)
    bv = w[:, 3 * gw + 1 : 3 * gw + 2].astype(F32)
    q_ref[...] = (p[:gw] + bq).astype(BF)
    k_ref[...] = p[gw : 2 * gw].astype(BF)
    v_ref[...] = (p[2 * gw :] + bv).astype(BF)
    nh = gw // hd
    inv_ref[...] = jnp.zeros_like(inv_ref)

    def run(span, step):
        ones = jnp.ones((16, span), BF)
        for h in range(nh):
            r = slice(h * hd, (h + 1) * hd)
            for s0 in range(0, LONG, span):
                ks = slice(s0, s0 + span)
                k = k_ref[r, ks]
                vx = jnp.concatenate([v_ref[r, ks], ones], 0)
                for c0 in range(s0, s0 + span, step):
                    cs = slice(c0, c0 + step)
                    q = q_ref[r, cs] * jnp.asarray(hd**-0.5, BF)
                    s = dg(k, q, 0, 0)
                    m = jnp.max(s, axis=0, keepdims=True)
                    e = jnp.exp(s - m).astype(BF)
                    e_ref[h, 0, ks, cs] = e
                    o = dg(vx, e, 1, 0)
                    inv = 1.0 / o[hd : hd + 1]
                    c_ref[r, cs] = (o[:hd] * inv).astype(BF)
                    inv_ref[h : h + 1, cs] = inv

    @pl.when(flag_ref[0] == 1)
    def _():
        run(LONG, qc)

    @pl.when(flag_ref[0] != 1)
    def _():
        run(SHORT, SHORT)


def attn_fwd(flag, xt, w, step, last, g0, ng, gw, hd, qc=256):
    toks = xt.shape[1]
    blocks = toks // LONG
    nh = gw // hd
    own = lambda: pl.BlockSpec((gw, LONG), lambda g, j, f: (g, j))
    return pl.pallas_call(
        functools.partial(attn_fwd_kernel, gw=gw, hd=hd, qc=qc),
        out_shape=[jax.ShapeDtypeStruct((ng * gw, toks), BF)] * 3
        + [
            jax.ShapeDtypeStruct((ng * nh, blocks, LONG, LONG), BF),
            jax.ShapeDtypeStruct((ng * gw, toks), BF),
            jax.ShapeDtypeStruct((ng * 8, toks), F32),
        ],
        grid_spec=pltpu.PrefetchScalarGridSpec(
            num_scalar_prefetch=1,
            grid=(ng, blocks),
            in_specs=[
                pl.BlockSpec((gw, LONG), lambda g, j, f: (g0 + g, j)),
                pl.BlockSpec((gw, w.shape[1]), lambda g, j, f: (g0 + g, 0)),
                pl.BlockSpec(memory_space=pl.ANY),
                pl.BlockSpec(memory_space=pl.ANY),
            ],
            out_specs=[
                own(),
                own(),
                own(),
                pl.BlockSpec((nh, 1, LONG, LONG), lambda g, j, f: (g, j, 0, 0)),
                own(),
                pl.BlockSpec((8, LONG), lambda g, j, f: (g, j)),
            ],
        ),
        compiler_params=params(),
        cost_estimate=cost(7 * ng),
        name="attention_forward",
    )(flag, xt, w, step, last)


def attn_bwd_kernel(
    flag_ref, q_ref, k_ref, v_ref, e_ref, c_ref, inv_ref, dc_ref, x_ref, w_ref, dy_ref, vg_ref,
    step_ref, last_ref, g_ref, keep_ref, send_ref, acc, dq, bacc, *, gw, hd, kc, rows,
):
    nh = gw // hd
    j = pl.program_id(1)

    def run(span, step):
        for h in range(nh):
            r = slice(h * hd, (h + 1) * hd)
            dc = dc_ref[r, :].astype(F32)
            total = jnp.sum(dc * c_ref[r, :].astype(F32), axis=0, keepdims=True)
            inv = inv_ref[h : h + 1, :]
            dci = (dc * inv).astype(BF)
            ti = total * inv
            qs = q_ref[r, :] * jnp.asarray(hd**-0.5, BF)
            for s0 in range(0, LONG, span):
                ts = slice(s0, s0 + span)
                dcs = dci[:, ts]
                tis = ti[:, ts]
                qss = qs[:, ts]
                a = None
                for c0 in range(s0, s0 + span, step):
                    cs = slice(c0, c0 + step)
                    e = e_ref[h, 0, cs, ts]
                    dp = dg(v_ref[r, cs], dcs, 0, 0)
                    ds = (e.astype(F32) * (dp - tis)).astype(BF)
                    dq[2 * gw + h * hd : 2 * gw + (h + 1) * hd, cs] = dg(dcs, e, 1, 1)
                    dq[gw + h * hd : gw + (h + 1) * hd, cs] = dg(qss, ds, 1, 1)
                    t = dg(k_ref[r, cs], ds, 1, 0)
                    a = t if a is None else a + t
                dq[r, ts] = a * (hd**-0.5)

    @pl.when(flag_ref[0] == 1)
    def _():
        run(LONG, kc)

    @pl.when(flag_ref[0] != 1)
    def _():
        run(SHORT, SHORT)

    d = dq[...]
    dl = d.astype(BF)
    w = w_ref[...]
    g_ref[...] = (dy_ref[...] + dg(w[:, : 3 * gw], dl, 1, 0)).astype(BF)
    dw = dg(x_ref[...], dl, 1, 1)
    bq = lane_sum(d[:gw])
    bv = lane_sum(d[2 * gw :])

    @pl.when(j == 0)
    def _():
        acc[:, : 3 * gw] = dw
        bacc[0] = bq
        bacc[1] = bv

    @pl.when(j > 0)
    def _():
        acc[:, : 3 * gw] += dw
        bacc[0] += bq
        bacc[1] += bv

    @pl.when(j == pl.num_programs(1) - 1)
    def _():
        rest = acc.shape[1] - 3 * gw
        bqc = jnp.sum(bacc[0], axis=1, keepdims=True)
        bvc = jnp.sum(bacc[1], axis=1, keepdims=True)
        lane = lax.broadcasted_iota(jnp.int32, (gw, rest), 1)
        vectors = jnp.where(lane == 0, bqc, jnp.where(lane == 1, bvc, vg_ref[...][:, :rest]))
        acc[:, 3 * gw :] = vectors
        write_halves(acc, keep_ref, send_ref, flag_ref[1], rows)


def attn_bwd(flag, saved, dct, xt, w, dyt, vg, step, last, g0, ng, gw, hd, rows, kc=256):
    q, k, v, e, c, inv = saved
    toks = xt.shape[1]
    blocks = toks // LONG
    nh = gw // hd
    cols = w.shape[1]
    keep, send = half_shapes(gw, rows, cols)
    own = lambda: pl.BlockSpec((gw, LONG), lambda g, j, f: (g, j))
    part = lambda: pl.BlockSpec((gw, LONG), lambda g, j, f: (g0 + g, j))
    return pl.pallas_call(
        functools.partial(attn_bwd_kernel, gw=gw, hd=hd, kc=kc, rows=rows),
        out_shape=[
            jax.ShapeDtypeStruct((ng * gw, toks), BF),
            jax.ShapeDtypeStruct((ng * keep[0],) + keep[1:], BF),
            jax.ShapeDtypeStruct((ng * send[0],) + send[1:], BF),
        ],
        grid_spec=pltpu.PrefetchScalarGridSpec(
            num_scalar_prefetch=1,
            grid=(ng, blocks),
            in_specs=[
                own(),
                own(),
                own(),
                pl.BlockSpec((nh, 1, LONG, LONG), lambda g, j, f: (g, j, 0, 0)),
                own(),
                pl.BlockSpec((8, LONG), lambda g, j, f: (g, j)),
                part(),
                part(),
                pl.BlockSpec((gw, cols), lambda g, j, f: (g0 + g, 0)),
                part(),
                pl.BlockSpec((gw, 128), lambda g, j, f: (g0 + g, 0)),
                pl.BlockSpec(memory_space=pl.ANY),
                pl.BlockSpec(memory_space=pl.ANY),
            ],
            out_specs=[
                own(),
                pl.BlockSpec(keep, lambda g, j, f: (g,) + (0,) * (len(keep) - 1)),
                pl.BlockSpec(send, lambda g, j, f: (g,) + (0,) * (len(send) - 1)),
            ],
            scratch_shapes=[
                pltpu.VMEM((gw, cols), F32),
                pltpu.VMEM((3 * gw, LONG), F32),
                pltpu.VMEM((2, gw, 128), F32),
            ],
        ),
        compiler_params=params(),
        cost_estimate=cost(7 * ng),
        name="attention_backward",
    )(flag, q, k, v, e, c, inv, dct, xt, w, dyt, vg, step, last)


def fill_context(ctx, refs):
    row = 0
    for ref in refs:
        ctx[row : row + ref.shape[0], :] = ref[...]
        row += ref.shape[0]


def ffn_kernel(x_ref, *refs, parts, shards, gw, vbase):
    ctx_refs = refs[:parts]
    vec_ref, wo_ref = refs[parts : parts + 2]
    wf_refs = refs[parts + 2 : parts + 2 + shards]
    cot_ref = refs[parts + 2 + shards]
    rest = refs[parts + 3 + shards :]
    out_ref, n1_ref, rs_ref, dh_ref = rest[:4]
    grad_refs = rest[4 : 4 + shards]
    vg_ref = rest[4 + shards]
    ctx, wf, h1x, h1t, ua, ub, act, slope, y2, dyl, dyt, acc1, acc2, accb, accv = rest[5 + shards :]
    j = pl.program_id(0)
    last = pl.num_programs(0) - 1
    groups = h1x.shape[0]
    toks = x_ref.shape[1]
    width = groups * gw
    inv_width = 1.0 / width

    def col(i):
        return vec_ref[:, vbase + i : vbase + i + 1].astype(F32)

    def mean(v):
        return jnp.sum(v, axis=0, keepdims=True) * inv_width

    @pl.when(j == 0)
    def _():
        for s in range(shards):
            wf[s] = wf_refs[s][...]
        acc1[...] = jnp.zeros_like(acc1)
        acc2[...] = jnp.zeros_like(acc2)
        accb[...] = jnp.zeros_like(accb)
        accv[...] = jnp.zeros_like(accv)

    fill_context(ctx, ctx_refs)
    y1 = x_ref[...].astype(F32) + dg(wo_ref[...], ctx[...], 0, 0) + col(2)
    center = y1 - mean(y1)
    rs1 = lax.rsqrt(mean(center * center) + EPS)
    rs_ref[...] = jnp.broadcast_to(rs1, rs_ref.shape)
    norm1 = center * rs1
    n1_ref[...] = norm1
    h1 = norm1 * col(3) + col(4)
    y2[...] = (h1 + col(5)).reshape(groups, gw, toks)
    h1x[:, :gw, :] = h1.astype(BF).reshape(groups, gw, toks)
    h1x[:, gw:, :] = jnp.ones((groups, PAD, toks), BF)
    for g in range(groups):
        h1t[g] = h1x[g, :gw, :].T

    chunks = groups * shards

    def first_dot(i, buf):
        buf[...] = dg(wf[i % shards, i // shards, :, :gw], h1x[i // shards], 0, 0)

    def second_dot(i):
        g = i // shards
        s = i % shards
        y2[g] += dg(wf[s, g, :gw, gw : 2 * gw], act[g, s], 0, 0)

    def gelu(i, buf):
        g = i // shards
        s = i % shards
        u = buf[...]
        phi = lax.erf(u * ROOT_HALF) * 0.5 + 0.5
        act[g, s] = (u * phi).astype(BF)
        slope[g, s] = phi + u * INV_ROOT_2PI * jnp.exp2(u * u * HALF_LOG2E)

    first_dot(0, ua)
    first_dot(1, ub)
    gelu(0, ua)

    def forward(k, carry):
        i = 2 * k + 1
        second_dot(i - 1)
        first_dot(i + 1, ua)
        gelu(i, ub)
        second_dot(i)
        first_dot(i + 2, ub)
        gelu(i + 1, ua)
        return carry

    lax.fori_loop(0, chunks // 2 - 1, forward, 0)
    second_dot(chunks - 2)
    gelu(chunks - 1, ub)
    second_dot(chunks - 1)

    yy = y2[...].reshape(width, toks)
    center = yy - mean(yy)
    rs2 = lax.rsqrt(mean(center * center) + EPS)
    norm2 = center * rs2
    out_ref[...] = (norm2 * col(6) + col(7)).astype(BF)
    cot = cot_ref[...].astype(F32)
    e2 = cot * col(6)
    dy2 = (e2 - mean(e2) - norm2 * mean(e2 * norm2)) * rs2
    accv[0] += lane_sum(dy2)
    accv[1] += lane_sum(cot * norm2)
    accv[2] += lane_sum(cot)
    y2[...] = dy2.reshape(groups, gw, toks)
    dyl[...] = dy2.astype(BF).reshape(groups, gw, toks)
    for g in range(groups):
        dyt[g] = dyl[g].T

    def backward(i, carry):
        g = i // shards
        s = i % shards
        dact = dg(wf[s, g, :gw, gw : 2 * gw], dyl[g], 1, 0)
        du = dact * slope[g, s]
        low = du.astype(BF)
        acc2[s, g] += dg(act[g, s], dyt[g], 1, 0)
        y2[g] += dg(wf[s, g, :gw, :gw], low, 1, 0)
        acc1[s, g] += dg(low, h1t[g], 1, 0)
        accb[s, g] += lane_sum(du)
        return carry

    lax.fori_loop(0, groups * shards, backward, 0, unroll=2)
    dh_ref[...] = y2[...].reshape(width, toks)

    @pl.when(j == last)
    def _():
        for s in range(shards):

            def write(g, carry, s=s):
                grad_refs[s][g, :gw, :gw] = acc1[s, g].astype(BF).T
                grad_refs[s][g, :gw, gw : 2 * gw] = acc2[s, g].astype(BF)
                row = jnp.sum(accb[s, g].T, axis=0, keepdims=True)
                tail = jnp.concatenate([row, jnp.zeros_like(row)], axis=1)
                grad_refs[s][g, gw:, :] = jnp.broadcast_to(tail, (PAD, 2 * gw)).astype(BF)
                return carry

            lax.fori_loop(0, groups, write, 0, unroll=2)
        vg_ref[...] = spread(accv, 5)


def spread(sums, first):
    count, width, lanes = sums.shape
    lane = lax.broadcasted_iota(jnp.int32, (width, lanes), 1)
    t = jnp.zeros((width, lanes), F32)
    for i in range(count):
        t = jnp.where(lane == i + first, jnp.sum(sums[i], axis=1, keepdims=True), t)
    return t


def write_halves(full, keep_ref, send_ref, mine, rows):
    if rows % 8:
        keep_ref[...] = full[...].astype(BF)
        send_ref[...] = jnp.zeros_like(send_ref)
        return
    for k in range(keep_ref.shape[0]):
        own = pl.multiple_of((2 * k + mine) * rows, 8)
        other = pl.multiple_of((2 * k + 1 - mine) * rows, 8)
        keep_ref[k] = full[pl.ds(own, rows), :].astype(BF)
        send_ref[k] = full[pl.ds(other, rows), :].astype(BF)


def half_shapes(total, rows, cols):
    if rows % 8:
        return (total, cols), (16, 128)
    return (total // rows // 2, rows, cols), (total // rows // 2, rows, cols)


def core_step(keep, send, rows, index, count):
    if rows % 8:
        keep, send = halves(keep.reshape(-1, rows, keep.shape[-1]), 0, index)
    return keep, swap(send, 0, count)


def norm_kernel(me_ref, *refs, parts, vbase, rows):
    ctx_refs = refs[:parts]
    n1_ref, rs_ref, dh_ref, vec_ref, wo_ref, vga_ref = refs[parts : parts + 6]
    dy1_ref, dct_ref, keep_ref, send_ref, vg_ref = refs[parts + 6 : parts + 11]
    ctx, acco, accv = refs[parts + 11 :]
    j = pl.program_id(0)
    last = pl.num_programs(0) - 1
    inv_width = 1.0 / n1_ref.shape[0]

    def mean(v):
        return jnp.sum(v, axis=0, keepdims=True) * inv_width

    fill_context(ctx, ctx_refs)
    norm1 = n1_ref[...]
    dh1 = dh_ref[...]
    e1 = dh1 * vec_ref[:, vbase + 3 : vbase + 4].astype(F32)
    dy1 = (e1 - mean(e1) - norm1 * mean(e1 * norm1)) * rs_ref[0:1, :]
    dy1_ref[...] = dy1
    low1 = dy1.astype(BF)
    dct_ref[...] = dg(wo_ref[...], low1, 1, 0).astype(BF)
    sums = (lane_sum(dy1), lane_sum(dh1 * norm1), lane_sum(dh1))
    dwo = dg(ctx[...], low1, 1, 1)

    @pl.when(j == 0)
    def _():
        acco[...] = dwo
        for i in range(3):
            accv[i] = sums[i]

    @pl.when(j > 0)
    def _():
        acco[...] += dwo
        for i in range(3):
            accv[i] += sums[i]

    @pl.when(j == last)
    def _():
        write_halves(acco, keep_ref, send_ref, me_ref[0], rows)
        vg_ref[...] = vga_ref[...] + spread(accv, 2)


def whole(shape):
    return pl.BlockSpec(shape, lambda j, *m: (0,) * len(shape), pipeline_mode=pl.Buffered(1))


def ffn_layer(xt, ctxs, w, wo, wfs, cott, gw):
    width, toks = xt.shape
    blk = min(LONG, toks)
    shards = len(wfs)
    groups = wfs[0].shape[0]
    vec_block = (3 * gw) // 128
    col_blk = lambda rows: pl.BlockSpec((rows, blk), lambda j: (0, j))
    return pl.pallas_call(
        functools.partial(ffn_kernel, parts=len(ctxs), shards=shards, gw=gw, vbase=3 * gw - 128 * vec_block),
        out_shape=[
            jax.ShapeDtypeStruct((width, toks), BF),
            jax.ShapeDtypeStruct((width, toks), F32),
            jax.ShapeDtypeStruct((8, toks), F32),
            jax.ShapeDtypeStruct((width, toks), F32),
        ]
        + [jax.ShapeDtypeStruct(wfs[0].shape, BF)] * shards
        + [jax.ShapeDtypeStruct((width, 128), F32)],
        grid=(toks // blk,),
        in_specs=[col_blk(width)]
        + [col_blk(c.shape[0]) for c in ctxs]
        + [pl.BlockSpec((width, 128), lambda j: (0, vec_block)), whole((width, width))]
        + [whole(wfs[0].shape) for _ in wfs]
        + [col_blk(width)],
        out_specs=[col_blk(width), col_blk(width), col_blk(8), col_blk(width)]
        + [whole(wfs[0].shape) for _ in wfs]
        + [whole((width, 128))],
        scratch_shapes=[
            pltpu.VMEM((width, blk), BF),
            pltpu.VMEM((shards,) + wfs[0].shape, BF),
            pltpu.VMEM((groups, gw + PAD, blk), BF),
            pltpu.VMEM((groups, blk, gw), BF),
            pltpu.VMEM((gw, blk), F32),
            pltpu.VMEM((gw, blk), F32),
            pltpu.VMEM((groups, shards, gw, blk), BF),
            pltpu.VMEM((groups, shards, gw, blk), F32),
            pltpu.VMEM((groups, gw, blk), F32),
            pltpu.VMEM((groups, gw, blk), BF),
            pltpu.VMEM((groups, blk, gw), BF),
            pltpu.VMEM((shards, groups, gw, gw), F32),
            pltpu.VMEM((shards, groups, gw, gw), F32),
            pltpu.VMEM((shards, groups, gw, 128), F32),
            pltpu.VMEM((3, width, 128), F32),
        ],
        compiler_params=params(),
        cost_estimate=cost(40),
        name="feed_forward",
    )(xt, *ctxs, w, wo, *wfs, cott)


def norm_layer(me, ctxs, n1, rs1, dh1, w, wo, vga, gw, rows):
    width, toks = n1.shape
    blk = min(LONG, toks)
    vec_block = (3 * gw) // 128
    col_blk = lambda rows: pl.BlockSpec((rows, blk), lambda j, m: (0, j))
    keep, send = half_shapes(width, rows, width)
    return pl.pallas_call(
        functools.partial(norm_kernel, parts=len(ctxs), vbase=3 * gw - 128 * vec_block, rows=rows),
        out_shape=[
            jax.ShapeDtypeStruct((width, toks), F32),
            jax.ShapeDtypeStruct((width, toks), BF),
            jax.ShapeDtypeStruct(keep, BF),
            jax.ShapeDtypeStruct(send, BF),
            jax.ShapeDtypeStruct((width, 128), F32),
        ],
        grid_spec=pltpu.PrefetchScalarGridSpec(
            num_scalar_prefetch=1,
            grid=(toks // blk,),
            in_specs=[col_blk(c.shape[0]) for c in ctxs]
            + [
                col_blk(width),
                col_blk(8),
                col_blk(width),
                pl.BlockSpec((width, 128), lambda j, m: (0, vec_block)),
                whole((width, width)),
                whole((width, 128)),
            ],
            out_specs=[col_blk(width), col_blk(width), whole(keep), whole(send), whole((width, 128))],
            scratch_shapes=[
                pltpu.VMEM((width, blk), BF),
                pltpu.VMEM((width, width), F32),
                pltpu.VMEM((3, width, 128), F32),
            ],
        ),
        compiler_params=params(),
        cost_estimate=cost(7),
        name="norm_backward",
    )(me, *ctxs, n1, rs1, dh1, w, wo, vga)


def swap(a, bit, count):
    return lax.ppermute(a, AXES, [(i, i ^ (1 << bit)) for i in range(count)])


def gather_bit(cur, b, index, count):
    return merge(cur, swap(cur, b, count), b, index)


def merge(cur, got, b, index):
    place = lax.broadcasted_iota(jnp.int32, (1, 2) + (1,) * (cur.ndim - 1), 1)
    new = jnp.where(place == ((index >> b) & 1), cur[:, None], got[:, None])
    return new.reshape((cur.shape[0] * 2,) + cur.shape[1:])


def halves(cur, b, index):
    pair = cur.reshape((cur.shape[0] // 2, 2) + cur.shape[1:])
    mine = (index >> b) & 1
    keep = lax.dynamic_index_in_dim(pair, mine, 1, keepdims=False)
    return keep, lax.dynamic_index_in_dim(pair, 1 - mine, 1, keepdims=False)


def reduce_bit(cur, b, index, count):
    keep, send = halves(cur, b, index)
    return keep.astype(F32) + swap(send, b, count).astype(F32)


def log2(n):
    return n.bit_length() - 1


def body(
    dp, ffn, tokens, long_seq, cotangent, query_weight, key_weight, value_weight, out_weight,
    query_bias, value_bias, out_bias, attn_gain, attn_shift, ffn_in_weight, ffn_in_bias,
    ffn_out_weight, ffn_out_bias, ffn_gain, ffn_shift,
):
    count = dp * ffn
    index = lax.axis_index("dp") * ffn + lax.axis_index("ffn")
    ffn_bits = list(range(log2(ffn)))
    dp_bits = list(range(log2(ffn), log2(count)))
    all_bits = ffn_bits + dp_bits
    width = tokens.shape[1]
    groups = ffn_in_weight.shape[0]
    gw = width // groups
    hd = width // HEADS
    rows = query_weight.shape[0]

    vectors = [query_bias, value_bias, out_bias, attn_gain, attn_shift, ffn_out_bias, ffn_gain, ffn_shift]
    used = 3 * gw + len(vectors)
    cols = -(-used // 128) * 128
    columns = jnp.pad(jnp.stack(vectors), ((0, cols - used), (0, 0))).T
    w = jnp.concatenate([query_weight, key_weight, value_weight, columns], axis=1)[None]
    wo = out_weight[None]
    top = ffn_bits[-1]
    first = jnp.concatenate([ffn_in_weight, ffn_in_bias[:, None, :], jnp.zeros((groups, PAD - 1, gw), BF)], axis=1)
    second = jnp.pad(ffn_out_weight, ((0, 0), (0, PAD), (0, 0)))
    wf = jnp.concatenate([first, second], axis=2)
    xt = tokens.T
    cott = cotangent.T
    flags = jnp.concatenate([long_seq, (index & 1).astype(jnp.int32)[None]])
    both = jnp.concatenate([w, wo], axis=2)
    for n, b in enumerate(reversed(dp_bits[1:])):
        both = gather_bit(both, b, index, count)
        if n == 0:
            both, xt = lax.optimization_barrier((both, xt))
        if n == 1:
            both, cott = lax.optimization_barrier((both, cott))
    w = both[:, :, :cols]
    wo = both[:, :, cols:]
    w = gather_bit(w, dp_bits[0], index, count)
    w = gather_bit(w, top, index, count)
    for b in reversed(ffn_bits[:-1]):
        w = gather_bit(w, b, index, count)
    w, wo, wf = lax.optimization_barrier((w, wo, wf))
    w = w.reshape(width, cols)
    got_wo = swap(wo, dp_bits[0], count)
    got_wf = swap(wf, top, count)
    slots = {0: wf}
    for b in ffn_bits[:-1]:
        slots[1 << b] = swap(wf, b, count)

    saved = []
    step = last = xt
    for i, (g0, ng) in enumerate(SPLITS):
        out = list(attn_fwd(flags, xt, w, step, last, g0, ng, gw, hd))
        if i == 0:
            got_wo, out[4] = lax.optimization_barrier((got_wo, out[4]))
            step = wo = merge(wo, got_wo, dp_bits[0], index)
            got_wo = swap(wo, top, count)
        if i == 1:
            got_wo, got_wf, out[4] = lax.optimization_barrier((got_wo, got_wf, out[4]))
            step = wo = merge(wo, got_wo, top, index)
        last = out[5]
        saved.append(out)
    slots[1 << top] = got_wf
    for b in reversed(ffn_bits[:-1]):
        wo = gather_bit(wo, b, index, count)
        slots[(1 << top) + (1 << b)] = swap(got_wf, b, count)
    wo = wo.reshape(width, width)
    ctxs = [s[4] for s in saved]
    wfs = [slots[s] for s in range(ffn)]
    outs = ffn_layer(xt, ctxs, w, wo, wfs, cott, gw)
    outt, n1, rs1, dh1 = outs[:4]
    gf = outs[4 : 4 + ffn]
    dyt, dct, keep_o, send_o, vg = norm_layer(flags[1:], ctxs, n1, rs1, dh1, w, wo, outs[4 + ffn], gw, rows)

    def add(keep, got):
        return (keep.astype(F32) + got.astype(F32)).astype(BF)

    got1 = swap(gf[1], 0, count)
    got3 = swap(gf[3], 0, count)
    send = add(gf[2], got3)
    got2 = swap(send, top, count)
    keep_o, got_o = core_step(keep_o, send_o, rows, index, count)

    grads = []
    step, last = send, dct
    for i, (g0, ng) in enumerate(SPLITS):
        out = list(attn_bwd(flags, saved[i], dct, xt, w, dyt, vg, step, last, g0, ng, gw, hd, rows))
        if i == 0:
            got_o, out[0] = lax.optimization_barrier((got_o, out[0]))
            keep_o, step = halves(add(keep_o, got_o), top, index)
            got_o = swap(step, top, count)
        if i == 1:
            got2, got_o, out[0] = lax.optimization_barrier((got2, got_o, out[0]))
            mine = (gf[0].astype(F32) + got1.astype(F32) + got2.astype(F32)).astype(BF)
            keep_f, step = halves(mine.reshape(dp, -1, mine.shape[-1]), dp_bits[0], index)
            got_f = swap(step, dp_bits[0], count)
            keep_o, send_o = halves(add(keep_o, got_o), dp_bits[0], index)
            got_o = swap(send_o, dp_bits[0], count)
        if i == 2:
            got_f, got_o, out[1] = lax.optimization_barrier((got_f, got_o, out[1]))
        last = out[1]
        grads.append(out)
    keep_w, send_w = [jnp.concatenate([item[n] for item in grads], axis=0) for n in (1, 2)]
    keep_w, got_w = core_step(keep_w, send_w, rows, index, count)
    keep_w, send_w = halves(add(keep_w, got_w), top, index)
    got_w = swap(send_w, top, count)
    output = outt.T
    got_w, output = lax.optimization_barrier((got_w, output))
    keep_w, send_w = halves(add(keep_w, got_w), dp_bits[0], index)
    got_w = swap(send_w, dp_bits[0], count)
    grad_tokens = jnp.concatenate([item[0] for item in grads], axis=0).T
    got_w, grad_tokens = lax.optimization_barrier((got_w, grad_tokens))

    ffn_sum = add(keep_f, got_f)
    for b in dp_bits[1:]:
        ffn_sum = reduce_bit(ffn_sum, b, index, count).astype(BF)
    for b in reversed(dp_bits):
        ffn_sum = gather_bit(ffn_sum, b, index, count)
    ffn_sum = ffn_sum.reshape(mine.shape).astype(F32)

    both = jnp.concatenate([add(keep_w, got_w), add(keep_o, got_o)], axis=2)
    for b in dp_bits[1:]:
        both = reduce_bit(both, b, index, count)
        if b != dp_bits[-1]:
            both = both.astype(BF)
    dw_sum = both[0, :, :cols]
    dwo_sum = both[0, :, cols:]
    vec = lambda i: dw_sum[:, 3 * gw + i]
    return (
        output,
        grad_tokens,
        dw_sum[:, :gw],
        dw_sum[:, gw : 2 * gw],
        dw_sum[:, 2 * gw : 3 * gw],
        dwo_sum,
        vec(0),
        vec(1),
        vec(2),
        vec(3),
        vec(4),
        ffn_sum[:, :gw, :gw],
        ffn_sum[:, gw, :gw],
        ffn_sum[:, :gw, gw:],
        vec(5),
        vec(6),
        vec(7),
    )


def solution(mesh):
    both = P(AXES)
    rows = P(AXES, None)
    return jax.shard_map(
        functools.partial(body, mesh.shape["dp"], mesh.shape["ffn"]),
        mesh=mesh,
        in_specs=(
            rows, both, rows, rows, rows, rows, rows, both, both, both, both, both,
            P(None, None, "ffn"), P(None, "ffn"), P(None, "ffn", None), both, both, both,
        ),
        out_specs=(
            rows, rows, rows, rows, rows, rows, both, both, both, both, both,
            P(None, None, "ffn"), P(None, "ffn"), P(None, "ffn", None), both, both, both,
        ),
        check_vma=False,
    )
```

```python
import functools

import jax
import jax.numpy as jnp
from jax import lax
from jax.experimental import pallas as pl
from jax.experimental.pallas import tpu as pltpu
from jax.sharding import PartitionSpec as P

F32 = jnp.float32
BF = jnp.bfloat16
HEADS = 12
LONG = 512
SHORT = 128
EPS = 1e-12
AXES = ("dp", "ffn")
PAD = 16

ROOT_HALF = 0.7071067811865476
INV_ROOT_2PI = 0.3989422804014327
HALF_LOG2E = -0.7213475204444817
FORWARD = ((0, 2), (2, 2))
BACKWARD = ((0, 2), (2, 1), (3, 1))


def dg(a, b, ca, cb):
    return lax.dot_general(a, b, (((ca,), (cb,)), ((), ())), preferred_element_type=F32)


def lane_sum(v):
    out = v[:, :128]
    for c in range(128, v.shape[1], 128):
        out = out + v[:, c : c + 128]
    return out


def params():
    return pltpu.CompilerParams(vmem_limit_bytes=63 << 20)


def cost(us):
    return pl.CostEstimate(flops=int(us * 1e9), bytes_accessed=int(us * 3e6), transcendentals=0)


def across(s, outside):
    rows = []
    for a in range(0, LONG, SHORT):
        cells = []
        for b in range(0, LONG, SHORT):
            cell = s[a : a + SHORT, b : b + SHORT]
            cells.append(cell if a == b else cell + outside)
        rows.append(jnp.concatenate(cells, axis=1))
    return jnp.concatenate(rows, axis=0)


def attn_fwd_kernel(flag_ref, x_ref, w_ref, step_ref, *refs, gw, hd):
    q_ref, k_ref, v_ref, e_ref, c_ref, inv_ref = refs[-6:]
    w = w_ref[...]
    p = dg(w[:, : 3 * gw], x_ref[...], 0, 0)
    bq = w[:, 3 * gw : 3 * gw + 1].astype(F32)
    bv = w[:, 3 * gw + 1 : 3 * gw + 2].astype(F32)
    q_ref[...] = (p[:gw] + bq).astype(BF)
    k_ref[...] = p[gw : 2 * gw].astype(BF)
    v_ref[...] = (p[2 * gw :] + bv).astype(BF)
    inv_ref[...] = jnp.zeros_like(inv_ref)
    outside = jnp.where(flag_ref[0] == 1, 0.0, -1e9).astype(F32)
    ones = jnp.ones((16, LONG), BF)
    for h in range(gw // hd):
        r = slice(h * hd, (h + 1) * hd)
        vx = jnp.concatenate([v_ref[r, :], ones], 0)
        q = q_ref[r, :] * jnp.asarray(hd**-0.5, BF)
        s = across(dg(k_ref[r, :], q, 0, 0), outside)
        m = jnp.max(s, axis=0, keepdims=True)
        e = jnp.exp(s - m).astype(BF)
        e_ref[h, 0] = e
        o = dg(vx, e, 1, 0)
        inv = 1.0 / o[hd : hd + 1]
        c_ref[r, :] = (o[:hd] * inv).astype(BF)
        inv_ref[h : h + 1, :] = inv


def anywhere(count):
    return [pl.BlockSpec(memory_space=pl.ANY) for _ in range(count)]


def attn_fwd(flag, xt, w, step, before, g0, ng, gw, hd):
    width, toks = xt.shape
    groups = width // gw
    blocks = toks // LONG
    nh = gw // hd
    own = lambda: pl.BlockSpec((gw, LONG), lambda g, j, f: (g0 + g, j))
    return pl.pallas_call(
        functools.partial(attn_fwd_kernel, gw=gw, hd=hd),
        out_shape=[jax.ShapeDtypeStruct((width, toks), BF)] * 3
        + [
            jax.ShapeDtypeStruct((groups * nh, blocks, LONG, LONG), BF),
            jax.ShapeDtypeStruct((width, toks), BF),
            jax.ShapeDtypeStruct((groups * 8, toks), F32),
        ],
        grid_spec=pltpu.PrefetchScalarGridSpec(
            num_scalar_prefetch=1,
            grid=(ng, blocks),
            in_specs=[own(), pl.BlockSpec((gw, w.shape[1]), lambda g, j, f: (g0 + g, 0))] + anywhere(1 + len(before)),
            out_specs=[
                own(),
                own(),
                own(),
                pl.BlockSpec((nh, 1, LONG, LONG), lambda g, j, f: (g0 + g, j, 0, 0)),
                own(),
                pl.BlockSpec((8, LONG), lambda g, j, f: (g0 + g, j)),
            ],
        ),
        input_output_aliases={4 + i: i for i in range(len(before))},
        compiler_params=params(),
        cost_estimate=cost(5 * ng),
        name="attention_forward",
    )(flag, xt, w, step, *before)


def attn_bwd_kernel(
    flag_ref, q_ref, k_ref, v_ref, e_ref, c_ref, inv_ref, dc_ref, x_ref, w_ref, dy_ref, vg_ref, step_ref,
    *refs, gw, hd, rows,
):
    g_ref, keep_ref, send_ref, acc, dq, bacc = refs[-6:]
    nh = gw // hd
    j = pl.program_id(1)
    for h in range(nh):
        r = slice(h * hd, (h + 1) * hd)
        dc = dc_ref[r, :].astype(F32)
        total = jnp.sum(dc * c_ref[r, :].astype(F32), axis=0, keepdims=True)
        inv = inv_ref[h : h + 1, :]
        dci = (dc * inv).astype(BF)
        qs = q_ref[r, :] * jnp.asarray(hd**-0.5, BF)
        e = e_ref[h, 0]
        dp = dg(v_ref[r, :], dci, 0, 0)
        ds = (e.astype(F32) * (dp - total * inv)).astype(BF)
        dq[2 * gw + h * hd : 2 * gw + (h + 1) * hd, :] = dg(dci, e, 1, 1)
        dq[gw + h * hd : gw + (h + 1) * hd, :] = dg(qs, ds, 1, 1)
        dq[r, :] = dg(k_ref[r, :], ds, 1, 0) * (hd**-0.5)

    d = dq[...]
    dl = d.astype(BF)
    w = w_ref[...]
    g_ref[...] = (dy_ref[...] + dg(w[:, : 3 * gw], dl, 1, 0)).astype(BF)
    dw = dg(x_ref[...], dl, 1, 1)
    bq = lane_sum(d[:gw])
    bv = lane_sum(d[2 * gw :])

    @pl.when(j == 0)
    def _():
        acc[:, : 3 * gw] = dw
        bacc[0] = bq
        bacc[1] = bv

    @pl.when(j > 0)
    def _():
        acc[:, : 3 * gw] += dw
        bacc[0] += bq
        bacc[1] += bv

    @pl.when(j == pl.num_programs(1) - 1)
    def _():
        rest = acc.shape[1] - 3 * gw
        bqc = jnp.sum(bacc[0], axis=1, keepdims=True)
        bvc = jnp.sum(bacc[1], axis=1, keepdims=True)
        lane = lax.broadcasted_iota(jnp.int32, (gw, rest), 1)
        vectors = jnp.where(lane == 0, bqc, jnp.where(lane == 1, bvc, vg_ref[...][:, :rest]))
        acc[:, 3 * gw :] = vectors
        write_halves(acc, keep_ref, send_ref, flag_ref[1], rows)


def attn_bwd(flag, saved, dct, xt, w, dyt, vg, step, before, g0, ng, gw, hd, rows):
    q, k, v, e, c, inv = saved
    width, toks = xt.shape
    groups = width // gw
    blocks = toks // LONG
    nh = gw // hd
    cols = w.shape[1]
    keep, send = half_shapes(gw, rows, cols)
    own = lambda: pl.BlockSpec((gw, LONG), lambda g, j, f: (g0 + g, j))
    return pl.pallas_call(
        functools.partial(attn_bwd_kernel, gw=gw, hd=hd, rows=rows),
        out_shape=[
            jax.ShapeDtypeStruct((width, toks), BF),
            jax.ShapeDtypeStruct((groups * keep[0],) + keep[1:], BF),
            jax.ShapeDtypeStruct((groups * send[0],) + send[1:], BF),
        ],
        grid_spec=pltpu.PrefetchScalarGridSpec(
            num_scalar_prefetch=1,
            grid=(ng, blocks),
            in_specs=[
                own(),
                own(),
                own(),
                pl.BlockSpec((nh, 1, LONG, LONG), lambda g, j, f: (g0 + g, j, 0, 0)),
                own(),
                pl.BlockSpec((8, LONG), lambda g, j, f: (g0 + g, j)),
                own(),
                own(),
                pl.BlockSpec((gw, cols), lambda g, j, f: (g0 + g, 0)),
                own(),
                pl.BlockSpec((gw, 128), lambda g, j, f: (g0 + g, 0)),
            ]
            + anywhere(1 + len(before)),
            out_specs=[
                own(),
                pl.BlockSpec(keep, lambda g, j, f: (g0 + g,) + (0,) * (len(keep) - 1)),
                pl.BlockSpec(send, lambda g, j, f: (g0 + g,) + (0,) * (len(send) - 1)),
            ],
            scratch_shapes=[
                pltpu.VMEM((gw, cols), F32),
                pltpu.VMEM((3 * gw, LONG), F32),
                pltpu.VMEM((2, gw, 128), F32),
            ],
        ),
        input_output_aliases={13 + i: i for i in range(len(before))},
        compiler_params=params(),
        cost_estimate=cost(7 * ng),
        name="attention_backward",
    )(flag, q, k, v, e, c, inv, dct, xt, w, dyt, vg, step, *before)


def ffn_kernel(x_ref, ctx, vec_ref, wo_ref, cot_ref, *refs, shards, gw, vbase):
    wf_refs = refs[:shards]
    rest = refs[shards:]
    out_ref, n1_ref, rs_ref, dh_ref = rest[:4]
    grad_refs = rest[4 : 4 + shards]
    vg_ref = rest[4 + shards]
    wf, h1x, h1t, ua, ub, act, slope, y2, dyl, dyt, acc1, acc2, accb, accv = rest[5 + shards :]
    j = pl.program_id(0)
    last = pl.num_programs(0) - 1
    groups = h1x.shape[0]
    toks = x_ref.shape[1]
    width = groups * gw
    inv_width = 1.0 / width

    def col(i):
        return vec_ref[:, vbase + i : vbase + i + 1].astype(F32)

    def mean(v):
        return jnp.sum(v, axis=0, keepdims=True) * inv_width

    @pl.when(j == 0)
    def _():
        for s in range(shards):
            wf[s] = wf_refs[s][...]
        acc1[...] = jnp.zeros_like(acc1)
        acc2[...] = jnp.zeros_like(acc2)
        accb[...] = jnp.zeros_like(accb)
        accv[...] = jnp.zeros_like(accv)

    y1 = x_ref[...].astype(F32) + dg(wo_ref[...], ctx[...], 0, 0) + col(2)
    center = y1 - mean(y1)
    rs1 = lax.rsqrt(mean(center * center) + EPS)
    rs_ref[...] = jnp.broadcast_to(rs1, rs_ref.shape)
    norm1 = center * rs1
    n1_ref[...] = norm1
    h1 = norm1 * col(3) + col(4)
    y2[...] = (h1 + col(5)).reshape(groups, gw, toks)
    h1x[:, :gw, :] = h1.astype(BF).reshape(groups, gw, toks)
    h1x[:, gw:, :] = jnp.ones((groups, PAD, toks), BF)
    for g in range(groups):
        h1t[g] = h1x[g, :gw, :].T

    chunks = groups * shards

    def first_dot(i, buf):
        buf[...] = dg(wf[i % shards, i // shards, :, :gw], h1x[i // shards], 0, 0)

    def second_dot(i):
        g = i // shards
        s = i % shards
        y2[g] += dg(wf[s, g, :gw, gw : 2 * gw], act[g, s], 0, 0)

    def gelu(i, buf):
        g = i // shards
        s = i % shards
        u = buf[...]
        phi = lax.erf(u * ROOT_HALF) * 0.5 + 0.5
        act[g, s] = (u * phi).astype(BF)
        slope[g, s] = phi + u * INV_ROOT_2PI * jnp.exp2(u * u * HALF_LOG2E)

    first_dot(0, ua)
    first_dot(1, ub)
    gelu(0, ua)

    def forward(k, carry):
        i = 2 * k + 1
        second_dot(i - 1)
        first_dot(i + 1, ua)
        gelu(i, ub)
        second_dot(i)
        first_dot(i + 2, ub)
        gelu(i + 1, ua)
        return carry

    lax.fori_loop(0, chunks // 2 - 1, forward, 0)
    second_dot(chunks - 2)
    gelu(chunks - 1, ub)
    second_dot(chunks - 1)

    yy = y2[...].reshape(width, toks)
    center = yy - mean(yy)
    rs2 = lax.rsqrt(mean(center * center) + EPS)
    norm2 = center * rs2
    out_ref[...] = (norm2 * col(6) + col(7)).astype(BF)
    cot = cot_ref[...].astype(F32)
    e2 = cot * col(6)
    dy2 = (e2 - mean(e2) - norm2 * mean(e2 * norm2)) * rs2
    accv[0] += lane_sum(dy2)
    accv[1] += lane_sum(cot * norm2)
    accv[2] += lane_sum(cot)
    y2[...] = dy2.reshape(groups, gw, toks)
    dyl[...] = dy2.astype(BF).reshape(groups, gw, toks)
    for g in range(groups):
        dyt[g] = dyl[g].T

    def backward(i, carry):
        g = i // shards
        s = i % shards
        dact = dg(wf[s, g, :gw, gw : 2 * gw], dyl[g], 1, 0)
        du = dact * slope[g, s]
        low = du.astype(BF)
        acc2[s, g] += dg(act[g, s], dyt[g], 1, 0)
        y2[g] += dg(wf[s, g, :gw, :gw], low, 1, 0)
        acc1[s, g] += dg(low, h1t[g], 1, 0)
        accb[s, g] += lane_sum(du)
        return carry

    lax.fori_loop(0, groups * shards, backward, 0, unroll=2)
    dh_ref[...] = y2[...].reshape(width, toks)

    @pl.when(j == last)
    def _():
        for s in range(shards):

            def write(g, carry, s=s):
                grad_refs[s][g, :gw, :gw] = acc1[s, g].astype(BF).T
                grad_refs[s][g, :gw, gw : 2 * gw] = acc2[s, g].astype(BF)
                row = jnp.sum(accb[s, g].T, axis=0, keepdims=True)
                tail = jnp.concatenate([row, jnp.zeros_like(row)], axis=1)
                grad_refs[s][g, gw:, :] = jnp.broadcast_to(tail, (PAD, 2 * gw)).astype(BF)
                return carry

            lax.fori_loop(0, groups, write, 0, unroll=2)
        vg_ref[...] = spread(accv, 5)


def spread(sums, first):
    count, width, lanes = sums.shape
    lane = lax.broadcasted_iota(jnp.int32, (width, lanes), 1)
    t = jnp.zeros((width, lanes), F32)
    for i in range(count):
        t = jnp.where(lane == i + first, jnp.sum(sums[i], axis=1, keepdims=True), t)
    return t


def write_halves(full, keep_ref, send_ref, mine, rows):
    if rows % 8:
        keep_ref[...] = full[...].astype(BF)
        send_ref[...] = jnp.zeros_like(send_ref)
        return
    for k in range(keep_ref.shape[0]):
        own = pl.multiple_of((2 * k + mine) * rows, 8)
        other = pl.multiple_of((2 * k + 1 - mine) * rows, 8)
        keep_ref[k] = full[pl.ds(own, rows), :].astype(BF)
        send_ref[k] = full[pl.ds(other, rows), :].astype(BF)


def half_shapes(total, rows, cols):
    if rows % 8:
        return (total, cols), (16, 128)
    return (total // rows // 2, rows, cols), (total // rows // 2, rows, cols)


def core_step(keep, send, rows, index, count):
    if rows % 8:
        keep, send = halves(keep.reshape(-1, rows, keep.shape[-1]), 0, index)
    return keep, swap(send, 0, count)


def norm_kernel(
    me_ref, ctx, n1_ref, rs_ref, dh_ref, vec_ref, wo_ref, vga_ref,
    dy1_ref, dct_ref, keep_ref, send_ref, vg_ref, acco, accv, *, vbase, rows,
):
    j = pl.program_id(0)
    last = pl.num_programs(0) - 1
    inv_width = 1.0 / n1_ref.shape[0]

    def mean(v):
        return jnp.sum(v, axis=0, keepdims=True) * inv_width

    norm1 = n1_ref[...]
    dh1 = dh_ref[...]
    e1 = dh1 * vec_ref[:, vbase + 3 : vbase + 4].astype(F32)
    dy1 = (e1 - mean(e1) - norm1 * mean(e1 * norm1)) * rs_ref[0:1, :]
    dy1_ref[...] = dy1
    low1 = dy1.astype(BF)
    dct_ref[...] = dg(wo_ref[...], low1, 1, 0).astype(BF)
    sums = (lane_sum(dy1), lane_sum(dh1 * norm1), lane_sum(dh1))
    dwo = dg(ctx[...], low1, 1, 1)

    @pl.when(j == 0)
    def _():
        acco[...] = dwo
        for i in range(3):
            accv[i] = sums[i]

    @pl.when(j > 0)
    def _():
        acco[...] += dwo
        for i in range(3):
            accv[i] += sums[i]

    @pl.when(j == last)
    def _():
        write_halves(acco, keep_ref, send_ref, me_ref[0], rows)
        vg_ref[...] = vga_ref[...] + spread(accv, 2)


def whole(shape):
    return pl.BlockSpec(shape, lambda j, *m: (0,) * len(shape), pipeline_mode=pl.Buffered(1))


def ffn_layer(xt, ctx, w, wo, wfs, cott, gw):
    width, toks = xt.shape
    blk = min(LONG, toks)
    shards = len(wfs)
    groups = wfs[0].shape[0]
    vec_block = (3 * gw) // 128
    col_blk = lambda rows: pl.BlockSpec((rows, blk), lambda j: (0, j))
    return pl.pallas_call(
        functools.partial(ffn_kernel, shards=shards, gw=gw, vbase=3 * gw - 128 * vec_block),
        out_shape=[
            jax.ShapeDtypeStruct((width, toks), BF),
            jax.ShapeDtypeStruct((width, toks), F32),
            jax.ShapeDtypeStruct((8, toks), F32),
            jax.ShapeDtypeStruct((width, toks), F32),
        ]
        + [jax.ShapeDtypeStruct(wfs[0].shape, BF)] * shards
        + [jax.ShapeDtypeStruct((width, 128), F32)],
        grid=(toks // blk,),
        in_specs=[
            col_blk(width),
            col_blk(width),
            pl.BlockSpec((width, 128), lambda j: (0, vec_block)),
            whole((width, width)),
            col_blk(width),
        ]
        + [whole(wfs[0].shape) for _ in wfs],
        out_specs=[col_blk(width), col_blk(width), col_blk(8), col_blk(width)]
        + [whole(wfs[0].shape) for _ in wfs]
        + [whole((width, 128))],
        scratch_shapes=[
            pltpu.VMEM((shards,) + wfs[0].shape, BF),
            pltpu.VMEM((groups, gw + PAD, blk), BF),
            pltpu.VMEM((groups, blk, gw), BF),
            pltpu.VMEM((gw, blk), F32),
            pltpu.VMEM((gw, blk), F32),
            pltpu.VMEM((groups, shards, gw, blk), BF),
            pltpu.VMEM((groups, shards, gw, blk), F32),
            pltpu.VMEM((groups, gw, blk), F32),
            pltpu.VMEM((groups, gw, blk), BF),
            pltpu.VMEM((groups, blk, gw), BF),
            pltpu.VMEM((shards, groups, gw, gw), F32),
            pltpu.VMEM((shards, groups, gw, gw), F32),
            pltpu.VMEM((shards, groups, gw, 128), F32),
            pltpu.VMEM((3, width, 128), F32),
        ],
        compiler_params=params(),
        cost_estimate=cost(40),
        name="feed_forward",
    )(xt, ctx, w, wo, cott, *wfs)


def norm_layer(me, ctx, n1, rs1, dh1, w, wo, vga, gw, rows):
    width, toks = n1.shape
    blk = min(LONG, toks)
    vec_block = (3 * gw) // 128
    col_blk = lambda rows: pl.BlockSpec((rows, blk), lambda j, m: (0, j))
    keep, send = half_shapes(width, rows, width)
    return pl.pallas_call(
        functools.partial(norm_kernel, vbase=3 * gw - 128 * vec_block, rows=rows),
        out_shape=[
            jax.ShapeDtypeStruct((width, toks), F32),
            jax.ShapeDtypeStruct((width, toks), BF),
            jax.ShapeDtypeStruct(keep, BF),
            jax.ShapeDtypeStruct(send, BF),
            jax.ShapeDtypeStruct((width, 128), F32),
        ],
        grid_spec=pltpu.PrefetchScalarGridSpec(
            num_scalar_prefetch=1,
            grid=(toks // blk,),
            in_specs=[
                col_blk(width),
                col_blk(width),
                col_blk(8),
                col_blk(width),
                pl.BlockSpec((width, 128), lambda j, m: (0, vec_block)),
                whole((width, width)),
                whole((width, 128)),
            ],
            out_specs=[col_blk(width), col_blk(width), whole(keep), whole(send), whole((width, 128))],
            scratch_shapes=[
                pltpu.VMEM((width, width), F32),
                pltpu.VMEM((3, width, 128), F32),
            ],
        ),
        compiler_params=params(),
        cost_estimate=cost(7),
        name="norm_backward",
    )(me, ctx, n1, rs1, dh1, w, wo, vga)


def swap(a, bit, count):
    return lax.ppermute(a, AXES, [(i, i ^ (1 << bit)) for i in range(count)])


def gather_bit(cur, b, index, count):
    return merge(cur, swap(cur, b, count), b, index)


def merge(cur, got, b, index):
    place = lax.broadcasted_iota(jnp.int32, (1, 2) + (1,) * (cur.ndim - 1), 1)
    new = jnp.where(place == ((index >> b) & 1), cur[:, None], got[:, None])
    return new.reshape((cur.shape[0] * 2,) + cur.shape[1:])


def halves(cur, b, index):
    pair = cur.reshape((cur.shape[0] // 2, 2) + cur.shape[1:])
    mine = (index >> b) & 1
    keep = lax.dynamic_index_in_dim(pair, mine, 1, keepdims=False)
    return keep, lax.dynamic_index_in_dim(pair, 1 - mine, 1, keepdims=False)


def reduce_bit(cur, b, index, count):
    keep, send = halves(cur, b, index)
    return keep.astype(F32) + swap(send, b, count).astype(F32)


def log2(n):
    return n.bit_length() - 1


def body(
    dp, ffn, tokens, long_seq, cotangent, query_weight, key_weight, value_weight, out_weight,
    query_bias, value_bias, out_bias, attn_gain, attn_shift, ffn_in_weight, ffn_in_bias,
    ffn_out_weight, ffn_out_bias, ffn_gain, ffn_shift,
):
    count = dp * ffn
    index = lax.axis_index("dp") * ffn + lax.axis_index("ffn")
    ffn_bits = list(range(log2(ffn)))
    dp_bits = list(range(log2(ffn), log2(count)))
    all_bits = ffn_bits + dp_bits
    width = tokens.shape[1]
    groups = ffn_in_weight.shape[0]
    gw = width // groups
    hd = width // HEADS
    rows = query_weight.shape[0]

    vectors = [query_bias, value_bias, out_bias, attn_gain, attn_shift, ffn_out_bias, ffn_gain, ffn_shift]
    used = 3 * gw + len(vectors)
    cols = -(-used // 128) * 128
    columns = jnp.pad(jnp.stack(vectors), ((0, cols - used), (0, 0))).T
    w = jnp.concatenate([query_weight, key_weight, value_weight, columns], axis=1)[None]
    wo = out_weight[None]
    top = ffn_bits[-1]
    first = jnp.concatenate([ffn_in_weight, ffn_in_bias[:, None, :], jnp.zeros((groups, PAD - 1, gw), BF)], axis=1)
    second = jnp.pad(ffn_out_weight, ((0, 0), (0, PAD), (0, 0)))
    wf = jnp.concatenate([first, second], axis=2)
    xt = tokens.T
    cott = cotangent.T
    flags = jnp.concatenate([long_seq, (index & 1).astype(jnp.int32)[None]])
    both = jnp.concatenate([w, wo], axis=2)
    for n, b in enumerate(reversed(dp_bits)):
        both = gather_bit(both, b, index, count)
        if n == 0:
            both, wf, flags = lax.optimization_barrier((both, wf, flags))
            got_wf = swap(wf, top, count)
        if n == 1:
            both, xt = lax.optimization_barrier((both, xt))
        if n == 2:
            both, cott = lax.optimization_barrier((both, cott))
    w = both[:, :, :cols]
    wo = both[:, :, cols:]
    w, got_wf = lax.optimization_barrier((w, got_wf))
    w = gather_bit(w, top, index, count)
    slots = {0: wf, 1 << top: got_wf}
    for b in reversed(ffn_bits[:-1]):
        w = gather_bit(w, b, index, count)
        slots[1 << b] = swap(wf, b, count)
        slots[(1 << top) + (1 << b)] = swap(got_wf, b, count)
    w, wo = lax.optimization_barrier((w, wo))
    w = w.reshape(width, cols)
    got_wo = swap(wo, top, count)

    saved = []
    step = flags
    for i, (g0, ng) in enumerate(FORWARD):
        saved = list(attn_fwd(flags, xt, w, step, saved, g0, ng, gw, hd))
        if i == 0:
            got_wo, saved[4] = lax.optimization_barrier((got_wo, saved[4]))
            step = wo = merge(wo, got_wo, top, index)
    for b in reversed(ffn_bits[:-1]):
        wo = gather_bit(wo, b, index, count)
    wo = wo.reshape(width, width)
    ctx = saved[4]
    wfs = [slots[s] for s in range(ffn)]
    outs = ffn_layer(xt, ctx, w, wo, wfs, cott, gw)
    outt, n1, rs1, dh1 = outs[:4]
    gf = outs[4 : 4 + ffn]
    dyt, dct, keep_o, send_o, vg = norm_layer(flags[1:], ctx, n1, rs1, dh1, w, wo, outs[4 + ffn], gw, rows)

    def add(keep, got):
        return (keep.astype(F32) + got.astype(F32)).astype(BF)

    got1 = swap(gf[1], 0, count)
    got3 = swap(gf[3], 0, count)
    send = add(gf[2], got3)
    got2 = swap(send, top, count)
    keep_o, got_o = core_step(keep_o, send_o, rows, index, count)

    grads = []
    step = send
    for i, (g0, ng) in enumerate(BACKWARD):
        grads = list(attn_bwd(flags, saved, dct, xt, w, dyt, vg, step, grads, g0, ng, gw, hd, rows))
        if i == 0:
            got2, got_o, grads[0] = lax.optimization_barrier((got2, got_o, grads[0]))
            mine = (gf[0].astype(F32) + got1.astype(F32) + got2.astype(F32)).astype(BF)
            keep_f, step = halves(mine.reshape(dp, -1, mine.shape[-1]), dp_bits[0], index)
            got_f = swap(step, dp_bits[0], count)
            keep_o, send_o = halves(add(keep_o, got_o), top, index)
            got_o = swap(send_o, top, count)
        if i == 1:
            got_f, got_o, grads[0] = lax.optimization_barrier((got_f, got_o, grads[0]))
            keep_f, step = halves(add(keep_f, got_f), dp_bits[1], index)
            got_f = swap(step, dp_bits[1], count)
            keep_o, send_o = halves(add(keep_o, got_o), dp_bits[0], index)
            got_o = swap(send_o, dp_bits[0], count)
        if i == 2:
            got_f, got_o, grads[1] = lax.optimization_barrier((got_f, got_o, grads[1]))
    keep_w, send_w = grads[1:]
    keep_w, got_w = core_step(keep_w, send_w, rows, index, count)
    keep_w, send_w = halves(add(keep_w, got_w), top, index)
    got_w = swap(send_w, top, count)
    output = outt.T
    got_w, output = lax.optimization_barrier((got_w, output))
    keep_w, send_w = halves(add(keep_w, got_w), dp_bits[0], index)
    got_w = swap(send_w, dp_bits[0], count)
    grad_tokens = grads[0].T
    got_w, grad_tokens = lax.optimization_barrier((got_w, grad_tokens))

    ffn_sum = add(keep_f, got_f)
    for b in dp_bits[2:]:
        ffn_sum = reduce_bit(ffn_sum, b, index, count).astype(BF)
    for b in reversed(dp_bits):
        ffn_sum = gather_bit(ffn_sum, b, index, count)
    ffn_sum = ffn_sum.reshape(mine.shape).astype(F32)

    both = jnp.concatenate([add(keep_w, got_w), add(keep_o, got_o)], axis=2)
    for b in dp_bits[1:]:
        both = reduce_bit(both, b, index, count)
        if b != dp_bits[-1]:
            both = both.astype(BF)
    dw_sum = both[0, :, :cols]
    dwo_sum = both[0, :, cols:]
    vec = lambda i: dw_sum[:, 3 * gw + i]
    return (
        output,
        grad_tokens,
        dw_sum[:, :gw],
        dw_sum[:, gw : 2 * gw],
        dw_sum[:, 2 * gw : 3 * gw],
        dwo_sum,
        vec(0),
        vec(1),
        vec(2),
        vec(3),
        vec(4),
        ffn_sum[:, :gw, :gw],
        ffn_sum[:, gw, :gw],
        ffn_sum[:, :gw, gw:],
        vec(5),
        vec(6),
        vec(7),
    )


def solution(mesh):
    both = P(AXES)
    rows = P(AXES, None)
    return jax.shard_map(
        functools.partial(body, mesh.shape["dp"], mesh.shape["ffn"]),
        mesh=mesh,
        in_specs=(
            rows, both, rows, rows, rows, rows, rows, both, both, both, both, both,
            P(None, None, "ffn"), P(None, "ffn"), P(None, "ffn", None), both, both, both,
        ),
        out_specs=(
            rows, rows, rows, rows, rows, rows, both, both, both, both, both,
            P(None, None, "ffn"), P(None, "ffn"), P(None, "ffn", None), both, both, both,
        ),
        check_vma=False,
    )
```

```python
import functools

import jax
import jax.numpy as jnp
from jax import lax
from jax.experimental import pallas as pl
from jax.experimental.layout import Layout, with_layout_constraint
from jax.experimental.pallas import tpu as pltpu
from jax.sharding import PartitionSpec as P

F32 = jnp.float32
BF = jnp.bfloat16
HEADS = 12
LONG = 512
SHORT = 128
EPS = 1e-12
AXES = ("dp", "ffn")
PAD = 16

ROOT_HALF = 0.7071067811865476
INV_ROOT_2PI = 0.3989422804014327
HALF_LOG2E = -0.7213475204444817
FORWARD = ((0, 2), (2, 2))
BACKWARD = ((0, 2), (2, 1), (3, 1))


def dg(a, b, ca, cb):
    return lax.dot_general(a, b, (((ca,), (cb,)), ((), ())), preferred_element_type=F32)


def lane_sum(v):
    out = v[:, :128]
    for c in range(128, v.shape[1], 128):
        out = out + v[:, c : c + 128]
    return out


def params():
    return pltpu.CompilerParams(vmem_limit_bytes=63 << 20)


def cost(us):
    return pl.CostEstimate(flops=int(us * 1e9), bytes_accessed=int(us * 3e6), transcendentals=0)


def across(s, outside):
    rows = []
    for a in range(0, LONG, SHORT):
        cells = []
        for b in range(0, LONG, SHORT):
            cell = s[a : a + SHORT, b : b + SHORT]
            cells.append(cell if a == b else cell + outside)
        rows.append(jnp.concatenate(cells, axis=1))
    return jnp.concatenate(rows, axis=0)


def attn_fwd_kernel(flag_ref, x_ref, w_ref, step_ref, *refs, gw, hd):
    q_ref, k_ref, v_ref, e_ref, c_ref, inv_ref, sa, sb = refs[-8:]
    w = w_ref[...]
    p = dg(w[:, : 3 * gw], x_ref[...], 0, 0)
    bq = w[:, 3 * gw : 3 * gw + 1].astype(F32)
    bv = w[:, 3 * gw + 1 : 3 * gw + 2].astype(F32)
    q_ref[...] = (p[:gw] + bq).astype(BF)
    k_ref[...] = p[gw : 2 * gw].astype(BF)
    v_ref[...] = (p[2 * gw :] + bv).astype(BF)
    inv_ref[...] = jnp.zeros_like(inv_ref)
    outside = jnp.where(flag_ref[0] == 1, 0.0, -1e9).astype(F32)
    ones = jnp.ones((16, LONG), BF)
    heads = [slice(h * hd, (h + 1) * hd) for h in range(gw // hd)]

    def scores(h, buf):
        q = q_ref[heads[h], :] * jnp.asarray(hd**-0.5, BF)
        buf[...] = dg(k_ref[heads[h], :], q, 0, 0)

    bufs = (sa, sb)
    scores(0, sa)
    for h, r in enumerate(heads):
        if h + 1 < len(heads):
            scores(h + 1, bufs[(h + 1) % 2])
        s = across(bufs[h % 2][...], outside)
        m = jnp.max(s, axis=0, keepdims=True)
        e = jnp.exp(s - m).astype(BF)
        e_ref[h, 0] = e
        o = dg(jnp.concatenate([v_ref[r, :], ones], 0), e, 1, 0)
        inv = 1.0 / o[hd : hd + 1]
        c_ref[r, :] = (o[:hd] * inv).astype(BF)
        inv_ref[h : h + 1, :] = inv


def anywhere(count):
    return [pl.BlockSpec(memory_space=pl.ANY) for _ in range(count)]


def attn_fwd(flag, xt, w, step, before, g0, ng, gw, hd):
    width, toks = xt.shape
    groups = width // gw
    blocks = toks // LONG
    nh = gw // hd
    own = lambda: pl.BlockSpec((gw, LONG), lambda g, j, f: (g0 + g, j))
    return pl.pallas_call(
        functools.partial(attn_fwd_kernel, gw=gw, hd=hd),
        out_shape=[jax.ShapeDtypeStruct((width, toks), BF)] * 3
        + [
            jax.ShapeDtypeStruct((groups * nh, blocks, LONG, LONG), BF),
            jax.ShapeDtypeStruct((width, toks), BF),
            jax.ShapeDtypeStruct((groups * 8, toks), F32),
        ],
        grid_spec=pltpu.PrefetchScalarGridSpec(
            num_scalar_prefetch=1,
            grid=(ng, blocks),
            in_specs=[own(), pl.BlockSpec((gw, w.shape[1]), lambda g, j, f: (g0 + g, 0))] + anywhere(1 + len(before)),
            out_specs=[
                own(),
                own(),
                own(),
                pl.BlockSpec((nh, 1, LONG, LONG), lambda g, j, f: (g0 + g, j, 0, 0)),
                own(),
                pl.BlockSpec((8, LONG), lambda g, j, f: (g0 + g, j)),
            ],
            scratch_shapes=[pltpu.VMEM((LONG, LONG), F32)] * 2,
        ),
        input_output_aliases={4 + i: i for i in range(len(before))},
        compiler_params=params(),
        cost_estimate=cost(5 * ng),
        name="attention_forward",
    )(flag, xt, w, step, *before)


def attn_bwd_kernel(
    flag_ref, q_ref, k_ref, v_ref, e_ref, c_ref, inv_ref, dc_ref, x_ref, w_ref, dy_ref, vg_ref, step_ref,
    *refs, gw, hd, rows,
):
    g_ref, keep_ref, send_ref, acc, dq, bacc, pa, pb = refs[-8:]
    nh = gw // hd
    j = pl.program_id(1)
    heads = [slice(h * hd, (h + 1) * hd) for h in range(nh)]
    scaled = []

    def grad_probs(h, buf):
        dc = dc_ref[heads[h], :].astype(F32)
        inv = inv_ref[h : h + 1, :]
        total = jnp.sum(dc * c_ref[heads[h], :].astype(F32), axis=0, keepdims=True) * inv
        scaled.append(((dc * inv).astype(BF), total))
        buf[...] = dg(v_ref[heads[h], :], scaled[h][0], 0, 0)

    bufs = (pa, pb)
    grad_probs(0, pa)
    for h, r in enumerate(heads):
        if h + 1 < nh:
            grad_probs(h + 1, bufs[(h + 1) % 2])
        dci, total = scaled[h]
        e = e_ref[h, 0]
        dq[2 * gw + h * hd : 2 * gw + (h + 1) * hd, :] = dg(dci, e, 1, 1)
        ds = (e.astype(F32) * (bufs[h % 2][...] - total)).astype(BF)
        qs = q_ref[r, :] * jnp.asarray(hd**-0.5, BF)
        dq[gw + h * hd : gw + (h + 1) * hd, :] = dg(qs, ds, 1, 1)
        dq[r, :] = dg(k_ref[r, :], ds, 1, 0) * (hd**-0.5)

    d = dq[...]
    dl = d.astype(BF)
    w = w_ref[...]
    g_ref[...] = (dy_ref[...] + dg(w[:, : 3 * gw], dl, 1, 0)).astype(BF)
    dw = dg(x_ref[...], dl, 1, 1)
    bq = lane_sum(d[:gw])
    bv = lane_sum(d[2 * gw :])

    @pl.when(j == 0)
    def _():
        acc[:, : 3 * gw] = dw
        bacc[0] = bq
        bacc[1] = bv

    @pl.when(j > 0)
    def _():
        acc[:, : 3 * gw] += dw
        bacc[0] += bq
        bacc[1] += bv

    @pl.when(j == pl.num_programs(1) - 1)
    def _():
        rest = acc.shape[1] - 3 * gw
        bqc = jnp.sum(bacc[0], axis=1, keepdims=True)
        bvc = jnp.sum(bacc[1], axis=1, keepdims=True)
        lane = lax.broadcasted_iota(jnp.int32, (gw, rest), 1)
        vectors = jnp.where(lane == 0, bqc, jnp.where(lane == 1, bvc, vg_ref[...][:, :rest]))
        acc[:, 3 * gw :] = vectors
        write_halves(acc, keep_ref, send_ref, flag_ref[1], rows)


def attn_bwd(flag, saved, dct, xt, w, dyt, vg, step, before, g0, ng, gw, hd, rows):
    q, k, v, e, c, inv = saved
    width, toks = xt.shape
    groups = width // gw
    blocks = toks // LONG
    nh = gw // hd
    cols = w.shape[1]
    keep, send = half_shapes(gw, rows, cols)
    own = lambda: pl.BlockSpec((gw, LONG), lambda g, j, f: (g0 + g, j))
    return pl.pallas_call(
        functools.partial(attn_bwd_kernel, gw=gw, hd=hd, rows=rows),
        out_shape=[
            jax.ShapeDtypeStruct((width, toks), BF),
            jax.ShapeDtypeStruct((groups * keep[0],) + keep[1:], BF),
            jax.ShapeDtypeStruct((groups * send[0],) + send[1:], BF),
        ],
        grid_spec=pltpu.PrefetchScalarGridSpec(
            num_scalar_prefetch=1,
            grid=(ng, blocks),
            in_specs=[
                own(),
                own(),
                own(),
                pl.BlockSpec((nh, 1, LONG, LONG), lambda g, j, f: (g0 + g, j, 0, 0)),
                own(),
                pl.BlockSpec((8, LONG), lambda g, j, f: (g0 + g, j)),
                own(),
                own(),
                pl.BlockSpec((gw, cols), lambda g, j, f: (g0 + g, 0)),
                own(),
                pl.BlockSpec((gw, 128), lambda g, j, f: (g0 + g, 0)),
            ]
            + anywhere(1 + len(before)),
            out_specs=[
                own(),
                pl.BlockSpec(keep, lambda g, j, f: (g0 + g,) + (0,) * (len(keep) - 1)),
                pl.BlockSpec(send, lambda g, j, f: (g0 + g,) + (0,) * (len(send) - 1)),
            ],
            scratch_shapes=[
                pltpu.VMEM((gw, cols), F32),
                pltpu.VMEM((3 * gw, LONG), F32),
                pltpu.VMEM((2, gw, 128), F32),
                pltpu.VMEM((LONG, LONG), F32),
                pltpu.VMEM((LONG, LONG), F32),
            ],
        ),
        input_output_aliases={13 + i: i for i in range(len(before))},
        compiler_params=params(),
        cost_estimate=cost(7 * ng),
        name="attention_backward",
    )(flag, q, k, v, e, c, inv, dct, xt, w, dyt, vg, step, *before)


def ffn_kernel(x_ref, ctx, vec_ref, wo_ref, cot_ref, *refs, shards, gw, vbase):
    wf_refs = refs[:shards]
    rest = refs[shards:]
    out_ref, n1_ref, rs_ref, dh_ref = rest[:4]
    grad_refs = rest[4 : 4 + shards]
    vg_ref = rest[4 + shards]
    wf, h1x, h1t, ua, ub, act, slope, y2, dyl, dyt, acc1, acc2, accb, accv = rest[5 + shards :]
    j = pl.program_id(0)
    last = pl.num_programs(0) - 1
    groups = h1x.shape[0]
    toks = x_ref.shape[1]
    width = groups * gw
    inv_width = 1.0 / width

    def col(i):
        return vec_ref[:, vbase + i : vbase + i + 1].astype(F32)

    def mean(v):
        return jnp.sum(v, axis=0, keepdims=True) * inv_width

    @pl.when(j == 0)
    def _():
        for s in range(shards):
            wf[s] = wf_refs[s][...]
        acc1[...] = jnp.zeros_like(acc1)
        acc2[...] = jnp.zeros_like(acc2)
        accb[...] = jnp.zeros_like(accb)
        accv[...] = jnp.zeros_like(accv)

    y1 = x_ref[...].astype(F32) + dg(wo_ref[...], ctx[...], 0, 0) + col(2)
    center = y1 - mean(y1)
    rs1 = lax.rsqrt(mean(center * center) + EPS)
    rs_ref[...] = jnp.broadcast_to(rs1, rs_ref.shape)
    norm1 = center * rs1
    n1_ref[...] = norm1
    h1 = norm1 * col(3) + col(4)
    y2[...] = (h1 + col(5)).reshape(groups, gw, toks)
    h1x[:, :gw, :] = h1.astype(BF).reshape(groups, gw, toks)
    h1x[:, gw:, :] = jnp.ones((groups, PAD, toks), BF)
    for g in range(groups):
        h1t[g] = h1x[g, :gw, :].T

    chunks = groups * shards

    def first_dot(i, buf):
        buf[...] = dg(wf[i % shards, i // shards, :, :gw], h1x[i // shards], 0, 0)

    def second_dot(i):
        g = i // shards
        s = i % shards
        y2[g] += dg(wf[s, g, :gw, gw : 2 * gw], act[g, s], 0, 0)

    def gelu(i, buf):
        g = i // shards
        s = i % shards
        u = buf[...]
        phi = lax.erf(u * ROOT_HALF) * 0.5 + 0.5
        act[g, s] = (u * phi).astype(BF)
        slope[g, s] = phi + u * INV_ROOT_2PI * jnp.exp2(u * u * HALF_LOG2E)

    first_dot(0, ua)
    first_dot(1, ub)
    gelu(0, ua)

    def forward(k, carry):
        i = 2 * k + 1
        second_dot(i - 1)
        first_dot(i + 1, ua)
        gelu(i, ub)
        second_dot(i)
        first_dot(i + 2, ub)
        gelu(i + 1, ua)
        return carry

    lax.fori_loop(0, chunks // 2 - 1, forward, 0)
    second_dot(chunks - 2)
    gelu(chunks - 1, ub)
    second_dot(chunks - 1)

    yy = y2[...].reshape(width, toks)
    center = yy - mean(yy)
    rs2 = lax.rsqrt(mean(center * center) + EPS)
    norm2 = center * rs2
    out_ref[...] = (norm2 * col(6) + col(7)).astype(BF)
    cot = cot_ref[...].astype(F32)
    e2 = cot * col(6)
    dy2 = (e2 - mean(e2) - norm2 * mean(e2 * norm2)) * rs2
    accv[0] += lane_sum(dy2)
    accv[1] += lane_sum(cot * norm2)
    accv[2] += lane_sum(cot)
    y2[...] = dy2.reshape(groups, gw, toks)
    dyl[...] = dy2.astype(BF).reshape(groups, gw, toks)
    for g in range(groups):
        dyt[g] = dyl[g].T

    def backward(i, carry):
        g = i // shards
        s = i % shards
        dact = dg(wf[s, g, :gw, gw : 2 * gw], dyl[g], 1, 0)
        du = dact * slope[g, s]
        low = du.astype(BF)
        acc2[s, g] += dg(act[g, s], dyt[g], 1, 0)
        y2[g] += dg(wf[s, g, :gw, :gw], low, 1, 0)
        acc1[s, g] += dg(low, h1t[g], 1, 0)
        accb[s, g] += lane_sum(du)
        return carry

    lax.fori_loop(0, groups * shards, backward, 0, unroll=2)
    dh_ref[...] = y2[...].reshape(width, toks)

    @pl.when(j == last)
    def _():
        for s in range(shards):

            def write(g, carry, s=s):
                grad_refs[s][g, :gw, :gw] = acc1[s, g].astype(BF).T
                grad_refs[s][g, :gw, gw : 2 * gw] = acc2[s, g].astype(BF)
                row = jnp.sum(accb[s, g].T, axis=0, keepdims=True)
                tail = jnp.concatenate([row, jnp.zeros_like(row)], axis=1)
                grad_refs[s][g, gw:, :] = jnp.broadcast_to(tail, (PAD, 2 * gw)).astype(BF)
                return carry

            lax.fori_loop(0, groups, write, 0, unroll=2)
        vg_ref[...] = spread(accv, 5)


def spread(sums, first):
    count, width, lanes = sums.shape
    lane = lax.broadcasted_iota(jnp.int32, (width, lanes), 1)
    t = jnp.zeros((width, lanes), F32)
    for i in range(count):
        t = jnp.where(lane == i + first, jnp.sum(sums[i], axis=1, keepdims=True), t)
    return t


def write_halves(full, keep_ref, send_ref, mine, rows):
    if rows % 8:
        keep_ref[...] = full[...].astype(BF)
        send_ref[...] = jnp.zeros_like(send_ref)
        return
    for k in range(keep_ref.shape[0]):
        own = pl.multiple_of((2 * k + mine) * rows, 8)
        other = pl.multiple_of((2 * k + 1 - mine) * rows, 8)
        keep_ref[k] = full[pl.ds(own, rows), :].astype(BF)
        send_ref[k] = full[pl.ds(other, rows), :].astype(BF)


def half_shapes(total, rows, cols):
    if rows % 8:
        return (total, cols), (16, 128)
    return (total // rows // 2, rows, cols), (total // rows // 2, rows, cols)


def core_step(keep, send, rows, index, count):
    if rows % 8:
        keep, send = halves(keep.reshape(-1, rows, keep.shape[-1]), 0, index)
    return keep, swap(send, 0, count)


def norm_kernel(
    me_ref, ctx, n1_ref, rs_ref, dh_ref, vec_ref, wo_ref, vga_ref,
    dy1_ref, dct_ref, keep_ref, send_ref, vg_ref, acco, accv, *, vbase, rows,
):
    j = pl.program_id(0)
    last = pl.num_programs(0) - 1
    inv_width = 1.0 / n1_ref.shape[0]

    def mean(v):
        return jnp.sum(v, axis=0, keepdims=True) * inv_width

    norm1 = n1_ref[...]
    dh1 = dh_ref[...]
    e1 = dh1 * vec_ref[:, vbase + 3 : vbase + 4].astype(F32)
    dy1 = (e1 - mean(e1) - norm1 * mean(e1 * norm1)) * rs_ref[0:1, :]
    dy1_ref[...] = dy1
    low1 = dy1.astype(BF)
    dct_ref[...] = dg(wo_ref[...], low1, 1, 0).astype(BF)
    sums = (lane_sum(dy1), lane_sum(dh1 * norm1), lane_sum(dh1))
    dwo = dg(ctx[...], low1, 1, 1)

    @pl.when(j == 0)
    def _():
        acco[...] = dwo
        for i in range(3):
            accv[i] = sums[i]

    @pl.when(j > 0)
    def _():
        acco[...] += dwo
        for i in range(3):
            accv[i] += sums[i]

    @pl.when(j == last)
    def _():
        write_halves(acco, keep_ref, send_ref, me_ref[1], rows)
        vg_ref[...] = vga_ref[...] + spread(accv, 2)


def whole(shape):
    return pl.BlockSpec(shape, lambda j, *m: (0,) * len(shape), pipeline_mode=pl.Buffered(1))


def ffn_layer(xt, ctx, w, wo, wfs, cott, gw):
    width, toks = xt.shape
    blk = min(LONG, toks)
    shards = len(wfs)
    groups = wfs[0].shape[0]
    vec_block = (3 * gw) // 128
    col_blk = lambda rows: pl.BlockSpec((rows, blk), lambda j: (0, j))
    return pl.pallas_call(
        functools.partial(ffn_kernel, shards=shards, gw=gw, vbase=3 * gw - 128 * vec_block),
        out_shape=[
            jax.ShapeDtypeStruct((width, toks), BF),
            jax.ShapeDtypeStruct((width, toks), F32),
            jax.ShapeDtypeStruct((8, toks), F32),
            jax.ShapeDtypeStruct((width, toks), F32),
        ]
        + [jax.ShapeDtypeStruct(wfs[0].shape, BF)] * shards
        + [jax.ShapeDtypeStruct((width, 128), F32)],
        grid=(toks // blk,),
        in_specs=[
            col_blk(width),
            col_blk(width),
            pl.BlockSpec((width, 128), lambda j: (0, vec_block)),
            whole((width, width)),
            col_blk(width),
        ]
        + [whole(wfs[0].shape) for _ in wfs],
        out_specs=[col_blk(width), col_blk(width), col_blk(8), col_blk(width)]
        + [whole(wfs[0].shape) for _ in wfs]
        + [whole((width, 128))],
        scratch_shapes=[
            pltpu.VMEM((shards,) + wfs[0].shape, BF),
            pltpu.VMEM((groups, gw + PAD, blk), BF),
            pltpu.VMEM((groups, blk, gw), BF),
            pltpu.VMEM((gw, blk), F32),
            pltpu.VMEM((gw, blk), F32),
            pltpu.VMEM((groups, shards, gw, blk), BF),
            pltpu.VMEM((groups, shards, gw, blk), F32),
            pltpu.VMEM((groups, gw, blk), F32),
            pltpu.VMEM((groups, gw, blk), BF),
            pltpu.VMEM((groups, blk, gw), BF),
            pltpu.VMEM((shards, groups, gw, gw), F32),
            pltpu.VMEM((shards, groups, gw, gw), F32),
            pltpu.VMEM((shards, groups, gw, 128), F32),
            pltpu.VMEM((3, width, 128), F32),
        ],
        compiler_params=params(),
        cost_estimate=cost(40),
        name="feed_forward",
    )(xt, ctx, w, wo, cott, *wfs)


def norm_layer(me, ctx, n1, rs1, dh1, w, wo, vga, gw, rows):
    width, toks = n1.shape
    blk = min(LONG, toks)
    vec_block = (3 * gw) // 128
    col_blk = lambda rows: pl.BlockSpec((rows, blk), lambda j, m: (0, j))
    keep, send = half_shapes(width, rows, width)
    return pl.pallas_call(
        functools.partial(norm_kernel, vbase=3 * gw - 128 * vec_block, rows=rows),
        out_shape=[
            jax.ShapeDtypeStruct((width, toks), F32),
            jax.ShapeDtypeStruct((width, toks), BF),
            jax.ShapeDtypeStruct(keep, BF),
            jax.ShapeDtypeStruct(send, BF),
            jax.ShapeDtypeStruct((width, 128), F32),
        ],
        grid_spec=pltpu.PrefetchScalarGridSpec(
            num_scalar_prefetch=1,
            grid=(toks // blk,),
            in_specs=[
                col_blk(width),
                col_blk(width),
                col_blk(8),
                col_blk(width),
                pl.BlockSpec((width, 128), lambda j, m: (0, vec_block)),
                whole((width, width)),
                whole((width, 128)),
            ],
            out_specs=[col_blk(width), col_blk(width), whole(keep), whole(send), whole((width, 128))],
            scratch_shapes=[
                pltpu.VMEM((width, width), F32),
                pltpu.VMEM((3, width, 128), F32),
            ],
        ),
        compiler_params=params(),
        cost_estimate=cost(7),
        name="norm_backward",
    )(me, ctx, n1, rs1, dh1, w, wo, vga)


def swap(a, bit, count):
    return lax.ppermute(a, AXES, [(i, i ^ (1 << bit)) for i in range(count)])


def gather_bit(cur, b, index, count):
    return merge(cur, swap(cur, b, count), b, index)


def merge(cur, got, b, index):
    place = lax.broadcasted_iota(jnp.int32, (1, 2) + (1,) * (cur.ndim - 1), 1)
    new = jnp.where(place == ((index >> b) & 1), cur[:, None], got[:, None])
    return new.reshape((cur.shape[0] * 2,) + cur.shape[1:])


def halves(cur, b, index):
    pair = cur.reshape((cur.shape[0] // 2, 2) + cur.shape[1:])
    mine = (index >> b) & 1
    keep = lax.dynamic_index_in_dim(pair, mine, 1, keepdims=False)
    return keep, lax.dynamic_index_in_dim(pair, 1 - mine, 1, keepdims=False)


def reduce_bit(cur, b, index, count):
    keep, send = halves(cur, b, index)
    return keep.astype(F32) + swap(send, b, count).astype(F32)


def log2(n):
    return n.bit_length() - 1


def body(
    dp, ffn, tokens, long_seq, cotangent, query_weight, key_weight, value_weight, out_weight,
    query_bias, value_bias, out_bias, attn_gain, attn_shift, ffn_in_weight, ffn_in_bias,
    ffn_out_weight, ffn_out_bias, ffn_gain, ffn_shift,
):
    count = dp * ffn
    index = lax.axis_index("dp") * ffn + lax.axis_index("ffn")
    ffn_bits = list(range(log2(ffn)))
    dp_bits = list(range(log2(ffn), log2(count)))
    all_bits = ffn_bits + dp_bits
    width = tokens.shape[1]
    groups = ffn_in_weight.shape[0]
    gw = width // groups
    hd = width // HEADS
    rows = query_weight.shape[0]

    vectors = [query_bias, value_bias, out_bias, attn_gain, attn_shift, ffn_out_bias, ffn_gain, ffn_shift]
    used = 3 * gw + len(vectors)
    cols = -(-used // 128) * 128
    columns = jnp.pad(jnp.stack(vectors), ((0, cols - used), (0, 0))).T
    w = jnp.concatenate([query_weight, key_weight, value_weight, columns], axis=1)[None]
    wo = out_weight[None]
    top = ffn_bits[-1]
    first = jnp.concatenate([ffn_in_weight, ffn_in_bias[:, None, :], jnp.zeros((groups, PAD - 1, gw), BF)], axis=1)
    second = jnp.pad(ffn_out_weight, ((0, 0), (0, PAD), (0, 0)))
    wf = jnp.concatenate([first, second], axis=2)
    xt = tokens.T
    cott = cotangent.T
    flags = jnp.concatenate([long_seq, (index & 1).astype(jnp.int32)[None]])
    both = jnp.concatenate([w, wo], axis=2)
    for n, b in enumerate(reversed(dp_bits)):
        both = gather_bit(both, b, index, count)
        if n == 0:
            both, wf, flags = lax.optimization_barrier((both, wf, flags))
            got_wf = swap(wf, top, count)
        if n == 1:
            both, xt = lax.optimization_barrier((both, xt))
        if n == 2:
            both, cott = lax.optimization_barrier((both, cott))
    w = both[:, :, :cols]
    wo = both[:, :, cols:]
    w, got_wf = lax.optimization_barrier((w, got_wf))
    w = gather_bit(w, top, index, count)
    for b in reversed(ffn_bits[:-1]):
        w = gather_bit(w, b, index, count)
    w, wo = lax.optimization_barrier((w, wo))
    w = w.reshape(width, cols)
    got_wo = swap(wo, top, count)

    saved = []
    step = flags
    for i, (g0, ng) in enumerate(FORWARD):
        saved = list(attn_fwd(flags, xt, w, step, saved, g0, ng, gw, hd))
        if i == 0:
            got_wo, saved[4] = lax.optimization_barrier((got_wo, saved[4]))
            step = wo = merge(wo, got_wo, top, index)
    slots = {0: wf, 1 << top: got_wf}
    for b in reversed(ffn_bits[:-1]):
        wo = gather_bit(wo, b, index, count)
        slots[1 << b] = swap(wf, b, count)
        slots[(1 << top) + (1 << b)] = swap(got_wf, b, count)
    wo = wo.reshape(width, width)
    ctx = saved[4]
    wfs = [slots[s] for s in range(ffn)]
    outs = ffn_layer(xt, ctx, w, wo, wfs, cott, gw)
    outt, n1, rs1, dh1 = outs[:4]
    gf = outs[4 : 4 + ffn]
    dyt, dct, keep_o, send_o, vg = norm_layer(flags, ctx, n1, rs1, dh1, w, wo, outs[4 + ffn], gw, rows)

    def add(keep, got):
        return (keep.astype(F32) + got.astype(F32)).astype(BF)

    got1 = swap(gf[1], 0, count)
    got3 = swap(gf[3], 0, count)
    send = add(gf[2], got3)
    got2 = swap(send, top, count)
    keep_o, got_o = core_step(keep_o, send_o, rows, index, count)

    grads = []
    step = send
    for i, (g0, ng) in enumerate(BACKWARD):
        grads = list(attn_bwd(flags, saved, dct, xt, w, dyt, vg, step, grads, g0, ng, gw, hd, rows))
        if i == 0:
            got_o, grads[0] = lax.optimization_barrier((got_o, grads[0]))
            keep_o, send_o = halves(add(keep_o, got_o), top, index)
            got2, send_o, grads[0] = lax.optimization_barrier((got2, send_o, grads[0]))
            got_o = swap(send_o, top, count)
            mine = (gf[0].astype(F32) + got1.astype(F32) + got2.astype(F32)).astype(BF)
            keep_f, step = halves(mine.reshape(dp, -1, mine.shape[-1]), dp_bits[0], index)
            got_f = swap(step, dp_bits[0], count)
        if i == 1:
            got_f, got_o, grads[0] = lax.optimization_barrier((got_f, got_o, grads[0]))
            keep_f, step = halves(add(keep_f, got_f), dp_bits[1], index)
            got_f = swap(step, dp_bits[1], count)
            keep_o, send_o = halves(add(keep_o, got_o), dp_bits[0], index)
            got_o = swap(send_o, dp_bits[0], count)
        if i == 2:
            got_f, got_o, grads[1] = lax.optimization_barrier((got_f, got_o, grads[1]))
    ffn_sum = add(keep_f, got_f)
    keep_f, send_f = halves(ffn_sum, dp_bits[2], index)
    got_f = swap(send_f, dp_bits[2], count)
    keep_w, got_w = core_step(grads[1], grads[2], rows, index, count)
    keep_w, send_w = halves(add(keep_w, got_w), top, index)
    keep_w, got_f, outt = lax.optimization_barrier((keep_w, got_f, outt))
    got_w = swap(send_w, top, count)
    ffn_sum = add(keep_f, got_f)
    for b in dp_bits[3:]:
        ffn_sum = reduce_bit(ffn_sum, b, index, count).astype(BF)
    rows_first = Layout(major_to_minor=(0, 1))
    output = with_layout_constraint(outt.T, rows_first)
    got_w, output = lax.optimization_barrier((got_w, output))
    keep_w, send_w = halves(add(keep_w, got_w), dp_bits[0], index)
    got_w = swap(send_w, dp_bits[0], count)
    keep_w, grads[0] = lax.optimization_barrier((keep_w, grads[0]))
    grad_tokens = with_layout_constraint(grads[0].T, rows_first)
    got_w, grad_tokens = lax.optimization_barrier((got_w, grad_tokens))

    for b in reversed(dp_bits):
        ffn_sum = gather_bit(ffn_sum, b, index, count)
    ffn_sum = ffn_sum.reshape(mine.shape).astype(F32)

    both = jnp.concatenate([add(keep_w, got_w), add(keep_o, got_o)], axis=2)
    for b in dp_bits[1:]:
        both = reduce_bit(both, b, index, count)
        if b != dp_bits[-1]:
            both = both.astype(BF)
    dw_sum = both[0, :, :cols]
    dwo_sum = both[0, :, cols:]
    vec = lambda i: dw_sum[:, 3 * gw + i]
    return (
        output,
        grad_tokens,
        dw_sum[:, :gw],
        dw_sum[:, gw : 2 * gw],
        dw_sum[:, 2 * gw : 3 * gw],
        dwo_sum,
        vec(0),
        vec(1),
        vec(2),
        vec(3),
        vec(4),
        ffn_sum[:, :gw, :gw],
        ffn_sum[:, gw, :gw],
        ffn_sum[:, :gw, gw:],
        vec(5),
        vec(6),
        vec(7),
    )


def solution(mesh):
    both = P(AXES)
    rows = P(AXES, None)
    return jax.shard_map(
        functools.partial(body, mesh.shape["dp"], mesh.shape["ffn"]),
        mesh=mesh,
        in_specs=(
            rows, both, rows, rows, rows, rows, rows, both, both, both, both, both,
            P(None, None, "ffn"), P(None, "ffn"), P(None, "ffn", None), both, both, both,
        ),
        out_specs=(
            rows, rows, rows, rows, rows, rows, both, both, both, both, both,
            P(None, None, "ffn"), P(None, "ffn"), P(None, "ffn", None), both, both, both,
        ),
        check_vma=False,
    )
```

```python
import functools

import jax
import jax.numpy as jnp
from jax import lax
from jax.experimental import pallas as pl
from jax.experimental.layout import Layout, with_layout_constraint
from jax.experimental.pallas import tpu as pltpu
from jax.sharding import PartitionSpec as P

F32 = jnp.float32
BF = jnp.bfloat16
HEADS = 12
LONG = 512
SHORT = 128
EPS = 1e-12
AXES = ("dp", "ffn")
PAD = 16

ROOT_HALF = 0.7071067811865476
INV_ROOT_2PI = 0.3989422804014327
HALF_LOG2E = -0.7213475204444817
FORWARD = ((0, 2), (2, 2))
BACKWARD = ((0, 2), (2, 1), (3, 1))


def dg(a, b, ca, cb):
    return lax.dot_general(a, b, (((ca,), (cb,)), ((), ())), preferred_element_type=F32)


def lane_sum(v):
    out = v[:, :128]
    for c in range(128, v.shape[1], 128):
        out = out + v[:, c : c + 128]
    return out


def params():
    return pltpu.CompilerParams(vmem_limit_bytes=63 << 20)


def cost(us):
    return pl.CostEstimate(flops=int(us * 1e9), bytes_accessed=int(us * 3e6), transcendentals=0)


def across(s, outside):
    rows = []
    for a in range(0, LONG, SHORT):
        cells = []
        for b in range(0, LONG, SHORT):
            cell = s[a : a + SHORT, b : b + SHORT]
            cells.append(cell if a == b else cell + outside)
        rows.append(jnp.concatenate(cells, axis=1))
    return jnp.concatenate(rows, axis=0)


def attn_fwd_kernel(flag_ref, x_ref, w_ref, step_ref, *refs, gw, hd):
    q_ref, k_ref, v_ref, e_ref, c_ref, inv_ref, sa, sb = refs[-8:]
    w = w_ref[...]
    p = dg(w[:, : 3 * gw], x_ref[...], 0, 0)
    bq = w[:, 3 * gw : 3 * gw + 1].astype(F32)
    bv = w[:, 3 * gw + 1 : 3 * gw + 2].astype(F32)
    q_ref[...] = (p[:gw] + bq).astype(BF)
    k_ref[...] = p[gw : 2 * gw].astype(BF)
    v_ref[...] = (p[2 * gw :] + bv).astype(BF)
    inv_ref[...] = jnp.zeros_like(inv_ref)
    outside = jnp.where(flag_ref[0] == 1, 0.0, -1e9).astype(F32)
    ones = jnp.ones((16, LONG), BF)
    heads = [slice(h * hd, (h + 1) * hd) for h in range(gw // hd)]

    def scores(h, buf):
        q = q_ref[heads[h], :] * jnp.asarray(hd**-0.5, BF)
        buf[...] = dg(k_ref[heads[h], :], q, 0, 0)

    bufs = (sa, sb)
    scores(0, sa)
    for h, r in enumerate(heads):
        if h + 1 < len(heads):
            scores(h + 1, bufs[(h + 1) % 2])
        s = across(bufs[h % 2][...], outside)
        m = jnp.max(s, axis=0, keepdims=True)
        e = jnp.exp(s - m).astype(BF)
        e_ref[h, 0] = e
        o = dg(jnp.concatenate([v_ref[r, :], ones], 0), e, 1, 0)
        inv = 1.0 / o[hd : hd + 1]
        c_ref[r, :] = (o[:hd] * inv).astype(BF)
        inv_ref[h : h + 1, :] = inv


def anywhere(count):
    return [pl.BlockSpec(memory_space=pl.ANY) for _ in range(count)]


def attn_fwd(flag, xt, w, step, before, g0, ng, gw, hd):
    width, toks = xt.shape
    groups = width // gw
    blocks = toks // LONG
    nh = gw // hd
    own = lambda: pl.BlockSpec((gw, LONG), lambda g, j, f: (g0 + g, j))
    return pl.pallas_call(
        functools.partial(attn_fwd_kernel, gw=gw, hd=hd),
        out_shape=[jax.ShapeDtypeStruct((width, toks), BF)] * 3
        + [
            jax.ShapeDtypeStruct((groups * nh, blocks, LONG, LONG), BF),
            jax.ShapeDtypeStruct((width, toks), BF),
            jax.ShapeDtypeStruct((groups * 8, toks), F32),
        ],
        grid_spec=pltpu.PrefetchScalarGridSpec(
            num_scalar_prefetch=1,
            grid=(ng, blocks),
            in_specs=[own(), pl.BlockSpec((gw, w.shape[1]), lambda g, j, f: (g0 + g, 0))] + anywhere(1 + len(before)),
            out_specs=[
                own(),
                own(),
                own(),
                pl.BlockSpec((nh, 1, LONG, LONG), lambda g, j, f: (g0 + g, j, 0, 0)),
                own(),
                pl.BlockSpec((8, LONG), lambda g, j, f: (g0 + g, j)),
            ],
            scratch_shapes=[pltpu.VMEM((LONG, LONG), F32)] * 2,
        ),
        input_output_aliases={4 + i: i for i in range(len(before))},
        compiler_params=params(),
        cost_estimate=cost(5 * ng),
        name="attention_forward",
    )(flag, xt, w, step, *before)


def attn_bwd_kernel(
    flag_ref, q_ref, k_ref, v_ref, e_ref, c_ref, inv_ref, dc_ref, x_ref, w_ref, dy_ref, vg_ref,
    *refs, gw, hd, rows,
):
    g_ref, keep_ref, send_ref, acc, dq, bacc, pa, pb = refs[-8:]
    nh = gw // hd
    j = pl.program_id(1)
    heads = [slice(h * hd, (h + 1) * hd) for h in range(nh)]
    scaled = []

    def grad_probs(h, buf):
        dc = dc_ref[heads[h], :].astype(F32)
        inv = inv_ref[h : h + 1, :]
        total = jnp.sum(dc * c_ref[heads[h], :].astype(F32), axis=0, keepdims=True) * inv
        scaled.append(((dc * inv).astype(BF), total))
        buf[...] = dg(v_ref[heads[h], :], scaled[h][0], 0, 0)

    bufs = (pa, pb)
    grad_probs(0, pa)
    for h, r in enumerate(heads):
        if h + 1 < nh:
            grad_probs(h + 1, bufs[(h + 1) % 2])
        dci, total = scaled[h]
        e = e_ref[h, 0]
        dq[2 * gw + h * hd : 2 * gw + (h + 1) * hd, :] = dg(dci, e, 1, 1)
        ds = (e.astype(F32) * (bufs[h % 2][...] - total)).astype(BF)
        qs = q_ref[r, :] * jnp.asarray(hd**-0.5, BF)
        dq[gw + h * hd : gw + (h + 1) * hd, :] = dg(qs, ds, 1, 1)
        dq[r, :] = dg(k_ref[r, :], ds, 1, 0) * (hd**-0.5)

    d = dq[...]
    dl = d.astype(BF)
    w = w_ref[...]
    g_ref[...] = (dy_ref[...] + dg(w[:, : 3 * gw], dl, 1, 0)).astype(BF)
    dw = dg(x_ref[...], dl, 1, 1)
    bq = lane_sum(d[:gw])
    bv = lane_sum(d[2 * gw :])

    @pl.when(j == 0)
    def _():
        acc[:, : 3 * gw] = dw
        bacc[0] = bq
        bacc[1] = bv

    @pl.when(j > 0)
    def _():
        acc[:, : 3 * gw] += dw
        bacc[0] += bq
        bacc[1] += bv

    @pl.when(j == pl.num_programs(1) - 1)
    def _():
        rest = acc.shape[1] - 3 * gw
        bqc = jnp.sum(bacc[0], axis=1, keepdims=True)
        bvc = jnp.sum(bacc[1], axis=1, keepdims=True)
        lane = lax.broadcasted_iota(jnp.int32, (gw, rest), 1)
        vectors = jnp.where(lane == 0, bqc, jnp.where(lane == 1, bvc, vg_ref[...][:, :rest]))
        acc[:, 3 * gw :] = vectors
        write_halves(acc, keep_ref, send_ref, flag_ref[1], rows)


def attn_bwd(flag, saved, dct, xt, w, dyt, vg, steps, before, g0, ng, gw, hd, rows):
    q, k, v, e, c, inv = saved
    width, toks = xt.shape
    groups = width // gw
    blocks = toks // LONG
    nh = gw // hd
    cols = w.shape[1]
    keep, send = half_shapes(gw, rows, cols)
    own = lambda: pl.BlockSpec((gw, LONG), lambda g, j, f: (g0 + g, j))
    return pl.pallas_call(
        functools.partial(attn_bwd_kernel, gw=gw, hd=hd, rows=rows),
        out_shape=[
            jax.ShapeDtypeStruct((width, toks), BF),
            jax.ShapeDtypeStruct((groups * keep[0],) + keep[1:], BF),
            jax.ShapeDtypeStruct((groups * send[0],) + send[1:], BF),
        ],
        grid_spec=pltpu.PrefetchScalarGridSpec(
            num_scalar_prefetch=1,
            grid=(ng, blocks),
            in_specs=[
                own(),
                own(),
                own(),
                pl.BlockSpec((nh, 1, LONG, LONG), lambda g, j, f: (g0 + g, j, 0, 0)),
                own(),
                pl.BlockSpec((8, LONG), lambda g, j, f: (g0 + g, j)),
                own(),
                own(),
                pl.BlockSpec((gw, cols), lambda g, j, f: (g0 + g, 0)),
                own(),
                pl.BlockSpec((gw, 128), lambda g, j, f: (g0 + g, 0)),
            ]
            + anywhere(len(steps) + len(before)),
            out_specs=[
                own(),
                pl.BlockSpec(keep, lambda g, j, f: (g0 + g,) + (0,) * (len(keep) - 1)),
                pl.BlockSpec(send, lambda g, j, f: (g0 + g,) + (0,) * (len(send) - 1)),
            ],
            scratch_shapes=[
                pltpu.VMEM((gw, cols), F32),
                pltpu.VMEM((3 * gw, LONG), F32),
                pltpu.VMEM((2, gw, 128), F32),
                pltpu.VMEM((LONG, LONG), F32),
                pltpu.VMEM((LONG, LONG), F32),
            ],
        ),
        input_output_aliases={12 + len(steps) + i: i for i in range(len(before))},
        compiler_params=params(),
        cost_estimate=cost(7 * ng),
        name="attention_backward",
    )(flag, q, k, v, e, c, inv, dct, xt, w, dyt, vg, *steps, *before)


def ffn_kernel(x_ref, ctx, vec_ref, wo_ref, cot_ref, *refs, shards, gw, vbase):
    wf_refs = refs[:shards]
    rest = refs[shards:]
    out_ref, n1_ref, rs_ref, dh_ref = rest[:4]
    grad_refs = rest[4 : 4 + shards]
    vg_ref = rest[4 + shards]
    wf, h1x, h1t, ua, ub, act, slope, y2, dyl, dyt, acc1, acc2, accb, accv = rest[5 + shards :]
    j = pl.program_id(0)
    last = pl.num_programs(0) - 1
    groups = h1x.shape[0]
    toks = x_ref.shape[1]
    width = groups * gw
    inv_width = 1.0 / width

    def col(i):
        return vec_ref[:, vbase + i : vbase + i + 1].astype(F32)

    def mean(v):
        return jnp.sum(v, axis=0, keepdims=True) * inv_width

    @pl.when(j == 0)
    def _():
        for s in range(shards):
            wf[s] = wf_refs[s][...]
        acc1[...] = jnp.zeros_like(acc1)
        acc2[...] = jnp.zeros_like(acc2)
        accb[...] = jnp.zeros_like(accb)
        accv[...] = jnp.zeros_like(accv)

    y1 = x_ref[...].astype(F32) + dg(wo_ref[...], ctx[...], 0, 0) + col(2)
    center = y1 - mean(y1)
    rs1 = lax.rsqrt(mean(center * center) + EPS)
    rs_ref[...] = jnp.broadcast_to(rs1, rs_ref.shape)
    norm1 = center * rs1
    n1_ref[...] = norm1
    h1 = norm1 * col(3) + col(4)
    y2[...] = (h1 + col(5)).reshape(groups, gw, toks)
    h1x[:, :gw, :] = h1.astype(BF).reshape(groups, gw, toks)
    h1x[:, gw:, :] = jnp.ones((groups, PAD, toks), BF)
    for g in range(groups):
        h1t[g] = h1x[g, :gw, :].T

    chunks = groups * shards

    def first_dot(i, buf):
        buf[...] = dg(wf[i % shards, i // shards, :, :gw], h1x[i // shards], 0, 0)

    def second_dot(i):
        g = i // shards
        s = i % shards
        y2[g] += dg(wf[s, g, :gw, gw : 2 * gw], act[g, s], 0, 0)

    def gelu(i, buf):
        g = i // shards
        s = i % shards
        u = buf[...]
        phi = lax.erf(u * ROOT_HALF) * 0.5 + 0.5
        act[g, s] = (u * phi).astype(BF)
        slope[g, s] = phi + u * INV_ROOT_2PI * jnp.exp2(u * u * HALF_LOG2E)

    first_dot(0, ua)
    first_dot(1, ub)
    gelu(0, ua)

    def forward(k, carry):
        i = 2 * k + 1
        second_dot(i - 1)
        first_dot(i + 1, ua)
        gelu(i, ub)
        second_dot(i)
        first_dot(i + 2, ub)
        gelu(i + 1, ua)
        return carry

    lax.fori_loop(0, chunks // 2 - 1, forward, 0)
    second_dot(chunks - 2)
    gelu(chunks - 1, ub)
    second_dot(chunks - 1)

    yy = y2[...].reshape(width, toks)
    center = yy - mean(yy)
    rs2 = lax.rsqrt(mean(center * center) + EPS)
    norm2 = center * rs2
    out_ref[...] = (norm2 * col(6) + col(7)).astype(BF)
    cot = cot_ref[...].astype(F32)
    e2 = cot * col(6)
    dy2 = (e2 - mean(e2) - norm2 * mean(e2 * norm2)) * rs2
    accv[0] += lane_sum(dy2)
    accv[1] += lane_sum(cot * norm2)
    accv[2] += lane_sum(cot)
    y2[...] = dy2.reshape(groups, gw, toks)
    dyl[...] = dy2.astype(BF).reshape(groups, gw, toks)
    for g in range(groups):
        dyt[g] = dyl[g].T

    def backward(i, carry):
        g = i // shards
        s = i % shards
        dact = dg(wf[s, g, :gw, gw : 2 * gw], dyl[g], 1, 0)
        du = dact * slope[g, s]
        low = du.astype(BF)
        acc2[s, g] += dg(act[g, s], dyt[g], 1, 0)
        y2[g] += dg(wf[s, g, :gw, :gw], low, 1, 0)
        acc1[s, g] += dg(low, h1t[g], 1, 0)
        accb[s, g] += lane_sum(du)
        return carry

    lax.fori_loop(0, groups * shards, backward, 0, unroll=2)
    dh_ref[...] = y2[...].reshape(width, toks)

    @pl.when(j == last)
    def _():
        for s in range(shards):

            def write(g, carry, s=s):
                grad_refs[s][g, :gw, :gw] = acc1[s, g].astype(BF).T
                grad_refs[s][g, :gw, gw : 2 * gw] = acc2[s, g].astype(BF)
                row = jnp.sum(accb[s, g].T, axis=0, keepdims=True)
                tail = jnp.concatenate([row, jnp.zeros_like(row)], axis=1)
                grad_refs[s][g, gw:, :] = jnp.broadcast_to(tail, (PAD, 2 * gw)).astype(BF)
                return carry

            lax.fori_loop(0, groups, write, 0, unroll=2)
        vg_ref[...] = spread(accv, 5)


def spread(sums, first):
    count, width, lanes = sums.shape
    lane = lax.broadcasted_iota(jnp.int32, (width, lanes), 1)
    t = jnp.zeros((width, lanes), F32)
    for i in range(count):
        t = jnp.where(lane == i + first, jnp.sum(sums[i], axis=1, keepdims=True), t)
    return t


def write_halves(full, keep_ref, send_ref, mine, rows):
    if rows % 8:
        keep_ref[...] = full[...].astype(BF)
        send_ref[...] = jnp.zeros_like(send_ref)
        return
    for k in range(keep_ref.shape[0]):
        own = pl.multiple_of((2 * k + mine) * rows, 8)
        other = pl.multiple_of((2 * k + 1 - mine) * rows, 8)
        keep_ref[k] = full[pl.ds(own, rows), :].astype(BF)
        send_ref[k] = full[pl.ds(other, rows), :].astype(BF)


def half_shapes(total, rows, cols):
    if rows % 8:
        return (total, cols), (16, 128)
    return (total // rows // 2, rows, cols), (total // rows // 2, rows, cols)


def core_step(keep, send, rows, index, count):
    if rows % 8:
        keep, send = halves(keep.reshape(-1, rows, keep.shape[-1]), 0, index)
    return keep, swap(send, 0, count)


def norm_kernel(
    me_ref, ctx, n1_ref, rs_ref, dh_ref, vec_ref, wo_ref, vga_ref,
    dy1_ref, dct_ref, keep_ref, send_ref, vg_ref, acco, accv, *, vbase, rows,
):
    j = pl.program_id(0)
    last = pl.num_programs(0) - 1
    inv_width = 1.0 / n1_ref.shape[0]

    def mean(v):
        return jnp.sum(v, axis=0, keepdims=True) * inv_width

    norm1 = n1_ref[...]
    dh1 = dh_ref[...]
    e1 = dh1 * vec_ref[:, vbase + 3 : vbase + 4].astype(F32)
    dy1 = (e1 - mean(e1) - norm1 * mean(e1 * norm1)) * rs_ref[0:1, :]
    dy1_ref[...] = dy1
    low1 = dy1.astype(BF)
    dct_ref[...] = dg(wo_ref[...], low1, 1, 0).astype(BF)
    sums = (lane_sum(dy1), lane_sum(dh1 * norm1), lane_sum(dh1))
    dwo = dg(ctx[...], low1, 1, 1)

    @pl.when(j == 0)
    def _():
        acco[...] = dwo
        for i in range(3):
            accv[i] = sums[i]

    @pl.when(j > 0)
    def _():
        acco[...] += dwo
        for i in range(3):
            accv[i] += sums[i]

    @pl.when(j == last)
    def _():
        write_halves(acco, keep_ref, send_ref, me_ref[1], rows)
        vg_ref[...] = vga_ref[...] + spread(accv, 2)


def whole(shape):
    return pl.BlockSpec(shape, lambda j, *m: (0,) * len(shape), pipeline_mode=pl.Buffered(1))


def ffn_layer(xt, ctx, w, wo, wfs, cott, gw):
    width, toks = xt.shape
    blk = min(LONG, toks)
    shards = len(wfs)
    groups = wfs[0].shape[0]
    vec_block = (3 * gw) // 128
    col_blk = lambda rows: pl.BlockSpec((rows, blk), lambda j: (0, j))
    return pl.pallas_call(
        functools.partial(ffn_kernel, shards=shards, gw=gw, vbase=3 * gw - 128 * vec_block),
        out_shape=[
            jax.ShapeDtypeStruct((width, toks), BF),
            jax.ShapeDtypeStruct((width, toks), F32),
            jax.ShapeDtypeStruct((8, toks), F32),
            jax.ShapeDtypeStruct((width, toks), F32),
        ]
        + [jax.ShapeDtypeStruct(wfs[0].shape, BF)] * shards
        + [jax.ShapeDtypeStruct((width, 128), F32)],
        grid=(toks // blk,),
        in_specs=[
            col_blk(width),
            col_blk(width),
            pl.BlockSpec((width, 128), lambda j: (0, vec_block)),
            whole((width, width)),
            col_blk(width),
        ]
        + [whole(wfs[0].shape) for _ in wfs],
        out_specs=[col_blk(width), col_blk(width), col_blk(8), col_blk(width)]
        + [whole(wfs[0].shape) for _ in wfs]
        + [whole((width, 128))],
        scratch_shapes=[
            pltpu.VMEM((shards,) + wfs[0].shape, BF),
            pltpu.VMEM((groups, gw + PAD, blk), BF),
            pltpu.VMEM((groups, blk, gw), BF),
            pltpu.VMEM((gw, blk), F32),
            pltpu.VMEM((gw, blk), F32),
            pltpu.VMEM((groups, shards, gw, blk), BF),
            pltpu.VMEM((groups, shards, gw, blk), F32),
            pltpu.VMEM((groups, gw, blk), F32),
            pltpu.VMEM((groups, gw, blk), BF),
            pltpu.VMEM((groups, blk, gw), BF),
            pltpu.VMEM((shards, groups, gw, gw), F32),
            pltpu.VMEM((shards, groups, gw, gw), F32),
            pltpu.VMEM((shards, groups, gw, 128), F32),
            pltpu.VMEM((3, width, 128), F32),
        ],
        compiler_params=params(),
        cost_estimate=cost(40),
        name="feed_forward",
    )(xt, ctx, w, wo, cott, *wfs)


def norm_layer(me, ctx, n1, rs1, dh1, w, wo, vga, gw, rows):
    width, toks = n1.shape
    blk = min(LONG, toks)
    vec_block = (3 * gw) // 128
    col_blk = lambda rows: pl.BlockSpec((rows, blk), lambda j, m: (0, j))
    keep, send = half_shapes(width, rows, width)
    return pl.pallas_call(
        functools.partial(norm_kernel, vbase=3 * gw - 128 * vec_block, rows=rows),
        out_shape=[
            jax.ShapeDtypeStruct((width, toks), F32),
            jax.ShapeDtypeStruct((width, toks), BF),
            jax.ShapeDtypeStruct(keep, BF),
            jax.ShapeDtypeStruct(send, BF),
            jax.ShapeDtypeStruct((width, 128), F32),
        ],
        grid_spec=pltpu.PrefetchScalarGridSpec(
            num_scalar_prefetch=1,
            grid=(toks // blk,),
            in_specs=[
                col_blk(width),
                col_blk(width),
                col_blk(8),
                col_blk(width),
                pl.BlockSpec((width, 128), lambda j, m: (0, vec_block)),
                whole((width, width)),
                whole((width, 128)),
            ],
            out_specs=[col_blk(width), col_blk(width), whole(keep), whole(send), whole((width, 128))],
            scratch_shapes=[
                pltpu.VMEM((width, width), F32),
                pltpu.VMEM((3, width, 128), F32),
            ],
        ),
        compiler_params=params(),
        cost_estimate=cost(7),
        name="norm_backward",
    )(me, ctx, n1, rs1, dh1, w, wo, vga)


def swap(a, bit, count):
    return lax.ppermute(a, AXES, [(i, i ^ (1 << bit)) for i in range(count)])


def gather_bit(cur, b, index, count):
    return merge(cur, swap(cur, b, count), b, index)


def merge(cur, got, b, index):
    place = lax.broadcasted_iota(jnp.int32, (1, 2) + (1,) * (cur.ndim - 1), 1)
    new = jnp.where(place == ((index >> b) & 1), cur[:, None], got[:, None])
    return new.reshape((cur.shape[0] * 2,) + cur.shape[1:])


def halves(cur, b, index):
    pair = cur.reshape((cur.shape[0] // 2, 2) + cur.shape[1:])
    mine = (index >> b) & 1
    keep = lax.dynamic_index_in_dim(pair, mine, 1, keepdims=False)
    return keep, lax.dynamic_index_in_dim(pair, 1 - mine, 1, keepdims=False)


def total(terms):
    return sum(t.astype(F32) for t in terms[1:]) + terms[0].astype(F32)


def split(terms, b, index):
    pairs = [halves(t, b, index) for t in terms]
    return [p[0] for p in pairs], total([p[1] for p in pairs]).astype(BF)


def log2(n):
    return n.bit_length() - 1


def body(
    dp, ffn, tokens, long_seq, cotangent, query_weight, key_weight, value_weight, out_weight,
    query_bias, value_bias, out_bias, attn_gain, attn_shift, ffn_in_weight, ffn_in_bias,
    ffn_out_weight, ffn_out_bias, ffn_gain, ffn_shift,
):
    count = dp * ffn
    index = lax.axis_index("dp") * ffn + lax.axis_index("ffn")
    ffn_bits = list(range(log2(ffn)))
    dp_bits = list(range(log2(ffn), log2(count)))
    all_bits = ffn_bits + dp_bits
    width = tokens.shape[1]
    groups = ffn_in_weight.shape[0]
    gw = width // groups
    hd = width // HEADS
    rows = query_weight.shape[0]

    vectors = [query_bias, value_bias, out_bias, attn_gain, attn_shift, ffn_out_bias, ffn_gain, ffn_shift]
    used = 3 * gw + len(vectors)
    cols = -(-used // 128) * 128
    columns = jnp.pad(jnp.stack(vectors), ((0, cols - used), (0, 0))).T
    w = jnp.concatenate([query_weight, key_weight, value_weight, columns], axis=1)[None]
    wo = out_weight[None]
    top = ffn_bits[-1]
    first = jnp.concatenate([ffn_in_weight, ffn_in_bias[:, None, :], jnp.zeros((groups, PAD - 1, gw), BF)], axis=1)
    second = jnp.pad(ffn_out_weight, ((0, 0), (0, PAD), (0, 0)))
    wf = jnp.concatenate([first, second], axis=2)
    xt = tokens.T
    cott = cotangent.T
    flags = jnp.concatenate([long_seq, (index & 1).astype(jnp.int32)[None]])
    both = jnp.concatenate([w, wo], axis=2)
    for n, b in enumerate(reversed(dp_bits[1:])):
        both = gather_bit(both, b, index, count)
        if n == 0:
            both, xt, flags = lax.optimization_barrier((both, xt, flags))
        if n == 1:
            both, cott = lax.optimization_barrier((both, cott))
    both = gather_bit(both, top, index, count)
    both, wf = lax.optimization_barrier((both, wf))
    got_wf = swap(wf, top, count)
    both = both.reshape(both.shape[0] // 2, 2 * rows, both.shape[2])
    w = gather_bit(both[:, :, :cols], dp_bits[0], index, count).reshape(-1, rows, cols)
    wo = both[:, :, cols:]
    for b in reversed(ffn_bits[:-1]):
        w = gather_bit(w, b, index, count)
    w, wo, got_wf = lax.optimization_barrier((w, wo, got_wf))
    w = w.reshape(width, cols)
    got_wo = swap(wo, dp_bits[0], count)
    slots = {0: wf, 1 << top: got_wf}
    for b in reversed(ffn_bits[:-1]):
        slots[1 << b] = swap(wf, b, count)
        slots[(1 << top) + (1 << b)] = swap(got_wf, b, count)

    saved = []
    step = flags
    for i, (g0, ng) in enumerate(FORWARD):
        saved = list(attn_fwd(flags, xt, w, step, saved, g0, ng, gw, hd))
        if i == 0:
            got_wo, saved[4] = lax.optimization_barrier((got_wo, saved[4]))
            wo = merge(wo, got_wo, dp_bits[0], index)
            step = wo = wo.reshape(-1, rows, width)
    for b in reversed(ffn_bits[:-1]):
        wo = gather_bit(wo, b, index, count)
    wo = wo.reshape(width, width)
    ctx = saved[4]
    wfs = [slots[s] for s in range(ffn)]
    outs = ffn_layer(xt, ctx, w, wo, wfs, cott, gw)
    outt, n1, rs1, dh1 = outs[:4]
    gf = outs[4 : 4 + ffn]
    dyt, dct, keep_o, send_o, vg = norm_layer(flags, ctx, n1, rs1, dh1, w, wo, outs[4 + ffn], gw, rows)

    got1 = swap(gf[1], 0, count)
    got3 = swap(gf[3], 0, count)
    step = total([gf[2], got3]).astype(BF)
    got2 = swap(step, top, count)
    keep_o, got_o = core_step(keep_o, send_o, rows, index, count)

    grads = []
    for i, (g0, ng) in enumerate(BACKWARD):
        steps = [step] if i < 2 else [step, send_o]
        grads = list(attn_bwd(flags, saved, dct, xt, w, dyt, vg, steps, grads, g0, ng, gw, hd, rows))
        if i == 0:
            got_o, grads[0] = lax.optimization_barrier((got_o, grads[0]))
            terms_o, send_o = split([keep_o, got_o], top, index)
            got2, send_o, grads[0] = lax.optimization_barrier((got2, send_o, grads[0]))
            got_o = swap(send_o, top, count)
            lead = gf[0].shape
            terms_f = [t.reshape(dp, -1, lead[-1]) for t in (gf[0], got1, got2)]
            terms_f, step = split(terms_f, dp_bits[0], index)
            got_f = swap(step, dp_bits[0], count)
        if i == 1:
            got_f, got_o, grads[0] = lax.optimization_barrier((got_f, got_o, grads[0]))
            terms_f, step = split(terms_f + [got_f], dp_bits[1], index)
            terms_o, send_o = split(terms_o + [got_o], dp_bits[0], index)
            got_f = swap(step, dp_bits[1], count)
            got_o = swap(send_o, dp_bits[0], count)
        if i == 2:
            got_f, got_o, grads[1], grads[2] = lax.optimization_barrier((got_f, got_o, grads[1], grads[2]))
    terms_f, send_f = split(terms_f + [got_f], dp_bits[2], index)
    got_f = swap(send_f, dp_bits[2], count)
    keep_w, got_w = core_step(grads[1], grads[2], rows, index, count)
    keep_w, send_w = halves(total([keep_w, got_w]).astype(BF), top, index)
    keep_w, got_f = lax.optimization_barrier((keep_w, got_f))
    got_w = swap(send_w, top, count)
    terms_f = terms_f + [got_f]
    for b in dp_bits[3:]:
        terms_f, send_f = split(terms_f, b, index)
        terms_f = terms_f + [swap(send_f, b, count)]
    ffn_sum = total(terms_f).astype(BF)
    ffn_sum, outt = lax.optimization_barrier((ffn_sum, outt))
    rows_first = Layout(major_to_minor=(0, 1))
    output = with_layout_constraint(outt.T, rows_first)
    got_f = swap(ffn_sum, dp_bits[-1], count)
    got_w, got_f, output = lax.optimization_barrier((got_w, got_f, output))
    ffn_sum = merge(ffn_sum, got_f, dp_bits[-1], index)
    terms_w, send_w = split([keep_w, got_w], dp_bits[0], index)
    got_w = swap(send_w, dp_bits[0], count)
    terms_w[0], grads[0] = lax.optimization_barrier((terms_w[0], grads[0]))
    grad_tokens = with_layout_constraint(grads[0].T, rows_first)
    got_f = swap(ffn_sum, dp_bits[-2], count)
    got_w, got_f, grad_tokens = lax.optimization_barrier((got_w, got_f, grad_tokens))
    ffn_sum = merge(ffn_sum, got_f, dp_bits[-2], index)

    terms = [jnp.concatenate([total(terms_w + [got_w]), total(terms_o + [got_o])], axis=2).astype(BF)]
    for b in dp_bits[1:]:
        terms, send_w = split(terms, b, index)
        terms = terms + [swap(send_w, b, count)]
    both = total(terms)[0]
    dw_sum = both[:, :cols]
    dwo_sum = both[:, cols:]
    rest = dw_sum[:, 3 * gw :].T
    head = [dw_sum[:, i * gw : (i + 1) * gw] for i in range(3)]

    for b in reversed(dp_bits[1:-2]):
        ffn_sum = gather_bit(ffn_sum, b, index, count)
    got_f = swap(ffn_sum, dp_bits[0], count)
    got_f, rest, head, dwo_sum = lax.optimization_barrier((got_f, rest, head, dwo_sum))
    ffn_sum = merge(ffn_sum, got_f, dp_bits[0], index).reshape(lead).astype(F32)
    vec = lambda i: rest[i]
    return (
        output,
        grad_tokens,
        head[0],
        head[1],
        head[2],
        dwo_sum,
        vec(0),
        vec(1),
        vec(2),
        vec(3),
        vec(4),
        ffn_sum[:, :gw, :gw],
        ffn_sum[:, gw, :gw],
        ffn_sum[:, :gw, gw:],
        vec(5),
        vec(6),
        vec(7),
    )


def solution(mesh):
    both = P(AXES)
    rows = P(AXES, None)
    return jax.shard_map(
        functools.partial(body, mesh.shape["dp"], mesh.shape["ffn"]),
        mesh=mesh,
        in_specs=(
            rows, both, rows, rows, rows, rows, rows, both, both, both, both, both,
            P(None, None, "ffn"), P(None, "ffn"), P(None, "ffn", None), both, both, both,
        ),
        out_specs=(
            rows, rows, rows, rows, rows, rows, both, both, both, both, both,
            P(None, None, "ffn"), P(None, "ffn"), P(None, "ffn", None), both, both, both,
        ),
        check_vma=False,
    )
```

```python
import functools

import jax
import jax.numpy as jnp
from jax import lax
from jax.experimental import pallas as pl
from jax.experimental.layout import Layout, with_layout_constraint
from jax.experimental.pallas import tpu as pltpu
from jax.sharding import PartitionSpec as P

F32 = jnp.float32
BF = jnp.bfloat16
HEADS = 12
LONG = 512
SHORT = 128
EPS = 1e-12
AXES = ("dp", "ffn")
PAD = 16

ROOT_HALF = 0.7071067811865476
INV_ROOT_2PI = 0.3989422804014327
HALF_LOG2E = -0.7213475204444817
FORWARD = ((0, 2), (2, 2))
BACKWARD = ((0, 2), (2, 1), (3, 1))


def dg(a, b, ca, cb):
    return lax.dot_general(a, b, (((ca,), (cb,)), ((), ())), preferred_element_type=F32)


def lane_sum(v):
    out = v[:, :128]
    for c in range(128, v.shape[1], 128):
        out = out + v[:, c : c + 128]
    return out


def params():
    return pltpu.CompilerParams(vmem_limit_bytes=63 << 20)


def cost(us):
    return pl.CostEstimate(flops=int(us * 1e9), bytes_accessed=int(us * 3e6), transcendentals=0)


def across(s, outside):
    rows = []
    for a in range(0, LONG, SHORT):
        cells = []
        for b in range(0, LONG, SHORT):
            cell = s[a : a + SHORT, b : b + SHORT]
            cells.append(cell if a == b else cell + outside)
        rows.append(jnp.concatenate(cells, axis=1))
    return jnp.concatenate(rows, axis=0)


def attn_fwd_kernel(flag_ref, x_ref, w_ref, step_ref, *refs, gw, hd):
    q_ref, k_ref, v_ref, e_ref, c_ref, inv_ref, sa, sb = refs[-8:]
    w = w_ref[...]
    p = dg(w[:, : 3 * gw], x_ref[...], 0, 0)
    bq = w[:, 3 * gw : 3 * gw + 1].astype(F32)
    bv = w[:, 3 * gw + 1 : 3 * gw + 2].astype(F32)
    q_ref[...] = (p[:gw] + bq).astype(BF)
    k_ref[...] = p[gw : 2 * gw].astype(BF)
    v_ref[...] = (p[2 * gw :] + bv).astype(BF)
    inv_ref[...] = jnp.zeros_like(inv_ref)
    outside = jnp.where(flag_ref[0] == 1, 0.0, -1e9).astype(F32)
    ones = jnp.ones((16, LONG), BF)
    heads = [slice(h * hd, (h + 1) * hd) for h in range(gw // hd)]

    def scores(h, buf):
        q = q_ref[heads[h], :] * jnp.asarray(hd**-0.5, BF)
        buf[...] = dg(k_ref[heads[h], :], q, 0, 0)

    bufs = (sa, sb)
    scores(0, sa)
    for h, r in enumerate(heads):
        if h + 1 < len(heads):
            scores(h + 1, bufs[(h + 1) % 2])
        s = across(bufs[h % 2][...], outside)
        m = jnp.max(s, axis=0, keepdims=True)
        e = jnp.exp(s - m).astype(BF)
        e_ref[h, 0] = e
        o = dg(jnp.concatenate([v_ref[r, :], ones], 0), e, 1, 0)
        inv = 1.0 / o[hd : hd + 1]
        c_ref[r, :] = (o[:hd] * inv).astype(BF)
        inv_ref[h : h + 1, :] = inv


def anywhere(count):
    return [pl.BlockSpec(memory_space=pl.ANY) for _ in range(count)]


def attn_fwd(flag, xt, w, step, before, g0, ng, gw, hd):
    width, toks = xt.shape
    groups = width // gw
    blocks = toks // LONG
    nh = gw // hd
    own = lambda: pl.BlockSpec((gw, LONG), lambda g, j, f: (g0 + g, j))
    return pl.pallas_call(
        functools.partial(attn_fwd_kernel, gw=gw, hd=hd),
        out_shape=[jax.ShapeDtypeStruct((width, toks), BF)] * 3
        + [
            jax.ShapeDtypeStruct((groups * nh, blocks, LONG, LONG), BF),
            jax.ShapeDtypeStruct((width, toks), BF),
            jax.ShapeDtypeStruct((groups * 8, toks), F32),
        ],
        grid_spec=pltpu.PrefetchScalarGridSpec(
            num_scalar_prefetch=1,
            grid=(ng, blocks),
            in_specs=[own(), pl.BlockSpec((gw, w.shape[1]), lambda g, j, f: (g0 + g, 0))] + anywhere(1 + len(before)),
            out_specs=[
                own(),
                own(),
                own(),
                pl.BlockSpec((nh, 1, LONG, LONG), lambda g, j, f: (g0 + g, j, 0, 0)),
                own(),
                pl.BlockSpec((8, LONG), lambda g, j, f: (g0 + g, j)),
            ],
            scratch_shapes=[pltpu.VMEM((LONG, LONG), F32)] * 2,
        ),
        input_output_aliases={4 + i: i for i in range(len(before))},
        compiler_params=params(),
        cost_estimate=cost(5 * ng),
        name="attention_forward",
    )(flag, xt, w, step, *before)


def attn_bwd_kernel(
    flag_ref, q_ref, k_ref, v_ref, e_ref, c_ref, inv_ref, dc_ref, x_ref, w_ref, dy_ref, vg_ref, step_ref,
    *refs, gw, hd, rows,
):
    g_ref, keep_ref, send_ref, acc, dq, bacc, pa, pb = refs[-8:]
    nh = gw // hd
    j = pl.program_id(1)
    heads = [slice(h * hd, (h + 1) * hd) for h in range(nh)]
    scaled = []

    def grad_probs(h, buf):
        dc = dc_ref[heads[h], :].astype(F32)
        inv = inv_ref[h : h + 1, :]
        total = jnp.sum(dc * c_ref[heads[h], :].astype(F32), axis=0, keepdims=True) * inv
        scaled.append(((dc * inv).astype(BF), total))
        buf[...] = dg(v_ref[heads[h], :], scaled[h][0], 0, 0)

    bufs = (pa, pb)
    grad_probs(0, pa)
    for h, r in enumerate(heads):
        if h + 1 < nh:
            grad_probs(h + 1, bufs[(h + 1) % 2])
        dci, total = scaled[h]
        e = e_ref[h, 0]
        dq[2 * gw + h * hd : 2 * gw + (h + 1) * hd, :] = dg(dci, e, 1, 1)
        ds = (e.astype(F32) * (bufs[h % 2][...] - total)).astype(BF)
        qs = q_ref[r, :] * jnp.asarray(hd**-0.5, BF)
        dq[gw + h * hd : gw + (h + 1) * hd, :] = dg(qs, ds, 1, 1)
        dq[r, :] = dg(k_ref[r, :], ds, 1, 0) * (hd**-0.5)

    d = dq[...]
    dl = d.astype(BF)
    w = w_ref[...]
    g_ref[...] = (dy_ref[...] + dg(w[:, : 3 * gw], dl, 1, 0)).astype(BF)
    dw = dg(x_ref[...], dl, 1, 1)
    bq = lane_sum(d[:gw])
    bv = lane_sum(d[2 * gw :])

    @pl.when(j == 0)
    def _():
        acc[:, : 3 * gw] = dw
        bacc[0] = bq
        bacc[1] = bv

    @pl.when(j > 0)
    def _():
        acc[:, : 3 * gw] += dw
        bacc[0] += bq
        bacc[1] += bv

    @pl.when(j == pl.num_programs(1) - 1)
    def _():
        rest = acc.shape[1] - 3 * gw
        bqc = jnp.sum(bacc[0], axis=1, keepdims=True)
        bvc = jnp.sum(bacc[1], axis=1, keepdims=True)
        lane = lax.broadcasted_iota(jnp.int32, (gw, rest), 1)
        vectors = jnp.where(lane == 0, bqc, jnp.where(lane == 1, bvc, vg_ref[...][:, :rest]))
        acc[:, 3 * gw :] = vectors
        write_halves(acc, keep_ref, send_ref, flag_ref[1], rows)


def attn_bwd(flag, saved, dct, xt, w, dyt, vg, step, before, g0, ng, gw, hd, rows):
    q, k, v, e, c, inv = saved
    width, toks = xt.shape
    groups = width // gw
    blocks = toks // LONG
    nh = gw // hd
    cols = w.shape[1]
    keep, send = half_shapes(gw, rows, cols)
    own = lambda: pl.BlockSpec((gw, LONG), lambda g, j, f: (g0 + g, j))
    return pl.pallas_call(
        functools.partial(attn_bwd_kernel, gw=gw, hd=hd, rows=rows),
        out_shape=[
            jax.ShapeDtypeStruct((width, toks), BF),
            jax.ShapeDtypeStruct((groups * keep[0],) + keep[1:], BF),
            jax.ShapeDtypeStruct((groups * send[0],) + send[1:], BF),
        ],
        grid_spec=pltpu.PrefetchScalarGridSpec(
            num_scalar_prefetch=1,
            grid=(ng, blocks),
            in_specs=[
                own(),
                own(),
                own(),
                pl.BlockSpec((nh, 1, LONG, LONG), lambda g, j, f: (g0 + g, j, 0, 0)),
                own(),
                pl.BlockSpec((8, LONG), lambda g, j, f: (g0 + g, j)),
                own(),
                own(),
                pl.BlockSpec((gw, cols), lambda g, j, f: (g0 + g, 0)),
                own(),
                pl.BlockSpec((gw, 128), lambda g, j, f: (g0 + g, 0)),
            ]
            + anywhere(1 + len(before)),
            out_specs=[
                own(),
                pl.BlockSpec(keep, lambda g, j, f: (g0 + g,) + (0,) * (len(keep) - 1)),
                pl.BlockSpec(send, lambda g, j, f: (g0 + g,) + (0,) * (len(send) - 1)),
            ],
            scratch_shapes=[
                pltpu.VMEM((gw, cols), F32),
                pltpu.VMEM((3 * gw, LONG), F32),
                pltpu.VMEM((2, gw, 128), F32),
                pltpu.VMEM((LONG, LONG), F32),
                pltpu.VMEM((LONG, LONG), F32),
            ],
        ),
        input_output_aliases={13 + i: i for i in range(len(before))},
        compiler_params=params(),
        cost_estimate=cost(7 * ng),
        name="attention_backward",
    )(flag, q, k, v, e, c, inv, dct, xt, w, dyt, vg, step, *before)


def ffn_kernel(x_ref, ctx, vec_ref, wo_ref, cot_ref, *refs, shards, gw, vbase):
    wf_refs = refs[:shards]
    rest = refs[shards:]
    out_ref, n1_ref, rs_ref, dh_ref = rest[:4]
    grad_refs = rest[4 : 4 + shards]
    vg_ref = rest[4 + shards]
    wf, h1x, h1t, ua, ub, act, slope, y2, dyl, dyt, acc1, acc2, accb, accv = rest[5 + shards :]
    j = pl.program_id(0)
    last = pl.num_programs(0) - 1
    groups = h1x.shape[0]
    toks = x_ref.shape[1]
    width = groups * gw
    inv_width = 1.0 / width

    def col(i):
        return vec_ref[:, vbase + i : vbase + i + 1].astype(F32)

    def mean(v):
        return jnp.sum(v, axis=0, keepdims=True) * inv_width

    @pl.when(j == 0)
    def _():
        for s in range(shards):
            wf[s] = wf_refs[s][...]
        acc1[...] = jnp.zeros_like(acc1)
        acc2[...] = jnp.zeros_like(acc2)
        accb[...] = jnp.zeros_like(accb)
        accv[...] = jnp.zeros_like(accv)

    y1 = x_ref[...].astype(F32) + dg(wo_ref[...], ctx[...], 0, 0) + col(2)
    center = y1 - mean(y1)
    rs1 = lax.rsqrt(mean(center * center) + EPS)
    rs_ref[...] = jnp.broadcast_to(rs1, rs_ref.shape)
    norm1 = center * rs1
    n1_ref[...] = norm1
    h1 = norm1 * col(3) + col(4)
    y2[...] = (h1 + col(5)).reshape(groups, gw, toks)
    h1x[:, :gw, :] = h1.astype(BF).reshape(groups, gw, toks)
    h1x[:, gw:, :] = jnp.ones((groups, PAD, toks), BF)
    for g in range(groups):
        h1t[g] = h1x[g, :gw, :].T

    chunks = groups * shards

    def first_dot(i, buf):
        buf[...] = dg(wf[i % shards, i // shards, :, :gw], h1x[i // shards], 0, 0)

    def second_dot(i):
        g = i // shards
        s = i % shards
        y2[g] += dg(wf[s, g, :gw, gw : 2 * gw], act[g, s], 0, 0)

    def gelu(i, buf):
        g = i // shards
        s = i % shards
        u = buf[...]
        phi = lax.erf(u * ROOT_HALF) * 0.5 + 0.5
        act[g, s] = (u * phi).astype(BF)
        slope[g, s] = phi + u * INV_ROOT_2PI * jnp.exp2(u * u * HALF_LOG2E)

    first_dot(0, ua)
    first_dot(1, ub)
    gelu(0, ua)

    def forward(k, carry):
        i = 2 * k + 1
        second_dot(i - 1)
        first_dot(i + 1, ua)
        gelu(i, ub)
        second_dot(i)
        first_dot(i + 2, ub)
        gelu(i + 1, ua)
        return carry

    lax.fori_loop(0, chunks // 2 - 1, forward, 0)
    second_dot(chunks - 2)
    gelu(chunks - 1, ub)
    second_dot(chunks - 1)

    yy = y2[...].reshape(width, toks)
    center = yy - mean(yy)
    rs2 = lax.rsqrt(mean(center * center) + EPS)
    norm2 = center * rs2
    out_ref[...] = (norm2 * col(6) + col(7)).astype(BF)
    cot = cot_ref[...].astype(F32)
    e2 = cot * col(6)
    dy2 = (e2 - mean(e2) - norm2 * mean(e2 * norm2)) * rs2
    accv[0] += lane_sum(dy2)
    accv[1] += lane_sum(cot * norm2)
    accv[2] += lane_sum(cot)
    y2[...] = dy2.reshape(groups, gw, toks)
    dyl[...] = dy2.astype(BF).reshape(groups, gw, toks)
    for g in range(groups):
        dyt[g] = dyl[g].T

    def backward(i, carry):
        g = i // shards
        s = i % shards
        dact = dg(wf[s, g, :gw, gw : 2 * gw], dyl[g], 1, 0)
        du = dact * slope[g, s]
        low = du.astype(BF)
        acc2[s, g] += dg(act[g, s], dyt[g], 1, 0)
        y2[g] += dg(wf[s, g, :gw, :gw], low, 1, 0)
        acc1[s, g] += dg(low, h1t[g], 1, 0)
        accb[s, g] += lane_sum(du)
        return carry

    lax.fori_loop(0, groups * shards, backward, 0, unroll=2)
    dh_ref[...] = y2[...].reshape(width, toks)

    @pl.when(j == last)
    def _():
        for s in range(shards):

            def write(g, carry, s=s):
                grad_refs[s][g, :gw, :gw] = acc1[s, g].astype(BF).T
                grad_refs[s][g, :gw, gw : 2 * gw] = acc2[s, g].astype(BF)
                row = jnp.sum(accb[s, g].T, axis=0, keepdims=True)
                tail = jnp.concatenate([row, jnp.zeros_like(row)], axis=1)
                grad_refs[s][g, gw:, :] = jnp.broadcast_to(tail, (PAD, 2 * gw)).astype(BF)
                return carry

            lax.fori_loop(0, groups, write, 0, unroll=2)
        vg_ref[...] = spread(accv, 5)


def spread(sums, first):
    count, width, lanes = sums.shape
    lane = lax.broadcasted_iota(jnp.int32, (width, lanes), 1)
    t = jnp.zeros((width, lanes), F32)
    for i in range(count):
        t = jnp.where(lane == i + first, jnp.sum(sums[i], axis=1, keepdims=True), t)
    return t


def write_halves(full, keep_ref, send_ref, mine, rows):
    if rows % 8:
        keep_ref[...] = full[...].astype(BF)
        send_ref[...] = jnp.zeros_like(send_ref)
        return
    for k in range(keep_ref.shape[0]):
        own = pl.multiple_of((2 * k + mine) * rows, 8)
        other = pl.multiple_of((2 * k + 1 - mine) * rows, 8)
        keep_ref[k] = full[pl.ds(own, rows), :].astype(BF)
        send_ref[k] = full[pl.ds(other, rows), :].astype(BF)


def half_shapes(total, rows, cols):
    if rows % 8:
        return (total, cols), (16, 128)
    return (total // rows // 2, rows, cols), (total // rows // 2, rows, cols)


def core_step(keep, send, rows, index, count):
    if rows % 8:
        keep, send = halves(keep.reshape(-1, rows, keep.shape[-1]), 0, index)
    return keep, swap(send, 0, count)


def norm_kernel(
    me_ref, ctx, n1_ref, rs_ref, dh_ref, vec_ref, wo_ref, vga_ref,
    dy1_ref, dct_ref, keep_ref, send_ref, vg_ref, acco, accv, *, vbase, rows,
):
    j = pl.program_id(0)
    last = pl.num_programs(0) - 1
    inv_width = 1.0 / n1_ref.shape[0]

    def mean(v):
        return jnp.sum(v, axis=0, keepdims=True) * inv_width

    norm1 = n1_ref[...]
    dh1 = dh_ref[...]
    e1 = dh1 * vec_ref[:, vbase + 3 : vbase + 4].astype(F32)
    dy1 = (e1 - mean(e1) - norm1 * mean(e1 * norm1)) * rs_ref[0:1, :]
    dy1_ref[...] = dy1
    low1 = dy1.astype(BF)
    dct_ref[...] = dg(wo_ref[...], low1, 1, 0).astype(BF)
    sums = (lane_sum(dy1), lane_sum(dh1 * norm1), lane_sum(dh1))
    dwo = dg(ctx[...], low1, 1, 1)

    @pl.when(j == 0)
    def _():
        acco[...] = dwo
        for i in range(3):
            accv[i] = sums[i]

    @pl.when(j > 0)
    def _():
        acco[...] += dwo
        for i in range(3):
            accv[i] += sums[i]

    @pl.when(j == last)
    def _():
        write_halves(acco, keep_ref, send_ref, me_ref[1], rows)
        vg_ref[...] = vga_ref[...] + spread(accv, 2)


def whole(shape):
    return pl.BlockSpec(shape, lambda j, *m: (0,) * len(shape), pipeline_mode=pl.Buffered(1))


def ffn_layer(xt, ctx, w, wo, wfs, cott, gw):
    width, toks = xt.shape
    blk = min(LONG, toks)
    shards = len(wfs)
    groups = wfs[0].shape[0]
    vec_block = (3 * gw) // 128
    col_blk = lambda rows: pl.BlockSpec((rows, blk), lambda j: (0, j))
    return pl.pallas_call(
        functools.partial(ffn_kernel, shards=shards, gw=gw, vbase=3 * gw - 128 * vec_block),
        out_shape=[
            jax.ShapeDtypeStruct((width, toks), BF),
            jax.ShapeDtypeStruct((width, toks), F32),
            jax.ShapeDtypeStruct((8, toks), F32),
            jax.ShapeDtypeStruct((width, toks), F32),
        ]
        + [jax.ShapeDtypeStruct(wfs[0].shape, BF)] * shards
        + [jax.ShapeDtypeStruct((width, 128), F32)],
        grid=(toks // blk,),
        in_specs=[
            col_blk(width),
            col_blk(width),
            pl.BlockSpec((width, 128), lambda j: (0, vec_block)),
            whole((width, width)),
            col_blk(width),
        ]
        + [whole(wfs[0].shape) for _ in wfs],
        out_specs=[col_blk(width), col_blk(width), col_blk(8), col_blk(width)]
        + [whole(wfs[0].shape) for _ in wfs]
        + [whole((width, 128))],
        scratch_shapes=[
            pltpu.VMEM((shards,) + wfs[0].shape, BF),
            pltpu.VMEM((groups, gw + PAD, blk), BF),
            pltpu.VMEM((groups, blk, gw), BF),
            pltpu.VMEM((gw, blk), F32),
            pltpu.VMEM((gw, blk), F32),
            pltpu.VMEM((groups, shards, gw, blk), BF),
            pltpu.VMEM((groups, shards, gw, blk), F32),
            pltpu.VMEM((groups, gw, blk), F32),
            pltpu.VMEM((groups, gw, blk), BF),
            pltpu.VMEM((groups, blk, gw), BF),
            pltpu.VMEM((shards, groups, gw, gw), F32),
            pltpu.VMEM((shards, groups, gw, gw), F32),
            pltpu.VMEM((shards, groups, gw, 128), F32),
            pltpu.VMEM((3, width, 128), F32),
        ],
        compiler_params=params(),
        cost_estimate=cost(40),
        name="feed_forward",
    )(xt, ctx, w, wo, cott, *wfs)


def norm_layer(me, ctx, n1, rs1, dh1, w, wo, vga, gw, rows):
    width, toks = n1.shape
    blk = min(LONG, toks)
    vec_block = (3 * gw) // 128
    col_blk = lambda rows: pl.BlockSpec((rows, blk), lambda j, m: (0, j))
    keep, send = half_shapes(width, rows, width)
    return pl.pallas_call(
        functools.partial(norm_kernel, vbase=3 * gw - 128 * vec_block, rows=rows),
        out_shape=[
            jax.ShapeDtypeStruct((width, toks), F32),
            jax.ShapeDtypeStruct((width, toks), BF),
            jax.ShapeDtypeStruct(keep, BF),
            jax.ShapeDtypeStruct(send, BF),
            jax.ShapeDtypeStruct((width, 128), F32),
        ],
        grid_spec=pltpu.PrefetchScalarGridSpec(
            num_scalar_prefetch=1,
            grid=(toks // blk,),
            in_specs=[
                col_blk(width),
                col_blk(width),
                col_blk(8),
                col_blk(width),
                pl.BlockSpec((width, 128), lambda j, m: (0, vec_block)),
                whole((width, width)),
                whole((width, 128)),
            ],
            out_specs=[col_blk(width), col_blk(width), whole(keep), whole(send), whole((width, 128))],
            scratch_shapes=[
                pltpu.VMEM((width, width), F32),
                pltpu.VMEM((3, width, 128), F32),
            ],
        ),
        compiler_params=params(),
        cost_estimate=cost(7),
        name="norm_backward",
    )(me, ctx, n1, rs1, dh1, w, wo, vga)


def swap(a, bit, count):
    return lax.ppermute(a, AXES, [(i, i ^ (1 << bit)) for i in range(count)])


def gather_bit(cur, b, index, count):
    return merge(cur, swap(cur, b, count), b, index)


def merge(cur, got, b, index):
    place = lax.broadcasted_iota(jnp.int32, (1, 2) + (1,) * (cur.ndim - 1), 1)
    new = jnp.where(place == ((index >> b) & 1), cur[:, None], got[:, None])
    return new.reshape((cur.shape[0] * 2,) + cur.shape[1:])


def halves(cur, b, index):
    pair = cur.reshape((cur.shape[0] // 2, 2) + cur.shape[1:])
    mine = (index >> b) & 1
    keep = lax.dynamic_index_in_dim(pair, mine, 1, keepdims=False)
    return keep, lax.dynamic_index_in_dim(pair, 1 - mine, 1, keepdims=False)


def reduce_bit(cur, b, index, count):
    keep, send = halves(cur, b, index)
    return keep.astype(F32) + swap(send, b, count).astype(F32)


def log2(n):
    return n.bit_length() - 1


def body(
    dp, ffn, tokens, long_seq, cotangent, query_weight, key_weight, value_weight, out_weight,
    query_bias, value_bias, out_bias, attn_gain, attn_shift, ffn_in_weight, ffn_in_bias,
    ffn_out_weight, ffn_out_bias, ffn_gain, ffn_shift,
):
    count = dp * ffn
    index = lax.axis_index("dp") * ffn + lax.axis_index("ffn")
    ffn_bits = list(range(log2(ffn)))
    dp_bits = list(range(log2(ffn), log2(count)))
    all_bits = ffn_bits + dp_bits
    width = tokens.shape[1]
    groups = ffn_in_weight.shape[0]
    gw = width // groups
    hd = width // HEADS
    rows = query_weight.shape[0]

    vectors = [query_bias, value_bias, out_bias, attn_gain, attn_shift, ffn_out_bias, ffn_gain, ffn_shift]
    used = 3 * gw + len(vectors)
    cols = -(-used // 128) * 128
    columns = jnp.pad(jnp.stack(vectors), ((0, cols - used), (0, 0))).T
    w = jnp.concatenate([query_weight, key_weight, value_weight, columns], axis=1)[None]
    wo = out_weight[None]
    top = ffn_bits[-1]
    first = jnp.concatenate([ffn_in_weight, ffn_in_bias[:, None, :], jnp.zeros((groups, PAD - 1, gw), BF)], axis=1)
    second = jnp.pad(ffn_out_weight, ((0, 0), (0, PAD), (0, 0)))
    wf = jnp.concatenate([first, second], axis=2)
    xt = tokens.T
    cott = cotangent.T
    flags = jnp.concatenate([long_seq, (index & 1).astype(jnp.int32)[None]])
    both = jnp.concatenate([w, wo], axis=2)
    for n, b in enumerate(reversed(dp_bits[1:])):
        both = gather_bit(both, b, index, count)
        if n == 0:
            both, xt, flags = lax.optimization_barrier((both, xt, flags))
        if n == 1:
            both, cott = lax.optimization_barrier((both, cott))
    both = gather_bit(both, top, index, count)
    both, wf = lax.optimization_barrier((both, wf))
    got_wf = swap(wf, top, count)
    both = both.reshape(both.shape[0] // 2, 2 * rows, both.shape[2])
    w = gather_bit(both[:, :, :cols], dp_bits[0], index, count).reshape(-1, rows, cols)
    wo = both[:, :, cols:]
    for b in reversed(ffn_bits[:-1]):
        w = gather_bit(w, b, index, count)
    w, wo = lax.optimization_barrier((w, wo))
    w = w.reshape(width, cols)
    got_wo = swap(wo, dp_bits[0], count)

    saved = []
    step = flags
    for i, (g0, ng) in enumerate(FORWARD):
        saved = list(attn_fwd(flags, xt, w, step, saved, g0, ng, gw, hd))
        if i == 0:
            got_wo, saved[4] = lax.optimization_barrier((got_wo, saved[4]))
            wo = merge(wo, got_wo, dp_bits[0], index)
            step = wo = wo.reshape(-1, rows, width)
            got_wo = swap(wo, 0, count)
        if i == 1:
            got_wf, got_wo, saved[4] = lax.optimization_barrier((got_wf, got_wo, saved[4]))
    wo = merge(wo, got_wo, 0, index).reshape(width, width)
    wfs = [wf, swap(wf, 0, count), got_wf, swap(got_wf, 0, count)]
    ctx = saved[4]
    outs = ffn_layer(xt, ctx, w, wo, wfs, cott, gw)
    outt, n1, rs1, dh1 = outs[:4]
    gf = outs[4 : 4 + ffn]
    dyt, dct, keep_o, send_o, vg = norm_layer(flags, ctx, n1, rs1, dh1, w, wo, outs[4 + ffn], gw, rows)

    def add(keep, got):
        return (keep.astype(F32) + got.astype(F32)).astype(BF)

    got1 = swap(gf[1], 0, count)
    got3 = swap(gf[3], 0, count)
    send = add(gf[2], got3)
    got2 = swap(send, top, count)
    keep_o, got_o = core_step(keep_o, send_o, rows, index, count)

    grads = []
    step = send
    for i, (g0, ng) in enumerate(BACKWARD):
        grads = list(attn_bwd(flags, saved, dct, xt, w, dyt, vg, step, grads, g0, ng, gw, hd, rows))
        if i == 0:
            got_o, grads[0] = lax.optimization_barrier((got_o, grads[0]))
            keep_o, send_o = halves(add(keep_o, got_o), top, index)
            got2, send_o, grads[0] = lax.optimization_barrier((got2, send_o, grads[0]))
            got_o = swap(send_o, top, count)
            mine = (gf[0].astype(F32) + got1.astype(F32) + got2.astype(F32)).astype(BF)
            keep_f, step = halves(mine.reshape(dp, -1, mine.shape[-1]), dp_bits[0], index)
            got_f = swap(step, dp_bits[0], count)
        if i == 1:
            got_f, got_o, grads[0] = lax.optimization_barrier((got_f, got_o, grads[0]))
            keep_f, step = halves(add(keep_f, got_f), dp_bits[1], index)
            got_f = swap(step, dp_bits[1], count)
            keep_o, send_o = halves(add(keep_o, got_o), dp_bits[0], index)
            got_o = swap(send_o, dp_bits[0], count)
        if i == 2:
            got_f, got_o, grads[1] = lax.optimization_barrier((got_f, got_o, grads[1]))
    ffn_sum = add(keep_f, got_f)
    keep_f, send_f = halves(ffn_sum, dp_bits[2], index)
    got_f = swap(send_f, dp_bits[2], count)
    keep_w, got_w = core_step(grads[1], grads[2], rows, index, count)
    keep_w, send_w = halves(add(keep_w, got_w), top, index)
    keep_w, got_f, outt = lax.optimization_barrier((keep_w, got_f, outt))
    got_w = swap(send_w, top, count)
    ffn_sum = add(keep_f, got_f)
    for b in dp_bits[3:]:
        ffn_sum = reduce_bit(ffn_sum, b, index, count).astype(BF)
    rows_first = Layout(major_to_minor=(0, 1))
    output = with_layout_constraint(outt.T, rows_first)
    got_w, output = lax.optimization_barrier((got_w, output))
    keep_w, send_w = halves(add(keep_w, got_w), dp_bits[0], index)
    got_w = swap(send_w, dp_bits[0], count)
    keep_w, grads[0] = lax.optimization_barrier((keep_w, grads[0]))
    grad_tokens = with_layout_constraint(grads[0].T, rows_first)
    got_w, grad_tokens = lax.optimization_barrier((got_w, grad_tokens))

    for b in reversed(dp_bits):
        ffn_sum = gather_bit(ffn_sum, b, index, count)
    ffn_sum = ffn_sum.reshape(mine.shape).astype(F32)

    both = jnp.concatenate([add(keep_w, got_w), add(keep_o, got_o)], axis=2)
    for b in dp_bits[1:]:
        both = reduce_bit(both, b, index, count)
        if b != dp_bits[-1]:
            both = both.astype(BF)
    dw_sum = both[0, :, :cols]
    dwo_sum = both[0, :, cols:]
    vec = lambda i: dw_sum[:, 3 * gw + i]
    return (
        output,
        grad_tokens,
        dw_sum[:, :gw],
        dw_sum[:, gw : 2 * gw],
        dw_sum[:, 2 * gw : 3 * gw],
        dwo_sum,
        vec(0),
        vec(1),
        vec(2),
        vec(3),
        vec(4),
        ffn_sum[:, :gw, :gw],
        ffn_sum[:, gw, :gw],
        ffn_sum[:, :gw, gw:],
        vec(5),
        vec(6),
        vec(7),
    )


def solution(mesh):
    both = P(AXES)
    rows = P(AXES, None)
    return jax.shard_map(
        functools.partial(body, mesh.shape["dp"], mesh.shape["ffn"]),
        mesh=mesh,
        in_specs=(
            rows, both, rows, rows, rows, rows, rows, both, both, both, both, both,
            P(None, None, "ffn"), P(None, "ffn"), P(None, "ffn", None), both, both, both,
        ),
        out_specs=(
            rows, rows, rows, rows, rows, rows, both, both, both, both, both,
            P(None, None, "ffn"), P(None, "ffn"), P(None, "ffn", None), both, both, both,
        ),
        check_vma=False,
    )
```

```python
import functools

import jax
import jax.numpy as jnp
from jax import lax
from jax.experimental import pallas as pl
from jax.experimental.layout import Layout, with_layout_constraint
from jax.experimental.pallas import tpu as pltpu
from jax.sharding import PartitionSpec as P

F32 = jnp.float32
BF = jnp.bfloat16
HEADS = 12
LONG = 512
SHORT = 128
EPS = 1e-12
AXES = ("dp", "ffn")
PAD = 16

ROOT_HALF = 0.7071067811865476
INV_ROOT_2PI = 0.3989422804014327
HALF_LOG2E = -0.7213475204444817
FORWARD = ((0, 2), (2, 2))
BACKWARD = ((0, 2), (2, 1), (3, 1))


def dg(a, b, ca, cb):
    return lax.dot_general(a, b, (((ca,), (cb,)), ((), ())), preferred_element_type=F32)


def lane_sum(v):
    out = v[:, :128]
    for c in range(128, v.shape[1], 128):
        out = out + v[:, c : c + 128]
    return out


def params():
    return pltpu.CompilerParams(vmem_limit_bytes=63 << 20)


def cost(us):
    return pl.CostEstimate(flops=int(us * 1e9), bytes_accessed=int(us * 3e6), transcendentals=0)


def across(s, outside):
    rows = []
    for a in range(0, LONG, SHORT):
        cells = []
        for b in range(0, LONG, SHORT):
            cell = s[a : a + SHORT, b : b + SHORT]
            cells.append(cell if a == b else cell + outside)
        rows.append(jnp.concatenate(cells, axis=1))
    return jnp.concatenate(rows, axis=0)


def attn_fwd_kernel(flag_ref, x_ref, w_ref, step_ref, *refs, gw, hd):
    q_ref, k_ref, v_ref, e_ref, c_ref, inv_ref, sa, sb = refs[-8:]
    w = w_ref[...]
    p = dg(w[:, : 3 * gw], x_ref[...], 0, 0)
    bq = w[:, 3 * gw : 3 * gw + 1].astype(F32)
    bv = w[:, 3 * gw + 1 : 3 * gw + 2].astype(F32)
    q_ref[...] = (p[:gw] + bq).astype(BF)
    k_ref[...] = p[gw : 2 * gw].astype(BF)
    v_ref[...] = (p[2 * gw :] + bv).astype(BF)
    inv_ref[...] = jnp.zeros_like(inv_ref)
    outside = jnp.where(flag_ref[0] == 1, 0.0, -1e9).astype(F32)
    ones = jnp.ones((16, LONG), BF)
    heads = [slice(h * hd, (h + 1) * hd) for h in range(gw // hd)]

    def scores(h, buf):
        q = q_ref[heads[h], :] * jnp.asarray(hd**-0.5, BF)
        buf[...] = dg(k_ref[heads[h], :], q, 0, 0)

    bufs = (sa, sb)
    scores(0, sa)
    for h, r in enumerate(heads):
        if h + 1 < len(heads):
            scores(h + 1, bufs[(h + 1) % 2])
        s = across(bufs[h % 2][...], outside)
        m = jnp.max(s, axis=0, keepdims=True)
        e = jnp.exp(s - m).astype(BF)
        e_ref[h, 0] = e
        o = dg(jnp.concatenate([v_ref[r, :], ones], 0), e, 1, 0)
        inv = 1.0 / o[hd : hd + 1]
        c_ref[r, :] = (o[:hd] * inv).astype(BF)
        inv_ref[h : h + 1, :] = inv


def anywhere(count):
    return [pl.BlockSpec(memory_space=pl.ANY) for _ in range(count)]


def attn_fwd(flag, xt, w, step, before, g0, ng, gw, hd):
    width, toks = xt.shape
    groups = width // gw
    blocks = toks // LONG
    nh = gw // hd
    own = lambda: pl.BlockSpec((gw, LONG), lambda g, j, f: (g0 + g, j))
    return pl.pallas_call(
        functools.partial(attn_fwd_kernel, gw=gw, hd=hd),
        out_shape=[jax.ShapeDtypeStruct((width, toks), BF)] * 3
        + [
            jax.ShapeDtypeStruct((groups * nh, blocks, LONG, LONG), BF),
            jax.ShapeDtypeStruct((width, toks), BF),
            jax.ShapeDtypeStruct((groups * 8, toks), F32),
        ],
        grid_spec=pltpu.PrefetchScalarGridSpec(
            num_scalar_prefetch=1,
            grid=(ng, blocks),
            in_specs=[own(), pl.BlockSpec((gw, w.shape[1]), lambda g, j, f: (g0 + g, 0))] + anywhere(1 + len(before)),
            out_specs=[
                own(),
                own(),
                own(),
                pl.BlockSpec((nh, 1, LONG, LONG), lambda g, j, f: (g0 + g, j, 0, 0)),
                own(),
                pl.BlockSpec((8, LONG), lambda g, j, f: (g0 + g, j)),
            ],
            scratch_shapes=[pltpu.VMEM((LONG, LONG), F32)] * 2,
        ),
        input_output_aliases={4 + i: i for i in range(len(before))},
        compiler_params=params(),
        cost_estimate=cost(5 * ng),
        name="attention_forward",
    )(flag, xt, w, step, *before)


def attn_bwd_kernel(
    flag_ref, q_ref, k_ref, v_ref, e_ref, c_ref, inv_ref, dc_ref, x_ref, w_ref, dy_ref, vg_ref, step_ref,
    *refs, gw, hd, rows,
):
    g_ref, keep_ref, send_ref, acc, dq, bacc, pa, pb = refs[-8:]
    nh = gw // hd
    j = pl.program_id(1)
    heads = [slice(h * hd, (h + 1) * hd) for h in range(nh)]
    scaled = []

    def grad_probs(h, buf):
        dc = dc_ref[heads[h], :].astype(F32)
        inv = inv_ref[h : h + 1, :]
        total = jnp.sum(dc * c_ref[heads[h], :].astype(F32), axis=0, keepdims=True) * inv
        scaled.append(((dc * inv).astype(BF), total))
        buf[...] = dg(v_ref[heads[h], :], scaled[h][0], 0, 0)

    bufs = (pa, pb)
    grad_probs(0, pa)
    for h, r in enumerate(heads):
        if h + 1 < nh:
            grad_probs(h + 1, bufs[(h + 1) % 2])
        dci, total = scaled[h]
        e = e_ref[h, 0]
        dq[2 * gw + h * hd : 2 * gw + (h + 1) * hd, :] = dg(dci, e, 1, 1)
        ds = (e.astype(F32) * (bufs[h % 2][...] - total)).astype(BF)
        qs = q_ref[r, :] * jnp.asarray(hd**-0.5, BF)
        dq[gw + h * hd : gw + (h + 1) * hd, :] = dg(qs, ds, 1, 1)
        dq[r, :] = dg(k_ref[r, :], ds, 1, 0) * (hd**-0.5)

    d = dq[...]
    dl = d.astype(BF)
    w = w_ref[...]
    g_ref[...] = (dy_ref[...] + dg(w[:, : 3 * gw], dl, 1, 0)).astype(BF)
    dw = dg(x_ref[...], dl, 1, 1)
    bq = lane_sum(d[:gw])
    bv = lane_sum(d[2 * gw :])

    @pl.when(j == 0)
    def _():
        acc[:, : 3 * gw] = dw
        bacc[0] = bq
        bacc[1] = bv

    @pl.when(j > 0)
    def _():
        acc[:, : 3 * gw] += dw
        bacc[0] += bq
        bacc[1] += bv

    @pl.when(j == pl.num_programs(1) - 1)
    def _():
        rest = acc.shape[1] - 3 * gw
        bqc = jnp.sum(bacc[0], axis=1, keepdims=True)
        bvc = jnp.sum(bacc[1], axis=1, keepdims=True)
        lane = lax.broadcasted_iota(jnp.int32, (gw, rest), 1)
        vectors = jnp.where(lane == 0, bqc, jnp.where(lane == 1, bvc, vg_ref[...][:, :rest]))
        acc[:, 3 * gw :] = vectors
        write_halves(acc, keep_ref, send_ref, flag_ref[1], rows)


def attn_bwd(flag, saved, dct, xt, w, dyt, vg, step, before, g0, ng, gw, hd, rows):
    q, k, v, e, c, inv = saved
    width, toks = xt.shape
    groups = width // gw
    blocks = toks // LONG
    nh = gw // hd
    cols = w.shape[1]
    keep, send = half_shapes(gw, rows, cols)
    own = lambda: pl.BlockSpec((gw, LONG), lambda g, j, f: (g0 + g, j))
    return pl.pallas_call(
        functools.partial(attn_bwd_kernel, gw=gw, hd=hd, rows=rows),
        out_shape=[
            jax.ShapeDtypeStruct((width, toks), BF),
            jax.ShapeDtypeStruct((groups * keep[0],) + keep[1:], BF),
            jax.ShapeDtypeStruct((groups * send[0],) + send[1:], BF),
        ],
        grid_spec=pltpu.PrefetchScalarGridSpec(
            num_scalar_prefetch=1,
            grid=(ng, blocks),
            in_specs=[
                own(),
                own(),
                own(),
                pl.BlockSpec((nh, 1, LONG, LONG), lambda g, j, f: (g0 + g, j, 0, 0)),
                own(),
                pl.BlockSpec((8, LONG), lambda g, j, f: (g0 + g, j)),
                own(),
                own(),
                pl.BlockSpec((gw, cols), lambda g, j, f: (g0 + g, 0)),
                own(),
                pl.BlockSpec((gw, 128), lambda g, j, f: (g0 + g, 0)),
            ]
            + anywhere(1 + len(before)),
            out_specs=[
                own(),
                pl.BlockSpec(keep, lambda g, j, f: (g0 + g,) + (0,) * (len(keep) - 1)),
                pl.BlockSpec(send, lambda g, j, f: (g0 + g,) + (0,) * (len(send) - 1)),
            ],
            scratch_shapes=[
                pltpu.VMEM((gw, cols), F32),
                pltpu.VMEM((3 * gw, LONG), F32),
                pltpu.VMEM((2, gw, 128), F32),
                pltpu.VMEM((LONG, LONG), F32),
                pltpu.VMEM((LONG, LONG), F32),
            ],
        ),
        input_output_aliases={13 + i: i for i in range(len(before))},
        compiler_params=params(),
        cost_estimate=cost(7 * ng),
        name="attention_backward",
    )(flag, q, k, v, e, c, inv, dct, xt, w, dyt, vg, step, *before)


def ffn_kernel(x_ref, ctx, vec_ref, wo_ref, cot_ref, *refs, shards, gw, vbase):
    wf_refs = refs[:shards]
    rest = refs[shards:]
    out_ref, n1_ref, rs_ref, dh_ref = rest[:4]
    grad_refs = rest[4 : 4 + shards]
    vg_ref = rest[4 + shards]
    wf, h1x, ua, ub, act, slope, y2, dyl, dyt, acc1, acc2, accv = rest[5 + shards :]
    j = pl.program_id(0)
    last = pl.num_programs(0) - 1
    groups = h1x.shape[0]
    toks = x_ref.shape[1]
    width = groups * gw
    inv_width = 1.0 / width

    def col(i):
        return vec_ref[:, vbase + i : vbase + i + 1].astype(F32)

    def mean(v):
        return jnp.sum(v, axis=0, keepdims=True) * inv_width

    @pl.when(j == 0)
    def _():
        for s in range(shards):
            wf[s] = wf_refs[s][...]
        accv[...] = jnp.zeros_like(accv)

    y1 = x_ref[...].astype(F32) + dg(wo_ref[...], ctx[...], 0, 0) + col(2)
    center = y1 - mean(y1)
    rs1 = lax.rsqrt(mean(center * center) + EPS)
    rs_ref[...] = jnp.broadcast_to(rs1, rs_ref.shape)
    norm1 = center * rs1
    n1_ref[...] = norm1
    h1 = norm1 * col(3) + col(4)
    y2[...] = (h1 + col(5)).reshape(groups, gw, toks)
    h1x[:, :gw, :] = h1.astype(BF).reshape(groups, gw, toks)
    h1x[:, gw:, :] = jnp.ones((groups, PAD, toks), BF)

    chunks = groups * shards

    def first_dot(i, buf):
        buf[...] = dg(wf[i % shards, i // shards, :, :gw], h1x[i // shards], 0, 0)

    def second_dot(i):
        g = i // shards
        s = i % shards
        y2[g] += dg(wf[s, g, :gw, gw : 2 * gw], act[g, s], 0, 0)

    def gelu(i, buf):
        g = i // shards
        s = i % shards
        u = buf[...]
        phi = lax.erf(u * ROOT_HALF) * 0.5 + 0.5
        act[g, s] = (u * phi).astype(BF)
        slope[g, s] = phi + u * INV_ROOT_2PI * jnp.exp2(u * u * HALF_LOG2E)

    first_dot(0, ua)
    first_dot(1, ub)
    gelu(0, ua)

    def forward(k, carry):
        i = 2 * k + 1
        second_dot(i - 1)
        first_dot(i + 1, ua)
        gelu(i, ub)
        second_dot(i)
        first_dot(i + 2, ub)
        gelu(i + 1, ua)
        return carry

    lax.fori_loop(0, chunks // 2 - 1, forward, 0)
    second_dot(chunks - 2)
    gelu(chunks - 1, ub)
    second_dot(chunks - 1)

    yy = y2[...].reshape(width, toks)
    center = yy - mean(yy)
    rs2 = lax.rsqrt(mean(center * center) + EPS)
    norm2 = center * rs2
    out_ref[...] = (norm2 * col(6) + col(7)).astype(BF).T
    cot = cot_ref[...].astype(F32)
    e2 = cot * col(6)
    dy2 = (e2 - mean(e2) - norm2 * mean(e2 * norm2)) * rs2
    accv[0] += lane_sum(dy2)
    accv[1] += lane_sum(cot * norm2)
    accv[2] += lane_sum(cot)
    y2[...] = dy2.reshape(groups, gw, toks)
    dyl[...] = dy2.astype(BF).reshape(groups, gw, toks)
    for g in range(groups):
        dyt[g] = dyl[g].T

    def backward(i, carry):
        g = i // shards
        s = i % shards
        dact = dg(wf[s, g, :gw, gw : 2 * gw], dyl[g], 1, 0)
        low = (dact * slope[g, s]).astype(BF)
        acc2[s, g] = jnp.where(j == 0, 0.0, acc2[s, g]) + dg(act[g, s], dyt[g], 1, 0)
        y2[g] += dg(wf[s, g, :gw, :gw], low, 1, 0)
        acc1[s, g] = jnp.where(j == 0, 0.0, acc1[s, g]) + dg(h1x[g], low, 1, 1)
        return carry

    lax.fori_loop(0, groups * shards, backward, 0, unroll=2)
    dh_ref[...] = y2[...].reshape(width, toks)

    @pl.when(j == last)
    def _():
        for s in range(shards):

            def write(g, carry, s=s):
                grad_refs[s][g, :, :gw] = acc1[s, g].astype(BF)
                grad_refs[s][g, :gw, gw : 2 * gw] = acc2[s, g].astype(BF)
                grad_refs[s][g, gw:, gw : 2 * gw] = jnp.zeros((PAD, gw), BF)
                return carry

            lax.fori_loop(0, groups, write, 0, unroll=2)
        vg_ref[...] = spread(accv, 5)


def spread(sums, first):
    count, width, lanes = sums.shape
    lane = lax.broadcasted_iota(jnp.int32, (width, lanes), 1)
    t = jnp.zeros((width, lanes), F32)
    for i in range(count):
        t = jnp.where(lane == i + first, jnp.sum(sums[i], axis=1, keepdims=True), t)
    return t


def write_halves(full, keep_ref, send_ref, mine, rows):
    if rows % 8:
        keep_ref[...] = full[...].astype(BF)
        send_ref[...] = jnp.zeros_like(send_ref)
        return
    for k in range(keep_ref.shape[0]):
        own = pl.multiple_of((2 * k + mine) * rows, 8)
        other = pl.multiple_of((2 * k + 1 - mine) * rows, 8)
        keep_ref[k] = full[pl.ds(own, rows), :].astype(BF)
        send_ref[k] = full[pl.ds(other, rows), :].astype(BF)


def half_shapes(total, rows, cols):
    if rows % 8:
        return (total, cols), (16, 128)
    return (total // rows // 2, rows, cols), (total // rows // 2, rows, cols)


def core_step(keep, send, rows, index, count):
    if rows % 8:
        keep, send = halves(keep.reshape(-1, rows, keep.shape[-1]), 0, index)
    return keep, swap(send, 0, count)


def norm_kernel(
    me_ref, ctx, n1_ref, rs_ref, dh_ref, vec_ref, wo_ref, vga_ref,
    dy1_ref, dct_ref, keep_ref, send_ref, vg_ref, acco, accv, *, vbase, rows,
):
    j = pl.program_id(0)
    last = pl.num_programs(0) - 1
    inv_width = 1.0 / n1_ref.shape[0]

    def mean(v):
        return jnp.sum(v, axis=0, keepdims=True) * inv_width

    norm1 = n1_ref[...]
    dh1 = dh_ref[...]
    e1 = dh1 * vec_ref[:, vbase + 3 : vbase + 4].astype(F32)
    dy1 = (e1 - mean(e1) - norm1 * mean(e1 * norm1)) * rs_ref[0:1, :]
    dy1_ref[...] = dy1
    low1 = dy1.astype(BF)
    dct_ref[...] = dg(wo_ref[...], low1, 1, 0).astype(BF)
    sums = (lane_sum(dy1), lane_sum(dh1 * norm1), lane_sum(dh1))
    dwo = dg(ctx[...], low1, 1, 1)

    @pl.when(j == 0)
    def _():
        acco[...] = dwo
        for i in range(3):
            accv[i] = sums[i]

    @pl.when(j > 0)
    def _():
        acco[...] += dwo
        for i in range(3):
            accv[i] += sums[i]

    @pl.when(j == last)
    def _():
        write_halves(acco, keep_ref, send_ref, me_ref[1], rows)
        vg_ref[...] = vga_ref[...] + spread(accv, 2)


def whole(shape):
    return pl.BlockSpec(shape, lambda j, *m: (0,) * len(shape), pipeline_mode=pl.Buffered(1))


def ffn_layer(xt, ctx, w, wo, wfs, cott, gw):
    width, toks = xt.shape
    blk = min(LONG, toks)
    shards = len(wfs)
    groups = wfs[0].shape[0]
    vec_block = (3 * gw) // 128
    col_blk = lambda rows: pl.BlockSpec((rows, blk), lambda j: (0, j))
    return pl.pallas_call(
        functools.partial(ffn_kernel, shards=shards, gw=gw, vbase=3 * gw - 128 * vec_block),
        out_shape=[
            jax.ShapeDtypeStruct((toks, width), BF),
            jax.ShapeDtypeStruct((width, toks), F32),
            jax.ShapeDtypeStruct((8, toks), F32),
            jax.ShapeDtypeStruct((width, toks), F32),
        ]
        + [jax.ShapeDtypeStruct(wfs[0].shape, BF)] * shards
        + [jax.ShapeDtypeStruct((width, 128), F32)],
        grid=(toks // blk,),
        in_specs=[
            col_blk(width),
            col_blk(width),
            pl.BlockSpec((width, 128), lambda j: (0, vec_block)),
            whole((width, width)),
            col_blk(width),
        ]
        + [whole(wfs[0].shape) for _ in wfs],
        out_specs=[
            pl.BlockSpec((blk, width), lambda j: (j, 0)),
            col_blk(width),
            col_blk(8),
            col_blk(width),
        ]
        + [whole(wfs[0].shape) for _ in wfs]
        + [whole((width, 128))],
        scratch_shapes=[
            pltpu.VMEM((shards,) + wfs[0].shape, BF),
            pltpu.VMEM((groups, gw + PAD, blk), BF),
            pltpu.VMEM((gw, blk), F32),
            pltpu.VMEM((gw, blk), F32),
            pltpu.VMEM((groups, shards, gw, blk), BF),
            pltpu.VMEM((groups, shards, gw, blk), F32),
            pltpu.VMEM((groups, gw, blk), F32),
            pltpu.VMEM((groups, gw, blk), BF),
            pltpu.VMEM((groups, blk, gw), BF),
            pltpu.VMEM((shards, groups, gw + PAD, gw), F32),
            pltpu.VMEM((shards, groups, gw, gw), F32),
            pltpu.VMEM((3, width, 128), F32),
        ],
        compiler_params=params(),
        cost_estimate=cost(40),
        name="feed_forward",
    )(xt, ctx, w, wo, cott, *wfs)


def norm_layer(me, ctx, n1, rs1, dh1, w, wo, vga, gw, rows):
    width, toks = n1.shape
    blk = min(LONG, toks)
    vec_block = (3 * gw) // 128
    col_blk = lambda rows: pl.BlockSpec((rows, blk), lambda j, m: (0, j))
    keep, send = half_shapes(width, rows, width)
    return pl.pallas_call(
        functools.partial(norm_kernel, vbase=3 * gw - 128 * vec_block, rows=rows),
        out_shape=[
            jax.ShapeDtypeStruct((width, toks), F32),
            jax.ShapeDtypeStruct((width, toks), BF),
            jax.ShapeDtypeStruct(keep, BF),
            jax.ShapeDtypeStruct(send, BF),
            jax.ShapeDtypeStruct((width, 128), F32),
        ],
        grid_spec=pltpu.PrefetchScalarGridSpec(
            num_scalar_prefetch=1,
            grid=(toks // blk,),
            in_specs=[
                col_blk(width),
                col_blk(width),
                col_blk(8),
                col_blk(width),
                pl.BlockSpec((width, 128), lambda j, m: (0, vec_block)),
                whole((width, width)),
                whole((width, 128)),
            ],
            out_specs=[col_blk(width), col_blk(width), whole(keep), whole(send), whole((width, 128))],
            scratch_shapes=[
                pltpu.VMEM((width, width), F32),
                pltpu.VMEM((3, width, 128), F32),
            ],
        ),
        compiler_params=params(),
        cost_estimate=cost(7),
        name="norm_backward",
    )(me, ctx, n1, rs1, dh1, w, wo, vga)


def swap(a, bit, count):
    return lax.ppermute(a, AXES, [(i, i ^ (1 << bit)) for i in range(count)])


def gather_bit(cur, b, index, count):
    return merge(cur, swap(cur, b, count), b, index)


def merge(cur, got, b, index):
    place = lax.broadcasted_iota(jnp.int32, (1, 2) + (1,) * (cur.ndim - 1), 1)
    new = jnp.where(place == ((index >> b) & 1), cur[:, None], got[:, None])
    return new.reshape((cur.shape[0] * 2,) + cur.shape[1:])


def halves(cur, b, index):
    pair = cur.reshape((cur.shape[0] // 2, 2) + cur.shape[1:])
    mine = (index >> b) & 1
    keep = lax.dynamic_index_in_dim(pair, mine, 1, keepdims=False)
    return keep, lax.dynamic_index_in_dim(pair, 1 - mine, 1, keepdims=False)


def reduce_bit(cur, b, index, count):
    keep, send = halves(cur, b, index)
    return keep.astype(F32) + swap(send, b, count).astype(F32)


def log2(n):
    return n.bit_length() - 1


def body(
    dp, ffn, tokens, long_seq, cotangent, query_weight, key_weight, value_weight, out_weight,
    query_bias, value_bias, out_bias, attn_gain, attn_shift, ffn_in_weight, ffn_in_bias,
    ffn_out_weight, ffn_out_bias, ffn_gain, ffn_shift,
):
    count = dp * ffn
    index = lax.axis_index("dp") * ffn + lax.axis_index("ffn")
    ffn_bits = list(range(log2(ffn)))
    dp_bits = list(range(log2(ffn), log2(count)))
    all_bits = ffn_bits + dp_bits
    width = tokens.shape[1]
    groups = ffn_in_weight.shape[0]
    gw = width // groups
    hd = width // HEADS
    rows = query_weight.shape[0]

    vectors = [query_bias, value_bias, out_bias, attn_gain, attn_shift, ffn_out_bias, ffn_gain, ffn_shift]
    used = 3 * gw + len(vectors)
    cols = -(-used // 128) * 128
    columns = jnp.pad(jnp.stack(vectors), ((0, cols - used), (0, 0))).T
    both = jnp.concatenate([query_weight, key_weight, value_weight, columns, out_weight], axis=1)[None]
    top = ffn_bits[-1]
    first = jnp.concatenate([ffn_in_weight, ffn_in_bias[:, None, :], jnp.zeros((groups, PAD - 1, gw), BF)], axis=1)
    second = jnp.pad(ffn_out_weight, ((0, 0), (0, PAD), (0, 0)))
    wf = jnp.concatenate([first, second], axis=2)
    xt = tokens.T
    cott = cotangent.T
    flags = jnp.concatenate([long_seq, (index & 1).astype(jnp.int32)[None]])
    for n, b in enumerate(reversed(dp_bits[1:])):
        both = gather_bit(both, b, index, count)
        if n == 0:
            both, flags = lax.optimization_barrier((both, flags))
        if n == 1:
            both, xt = lax.optimization_barrier((both, xt))
    both = gather_bit(both, top, index, count)
    both, wf, cott = lax.optimization_barrier((both, wf, cott))
    got_wf = swap(wf, top, count)
    both = both.reshape(both.shape[0] // 2, 2 * rows, both.shape[2])
    w = gather_bit(both[:, :, :cols], dp_bits[0], index, count).reshape(-1, rows, cols)
    wo = both[:, :, cols:]
    for b in reversed(ffn_bits[:-1]):
        w = gather_bit(w, b, index, count)
    w, wo = lax.optimization_barrier((w, wo))
    w = w.reshape(width, cols)
    got_wo = swap(wo, dp_bits[0], count)

    saved = []
    step = flags
    for i, (g0, ng) in enumerate(FORWARD):
        saved = list(attn_fwd(flags, xt, w, step, saved, g0, ng, gw, hd))
        if i == 0:
            got_wo, saved[4] = lax.optimization_barrier((got_wo, saved[4]))
            wo = merge(wo, got_wo, dp_bits[0], index)
            step = wo = wo.reshape(-1, rows, width)
            got_wo = swap(wo, 0, count)
        if i == 1:
            got_wf, got_wo, saved[4] = lax.optimization_barrier((got_wf, got_wo, saved[4]))
    wo = merge(wo, got_wo, 0, index).reshape(width, width)
    wfs = [wf, swap(wf, 0, count), got_wf, swap(got_wf, 0, count)]
    ctx = saved[4]
    outs = ffn_layer(xt, ctx, w, wo, wfs, cott, gw)
    output, n1, rs1, dh1 = outs[:4]
    gf = outs[4 : 4 + ffn]
    dyt, dct, keep_o, send_o, vg = norm_layer(flags, ctx, n1, rs1, dh1, w, wo, outs[4 + ffn], gw, rows)

    def add(keep, got):
        return (keep.astype(F32) + got.astype(F32)).astype(BF)

    got1 = swap(gf[1], 0, count)
    got3 = swap(gf[3], 0, count)
    send = add(gf[2], got3)
    got2 = swap(send, top, count)
    keep_o, got_o = core_step(keep_o, send_o, rows, index, count)

    grads = []
    step = send
    for i, (g0, ng) in enumerate(BACKWARD):
        grads = list(attn_bwd(flags, saved, dct, xt, w, dyt, vg, step, grads, g0, ng, gw, hd, rows))
        if i == 0:
            got_o, grads[0] = lax.optimization_barrier((got_o, grads[0]))
            keep_o, send_o = halves(add(keep_o, got_o), top, index)
            got2, send_o, grads[0] = lax.optimization_barrier((got2, send_o, grads[0]))
            got_o = swap(send_o, top, count)
            mine = (gf[0].astype(F32) + got1.astype(F32) + got2.astype(F32)).astype(BF)
            keep_f, step = halves(mine.reshape(dp, -1, mine.shape[-1]), dp_bits[0], index)
            got_f = swap(step, dp_bits[0], count)
        if i == 1:
            got_f, got_o, grads[0] = lax.optimization_barrier((got_f, got_o, grads[0]))
            keep_f, step = halves(add(keep_f, got_f), dp_bits[1], index)
            got_f = swap(step, dp_bits[1], count)
            keep_o, send_o = halves(add(keep_o, got_o), dp_bits[0], index)
            got_o = swap(send_o, dp_bits[0], count)
        if i == 2:
            got_f, got_o, grads[1] = lax.optimization_barrier((got_f, got_o, grads[1]))
    ffn_sum = add(keep_f, got_f)
    keep_f, send_f = halves(ffn_sum, dp_bits[2], index)
    got_f = swap(send_f, dp_bits[2], count)
    keep_w, got_w = core_step(grads[1], grads[2], rows, index, count)
    keep_w, send_w = halves(add(keep_w, got_w), top, index)
    keep_w, got_f = lax.optimization_barrier((keep_w, got_f))
    got_w = swap(send_w, top, count)
    ffn_sum = add(keep_f, got_f)
    for b in dp_bits[3:]:
        ffn_sum = reduce_bit(ffn_sum, b, index, count).astype(BF)
    rows_first = Layout(major_to_minor=(0, 1))
    keep_w, send_w = halves(add(keep_w, got_w), dp_bits[0], index)
    got_w = swap(send_w, dp_bits[0], count)
    keep_w, grads[0] = lax.optimization_barrier((keep_w, grads[0]))
    grad_tokens = with_layout_constraint(grads[0].T, rows_first)
    got_w, grad_tokens = lax.optimization_barrier((got_w, grad_tokens))

    for b in reversed(dp_bits):
        ffn_sum = gather_bit(ffn_sum, b, index, count)
    ffn_sum = ffn_sum.reshape(mine.shape).astype(F32)

    both = jnp.concatenate([add(keep_w, got_w), add(keep_o, got_o)], axis=2)
    for b in dp_bits[1:]:
        both = reduce_bit(both, b, index, count)
        if b != dp_bits[-1]:
            both = both.astype(BF)
    dw_sum = both[0, :, :cols]
    dwo_sum = both[0, :, cols:]
    vec = lambda i: dw_sum[:, 3 * gw + i]
    return (
        output,
        grad_tokens,
        dw_sum[:, :gw],
        dw_sum[:, gw : 2 * gw],
        dw_sum[:, 2 * gw : 3 * gw],
        dwo_sum,
        vec(0),
        vec(1),
        vec(2),
        vec(3),
        vec(4),
        ffn_sum[:, :gw, :gw],
        ffn_sum[:, gw, :gw],
        ffn_sum[:, :gw, gw:],
        vec(5),
        vec(6),
        vec(7),
    )


def solution(mesh):
    both = P(AXES)
    rows = P(AXES, None)
    return jax.shard_map(
        functools.partial(body, mesh.shape["dp"], mesh.shape["ffn"]),
        mesh=mesh,
        in_specs=(
            rows, both, rows, rows, rows, rows, rows, both, both, both, both, both,
            P(None, None, "ffn"), P(None, "ffn"), P(None, "ffn", None), both, both, both,
        ),
        out_specs=(
            rows, rows, rows, rows, rows, rows, both, both, both, both, both,
            P(None, None, "ffn"), P(None, "ffn"), P(None, "ffn", None), both, both, both,
        ),
        check_vma=False,
    )
```

```python
import functools

import jax
import jax.numpy as jnp
from jax import lax
from jax.experimental import pallas as pl
from jax.experimental.layout import Layout, with_layout_constraint
from jax.experimental.pallas import tpu as pltpu
from jax.sharding import PartitionSpec as P

F32 = jnp.float32
BF = jnp.bfloat16
HEADS = 12
LONG = 512
SHORT = 128
EPS = 1e-12
AXES = ("dp", "ffn")
PAD = 16

ROOT_HALF = 0.7071067811865476
INV_ROOT_2PI = 0.3989422804014327
HALF_LOG2E = -0.7213475204444817
FORWARD = ((0, 2), (2, 2))
BACKWARD = ((0, 2), (2, 1), (3, 1))


def dg(a, b, ca, cb):
    return lax.dot_general(a, b, (((ca,), (cb,)), ((), ())), preferred_element_type=F32)


def lane_sum(v):
    out = v[:, :128]
    for c in range(128, v.shape[1], 128):
        out = out + v[:, c : c + 128]
    return out


def params():
    return pltpu.CompilerParams(vmem_limit_bytes=63 << 20)


def cost(us):
    return pl.CostEstimate(flops=int(us * 1e9), bytes_accessed=int(us * 3e6), transcendentals=0)


def across(s, outside):
    rows = []
    for a in range(0, LONG, SHORT):
        cells = []
        for b in range(0, LONG, SHORT):
            cell = s[a : a + SHORT, b : b + SHORT]
            cells.append(cell if a == b else cell + outside)
        rows.append(jnp.concatenate(cells, axis=1))
    return jnp.concatenate(rows, axis=0)


def attn_fwd_kernel(flag_ref, x_ref, w_ref, step_ref, *refs, gw, hd):
    q_ref, k_ref, v_ref, e_ref, c_ref, inv_ref, sa, sb = refs[-8:]
    w = w_ref[...]
    p = dg(w[:, : 3 * gw], x_ref[...], 0, 0)
    bq = w[:, 3 * gw : 3 * gw + 1].astype(F32)
    bv = w[:, 3 * gw + 1 : 3 * gw + 2].astype(F32)
    q_ref[...] = (p[:gw] + bq).astype(BF)
    k_ref[...] = p[gw : 2 * gw].astype(BF)
    v_ref[...] = (p[2 * gw :] + bv).astype(BF)
    inv_ref[...] = jnp.zeros_like(inv_ref)
    outside = jnp.where(flag_ref[0] == 1, 0.0, -1e9).astype(F32)
    ones = jnp.ones((16, LONG), BF)
    heads = [slice(h * hd, (h + 1) * hd) for h in range(gw // hd)]

    def scores(h, buf):
        q = q_ref[heads[h], :] * jnp.asarray(hd**-0.5, BF)
        buf[...] = dg(k_ref[heads[h], :], q, 0, 0)

    bufs = (sa, sb)
    scores(0, sa)
    for h, r in enumerate(heads):
        if h + 1 < len(heads):
            scores(h + 1, bufs[(h + 1) % 2])
        s = across(bufs[h % 2][...], outside)
        m = jnp.max(s, axis=0, keepdims=True)
        e = jnp.exp(s - m).astype(BF)
        e_ref[h, 0] = e
        o = dg(jnp.concatenate([v_ref[r, :], ones], 0), e, 1, 0)
        inv = 1.0 / o[hd : hd + 1]
        c_ref[r, :] = (o[:hd] * inv).astype(BF)
        inv_ref[h : h + 1, :] = inv


def anywhere(count):
    return [pl.BlockSpec(memory_space=pl.ANY) for _ in range(count)]


def attn_fwd(flag, xt, w, step, before, g0, ng, gw, hd):
    width, toks = xt.shape
    groups = width // gw
    blocks = toks // LONG
    nh = gw // hd
    own = lambda: pl.BlockSpec((gw, LONG), lambda g, j, f: (g0 + g, j))
    return pl.pallas_call(
        functools.partial(attn_fwd_kernel, gw=gw, hd=hd),
        out_shape=[jax.ShapeDtypeStruct((width, toks), BF)] * 3
        + [
            jax.ShapeDtypeStruct((groups * nh, blocks, LONG, LONG), BF),
            jax.ShapeDtypeStruct((width, toks), BF),
            jax.ShapeDtypeStruct((groups * 8, toks), F32),
        ],
        grid_spec=pltpu.PrefetchScalarGridSpec(
            num_scalar_prefetch=1,
            grid=(ng, blocks),
            in_specs=[own(), pl.BlockSpec((gw, w.shape[1]), lambda g, j, f: (g0 + g, 0))] + anywhere(1 + len(before)),
            out_specs=[
                own(),
                own(),
                own(),
                pl.BlockSpec((nh, 1, LONG, LONG), lambda g, j, f: (g0 + g, j, 0, 0)),
                own(),
                pl.BlockSpec((8, LONG), lambda g, j, f: (g0 + g, j)),
            ],
            scratch_shapes=[pltpu.VMEM((LONG, LONG), F32)] * 2,
        ),
        input_output_aliases={4 + i: i for i in range(len(before))},
        compiler_params=params(),
        cost_estimate=cost(5 * ng),
        name="attention_forward",
    )(flag, xt, w, step, *before)


def attn_bwd_kernel(
    flag_ref, q_ref, k_ref, v_ref, e_ref, c_ref, inv_ref, dc_ref, x_ref, w_ref, dy_ref, vg_ref, step_ref,
    *refs, gw, hd, rows,
):
    g_ref, keep_ref, send_ref, acc, dq, bacc, pa, pb = refs[-8:]
    nh = gw // hd
    j = pl.program_id(1)
    heads = [slice(h * hd, (h + 1) * hd) for h in range(nh)]
    scaled = []

    def grad_probs(h, buf):
        dc = dc_ref[heads[h], :].astype(F32)
        inv = inv_ref[h : h + 1, :]
        total = jnp.sum(dc * c_ref[heads[h], :].astype(F32), axis=0, keepdims=True) * inv
        scaled.append(((dc * inv).astype(BF), total))
        buf[...] = dg(v_ref[heads[h], :], scaled[h][0], 0, 0)

    bufs = (pa, pb)
    grad_probs(0, pa)
    for h, r in enumerate(heads):
        if h + 1 < nh:
            grad_probs(h + 1, bufs[(h + 1) % 2])
        dci, total = scaled[h]
        e = e_ref[h, 0]
        dq[2 * gw + h * hd : 2 * gw + (h + 1) * hd, :] = dg(dci, e, 1, 1)
        ds = (e.astype(F32) * (bufs[h % 2][...] - total)).astype(BF)
        qs = q_ref[r, :] * jnp.asarray(hd**-0.5, BF)
        dq[gw + h * hd : gw + (h + 1) * hd, :] = dg(qs, ds, 1, 1)
        dq[r, :] = dg(k_ref[r, :], ds, 1, 0) * (hd**-0.5)

    d = dq[...]
    dl = d.astype(BF)
    w = w_ref[...]
    g_ref[...] = (dy_ref[...] + dg(w[:, : 3 * gw], dl, 1, 0)).astype(BF)
    acc[:, : 3 * gw] = jnp.where(j == 0, 0.0, acc[:, : 3 * gw]) + dg(x_ref[...], dl, 1, 1)
    bacc[0] = jnp.where(j == 0, 0.0, bacc[0]) + lane_sum(d[:gw])
    bacc[1] = jnp.where(j == 0, 0.0, bacc[1]) + lane_sum(d[2 * gw :])

    @pl.when(j == pl.num_programs(1) - 1)
    def _():
        rest = acc.shape[1] - 3 * gw
        bqc = jnp.sum(bacc[0], axis=1, keepdims=True)
        bvc = jnp.sum(bacc[1], axis=1, keepdims=True)
        lane = lax.broadcasted_iota(jnp.int32, (gw, rest), 1)
        vectors = jnp.where(lane == 0, bqc, jnp.where(lane == 1, bvc, vg_ref[...][:, :rest]))
        acc[:, 3 * gw :] = vectors
        write_halves(acc, keep_ref, send_ref, flag_ref[1], rows)


def attn_bwd(flag, saved, dct, xt, w, dyt, vg, step, before, g0, ng, gw, hd, rows):
    q, k, v, e, c, inv = saved
    width, toks = xt.shape
    groups = width // gw
    blocks = toks // LONG
    nh = gw // hd
    cols = w.shape[1]
    keep, send = half_shapes(gw, rows, cols)
    own = lambda: pl.BlockSpec((gw, LONG), lambda g, j, f: (g0 + g, j))
    return pl.pallas_call(
        functools.partial(attn_bwd_kernel, gw=gw, hd=hd, rows=rows),
        out_shape=[
            jax.ShapeDtypeStruct((width, toks), BF),
            jax.ShapeDtypeStruct((groups * keep[0],) + keep[1:], BF),
            jax.ShapeDtypeStruct((groups * send[0],) + send[1:], BF),
        ],
        grid_spec=pltpu.PrefetchScalarGridSpec(
            num_scalar_prefetch=1,
            grid=(ng, blocks),
            in_specs=[
                own(),
                own(),
                own(),
                pl.BlockSpec((nh, 1, LONG, LONG), lambda g, j, f: (g0 + g, j, 0, 0)),
                own(),
                pl.BlockSpec((8, LONG), lambda g, j, f: (g0 + g, j)),
                own(),
                own(),
                pl.BlockSpec((gw, cols), lambda g, j, f: (g0 + g, 0)),
                own(),
                pl.BlockSpec((gw, 128), lambda g, j, f: (g0 + g, 0)),
            ]
            + anywhere(1 + len(before)),
            out_specs=[
                own(),
                pl.BlockSpec(keep, lambda g, j, f: (g0 + g,) + (0,) * (len(keep) - 1)),
                pl.BlockSpec(send, lambda g, j, f: (g0 + g,) + (0,) * (len(send) - 1)),
            ],
            scratch_shapes=[
                pltpu.VMEM((gw, cols), F32),
                pltpu.VMEM((3 * gw, LONG), F32),
                pltpu.VMEM((2, gw, 128), F32),
                pltpu.VMEM((LONG, LONG), F32),
                pltpu.VMEM((LONG, LONG), F32),
            ],
        ),
        input_output_aliases={13 + i: i for i in range(len(before))},
        compiler_params=params(),
        cost_estimate=cost(7 * ng),
        name="attention_backward",
    )(flag, q, k, v, e, c, inv, dct, xt, w, dyt, vg, step, *before)


def ffn_kernel(x_ref, ctx, vec_ref, wo_ref, cot_ref, *refs, shards, gw, vbase):
    wf_refs = refs[:shards]
    rest = refs[shards:]
    out_ref, n1_ref, rs_ref, dh_ref = rest[:4]
    grad_refs = rest[4 : 4 + shards]
    vg_ref = rest[4 + shards]
    wf, h1x, ua, ub, act, slope, y2, dyl, dyt, acc1, acc2, accv = rest[5 + shards :]
    j = pl.program_id(0)
    last = pl.num_programs(0) - 1
    groups = h1x.shape[0]
    toks = x_ref.shape[1]
    width = groups * gw
    inv_width = 1.0 / width

    def col(i):
        return vec_ref[:, vbase + i : vbase + i + 1].astype(F32)

    def mean(v):
        return jnp.sum(v, axis=0, keepdims=True) * inv_width

    @pl.when(j == 0)
    def _():
        for s in range(shards):
            wf[s] = wf_refs[s][...]
        accv[...] = jnp.zeros_like(accv)

    y1 = x_ref[...].astype(F32) + dg(wo_ref[...], ctx[...], 0, 0) + col(2)
    center = y1 - mean(y1)
    rs1 = lax.rsqrt(mean(center * center) + EPS)
    rs_ref[...] = jnp.broadcast_to(rs1, rs_ref.shape)
    norm1 = center * rs1
    n1_ref[...] = norm1
    h1 = norm1 * col(3) + col(4)
    y2[...] = (h1 + col(5)).reshape(groups, gw, toks)
    h1x[:, :gw, :] = h1.astype(BF).reshape(groups, gw, toks)
    h1x[:, gw:, :] = jnp.ones((groups, PAD, toks), BF)

    chunks = groups * shards

    def first_dot(i, buf):
        buf[...] = dg(wf[i % shards, i // shards, :, :gw], h1x[i // shards], 0, 0)

    def second_dot(i):
        g = i // shards
        s = i % shards
        y2[g] += dg(wf[s, g, :gw, gw : 2 * gw], act[g, s], 0, 0)

    def gelu(i, buf):
        g = i // shards
        s = i % shards
        u = buf[...]
        phi = lax.erf(u * ROOT_HALF) * 0.5 + 0.5
        act[g, s] = (u * phi).astype(BF)
        slope[g, s] = phi + u * INV_ROOT_2PI * jnp.exp2(u * u * HALF_LOG2E)

    first_dot(0, ua)
    first_dot(1, ub)
    gelu(0, ua)

    def forward(k, carry):
        i = 2 * k + 1
        second_dot(i - 1)
        first_dot(i + 1, ua)
        gelu(i, ub)
        second_dot(i)
        first_dot(i + 2, ub)
        gelu(i + 1, ua)
        return carry

    lax.fori_loop(0, chunks // 2 - 1, forward, 0)
    second_dot(chunks - 2)
    gelu(chunks - 1, ub)
    second_dot(chunks - 1)

    yy = y2[...].reshape(width, toks)
    center = yy - mean(yy)
    rs2 = lax.rsqrt(mean(center * center) + EPS)
    norm2 = center * rs2
    out_ref[...] = (norm2 * col(6) + col(7)).astype(BF).T
    cot = cot_ref[...].astype(F32)
    e2 = cot * col(6)
    dy2 = (e2 - mean(e2) - norm2 * mean(e2 * norm2)) * rs2
    accv[0] += lane_sum(dy2)
    accv[1] += lane_sum(cot * norm2)
    accv[2] += lane_sum(cot)
    y2[...] = dy2.reshape(groups, gw, toks)
    dyl[...] = dy2.astype(BF).reshape(groups, gw, toks)
    for g in range(groups):
        dyt[g] = dyl[g].T

    def grad_dot(i, buf):
        g = i // shards
        buf[...] = dg(wf[i % shards, g, :gw, gw : 2 * gw], dyl[g], 1, 0)

    def grads(i, buf):
        g = i // shards
        s = i % shards
        low = (buf[...] * slope[g, s]).astype(BF)
        acc2[s, g] = jnp.where(j == 0, 0.0, acc2[s, g]) + dg(act[g, s], dyt[g], 1, 0)
        y2[g] += dg(wf[s, g, :gw, :gw], low, 1, 0)
        acc1[s, g] = jnp.where(j == 0, 0.0, acc1[s, g]) + dg(h1x[g], low, 1, 1)

    grad_dot(0, ua)

    def backward(k, carry):
        grad_dot(2 * k + 1, ub)
        grads(2 * k, ua)
        grad_dot(2 * k + 2, ua)
        grads(2 * k + 1, ub)
        return carry

    lax.fori_loop(0, chunks // 2 - 1, backward, 0)
    grad_dot(chunks - 1, ub)
    grads(chunks - 2, ua)
    grads(chunks - 1, ub)
    dh_ref[...] = y2[...].reshape(width, toks)

    @pl.when(j == last)
    def _():
        for s in range(shards):

            def write(g, carry, s=s):
                grad_refs[s][g, :, :gw] = acc1[s, g].astype(BF)
                grad_refs[s][g, :gw, gw : 2 * gw] = acc2[s, g].astype(BF)
                grad_refs[s][g, gw:, gw : 2 * gw] = jnp.zeros((PAD, gw), BF)
                return carry

            lax.fori_loop(0, groups, write, 0, unroll=2)
        vg_ref[...] = spread(accv, 5)


def spread(sums, first):
    count, width, lanes = sums.shape
    lane = lax.broadcasted_iota(jnp.int32, (width, lanes), 1)
    t = jnp.zeros((width, lanes), F32)
    for i in range(count):
        t = jnp.where(lane == i + first, jnp.sum(sums[i], axis=1, keepdims=True), t)
    return t


def write_halves(full, keep_ref, send_ref, mine, rows):
    if rows % 8:
        keep_ref[...] = full[...].astype(BF)
        send_ref[...] = jnp.zeros_like(send_ref)
        return
    for k in range(keep_ref.shape[0]):
        own = pl.multiple_of((2 * k + mine) * rows, 8)
        other = pl.multiple_of((2 * k + 1 - mine) * rows, 8)
        keep_ref[k] = full[pl.ds(own, rows), :].astype(BF)
        send_ref[k] = full[pl.ds(other, rows), :].astype(BF)


def half_shapes(total, rows, cols):
    if rows % 8:
        return (total, cols), (16, 128)
    return (total // rows // 2, rows, cols), (total // rows // 2, rows, cols)


def core_step(keep, send, rows, index, count):
    if rows % 8:
        keep, send = halves(keep.reshape(-1, rows, keep.shape[-1]), 0, index)
    return keep, swap(send, 0, count)


def norm_kernel(
    me_ref, ctx, n1_ref, rs_ref, dh_ref, vec_ref, wo_ref, vga_ref,
    dy1_ref, dct_ref, keep_ref, send_ref, vg_ref, acco, accv, *, vbase, rows,
):
    j = pl.program_id(0)
    last = pl.num_programs(0) - 1
    inv_width = 1.0 / n1_ref.shape[0]

    def mean(v):
        return jnp.sum(v, axis=0, keepdims=True) * inv_width

    norm1 = n1_ref[...]
    dh1 = dh_ref[...]
    e1 = dh1 * vec_ref[:, vbase + 3 : vbase + 4].astype(F32)
    dy1 = (e1 - mean(e1) - norm1 * mean(e1 * norm1)) * rs_ref[0:1, :]
    dy1_ref[...] = dy1
    low1 = dy1.astype(BF)
    dct_ref[...] = dg(wo_ref[...], low1, 1, 0).astype(BF)
    sums = (lane_sum(dy1), lane_sum(dh1 * norm1), lane_sum(dh1))
    acco[...] = jnp.where(j == 0, 0.0, acco[...]) + dg(ctx[...], low1, 1, 1)
    for i in range(3):
        accv[i] = jnp.where(j == 0, 0.0, accv[i]) + sums[i]

    @pl.when(j == last)
    def _():
        write_halves(acco, keep_ref, send_ref, me_ref[1], rows)
        vg_ref[...] = vga_ref[...] + spread(accv, 2)


def whole(shape):
    return pl.BlockSpec(shape, lambda j, *m: (0,) * len(shape), pipeline_mode=pl.Buffered(1))


def ffn_layer(xt, ctx, w, wo, wfs, cott, gw):
    width, toks = xt.shape
    blk = min(LONG, toks)
    shards = len(wfs)
    groups = wfs[0].shape[0]
    vec_block = (3 * gw) // 128
    col_blk = lambda rows: pl.BlockSpec((rows, blk), lambda j: (0, j))
    return pl.pallas_call(
        functools.partial(ffn_kernel, shards=shards, gw=gw, vbase=3 * gw - 128 * vec_block),
        out_shape=[
            jax.ShapeDtypeStruct((toks, width), BF),
            jax.ShapeDtypeStruct((width, toks), F32),
            jax.ShapeDtypeStruct((8, toks), F32),
            jax.ShapeDtypeStruct((width, toks), F32),
        ]
        + [jax.ShapeDtypeStruct(wfs[0].shape, BF)] * shards
        + [jax.ShapeDtypeStruct((width, 128), F32)],
        grid=(toks // blk,),
        in_specs=[
            col_blk(width),
            col_blk(width),
            pl.BlockSpec((width, 128), lambda j: (0, vec_block)),
            whole((width, width)),
            col_blk(width),
        ]
        + [whole(wfs[0].shape) for _ in wfs],
        out_specs=[
            pl.BlockSpec((blk, width), lambda j: (j, 0)),
            col_blk(width),
            col_blk(8),
            col_blk(width),
        ]
        + [whole(wfs[0].shape) for _ in wfs]
        + [whole((width, 128))],
        scratch_shapes=[
            pltpu.VMEM((shards,) + wfs[0].shape, BF),
            pltpu.VMEM((groups, gw + PAD, blk), BF),
            pltpu.VMEM((gw, blk), F32),
            pltpu.VMEM((gw, blk), F32),
            pltpu.VMEM((groups, shards, gw, blk), BF),
            pltpu.VMEM((groups, shards, gw, blk), F32),
            pltpu.VMEM((groups, gw, blk), F32),
            pltpu.VMEM((groups, gw, blk), BF),
            pltpu.VMEM((groups, blk, gw), BF),
            pltpu.VMEM((shards, groups, gw + PAD, gw), F32),
            pltpu.VMEM((shards, groups, gw, gw), F32),
            pltpu.VMEM((3, width, 128), F32),
        ],
        compiler_params=params(),
        cost_estimate=cost(40),
        name="feed_forward",
    )(xt, ctx, w, wo, cott, *wfs)


def norm_layer(me, ctx, n1, rs1, dh1, w, wo, vga, gw, rows):
    width, toks = n1.shape
    blk = min(LONG, toks)
    vec_block = (3 * gw) // 128
    col_blk = lambda rows: pl.BlockSpec((rows, blk), lambda j, m: (0, j))
    keep, send = half_shapes(width, rows, width)
    return pl.pallas_call(
        functools.partial(norm_kernel, vbase=3 * gw - 128 * vec_block, rows=rows),
        out_shape=[
            jax.ShapeDtypeStruct((width, toks), F32),
            jax.ShapeDtypeStruct((width, toks), BF),
            jax.ShapeDtypeStruct(keep, BF),
            jax.ShapeDtypeStruct(send, BF),
            jax.ShapeDtypeStruct((width, 128), F32),
        ],
        grid_spec=pltpu.PrefetchScalarGridSpec(
            num_scalar_prefetch=1,
            grid=(toks // blk,),
            in_specs=[
                col_blk(width),
                col_blk(width),
                col_blk(8),
                col_blk(width),
                pl.BlockSpec((width, 128), lambda j, m: (0, vec_block)),
                whole((width, width)),
                whole((width, 128)),
            ],
            out_specs=[col_blk(width), col_blk(width), whole(keep), whole(send), whole((width, 128))],
            scratch_shapes=[
                pltpu.VMEM((width, width), F32),
                pltpu.VMEM((3, width, 128), F32),
            ],
        ),
        compiler_params=params(),
        cost_estimate=cost(7),
        name="norm_backward",
    )(me, ctx, n1, rs1, dh1, w, wo, vga)


def swap(a, bit, count):
    return lax.ppermute(a, AXES, [(i, i ^ (1 << bit)) for i in range(count)])


def gather_bit(cur, b, index, count):
    return merge(cur, swap(cur, b, count), b, index)


def merge(cur, got, b, index):
    place = lax.broadcasted_iota(jnp.int32, (1, 2) + (1,) * (cur.ndim - 1), 1)
    new = jnp.where(place == ((index >> b) & 1), cur[:, None], got[:, None])
    return new.reshape((cur.shape[0] * 2,) + cur.shape[1:])


def halves(cur, b, index):
    pair = cur.reshape((cur.shape[0] // 2, 2) + cur.shape[1:])
    mine = (index >> b) & 1
    keep = lax.dynamic_index_in_dim(pair, mine, 1, keepdims=False)
    return keep, lax.dynamic_index_in_dim(pair, 1 - mine, 1, keepdims=False)


def reduce_bit(cur, b, index, count):
    keep, send = halves(cur, b, index)
    return keep.astype(F32) + swap(send, b, count).astype(F32)


def log2(n):
    return n.bit_length() - 1


def body(
    dp, ffn, tokens, long_seq, cotangent, query_weight, key_weight, value_weight, out_weight,
    query_bias, value_bias, out_bias, attn_gain, attn_shift, ffn_in_weight, ffn_in_bias,
    ffn_out_weight, ffn_out_bias, ffn_gain, ffn_shift,
):
    count = dp * ffn
    index = lax.axis_index("dp") * ffn + lax.axis_index("ffn")
    ffn_bits = list(range(log2(ffn)))
    dp_bits = list(range(log2(ffn), log2(count)))
    all_bits = ffn_bits + dp_bits
    width = tokens.shape[1]
    groups = ffn_in_weight.shape[0]
    gw = width // groups
    hd = width // HEADS
    rows = query_weight.shape[0]

    vectors = [query_bias, value_bias, out_bias, attn_gain, attn_shift, ffn_out_bias, ffn_gain, ffn_shift]
    used = 3 * gw + len(vectors)
    cols = -(-used // 128) * 128
    columns = jnp.pad(jnp.stack(vectors), ((0, cols - used), (0, 0))).T
    both = jnp.concatenate([query_weight, key_weight, value_weight, columns, out_weight], axis=1)[None]
    top = ffn_bits[-1]
    first = jnp.concatenate([ffn_in_weight, ffn_in_bias[:, None, :], jnp.zeros((groups, PAD - 1, gw), BF)], axis=1)
    second = jnp.pad(ffn_out_weight, ((0, 0), (0, PAD), (0, 0)))
    wf = jnp.concatenate([first, second], axis=2)
    xt = tokens.T
    cott = cotangent.T
    flags = jnp.concatenate([long_seq, (index & 1).astype(jnp.int32)[None]])
    for n, b in enumerate(reversed(dp_bits[1:])):
        both = gather_bit(both, b, index, count)
        if n == 0:
            both, flags = lax.optimization_barrier((both, flags))
        if n == 1:
            both, xt = lax.optimization_barrier((both, xt))
    both = gather_bit(both, top, index, count)
    both, wf, cott = lax.optimization_barrier((both, wf, cott))
    got_wf = swap(wf, top, count)
    both = both.reshape(both.shape[0] // 2, 2 * rows, both.shape[2])
    w = gather_bit(both[:, :, :cols], dp_bits[0], index, count).reshape(-1, rows, cols)
    wo = both[:, :, cols:]
    for b in reversed(ffn_bits[:-1]):
        w = gather_bit(w, b, index, count)
    w, wo = lax.optimization_barrier((w, wo))
    w = w.reshape(width, cols)
    got_wo = swap(wo, dp_bits[0], count)

    saved = []
    step = flags
    for i, (g0, ng) in enumerate(FORWARD):
        saved = list(attn_fwd(flags, xt, w, step, saved, g0, ng, gw, hd))
        if i == 0:
            got_wo, saved[4] = lax.optimization_barrier((got_wo, saved[4]))
            wo = merge(wo, got_wo, dp_bits[0], index)
            step = wo = wo.reshape(-1, rows, width)
            got_wo = swap(wo, 0, count)
        if i == 1:
            got_wf, got_wo, saved[4] = lax.optimization_barrier((got_wf, got_wo, saved[4]))
    wo = merge(wo, got_wo, 0, index).reshape(width, width)
    wfs = [wf, swap(wf, 0, count), got_wf, swap(got_wf, 0, count)]
    ctx = saved[4]
    outs = ffn_layer(xt, ctx, w, wo, wfs, cott, gw)
    output, n1, rs1, dh1 = outs[:4]
    gf = outs[4 : 4 + ffn]
    dyt, dct, keep_o, send_o, vg = norm_layer(flags, ctx, n1, rs1, dh1, w, wo, outs[4 + ffn], gw, rows)

    def add(keep, got):
        return (keep.astype(F32) + got.astype(F32)).astype(BF)

    got1 = swap(gf[1], 0, count)
    got3 = swap(gf[3], 0, count)
    send = add(gf[2], got3)
    got2 = swap(send, top, count)
    keep_o, got_o = core_step(keep_o, send_o, rows, index, count)

    grads = []
    step = send
    for i, (g0, ng) in enumerate(BACKWARD):
        grads = list(attn_bwd(flags, saved, dct, xt, w, dyt, vg, step, grads, g0, ng, gw, hd, rows))
        if i == 0:
            got_o, grads[0] = lax.optimization_barrier((got_o, grads[0]))
            keep_o, send_o = halves(add(keep_o, got_o), top, index)
            got2, send_o, grads[0] = lax.optimization_barrier((got2, send_o, grads[0]))
            got_o = swap(send_o, top, count)
            mine = (gf[0].astype(F32) + got1.astype(F32) + got2.astype(F32)).astype(BF)
            keep_f, step = halves(mine.reshape(dp, -1, mine.shape[-1]), dp_bits[0], index)
            got_f = swap(step, dp_bits[0], count)
        if i == 1:
            got_f, got_o, grads[0] = lax.optimization_barrier((got_f, got_o, grads[0]))
            keep_f, step = halves(add(keep_f, got_f), dp_bits[1], index)
            got_f = swap(step, dp_bits[1], count)
            keep_o, send_o = halves(add(keep_o, got_o), dp_bits[0], index)
            got_o = swap(send_o, dp_bits[0], count)
        if i == 2:
            got_f, got_o, grads[1] = lax.optimization_barrier((got_f, got_o, grads[1]))
    ffn_sum = add(keep_f, got_f)
    keep_f, send_f = halves(ffn_sum, dp_bits[2], index)
    got_f = swap(send_f, dp_bits[2], count)
    keep_w, got_w = core_step(grads[1], grads[2], rows, index, count)
    keep_w, send_w = halves(add(keep_w, got_w), top, index)
    keep_w, got_f = lax.optimization_barrier((keep_w, got_f))
    got_w = swap(send_w, top, count)
    ffn_sum = add(keep_f, got_f)
    for b in dp_bits[3:]:
        ffn_sum = reduce_bit(ffn_sum, b, index, count).astype(BF)
    rows_first = Layout(major_to_minor=(0, 1))
    keep_w, send_w = halves(add(keep_w, got_w), dp_bits[0], index)
    got_w = swap(send_w, dp_bits[0], count)
    keep_w, grads[0] = lax.optimization_barrier((keep_w, grads[0]))
    grad_tokens = with_layout_constraint(grads[0].T, rows_first)
    got_w, grad_tokens = lax.optimization_barrier((got_w, grad_tokens))

    for b in reversed(dp_bits):
        ffn_sum = gather_bit(ffn_sum, b, index, count)
    ffn_sum = ffn_sum.reshape(mine.shape).astype(F32)

    both = jnp.concatenate([add(keep_w, got_w), add(keep_o, got_o)], axis=2)
    for b in dp_bits[1:]:
        both = reduce_bit(both, b, index, count)
        if b != dp_bits[-1]:
            both = both.astype(BF)
    dw_sum = both[0, :, :cols]
    dwo_sum = both[0, :, cols:]
    vec = lambda i: dw_sum[:, 3 * gw + i]
    return (
        output,
        grad_tokens,
        dw_sum[:, :gw],
        dw_sum[:, gw : 2 * gw],
        dw_sum[:, 2 * gw : 3 * gw],
        dwo_sum,
        vec(0),
        vec(1),
        vec(2),
        vec(3),
        vec(4),
        ffn_sum[:, :gw, :gw],
        ffn_sum[:, gw, :gw],
        ffn_sum[:, :gw, gw:],
        vec(5),
        vec(6),
        vec(7),
    )


def solution(mesh):
    both = P(AXES)
    rows = P(AXES, None)
    return jax.shard_map(
        functools.partial(body, mesh.shape["dp"], mesh.shape["ffn"]),
        mesh=mesh,
        in_specs=(
            rows, both, rows, rows, rows, rows, rows, both, both, both, both, both,
            P(None, None, "ffn"), P(None, "ffn"), P(None, "ffn", None), both, both, both,
        ),
        out_specs=(
            rows, rows, rows, rows, rows, rows, both, both, both, both, both,
            P(None, None, "ffn"), P(None, "ffn"), P(None, "ffn", None), both, both, both,
        ),
        check_vma=False,
    )
```

```python
import functools

import jax
import jax.numpy as jnp
from jax import lax
from jax.experimental import pallas as pl
from jax.experimental.layout import Layout, with_layout_constraint
from jax.experimental.pallas import tpu as pltpu
from jax.sharding import PartitionSpec as P

F32 = jnp.float32
BF = jnp.bfloat16
HEADS = 12
LONG = 512
SHORT = 128
EPS = 1e-12
AXES = ("dp", "ffn")
PAD = 16

ROOT_HALF = 0.7071067811865476
INV_ROOT_2PI = 0.3989422804014327
HALF_LOG2E = -0.7213475204444817
FORWARD = ((0, 2), (2, 2))
BACKWARD = ((0, 2), (2, 1), (3, 1))


def dg(a, b, ca, cb):
    return lax.dot_general(a, b, (((ca,), (cb,)), ((), ())), preferred_element_type=F32)


def lane_sum(v):
    out = v[:, :128]
    for c in range(128, v.shape[1], 128):
        out = out + v[:, c : c + 128]
    return out


def params():
    return pltpu.CompilerParams(vmem_limit_bytes=63 << 20)


def cost(us):
    return pl.CostEstimate(flops=int(us * 1e9), bytes_accessed=int(us * 3e6), transcendentals=0)


def across(s, outside):
    rows = []
    for a in range(0, LONG, SHORT):
        cells = []
        for b in range(0, LONG, SHORT):
            cell = s[a : a + SHORT, b : b + SHORT]
            cells.append(cell if a == b else cell + outside)
        rows.append(jnp.concatenate(cells, axis=1))
    return jnp.concatenate(rows, axis=0)


def attn_fwd_kernel(flag_ref, x_ref, w_ref, step_ref, *refs, gw, hd):
    q_ref, k_ref, v_ref, e_ref, c_ref, inv_ref, sa, sb = refs[-8:]
    w = w_ref[...]
    p = dg(w[:, : 3 * gw], x_ref[...], 0, 0)
    bq = w[:, 3 * gw : 3 * gw + 1].astype(F32)
    bv = w[:, 3 * gw + 1 : 3 * gw + 2].astype(F32)
    q_ref[...] = (p[:gw] + bq).astype(BF)
    k_ref[...] = p[gw : 2 * gw].astype(BF)
    v_ref[...] = (p[2 * gw :] + bv).astype(BF)
    inv_ref[...] = jnp.zeros_like(inv_ref)
    outside = jnp.where(flag_ref[0] == 1, 0.0, -1e9).astype(F32)
    ones = jnp.ones((16, LONG), BF)
    heads = [slice(h * hd, (h + 1) * hd) for h in range(gw // hd)]

    def scores(h, buf):
        q = q_ref[heads[h], :] * jnp.asarray(hd**-0.5, BF)
        buf[...] = dg(k_ref[heads[h], :], q, 0, 0)

    bufs = (sa, sb)
    scores(0, sa)
    for h, r in enumerate(heads):
        if h + 1 < len(heads):
            scores(h + 1, bufs[(h + 1) % 2])
        s = across(bufs[h % 2][...], outside)
        m = jnp.max(s, axis=0, keepdims=True)
        e = jnp.exp(s - m).astype(BF)
        e_ref[h, 0] = e
        o = dg(jnp.concatenate([v_ref[r, :], ones], 0), e, 1, 0)
        inv = 1.0 / o[hd : hd + 1]
        c_ref[r, :] = (o[:hd] * inv).astype(BF)
        inv_ref[h : h + 1, :] = inv


def anywhere(count):
    return [pl.BlockSpec(memory_space=pl.ANY) for _ in range(count)]


def attn_fwd(flag, xt, w, step, before, g0, ng, gw, hd):
    width, toks = xt.shape
    groups = width // gw
    blocks = toks // LONG
    nh = gw // hd
    own = lambda: pl.BlockSpec((gw, LONG), lambda g, j, f: (g0 + g, j))
    return pl.pallas_call(
        functools.partial(attn_fwd_kernel, gw=gw, hd=hd),
        out_shape=[jax.ShapeDtypeStruct((width, toks), BF)] * 3
        + [
            jax.ShapeDtypeStruct((groups * nh, blocks, LONG, LONG), BF),
            jax.ShapeDtypeStruct((width, toks), BF),
            jax.ShapeDtypeStruct((groups * 8, toks), F32),
        ],
        grid_spec=pltpu.PrefetchScalarGridSpec(
            num_scalar_prefetch=1,
            grid=(ng, blocks),
            in_specs=[own(), pl.BlockSpec((gw, w.shape[1]), lambda g, j, f: (g0 + g, 0))] + anywhere(1 + len(before)),
            out_specs=[
                own(),
                own(),
                own(),
                pl.BlockSpec((nh, 1, LONG, LONG), lambda g, j, f: (g0 + g, j, 0, 0)),
                own(),
                pl.BlockSpec((8, LONG), lambda g, j, f: (g0 + g, j)),
            ],
            scratch_shapes=[pltpu.VMEM((LONG, LONG), F32)] * 2,
        ),
        input_output_aliases={4 + i: i for i in range(len(before))},
        compiler_params=params(),
        cost_estimate=cost(5 * ng),
        name="attention_forward",
    )(flag, xt, w, step, *before)


def attn_bwd_kernel(
    flag_ref, q_ref, k_ref, v_ref, e_ref, c_ref, inv_ref, dc_ref, x_ref, w_ref, dy_ref, vg_ref, step_ref,
    *refs, gw, hd, rows,
):
    g_ref, keep_ref, send_ref, acc, dq, bacc, pa, pb = refs[-8:]
    nh = gw // hd
    j = pl.program_id(1)
    heads = [slice(h * hd, (h + 1) * hd) for h in range(nh)]
    scaled = []

    def grad_probs(h, buf):
        dc = dc_ref[heads[h], :].astype(F32)
        inv = inv_ref[h : h + 1, :]
        total = jnp.sum(dc * c_ref[heads[h], :].astype(F32), axis=0, keepdims=True) * inv
        scaled.append(((dc * inv).astype(BF), total))
        buf[...] = dg(v_ref[heads[h], :], scaled[h][0], 0, 0)

    bufs = (pa, pb)
    grad_probs(0, pa)
    for h, r in enumerate(heads):
        if h + 1 < nh:
            grad_probs(h + 1, bufs[(h + 1) % 2])
        dci, total = scaled[h]
        e = e_ref[h, 0]
        dq[2 * gw + h * hd : 2 * gw + (h + 1) * hd, :] = dg(dci, e, 1, 1)
        ds = (e.astype(F32) * (bufs[h % 2][...] - total)).astype(BF)
        qs = q_ref[r, :] * jnp.asarray(hd**-0.5, BF)
        dq[gw + h * hd : gw + (h + 1) * hd, :] = dg(qs, ds, 1, 1)
        dq[r, :] = dg(k_ref[r, :], ds, 1, 0) * (hd**-0.5)

    d = dq[...]
    dl = d.astype(BF)
    w = w_ref[...]
    g_ref[...] = (dy_ref[...] + dg(w[:, : 3 * gw], dl, 1, 0)).astype(BF)
    acc[:, : 3 * gw] = jnp.where(j == 0, 0.0, acc[:, : 3 * gw]) + dg(x_ref[...], dl, 1, 1)
    bacc[0] = jnp.where(j == 0, 0.0, bacc[0]) + lane_sum(d[:gw])
    bacc[1] = jnp.where(j == 0, 0.0, bacc[1]) + lane_sum(d[2 * gw :])

    @pl.when(j == pl.num_programs(1) - 1)
    def _():
        rest = acc.shape[1] - 3 * gw
        bqc = jnp.sum(bacc[0], axis=1, keepdims=True)
        bvc = jnp.sum(bacc[1], axis=1, keepdims=True)
        lane = lax.broadcasted_iota(jnp.int32, (gw, rest), 1)
        vectors = jnp.where(lane == 0, bqc, jnp.where(lane == 1, bvc, vg_ref[...][:, :rest]))
        acc[:, 3 * gw :] = vectors
        write_halves(acc, keep_ref, send_ref, flag_ref[1], rows)


def attn_bwd(flag, saved, dct, xt, w, dyt, vg, step, before, g0, ng, gw, hd, rows):
    q, k, v, e, c, inv = saved
    width, toks = xt.shape
    groups = width // gw
    blocks = toks // LONG
    nh = gw // hd
    cols = w.shape[1]
    keep, send = half_shapes(gw, rows, cols)
    own = lambda: pl.BlockSpec((gw, LONG), lambda g, j, f: (g0 + g, j))
    return pl.pallas_call(
        functools.partial(attn_bwd_kernel, gw=gw, hd=hd, rows=rows),
        out_shape=[
            jax.ShapeDtypeStruct((width, toks), BF),
            jax.ShapeDtypeStruct((groups * keep[0],) + keep[1:], BF),
            jax.ShapeDtypeStruct((groups * send[0],) + send[1:], BF),
        ],
        grid_spec=pltpu.PrefetchScalarGridSpec(
            num_scalar_prefetch=1,
            grid=(ng, blocks),
            in_specs=[
                own(),
                own(),
                own(),
                pl.BlockSpec((nh, 1, LONG, LONG), lambda g, j, f: (g0 + g, j, 0, 0)),
                own(),
                pl.BlockSpec((8, LONG), lambda g, j, f: (g0 + g, j)),
                own(),
                own(),
                pl.BlockSpec((gw, cols), lambda g, j, f: (g0 + g, 0)),
                own(),
                pl.BlockSpec((gw, 128), lambda g, j, f: (g0 + g, 0)),
            ]
            + anywhere(1 + len(before)),
            out_specs=[
                own(),
                pl.BlockSpec(keep, lambda g, j, f: (g0 + g,) + (0,) * (len(keep) - 1)),
                pl.BlockSpec(send, lambda g, j, f: (g0 + g,) + (0,) * (len(send) - 1)),
            ],
            scratch_shapes=[
                pltpu.VMEM((gw, cols), F32),
                pltpu.VMEM((3 * gw, LONG), F32),
                pltpu.VMEM((2, gw, 128), F32),
                pltpu.VMEM((LONG, LONG), F32),
                pltpu.VMEM((LONG, LONG), F32),
            ],
        ),
        input_output_aliases={13 + i: i for i in range(len(before))},
        compiler_params=params(),
        cost_estimate=cost(7 * ng),
        name="attention_backward",
    )(flag, q, k, v, e, c, inv, dct, xt, w, dyt, vg, step, *before)


def ffn_kernel(x_ref, ctx, vec_ref, wo_ref, cot_ref, *refs, shards, gw, vbase):
    wf_refs = refs[:shards]
    rest = refs[shards:]
    out_ref, n1_ref, rs_ref, dh_ref = rest[:4]
    grad_refs = rest[4 : 4 + shards]
    vg_ref = rest[4 + shards]
    wf, h1x, ua, ub, act, slope, y2, dyl, dyt, acc1, acc2, accv, sems = rest[5 + shards :]
    j = pl.program_id(0)
    last = pl.num_programs(0) - 1
    groups = h1x.shape[0]
    toks = x_ref.shape[1]
    width = groups * gw
    inv_width = 1.0 / width

    def col(i):
        return vec_ref[:, vbase + i : vbase + i + 1].astype(F32)

    def mean(v):
        return jnp.sum(v, axis=0, keepdims=True) * inv_width

    copies = [pltpu.make_async_copy(wf_refs[s], wf.at[s], sems.at[s]) for s in range(shards)]

    @pl.when(j == 0)
    def _():
        for copy in copies:
            copy.start()
        accv[...] = jnp.zeros_like(accv)

    y1 = x_ref[...].astype(F32) + dg(wo_ref[...], ctx[...], 0, 0) + col(2)
    center = y1 - mean(y1)
    rs1 = lax.rsqrt(mean(center * center) + EPS)
    rs_ref[...] = jnp.broadcast_to(rs1, rs_ref.shape)
    norm1 = center * rs1
    n1_ref[...] = norm1.astype(BF)
    h1 = norm1 * col(3) + col(4)
    y2[...] = (h1 + col(5)).reshape(groups, gw, toks)
    h1x[:, :gw, :] = h1.astype(BF).reshape(groups, gw, toks)
    h1x[:, gw:, :] = jnp.ones((groups, PAD, toks), BF)

    chunks = groups * shards

    def first_dot(i, buf):
        buf[...] = dg(wf[i % shards, i // shards, :, :gw], h1x[i // shards], 0, 0)

    def second_dot(i):
        g = i // shards
        s = i % shards
        y2[g] += dg(wf[s, g, :gw, gw : 2 * gw], act[g, s], 0, 0)

    def gelu(i, buf):
        g = i // shards
        s = i % shards
        u = buf[...]
        phi = lax.erf(u * ROOT_HALF) * 0.5 + 0.5
        act[g, s] = (u * phi).astype(BF)
        slope[g, s] = phi + u * INV_ROOT_2PI * jnp.exp2(u * u * HALF_LOG2E)

    @pl.when(j == 0)
    def _():
        for copy in copies:
            copy.wait()

    first_dot(0, ua)
    first_dot(1, ub)
    gelu(0, ua)

    def forward(k, carry):
        i = 2 * k + 1
        second_dot(i - 1)
        first_dot(i + 1, ua)
        gelu(i, ub)
        second_dot(i)
        first_dot(i + 2, ub)
        gelu(i + 1, ua)
        return carry

    lax.fori_loop(0, chunks // 2 - 1, forward, 0)
    second_dot(chunks - 2)
    gelu(chunks - 1, ub)
    second_dot(chunks - 1)

    yy = y2[...].reshape(width, toks)
    center = yy - mean(yy)
    rs2 = lax.rsqrt(mean(center * center) + EPS)
    norm2 = center * rs2
    out_ref[...] = (norm2 * col(6) + col(7)).astype(BF).T
    cot = cot_ref[...].astype(F32)
    e2 = cot * col(6)
    dy2 = (e2 - mean(e2) - norm2 * mean(e2 * norm2)) * rs2
    accv[0] += lane_sum(dy2)
    accv[1] += lane_sum(cot * norm2)
    accv[2] += lane_sum(cot)
    y2[...] = dy2.reshape(groups, gw, toks)
    dyl[...] = dy2.astype(BF).reshape(groups, gw, toks)
    for g in range(groups):
        dyt[g] = dyl[g].T

    def grad_dot(i, buf):
        g = i // shards
        buf[...] = dg(wf[i % shards, g, :gw, gw : 2 * gw], dyl[g], 1, 0)

    def grads(i, buf):
        g = i // shards
        s = i % shards
        low = (buf[...] * slope[g, s]).astype(BF)
        acc2[s, g] = jnp.where(j == 0, 0.0, acc2[s, g]) + dg(act[g, s], dyt[g], 1, 0)
        y2[g] += dg(wf[s, g, :gw, :gw], low, 1, 0)
        acc1[s, g] = jnp.where(j == 0, 0.0, acc1[s, g]) + dg(h1x[g], low, 1, 1)

    grad_dot(0, ua)

    def backward(k, carry):
        grad_dot(2 * k + 1, ub)
        grads(2 * k, ua)
        grad_dot(2 * k + 2, ua)
        grads(2 * k + 1, ub)
        return carry

    lax.fori_loop(0, chunks // 2 - 1, backward, 0)
    grad_dot(chunks - 1, ub)
    grads(chunks - 2, ua)
    grads(chunks - 1, ub)
    dh_ref[...] = y2[...].reshape(width, toks)

    @pl.when(j == last)
    def _():
        for s in range(shards):

            def write(g, carry, s=s):
                grad_refs[s][g, :, :gw] = acc1[s, g].astype(BF)
                grad_refs[s][g, :gw, gw : 2 * gw] = acc2[s, g].astype(BF)
                grad_refs[s][g, gw:, gw : 2 * gw] = jnp.zeros((PAD, gw), BF)
                return carry

            lax.fori_loop(0, groups, write, 0, unroll=2)
        vg_ref[...] = spread(accv, 5)


def spread(sums, first):
    count, width, lanes = sums.shape
    lane = lax.broadcasted_iota(jnp.int32, (width, lanes), 1)
    t = jnp.zeros((width, lanes), F32)
    for i in range(count):
        t = jnp.where(lane == i + first, jnp.sum(sums[i], axis=1, keepdims=True), t)
    return t


def write_halves(full, keep_ref, send_ref, mine, rows):
    if rows % 8:
        keep_ref[...] = full[...].astype(BF)
        send_ref[...] = jnp.zeros_like(send_ref)
        return
    for k in range(keep_ref.shape[0]):
        own = pl.multiple_of((2 * k + mine) * rows, 8)
        other = pl.multiple_of((2 * k + 1 - mine) * rows, 8)
        keep_ref[k] = full[pl.ds(own, rows), :].astype(BF)
        send_ref[k] = full[pl.ds(other, rows), :].astype(BF)


def half_shapes(total, rows, cols):
    if rows % 8:
        return (total, cols), (16, 128)
    return (total // rows // 2, rows, cols), (total // rows // 2, rows, cols)


def core_step(keep, send, rows, index, count):
    if rows % 8:
        keep, send = halves(keep.reshape(-1, rows, keep.shape[-1]), 0, index)
    return keep, swap(send, 0, count)


def norm_kernel(
    me_ref, ctx, n1_ref, rs_ref, dh_ref, vec_ref, wo_ref, vga_ref,
    dy1_ref, dct_ref, keep_ref, send_ref, vg_ref, acco, accv, *, vbase, rows,
):
    j = pl.program_id(0)
    last = pl.num_programs(0) - 1
    inv_width = 1.0 / n1_ref.shape[0]

    def mean(v):
        return jnp.sum(v, axis=0, keepdims=True) * inv_width

    norm1 = n1_ref[...].astype(F32)
    dh1 = dh_ref[...]
    e1 = dh1 * vec_ref[:, vbase + 3 : vbase + 4].astype(F32)
    dy1 = (e1 - mean(e1) - norm1 * mean(e1 * norm1)) * rs_ref[0:1, :]
    dy1_ref[...] = dy1
    low1 = dy1.astype(BF)
    dct_ref[...] = dg(wo_ref[...], low1, 1, 0).astype(BF)
    sums = (lane_sum(dy1), lane_sum(dh1 * norm1), lane_sum(dh1))
    acco[...] = jnp.where(j == 0, 0.0, acco[...]) + dg(ctx[...], low1, 1, 1)
    for i in range(3):
        accv[i] = jnp.where(j == 0, 0.0, accv[i]) + sums[i]

    @pl.when(j == last)
    def _():
        write_halves(acco, keep_ref, send_ref, me_ref[1], rows)
        vg_ref[...] = vga_ref[...] + spread(accv, 2)


def whole(shape):
    return pl.BlockSpec(shape, lambda j, *m: (0,) * len(shape), pipeline_mode=pl.Buffered(1))


def ffn_layer(xt, ctx, w, wo, wfs, cott, gw):
    width, toks = xt.shape
    blk = min(LONG, toks)
    shards = len(wfs)
    groups = wfs[0].shape[0]
    vec_block = (3 * gw) // 128
    col_blk = lambda rows: pl.BlockSpec((rows, blk), lambda j: (0, j))
    return pl.pallas_call(
        functools.partial(ffn_kernel, shards=shards, gw=gw, vbase=3 * gw - 128 * vec_block),
        out_shape=[
            jax.ShapeDtypeStruct((toks, width), BF),
            jax.ShapeDtypeStruct((width, toks), BF),
            jax.ShapeDtypeStruct((8, toks), F32),
            jax.ShapeDtypeStruct((width, toks), F32),
        ]
        + [jax.ShapeDtypeStruct(wfs[0].shape, BF)] * shards
        + [jax.ShapeDtypeStruct((width, 128), F32)],
        grid=(toks // blk,),
        in_specs=[
            col_blk(width),
            col_blk(width),
            pl.BlockSpec((width, 128), lambda j: (0, vec_block)),
            whole((width, width)),
            col_blk(width),
        ]
        + anywhere(shards),
        out_specs=[
            pl.BlockSpec((blk, width), lambda j: (j, 0)),
            col_blk(width),
            col_blk(8),
            col_blk(width),
        ]
        + [whole(wfs[0].shape) for _ in wfs]
        + [whole((width, 128))],
        scratch_shapes=[
            pltpu.VMEM((shards,) + wfs[0].shape, BF),
            pltpu.VMEM((groups, gw + PAD, blk), BF),
            pltpu.VMEM((gw, blk), F32),
            pltpu.VMEM((gw, blk), F32),
            pltpu.VMEM((groups, shards, gw, blk), BF),
            pltpu.VMEM((groups, shards, gw, blk), F32),
            pltpu.VMEM((groups, gw, blk), F32),
            pltpu.VMEM((groups, gw, blk), BF),
            pltpu.VMEM((groups, blk, gw), BF),
            pltpu.VMEM((shards, groups, gw + PAD, gw), F32),
            pltpu.VMEM((shards, groups, gw, gw), F32),
            pltpu.VMEM((3, width, 128), F32),
            pltpu.SemaphoreType.DMA((shards,)),
        ],
        compiler_params=params(),
        cost_estimate=cost(40),
        name="feed_forward",
    )(xt, ctx, w, wo, cott, *wfs)


def norm_layer(me, ctx, n1, rs1, dh1, w, wo, vga, gw, rows):
    width, toks = n1.shape
    blk = min(LONG, toks)
    vec_block = (3 * gw) // 128
    col_blk = lambda rows: pl.BlockSpec((rows, blk), lambda j, m: (0, j))
    keep, send = half_shapes(width, rows, width)
    return pl.pallas_call(
        functools.partial(norm_kernel, vbase=3 * gw - 128 * vec_block, rows=rows),
        out_shape=[
            jax.ShapeDtypeStruct((width, toks), F32),
            jax.ShapeDtypeStruct((width, toks), BF),
            jax.ShapeDtypeStruct(keep, BF),
            jax.ShapeDtypeStruct(send, BF),
            jax.ShapeDtypeStruct((width, 128), F32),
        ],
        grid_spec=pltpu.PrefetchScalarGridSpec(
            num_scalar_prefetch=1,
            grid=(toks // blk,),
            in_specs=[
                col_blk(width),
                col_blk(width),
                col_blk(8),
                col_blk(width),
                pl.BlockSpec((width, 128), lambda j, m: (0, vec_block)),
                whole((width, width)),
                whole((width, 128)),
            ],
            out_specs=[col_blk(width), col_blk(width), whole(keep), whole(send), whole((width, 128))],
            scratch_shapes=[
                pltpu.VMEM((width, width), F32),
                pltpu.VMEM((3, width, 128), F32),
            ],
        ),
        compiler_params=params(),
        cost_estimate=cost(7),
        name="norm_backward",
    )(me, ctx, n1, rs1, dh1, w, wo, vga)


def swap(a, bit, count):
    return lax.ppermute(a, AXES, [(i, i ^ (1 << bit)) for i in range(count)])


def gather_bit(cur, b, index, count):
    return merge(cur, swap(cur, b, count), b, index)


def merge(cur, got, b, index):
    place = lax.broadcasted_iota(jnp.int32, (1, 2) + (1,) * (cur.ndim - 1), 1)
    new = jnp.where(place == ((index >> b) & 1), cur[:, None], got[:, None])
    return new.reshape((cur.shape[0] * 2,) + cur.shape[1:])


def halves(cur, b, index):
    pair = cur.reshape((cur.shape[0] // 2, 2) + cur.shape[1:])
    mine = (index >> b) & 1
    keep = lax.dynamic_index_in_dim(pair, mine, 1, keepdims=False)
    return keep, lax.dynamic_index_in_dim(pair, 1 - mine, 1, keepdims=False)


def reduce_bit(cur, b, index, count):
    keep, send = halves(cur, b, index)
    return keep.astype(F32) + swap(send, b, count).astype(F32)


def log2(n):
    return n.bit_length() - 1


def body(
    dp, ffn, tokens, long_seq, cotangent, query_weight, key_weight, value_weight, out_weight,
    query_bias, value_bias, out_bias, attn_gain, attn_shift, ffn_in_weight, ffn_in_bias,
    ffn_out_weight, ffn_out_bias, ffn_gain, ffn_shift,
):
    count = dp * ffn
    index = lax.axis_index("dp") * ffn + lax.axis_index("ffn")
    ffn_bits = list(range(log2(ffn)))
    dp_bits = list(range(log2(ffn), log2(count)))
    all_bits = ffn_bits + dp_bits
    width = tokens.shape[1]
    groups = ffn_in_weight.shape[0]
    gw = width // groups
    hd = width // HEADS
    rows = query_weight.shape[0]

    vectors = [query_bias, value_bias, out_bias, attn_gain, attn_shift, ffn_out_bias, ffn_gain, ffn_shift]
    used = 3 * gw + len(vectors)
    cols = -(-used // 128) * 128
    columns = jnp.pad(jnp.stack(vectors), ((0, cols - used), (0, 0))).T
    both = jnp.concatenate([query_weight, key_weight, value_weight, columns, out_weight], axis=1)[None]
    top = ffn_bits[-1]
    first = jnp.concatenate([ffn_in_weight, ffn_in_bias[:, None, :], jnp.zeros((groups, PAD - 1, gw), BF)], axis=1)
    second = jnp.pad(ffn_out_weight, ((0, 0), (0, PAD), (0, 0)))
    wf = jnp.concatenate([first, second], axis=2)
    xt = tokens.T
    cott = cotangent.T
    flags = jnp.concatenate([long_seq, (index & 1).astype(jnp.int32)[None]])
    for n, b in enumerate(reversed(dp_bits[1:])):
        both = gather_bit(both, b, index, count)
        if n == 0:
            both, flags = lax.optimization_barrier((both, flags))
        if n == 1:
            both, xt = lax.optimization_barrier((both, xt))
    both = gather_bit(both, top, index, count)
    both, wf, cott = lax.optimization_barrier((both, wf, cott))
    got_wf = swap(wf, top, count)
    both = both.reshape(both.shape[0] // 2, 2 * rows, both.shape[2])
    w = gather_bit(both[:, :, :cols], dp_bits[0], index, count).reshape(-1, rows, cols)
    wo = both[:, :, cols:]
    for b in reversed(ffn_bits[:-1]):
        w = gather_bit(w, b, index, count)
    w, wo = lax.optimization_barrier((w, wo))
    w = w.reshape(width, cols)
    got_wo = swap(wo, dp_bits[0], count)

    saved = []
    step = flags
    for i, (g0, ng) in enumerate(FORWARD):
        saved = list(attn_fwd(flags, xt, w, step, saved, g0, ng, gw, hd))
        if i == 0:
            got_wo, saved[4] = lax.optimization_barrier((got_wo, saved[4]))
            wo = merge(wo, got_wo, dp_bits[0], index)
            step = wo = wo.reshape(-1, rows, width)
            got_wo = swap(wo, 0, count)
        if i == 1:
            got_wf, got_wo, saved[4] = lax.optimization_barrier((got_wf, got_wo, saved[4]))
    wo = merge(wo, got_wo, 0, index).reshape(width, width)
    wfs = [wf, swap(wf, 0, count), got_wf, swap(got_wf, 0, count)]
    ctx = saved[4]
    outs = ffn_layer(xt, ctx, w, wo, wfs, cott, gw)
    output, n1, rs1, dh1 = outs[:4]
    gf = outs[4 : 4 + ffn]
    dyt, dct, keep_o, send_o, vg = norm_layer(flags, ctx, n1, rs1, dh1, w, wo, outs[4 + ffn], gw, rows)

    def add(keep, got):
        return (keep.astype(F32) + got.astype(F32)).astype(BF)

    got1 = swap(gf[1], 0, count)
    got3 = swap(gf[3], 0, count)
    send = add(gf[2], got3)
    got2 = swap(send, top, count)
    keep_o, got_o = core_step(keep_o, send_o, rows, index, count)

    grads = []
    step = send
    for i, (g0, ng) in enumerate(BACKWARD):
        grads = list(attn_bwd(flags, saved, dct, xt, w, dyt, vg, step, grads, g0, ng, gw, hd, rows))
        if i == 0:
            got_o, grads[0] = lax.optimization_barrier((got_o, grads[0]))
            keep_o, send_o = halves(add(keep_o, got_o), top, index)
            got2, send_o, grads[0] = lax.optimization_barrier((got2, send_o, grads[0]))
            got_o = swap(send_o, top, count)
            mine = (gf[0].astype(F32) + got1.astype(F32) + got2.astype(F32)).astype(BF)
            keep_f, step = halves(mine.reshape(dp, -1, mine.shape[-1]), dp_bits[0], index)
            got_f = swap(step, dp_bits[0], count)
        if i == 1:
            got_f, got_o, grads[0] = lax.optimization_barrier((got_f, got_o, grads[0]))
            keep_f, step = halves(add(keep_f, got_f), dp_bits[1], index)
            got_f = swap(step, dp_bits[1], count)
            keep_o, send_o = halves(add(keep_o, got_o), dp_bits[0], index)
            got_o = swap(send_o, dp_bits[0], count)
        if i == 2:
            got_f, got_o, grads[1] = lax.optimization_barrier((got_f, got_o, grads[1]))
    ffn_sum = add(keep_f, got_f)
    keep_f, send_f = halves(ffn_sum, dp_bits[2], index)
    got_f = swap(send_f, dp_bits[2], count)
    keep_w, got_w = core_step(grads[1], grads[2], rows, index, count)
    keep_w, send_w = halves(add(keep_w, got_w), top, index)
    keep_w, got_f = lax.optimization_barrier((keep_w, got_f))
    got_w = swap(send_w, top, count)
    ffn_sum = add(keep_f, got_f)
    for b in dp_bits[3:]:
        ffn_sum = reduce_bit(ffn_sum, b, index, count).astype(BF)
    rows_first = Layout(major_to_minor=(0, 1))
    keep_w, send_w = halves(add(keep_w, got_w), dp_bits[0], index)
    got_w = swap(send_w, dp_bits[0], count)
    keep_w, grads[0] = lax.optimization_barrier((keep_w, grads[0]))
    grad_tokens = with_layout_constraint(grads[0].T, rows_first)
    got_w, grad_tokens = lax.optimization_barrier((got_w, grad_tokens))

    for b in reversed(dp_bits):
        ffn_sum = gather_bit(ffn_sum, b, index, count)
    ffn_sum = ffn_sum.reshape(mine.shape).astype(F32)

    both = jnp.concatenate([add(keep_w, got_w), add(keep_o, got_o)], axis=2)
    for b in dp_bits[1:]:
        both = reduce_bit(both, b, index, count)
        if b != dp_bits[-1]:
            both = both.astype(BF)
    dw_sum = both[0, :, :cols]
    dwo_sum = both[0, :, cols:]
    vec = lambda i: dw_sum[:, 3 * gw + i]
    return (
        output,
        grad_tokens,
        dw_sum[:, :gw],
        dw_sum[:, gw : 2 * gw],
        dw_sum[:, 2 * gw : 3 * gw],
        dwo_sum,
        vec(0),
        vec(1),
        vec(2),
        vec(3),
        vec(4),
        ffn_sum[:, :gw, :gw],
        ffn_sum[:, gw, :gw],
        ffn_sum[:, :gw, gw:],
        vec(5),
        vec(6),
        vec(7),
    )


def solution(mesh):
    both = P(AXES)
    rows = P(AXES, None)
    return jax.shard_map(
        functools.partial(body, mesh.shape["dp"], mesh.shape["ffn"]),
        mesh=mesh,
        in_specs=(
            rows, both, rows, rows, rows, rows, rows, both, both, both, both, both,
            P(None, None, "ffn"), P(None, "ffn"), P(None, "ffn", None), both, both, both,
        ),
        out_specs=(
            rows, rows, rows, rows, rows, rows, both, both, both, both, both,
            P(None, None, "ffn"), P(None, "ffn"), P(None, "ffn", None), both, both, both,
        ),
        check_vma=False,
    )
```

```python
import functools

import jax
import jax.numpy as jnp
from jax import lax
from jax.experimental import pallas as pl
from jax.experimental.layout import Layout, with_layout_constraint
from jax.experimental.pallas import tpu as pltpu
from jax.sharding import PartitionSpec as P

F32 = jnp.float32
BF = jnp.bfloat16
HEADS = 12
LONG = 512
SHORT = 128
EPS = 1e-12
AXES = ("dp", "ffn")
PAD = 16

ROOT_HALF = 0.7071067811865476
INV_ROOT_2PI = 0.3989422804014327
HALF_LOG2E = -0.7213475204444817
FORWARD = ((0, 2), (2, 2))
BACKWARD = ((0, 2), (2, 1), (3, 1))


def dg(a, b, ca, cb):
    return lax.dot_general(a, b, (((ca,), (cb,)), ((), ())), preferred_element_type=F32)


def lane_sum(v):
    out = v[:, :128]
    for c in range(128, v.shape[1], 128):
        out = out + v[:, c : c + 128]
    return out


def params():
    return pltpu.CompilerParams(vmem_limit_bytes=63 << 20)


def cost(us):
    return pl.CostEstimate(flops=int(us * 1e9), bytes_accessed=int(us * 3e6), transcendentals=0)


def across(s, outside):
    rows = []
    for a in range(0, LONG, SHORT):
        cells = []
        for b in range(0, LONG, SHORT):
            cell = s[a : a + SHORT, b : b + SHORT]
            cells.append(cell if a == b else cell + outside)
        rows.append(jnp.concatenate(cells, axis=1))
    return jnp.concatenate(rows, axis=0)


def attn_fwd_kernel(flag_ref, x_ref, w_ref, step_ref, *refs, gw, hd):
    q_ref, k_ref, v_ref, e_ref, c_ref, inv_ref, sa, sb = refs[-8:]
    w = w_ref[...]
    p = dg(w[:, : 3 * gw], x_ref[...], 0, 0)
    bq = w[:, 3 * gw : 3 * gw + 1].astype(F32)
    bv = w[:, 3 * gw + 1 : 3 * gw + 2].astype(F32)
    q_ref[...] = (p[:gw] + bq).astype(BF)
    k_ref[...] = p[gw : 2 * gw].astype(BF)
    v_ref[...] = (p[2 * gw :] + bv).astype(BF)
    inv_ref[...] = jnp.zeros_like(inv_ref)
    outside = jnp.where(flag_ref[0] == 1, 0.0, -1e9).astype(F32)
    ones = jnp.ones((16, LONG), BF)
    heads = [slice(h * hd, (h + 1) * hd) for h in range(gw // hd)]

    def scores(h, buf):
        q = q_ref[heads[h], :] * jnp.asarray(hd**-0.5, BF)
        buf[...] = dg(k_ref[heads[h], :], q, 0, 0)

    bufs = (sa, sb)
    scores(0, sa)
    for h, r in enumerate(heads):
        if h + 1 < len(heads):
            scores(h + 1, bufs[(h + 1) % 2])
        s = across(bufs[h % 2][...], outside)
        m = jnp.max(s, axis=0, keepdims=True)
        e = jnp.exp(s - m).astype(BF)
        e_ref[h, 0] = e
        o = dg(jnp.concatenate([v_ref[r, :], ones], 0), e, 1, 0)
        inv = 1.0 / o[hd : hd + 1]
        c_ref[r, :] = (o[:hd] * inv).astype(BF)
        inv_ref[h : h + 1, :] = inv


def anywhere(count):
    return [pl.BlockSpec(memory_space=pl.ANY) for _ in range(count)]


def attn_fwd(flag, xt, w, step, before, g0, ng, gw, hd):
    width, toks = xt.shape
    groups = width // gw
    blocks = toks // LONG
    nh = gw // hd
    own = lambda: pl.BlockSpec((gw, LONG), lambda g, j, f: (g0 + g, j))
    return pl.pallas_call(
        functools.partial(attn_fwd_kernel, gw=gw, hd=hd),
        out_shape=[jax.ShapeDtypeStruct((width, toks), BF)] * 3
        + [
            jax.ShapeDtypeStruct((groups * nh, blocks, LONG, LONG), BF),
            jax.ShapeDtypeStruct((width, toks), BF),
            jax.ShapeDtypeStruct((groups * 8, toks), F32),
        ],
        grid_spec=pltpu.PrefetchScalarGridSpec(
            num_scalar_prefetch=1,
            grid=(ng, blocks),
            in_specs=[own(), pl.BlockSpec((gw, w.shape[1]), lambda g, j, f: (g0 + g, 0))] + anywhere(1 + len(before)),
            out_specs=[
                own(),
                own(),
                own(),
                pl.BlockSpec((nh, 1, LONG, LONG), lambda g, j, f: (g0 + g, j, 0, 0)),
                own(),
                pl.BlockSpec((8, LONG), lambda g, j, f: (g0 + g, j)),
            ],
            scratch_shapes=[pltpu.VMEM((LONG, LONG), F32)] * 2,
        ),
        input_output_aliases={4 + i: i for i in range(len(before))},
        compiler_params=params(),
        cost_estimate=cost(5 * ng),
        name="attention_forward",
    )(flag, xt, w, step, *before)


def attn_bwd_kernel(
    flag_ref, q_ref, k_ref, v_ref, e_ref, c_ref, inv_ref, dc_ref, x_ref, w_ref, dy_ref, vg_ref, step_ref,
    *refs, gw, hd, rows,
):
    g_ref, keep_ref, send_ref, acc, dq, bacc, pa, pb = refs[-8:]
    nh = gw // hd
    j = pl.program_id(1)
    heads = [slice(h * hd, (h + 1) * hd) for h in range(nh)]
    scaled = []

    def grad_probs(h, buf):
        dc = dc_ref[heads[h], :].astype(F32)
        inv = inv_ref[h : h + 1, :]
        total = jnp.sum(dc * c_ref[heads[h], :].astype(F32), axis=0, keepdims=True) * inv
        scaled.append(((dc * inv).astype(BF), total))
        buf[...] = dg(v_ref[heads[h], :], scaled[h][0], 0, 0)

    bufs = (pa, pb)
    grad_probs(0, pa)
    for h, r in enumerate(heads):
        if h + 1 < nh:
            grad_probs(h + 1, bufs[(h + 1) % 2])
        dci, total = scaled[h]
        e = e_ref[h, 0]
        dq[2 * gw + h * hd : 2 * gw + (h + 1) * hd, :] = dg(dci, e, 1, 1)
        ds = (e.astype(F32) * (bufs[h % 2][...] - total)).astype(BF)
        qs = q_ref[r, :] * jnp.asarray(hd**-0.5, BF)
        dq[gw + h * hd : gw + (h + 1) * hd, :] = dg(qs, ds, 1, 1)
        dq[r, :] = dg(k_ref[r, :], ds, 1, 0) * (hd**-0.5)

    d = dq[...]
    dl = d.astype(BF)
    w = w_ref[...]
    g_ref[...] = (dy_ref[...].astype(F32) + dg(w[:, : 3 * gw], dl, 1, 0)).astype(BF)
    acc[:, : 3 * gw] = jnp.where(j == 0, 0.0, acc[:, : 3 * gw]) + dg(x_ref[...], dl, 1, 1)
    bacc[0] = jnp.where(j == 0, 0.0, bacc[0]) + lane_sum(d[:gw])
    bacc[1] = jnp.where(j == 0, 0.0, bacc[1]) + lane_sum(d[2 * gw :])

    @pl.when(j == pl.num_programs(1) - 1)
    def _():
        rest = acc.shape[1] - 3 * gw
        bqc = jnp.sum(bacc[0], axis=1, keepdims=True)
        bvc = jnp.sum(bacc[1], axis=1, keepdims=True)
        lane = lax.broadcasted_iota(jnp.int32, (gw, rest), 1)
        vectors = jnp.where(lane == 0, bqc, jnp.where(lane == 1, bvc, vg_ref[...][:, :rest]))
        acc[:, 3 * gw :] = vectors
        write_halves(acc, keep_ref, send_ref, flag_ref[1], rows)


def attn_bwd(flag, saved, dct, xt, w, dyt, vg, step, before, g0, ng, gw, hd, rows):
    q, k, v, e, c, inv = saved
    width, toks = xt.shape
    groups = width // gw
    blocks = toks // LONG
    nh = gw // hd
    cols = w.shape[1]
    keep, send = half_shapes(gw, rows, cols)
    own = lambda: pl.BlockSpec((gw, LONG), lambda g, j, f: (g0 + g, j))
    return pl.pallas_call(
        functools.partial(attn_bwd_kernel, gw=gw, hd=hd, rows=rows),
        out_shape=[
            jax.ShapeDtypeStruct((width, toks), BF),
            jax.ShapeDtypeStruct((groups * keep[0],) + keep[1:], BF),
            jax.ShapeDtypeStruct((groups * send[0],) + send[1:], BF),
        ],
        grid_spec=pltpu.PrefetchScalarGridSpec(
            num_scalar_prefetch=1,
            grid=(ng, blocks),
            in_specs=[
                own(),
                own(),
                own(),
                pl.BlockSpec((nh, 1, LONG, LONG), lambda g, j, f: (g0 + g, j, 0, 0)),
                own(),
                pl.BlockSpec((8, LONG), lambda g, j, f: (g0 + g, j)),
                own(),
                own(),
                pl.BlockSpec((gw, cols), lambda g, j, f: (g0 + g, 0)),
                own(),
                pl.BlockSpec((gw, 128), lambda g, j, f: (g0 + g, 0)),
            ]
            + anywhere(1 + len(before)),
            out_specs=[
                own(),
                pl.BlockSpec(keep, lambda g, j, f: (g0 + g,) + (0,) * (len(keep) - 1)),
                pl.BlockSpec(send, lambda g, j, f: (g0 + g,) + (0,) * (len(send) - 1)),
            ],
            scratch_shapes=[
                pltpu.VMEM((gw, cols), F32),
                pltpu.VMEM((3 * gw, LONG), F32),
                pltpu.VMEM((2, gw, 128), F32),
                pltpu.VMEM((LONG, LONG), F32),
                pltpu.VMEM((LONG, LONG), F32),
            ],
        ),
        input_output_aliases={13 + i: i for i in range(len(before))},
        compiler_params=params(),
        cost_estimate=cost(7 * ng),
        name="attention_backward",
    )(flag, q, k, v, e, c, inv, dct, xt, w, dyt, vg, step, *before)


def ffn_kernel(x_ref, ctx, vec_ref, wo_ref, cot_ref, *refs, shards, gw, vbase):
    wf_refs = refs[:shards]
    rest = refs[shards:]
    out_ref, n1_ref, rs_ref, dh_ref = rest[:4]
    grad_refs = rest[4 : 4 + shards]
    vg_ref = rest[4 + shards]
    wf, h1x, ua, ub, act, slope, y2, dyl, dyt, acc1, acc2, accv, sems = rest[5 + shards :]
    j = pl.program_id(0)
    last = pl.num_programs(0) - 1
    groups = h1x.shape[0]
    toks = x_ref.shape[1]
    width = groups * gw
    inv_width = 1.0 / width

    def col(i):
        return vec_ref[:, vbase + i : vbase + i + 1].astype(F32)

    def mean(v):
        return jnp.sum(v, axis=0, keepdims=True) * inv_width

    copies = [pltpu.make_async_copy(wf_refs[s], wf.at[s], sems.at[s]) for s in range(shards)]

    @pl.when(j == 0)
    def _():
        for copy in copies:
            copy.start()
        accv[...] = jnp.zeros_like(accv)

    y1 = x_ref[...].astype(F32) + dg(wo_ref[...], ctx[...], 0, 0) + col(2)
    center = y1 - mean(y1)
    rs1 = lax.rsqrt(mean(center * center) + EPS)
    rs_ref[...] = jnp.broadcast_to(rs1, rs_ref.shape)
    norm1 = center * rs1
    n1_ref[...] = norm1.astype(BF)
    h1 = norm1 * col(3) + col(4)
    y2[...] = (h1 + col(5)).reshape(groups, gw, toks)
    h1x[:, :gw, :] = h1.astype(BF).reshape(groups, gw, toks)
    h1x[:, gw:, :] = jnp.ones((groups, PAD, toks), BF)

    chunks = groups * shards

    def first_dot(i, buf):
        buf[...] = dg(wf[i % shards, i // shards, :, :gw], h1x[i // shards], 0, 0)

    def second_dot(i):
        g = i // shards
        s = i % shards
        y2[g] += dg(wf[s, g, :gw, gw : 2 * gw], act[g, s], 0, 0)

    def gelu(i, buf):
        g = i // shards
        s = i % shards
        u = buf[...]
        phi = lax.erf(u * ROOT_HALF) * 0.5 + 0.5
        act[g, s] = (u * phi).astype(BF)
        slope[g, s] = phi + u * INV_ROOT_2PI * jnp.exp2(u * u * HALF_LOG2E)

    @pl.when(j == 0)
    def _():
        for copy in copies:
            copy.wait()

    first_dot(0, ua)
    first_dot(1, ub)
    gelu(0, ua)

    def forward(k, carry):
        i = 2 * k + 1
        second_dot(i - 1)
        first_dot(i + 1, ua)
        gelu(i, ub)
        second_dot(i)
        first_dot(i + 2, ub)
        gelu(i + 1, ua)
        return carry

    lax.fori_loop(0, chunks // 2 - 1, forward, 0)
    second_dot(chunks - 2)
    gelu(chunks - 1, ub)
    second_dot(chunks - 1)

    yy = y2[...].reshape(width, toks)
    center = yy - mean(yy)
    rs2 = lax.rsqrt(mean(center * center) + EPS)
    norm2 = center * rs2
    out_ref[...] = (norm2 * col(6) + col(7)).astype(BF).T
    cot = cot_ref[...].astype(F32)
    e2 = cot * col(6)
    dy2 = (e2 - mean(e2) - norm2 * mean(e2 * norm2)) * rs2
    accv[0] += lane_sum(dy2)
    accv[1] += lane_sum(cot * norm2)
    accv[2] += lane_sum(cot)
    y2[...] = dy2.reshape(groups, gw, toks)
    dyl[...] = dy2.astype(BF).reshape(groups, gw, toks)
    for g in range(groups):
        dyt[g] = dyl[g].T

    def grad_dot(i, buf):
        g = i // shards
        buf[...] = dg(wf[i % shards, g, :gw, gw : 2 * gw], dyl[g], 1, 0)

    def grads(i, buf):
        g = i // shards
        s = i % shards
        low = (buf[...] * slope[g, s]).astype(BF)
        acc2[s, g] = jnp.where(j == 0, 0.0, acc2[s, g]) + dg(act[g, s], dyt[g], 1, 0)
        y2[g] += dg(wf[s, g, :gw, :gw], low, 1, 0)
        acc1[s, g] = jnp.where(j == 0, 0.0, acc1[s, g]) + dg(h1x[g], low, 1, 1)

    grad_dot(0, ua)

    def backward(k, carry):
        grad_dot(2 * k + 1, ub)
        grads(2 * k, ua)
        grad_dot(2 * k + 2, ua)
        grads(2 * k + 1, ub)
        return carry

    lax.fori_loop(0, chunks // 2 - 1, backward, 0)
    grad_dot(chunks - 1, ub)
    grads(chunks - 2, ua)
    grads(chunks - 1, ub)
    dh_ref[...] = y2[...].reshape(width, toks).astype(BF)

    @pl.when(j == last)
    def _():
        for s in range(shards):

            def write(g, carry, s=s):
                grad_refs[s][g, :, :gw] = acc1[s, g].astype(BF)
                grad_refs[s][g, :gw, gw : 2 * gw] = acc2[s, g].astype(BF)
                grad_refs[s][g, gw:, gw : 2 * gw] = jnp.zeros((PAD, gw), BF)
                return carry

            lax.fori_loop(0, groups, write, 0, unroll=2)
        vg_ref[...] = spread(accv, 5)


def spread(sums, first):
    count, width, lanes = sums.shape
    lane = lax.broadcasted_iota(jnp.int32, (width, lanes), 1)
    t = jnp.zeros((width, lanes), F32)
    for i in range(count):
        t = jnp.where(lane == i + first, jnp.sum(sums[i], axis=1, keepdims=True), t)
    return t


def write_halves(full, keep_ref, send_ref, mine, rows):
    if rows % 8:
        keep_ref[...] = full[...].astype(BF)
        send_ref[...] = jnp.zeros_like(send_ref)
        return
    for k in range(keep_ref.shape[0]):
        own = pl.multiple_of((2 * k + mine) * rows, 8)
        other = pl.multiple_of((2 * k + 1 - mine) * rows, 8)
        keep_ref[k] = full[pl.ds(own, rows), :].astype(BF)
        send_ref[k] = full[pl.ds(other, rows), :].astype(BF)


def half_shapes(total, rows, cols):
    if rows % 8:
        return (total, cols), (16, 128)
    return (total // rows // 2, rows, cols), (total // rows // 2, rows, cols)


def core_step(keep, send, rows, index, count):
    if rows % 8:
        keep, send = halves(keep.reshape(-1, rows, keep.shape[-1]), 0, index)
    return keep, swap(send, 0, count)


def norm_kernel(
    me_ref, ctx, n1_ref, rs_ref, dh_ref, vec_ref, wo_ref, vga_ref,
    dy1_ref, dct_ref, keep_ref, send_ref, vg_ref, acco, accv, wo, sem, *, vbase, rows,
):
    j = pl.program_id(0)
    last = pl.num_programs(0) - 1
    inv_width = 1.0 / n1_ref.shape[0]

    def mean(v):
        return jnp.sum(v, axis=0, keepdims=True) * inv_width

    copy = pltpu.make_async_copy(wo_ref, wo, sem)

    @pl.when(j == 0)
    def _():
        copy.start()

    norm1 = n1_ref[...].astype(F32)
    dh1 = dh_ref[...].astype(F32)
    e1 = dh1 * vec_ref[:, vbase + 3 : vbase + 4].astype(F32)
    dy1 = (e1 - mean(e1) - norm1 * mean(e1 * norm1)) * rs_ref[0:1, :]
    low1 = dy1.astype(BF)
    dy1_ref[...] = low1

    @pl.when(j == 0)
    def _():
        copy.wait()

    dct_ref[...] = dg(wo[...], low1, 1, 0).astype(BF)
    sums = (lane_sum(dy1), lane_sum(dh1 * norm1), lane_sum(dh1))
    acco[...] = jnp.where(j == 0, 0.0, acco[...]) + dg(ctx[...], low1, 1, 1)
    for i in range(3):
        accv[i] = jnp.where(j == 0, 0.0, accv[i]) + sums[i]

    @pl.when(j == last)
    def _():
        write_halves(acco, keep_ref, send_ref, me_ref[1], rows)
        vg_ref[...] = vga_ref[...] + spread(accv, 2)


def whole(shape):
    return pl.BlockSpec(shape, lambda j, *m: (0,) * len(shape), pipeline_mode=pl.Buffered(1))


def ffn_layer(xt, ctx, w, wo, wfs, cott, gw):
    width, toks = xt.shape
    blk = min(LONG, toks)
    shards = len(wfs)
    groups = wfs[0].shape[0]
    vec_block = (3 * gw) // 128
    col_blk = lambda rows: pl.BlockSpec((rows, blk), lambda j: (0, j))
    return pl.pallas_call(
        functools.partial(ffn_kernel, shards=shards, gw=gw, vbase=3 * gw - 128 * vec_block),
        out_shape=[
            jax.ShapeDtypeStruct((toks, width), BF),
            jax.ShapeDtypeStruct((width, toks), BF),
            jax.ShapeDtypeStruct((8, toks), F32),
            jax.ShapeDtypeStruct((width, toks), BF),
        ]
        + [jax.ShapeDtypeStruct(wfs[0].shape, BF)] * shards
        + [jax.ShapeDtypeStruct((width, 128), F32)],
        grid=(toks // blk,),
        in_specs=[
            col_blk(width),
            col_blk(width),
            pl.BlockSpec((width, 128), lambda j: (0, vec_block)),
            whole((width, width)),
            col_blk(width),
        ]
        + anywhere(shards),
        out_specs=[
            pl.BlockSpec((blk, width), lambda j: (j, 0)),
            col_blk(width),
            col_blk(8),
            col_blk(width),
        ]
        + [whole(wfs[0].shape) for _ in wfs]
        + [whole((width, 128))],
        scratch_shapes=[
            pltpu.VMEM((shards,) + wfs[0].shape, BF),
            pltpu.VMEM((groups, gw + PAD, blk), BF),
            pltpu.VMEM((gw, blk), F32),
            pltpu.VMEM((gw, blk), F32),
            pltpu.VMEM((groups, shards, gw, blk), BF),
            pltpu.VMEM((groups, shards, gw, blk), F32),
            pltpu.VMEM((groups, gw, blk), F32),
            pltpu.VMEM((groups, gw, blk), BF),
            pltpu.VMEM((groups, blk, gw), BF),
            pltpu.VMEM((shards, groups, gw + PAD, gw), F32),
            pltpu.VMEM((shards, groups, gw, gw), F32),
            pltpu.VMEM((3, width, 128), F32),
            pltpu.SemaphoreType.DMA((shards,)),
        ],
        compiler_params=params(),
        cost_estimate=cost(40),
        name="feed_forward",
    )(xt, ctx, w, wo, cott, *wfs)


def norm_layer(me, ctx, n1, rs1, dh1, w, wo, vga, gw, rows):
    width, toks = n1.shape
    blk = min(LONG, toks)
    vec_block = (3 * gw) // 128
    col_blk = lambda rows: pl.BlockSpec((rows, blk), lambda j, m: (0, j))
    keep, send = half_shapes(width, rows, width)
    return pl.pallas_call(
        functools.partial(norm_kernel, vbase=3 * gw - 128 * vec_block, rows=rows),
        out_shape=[
            jax.ShapeDtypeStruct((width, toks), BF),
            jax.ShapeDtypeStruct((width, toks), BF),
            jax.ShapeDtypeStruct(keep, BF),
            jax.ShapeDtypeStruct(send, BF),
            jax.ShapeDtypeStruct((width, 128), F32),
        ],
        grid_spec=pltpu.PrefetchScalarGridSpec(
            num_scalar_prefetch=1,
            grid=(toks // blk,),
            in_specs=[
                col_blk(width),
                col_blk(width),
                col_blk(8),
                col_blk(width),
                pl.BlockSpec((width, 128), lambda j, m: (0, vec_block)),
                pl.BlockSpec(memory_space=pl.ANY),
                whole((width, 128)),
            ],
            out_specs=[col_blk(width), col_blk(width), whole(keep), whole(send), whole((width, 128))],
            scratch_shapes=[
                pltpu.VMEM((width, width), F32),
                pltpu.VMEM((3, width, 128), F32),
                pltpu.VMEM((width, width), BF),
                pltpu.SemaphoreType.DMA,
            ],
        ),
        compiler_params=params(),
        cost_estimate=cost(7),
        name="norm_backward",
    )(me, ctx, n1, rs1, dh1, w, wo, vga)


def swap(a, bit, count):
    return lax.ppermute(a, AXES, [(i, i ^ (1 << bit)) for i in range(count)])


def gather_bit(cur, b, index, count):
    return merge(cur, swap(cur, b, count), b, index)


def merge(cur, got, b, index):
    place = lax.broadcasted_iota(jnp.int32, (1, 2) + (1,) * (cur.ndim - 1), 1)
    new = jnp.where(place == ((index >> b) & 1), cur[:, None], got[:, None])
    return new.reshape((cur.shape[0] * 2,) + cur.shape[1:])


def halves(cur, b, index):
    pair = cur.reshape((cur.shape[0] // 2, 2) + cur.shape[1:])
    mine = (index >> b) & 1
    keep = lax.dynamic_index_in_dim(pair, mine, 1, keepdims=False)
    return keep, lax.dynamic_index_in_dim(pair, 1 - mine, 1, keepdims=False)


def reduce_bit(cur, b, index, count):
    keep, send = halves(cur, b, index)
    return keep.astype(F32) + swap(send, b, count).astype(F32)


def log2(n):
    return n.bit_length() - 1


def body(
    dp, ffn, tokens, long_seq, cotangent, query_weight, key_weight, value_weight, out_weight,
    query_bias, value_bias, out_bias, attn_gain, attn_shift, ffn_in_weight, ffn_in_bias,
    ffn_out_weight, ffn_out_bias, ffn_gain, ffn_shift,
):
    count = dp * ffn
    index = lax.axis_index("dp") * ffn + lax.axis_index("ffn")
    ffn_bits = list(range(log2(ffn)))
    dp_bits = list(range(log2(ffn), log2(count)))
    all_bits = ffn_bits + dp_bits
    width = tokens.shape[1]
    groups = ffn_in_weight.shape[0]
    gw = width // groups
    hd = width // HEADS
    rows = query_weight.shape[0]

    vectors = [query_bias, value_bias, out_bias, attn_gain, attn_shift, ffn_out_bias, ffn_gain, ffn_shift]
    used = 3 * gw + len(vectors)
    cols = -(-used // 128) * 128
    columns = jnp.pad(jnp.stack(vectors), ((0, cols - used), (0, 0))).T
    both = jnp.concatenate([query_weight, key_weight, value_weight, columns, out_weight], axis=1)[None]
    top = ffn_bits[-1]
    first = jnp.concatenate([ffn_in_weight, ffn_in_bias[:, None, :], jnp.zeros((groups, PAD - 1, gw), BF)], axis=1)
    second = jnp.pad(ffn_out_weight, ((0, 0), (0, PAD), (0, 0)))
    wf = jnp.concatenate([first, second], axis=2)
    xt = tokens.T
    cott = cotangent.T
    flags = jnp.concatenate([long_seq, (index & 1).astype(jnp.int32)[None]])
    for n, b in enumerate(reversed(dp_bits[1:])):
        both = gather_bit(both, b, index, count)
        if n == 0:
            both, flags = lax.optimization_barrier((both, flags))
        if n == 1:
            both, xt = lax.optimization_barrier((both, xt))
    both = gather_bit(both, top, index, count)
    both, wf, cott = lax.optimization_barrier((both, wf, cott))
    got_wf = swap(wf, top, count)
    both = both.reshape(both.shape[0] // 2, 2 * rows, both.shape[2])
    w = gather_bit(both[:, :, :cols], dp_bits[0], index, count).reshape(-1, rows, cols)
    wo = both[:, :, cols:]
    for b in reversed(ffn_bits[:-1]):
        w = gather_bit(w, b, index, count)
    w, wo = lax.optimization_barrier((w, wo))
    w = w.reshape(width, cols)
    got_wo = swap(wo, dp_bits[0], count)

    saved = []
    step = flags
    for i, (g0, ng) in enumerate(FORWARD):
        saved = list(attn_fwd(flags, xt, w, step, saved, g0, ng, gw, hd))
        if i == 0:
            got_wo, saved[4] = lax.optimization_barrier((got_wo, saved[4]))
            wo = merge(wo, got_wo, dp_bits[0], index)
            step = wo = wo.reshape(-1, rows, width)
            got_wo = swap(wo, 0, count)
        if i == 1:
            got_wf, got_wo, saved[4] = lax.optimization_barrier((got_wf, got_wo, saved[4]))
    wo = merge(wo, got_wo, 0, index).reshape(width, width)
    wfs = [wf, swap(wf, 0, count), got_wf, swap(got_wf, 0, count)]
    ctx = saved[4]
    outs = ffn_layer(xt, ctx, w, wo, wfs, cott, gw)
    output, n1, rs1, dh1 = outs[:4]
    gf = outs[4 : 4 + ffn]
    dyt, dct, keep_o, send_o, vg = norm_layer(flags, ctx, n1, rs1, dh1, w, wo, outs[4 + ffn], gw, rows)

    def add(keep, got):
        return (keep.astype(F32) + got.astype(F32)).astype(BF)

    got1 = swap(gf[1], 0, count)
    got3 = swap(gf[3], 0, count)
    send = add(gf[2], got3)
    got2 = swap(send, top, count)
    keep_o, got_o = core_step(keep_o, send_o, rows, index, count)

    grads = []
    step = send
    for i, (g0, ng) in enumerate(BACKWARD):
        grads = list(attn_bwd(flags, saved, dct, xt, w, dyt, vg, step, grads, g0, ng, gw, hd, rows))
        if i == 0:
            got_o, grads[0] = lax.optimization_barrier((got_o, grads[0]))
            keep_o, send_o = halves(add(keep_o, got_o), top, index)
            got2, send_o, grads[0] = lax.optimization_barrier((got2, send_o, grads[0]))
            got_o = swap(send_o, top, count)
            mine = (gf[0].astype(F32) + got1.astype(F32) + got2.astype(F32)).astype(BF)
            keep_f, step = halves(mine.reshape(dp, -1, mine.shape[-1]), dp_bits[0], index)
            got_f = swap(step, dp_bits[0], count)
        if i == 1:
            got_f, got_o, grads[0] = lax.optimization_barrier((got_f, got_o, grads[0]))
            keep_f, step = halves(add(keep_f, got_f), dp_bits[1], index)
            got_f = swap(step, dp_bits[1], count)
            keep_o, send_o = halves(add(keep_o, got_o), dp_bits[0], index)
            got_o = swap(send_o, dp_bits[0], count)
        if i == 2:
            got_f, got_o, grads[1] = lax.optimization_barrier((got_f, got_o, grads[1]))
    ffn_sum = add(keep_f, got_f)
    keep_f, send_f = halves(ffn_sum, dp_bits[2], index)
    got_f = swap(send_f, dp_bits[2], count)
    keep_w, got_w = core_step(grads[1], grads[2], rows, index, count)
    keep_w, send_w = halves(add(keep_w, got_w), top, index)
    keep_w, got_f = lax.optimization_barrier((keep_w, got_f))
    got_w = swap(send_w, top, count)
    ffn_sum = add(keep_f, got_f)
    for b in dp_bits[3:]:
        ffn_sum = reduce_bit(ffn_sum, b, index, count).astype(BF)
    rows_first = Layout(major_to_minor=(0, 1))
    keep_w, send_w = halves(add(keep_w, got_w), dp_bits[0], index)
    got_w = swap(send_w, dp_bits[0], count)
    keep_w, grads[0] = lax.optimization_barrier((keep_w, grads[0]))
    grad_tokens = with_layout_constraint(grads[0].T, rows_first)
    got_w, grad_tokens = lax.optimization_barrier((got_w, grad_tokens))

    for b in reversed(dp_bits):
        ffn_sum = gather_bit(ffn_sum, b, index, count)
    ffn_sum = ffn_sum.reshape(mine.shape).astype(F32)

    both = jnp.concatenate([add(keep_w, got_w), add(keep_o, got_o)], axis=2)
    for b in dp_bits[1:]:
        both = reduce_bit(both, b, index, count)
        if b != dp_bits[-1]:
            both = both.astype(BF)
    dw_sum = both[0, :, :cols]
    dwo_sum = both[0, :, cols:]
    vec = lambda i: dw_sum[:, 3 * gw + i]
    return (
        output,
        grad_tokens,
        dw_sum[:, :gw],
        dw_sum[:, gw : 2 * gw],
        dw_sum[:, 2 * gw : 3 * gw],
        dwo_sum,
        vec(0),
        vec(1),
        vec(2),
        vec(3),
        vec(4),
        ffn_sum[:, :gw, :gw],
        ffn_sum[:, gw, :gw],
        ffn_sum[:, :gw, gw:],
        vec(5),
        vec(6),
        vec(7),
    )


def solution(mesh):
    both = P(AXES)
    rows = P(AXES, None)
    return jax.shard_map(
        functools.partial(body, mesh.shape["dp"], mesh.shape["ffn"]),
        mesh=mesh,
        in_specs=(
            rows, both, rows, rows, rows, rows, rows, both, both, both, both, both,
            P(None, None, "ffn"), P(None, "ffn"), P(None, "ffn", None), both, both, both,
        ),
        out_specs=(
            rows, rows, rows, rows, rows, rows, both, both, both, both, both,
            P(None, None, "ffn"), P(None, "ffn"), P(None, "ffn", None), both, both, both,
        ),
        check_vma=False,
    )
```

```python
import functools

import jax
import jax.numpy as jnp
from jax import lax
from jax.experimental import pallas as pl
from jax.experimental.layout import Layout, with_layout_constraint
from jax.experimental.pallas import tpu as pltpu
from jax.sharding import PartitionSpec as P

F32 = jnp.float32
BF = jnp.bfloat16
HEADS = 12
LONG = 512
SHORT = 128
EPS = 1e-12
AXES = ("dp", "ffn")
PAD = 16

ROOT_HALF = 0.7071067811865476
INV_ROOT_2PI = 0.3989422804014327
HALF_LOG2E = -0.7213475204444817
FORWARD = ((0, 2), (2, 2))
BACKWARD = ((0, 2), (2, 1), (3, 1))


def dg(a, b, ca, cb):
    return lax.dot_general(a, b, (((ca,), (cb,)), ((), ())), preferred_element_type=F32)


def lane_sum(v):
    out = v[:, :128]
    for c in range(128, v.shape[1], 128):
        out = out + v[:, c : c + 128]
    return out


def params():
    return pltpu.CompilerParams(vmem_limit_bytes=63 << 20)


def cost(us):
    return pl.CostEstimate(flops=int(us * 1e9), bytes_accessed=int(us * 3e6), transcendentals=0)


def across(s, outside):
    rows = []
    for a in range(0, LONG, SHORT):
        cells = []
        for b in range(0, LONG, SHORT):
            cell = s[a : a + SHORT, b : b + SHORT]
            cells.append(cell if a == b else cell + outside)
        rows.append(jnp.concatenate(cells, axis=1))
    return jnp.concatenate(rows, axis=0)


def attn_fwd_kernel(flag_ref, x_ref, w_ref, step_ref, *refs, gw, hd):
    q_ref, k_ref, v_ref, e_ref, c_ref, inv_ref, sa, sb = refs[-8:]
    w = w_ref[...]
    p = dg(w[:, : 3 * gw], x_ref[...], 0, 0)
    bq = w[:, 3 * gw : 3 * gw + 1].astype(F32)
    bv = w[:, 3 * gw + 1 : 3 * gw + 2].astype(F32)
    q_ref[...] = (p[:gw] + bq).astype(BF)
    k_ref[...] = p[gw : 2 * gw].astype(BF)
    v_ref[...] = (p[2 * gw :] + bv).astype(BF)
    inv_ref[...] = jnp.zeros_like(inv_ref)
    outside = jnp.where(flag_ref[0] == 1, 0.0, -1e9).astype(F32)
    ones = jnp.ones((16, LONG), BF)
    heads = [slice(h * hd, (h + 1) * hd) for h in range(gw // hd)]

    def scores(h, buf):
        q = q_ref[heads[h], :] * jnp.asarray(hd**-0.5, BF)
        buf[...] = dg(k_ref[heads[h], :], q, 0, 0)

    bufs = (sa, sb)
    scores(0, sa)
    for h, r in enumerate(heads):
        if h + 1 < len(heads):
            scores(h + 1, bufs[(h + 1) % 2])
        s = across(bufs[h % 2][...], outside)
        m = jnp.max(s, axis=0, keepdims=True)
        e = jnp.exp(s - m).astype(BF)
        e_ref[h, 0] = e
        o = dg(jnp.concatenate([v_ref[r, :], ones], 0), e, 1, 0)
        inv = 1.0 / o[hd : hd + 1]
        c_ref[r, :] = (o[:hd] * inv).astype(BF)
        inv_ref[h : h + 1, :] = inv


def anywhere(count):
    return [pl.BlockSpec(memory_space=pl.ANY) for _ in range(count)]


def attn_fwd(flag, xt, w, step, before, g0, ng, gw, hd):
    width, toks = xt.shape
    groups = width // gw
    blocks = toks // LONG
    nh = gw // hd
    own = lambda: pl.BlockSpec((gw, LONG), lambda g, j, f: (g0 + g, j))
    return pl.pallas_call(
        functools.partial(attn_fwd_kernel, gw=gw, hd=hd),
        out_shape=[jax.ShapeDtypeStruct((width, toks), BF)] * 3
        + [
            jax.ShapeDtypeStruct((groups * nh, blocks, LONG, LONG), BF),
            jax.ShapeDtypeStruct((width, toks), BF),
            jax.ShapeDtypeStruct((groups * 8, toks), F32),
        ],
        grid_spec=pltpu.PrefetchScalarGridSpec(
            num_scalar_prefetch=1,
            grid=(ng, blocks),
            in_specs=[own(), pl.BlockSpec((gw, w.shape[1]), lambda g, j, f: (g0 + g, 0))] + anywhere(1 + len(before)),
            out_specs=[
                own(),
                own(),
                own(),
                pl.BlockSpec((nh, 1, LONG, LONG), lambda g, j, f: (g0 + g, j, 0, 0)),
                own(),
                pl.BlockSpec((8, LONG), lambda g, j, f: (g0 + g, j)),
            ],
            scratch_shapes=[pltpu.VMEM((LONG, LONG), F32)] * 2,
        ),
        input_output_aliases={4 + i: i for i in range(len(before))},
        compiler_params=params(),
        cost_estimate=cost(5 * ng),
        name="attention_forward",
    )(flag, xt, w, step, *before)


def attn_bwd_kernel(
    flag_ref, q_ref, k_ref, v_ref, e_ref, c_ref, inv_ref, dc_ref, x_ref, w_ref, dy_ref, vg_ref, step_ref,
    *refs, gw, hd, rows,
):
    g_ref, keep_ref, send_ref, acc, dq, bacc, pa, pb = refs[-8:]
    nh = gw // hd
    j = pl.program_id(1)
    heads = [slice(h * hd, (h + 1) * hd) for h in range(nh)]
    scaled = []

    def grad_probs(h, buf):
        dc = dc_ref[heads[h], :].astype(F32)
        inv = inv_ref[h : h + 1, :]
        total = jnp.sum(dc * c_ref[heads[h], :].astype(F32), axis=0, keepdims=True) * inv
        scaled.append(((dc * inv).astype(BF), total))
        buf[...] = dg(v_ref[heads[h], :], scaled[h][0], 0, 0)

    bufs = (pa, pb)
    grad_probs(0, pa)
    for h, r in enumerate(heads):
        if h + 1 < nh:
            grad_probs(h + 1, bufs[(h + 1) % 2])
        dci, total = scaled[h]
        e = e_ref[h, 0]
        dq[2 * gw + h * hd : 2 * gw + (h + 1) * hd, :] = dg(dci, e, 1, 1)
        ds = (e.astype(F32) * (bufs[h % 2][...] - total)).astype(BF)
        qs = q_ref[r, :] * jnp.asarray(hd**-0.5, BF)
        dq[gw + h * hd : gw + (h + 1) * hd, :] = dg(qs, ds, 1, 1)
        dq[r, :] = dg(k_ref[r, :], ds, 1, 0) * (hd**-0.5)

    d = dq[...]
    dl = d.astype(BF)
    w = w_ref[...]
    g_ref[...] = (dy_ref[...] + dg(w[:, : 3 * gw], dl, 1, 0)).astype(BF)
    acc[:, : 3 * gw] = jnp.where(j == 0, 0.0, acc[:, : 3 * gw]) + dg(x_ref[...], dl, 1, 1)
    bacc[0] = jnp.where(j == 0, 0.0, bacc[0]) + lane_sum(d[:gw])
    bacc[1] = jnp.where(j == 0, 0.0, bacc[1]) + lane_sum(d[2 * gw :])

    @pl.when(j == pl.num_programs(1) - 1)
    def _():
        rest = acc.shape[1] - 3 * gw
        bqc = jnp.sum(bacc[0], axis=1, keepdims=True)
        bvc = jnp.sum(bacc[1], axis=1, keepdims=True)
        lane = lax.broadcasted_iota(jnp.int32, (gw, rest), 1)
        vectors = jnp.where(lane == 0, bqc, jnp.where(lane == 1, bvc, vg_ref[...][:, :rest]))
        acc[:, 3 * gw :] = vectors
        write_halves(acc, keep_ref, send_ref, flag_ref[1], rows)


def attn_bwd(flag, saved, dct, xt, w, dyt, vg, step, before, g0, ng, gw, hd, rows):
    q, k, v, e, c, inv = saved
    width, toks = xt.shape
    groups = width // gw
    blocks = toks // LONG
    nh = gw // hd
    cols = w.shape[1]
    keep, send = half_shapes(gw, rows, cols)
    own = lambda: pl.BlockSpec((gw, LONG), lambda g, j, f: (g0 + g, j))
    return pl.pallas_call(
        functools.partial(attn_bwd_kernel, gw=gw, hd=hd, rows=rows),
        out_shape=[
            jax.ShapeDtypeStruct((width, toks), BF),
            jax.ShapeDtypeStruct((groups * keep[0],) + keep[1:], BF),
            jax.ShapeDtypeStruct((groups * send[0],) + send[1:], BF),
        ],
        grid_spec=pltpu.PrefetchScalarGridSpec(
            num_scalar_prefetch=1,
            grid=(ng, blocks),
            in_specs=[
                own(),
                own(),
                own(),
                pl.BlockSpec((nh, 1, LONG, LONG), lambda g, j, f: (g0 + g, j, 0, 0)),
                own(),
                pl.BlockSpec((8, LONG), lambda g, j, f: (g0 + g, j)),
                own(),
                own(),
                pl.BlockSpec((gw, cols), lambda g, j, f: (g0 + g, 0)),
                own(),
                pl.BlockSpec((gw, 128), lambda g, j, f: (g0 + g, 0)),
            ]
            + anywhere(1 + len(before)),
            out_specs=[
                own(),
                pl.BlockSpec(keep, lambda g, j, f: (g0 + g,) + (0,) * (len(keep) - 1)),
                pl.BlockSpec(send, lambda g, j, f: (g0 + g,) + (0,) * (len(send) - 1)),
            ],
            scratch_shapes=[
                pltpu.VMEM((gw, cols), F32),
                pltpu.VMEM((3 * gw, LONG), F32),
                pltpu.VMEM((2, gw, 128), F32),
                pltpu.VMEM((LONG, LONG), F32),
                pltpu.VMEM((LONG, LONG), F32),
            ],
        ),
        input_output_aliases={13 + i: i for i in range(len(before))},
        compiler_params=params(),
        cost_estimate=cost(7 * ng),
        name="attention_backward",
    )(flag, q, k, v, e, c, inv, dct, xt, w, dyt, vg, step, *before)


def ffn_kernel(x_ref, ctx, vec_ref, wo_ref, cot_ref, *refs, shards, gw, vbase):
    wf_refs = refs[:shards]
    rest = refs[shards:]
    out_ref, n1_ref, rs_ref, dh_ref = rest[:4]
    grad_refs = rest[4 : 4 + shards]
    vg_ref = rest[4 + shards]
    wf, h1x, ua, ub, act, slope, y2, dyl, dyt, acc1, acc2, accv, sems = rest[5 + shards :]
    j = pl.program_id(0)
    last = pl.num_programs(0) - 1
    groups = h1x.shape[0]
    toks = x_ref.shape[1]
    width = groups * gw
    inv_width = 1.0 / width

    def col(i):
        return vec_ref[:, vbase + i : vbase + i + 1].astype(F32)

    def mean(v):
        return jnp.sum(v, axis=0, keepdims=True) * inv_width

    copies = [pltpu.make_async_copy(wf_refs[s], wf.at[s], sems.at[s]) for s in range(shards)]

    @pl.when(j == 0)
    def _():
        for copy in copies:
            copy.start()
        accv[...] = jnp.zeros_like(accv)

    y1 = x_ref[...].astype(F32) + dg(wo_ref[...], ctx[...], 0, 0) + col(2)
    center = y1 - mean(y1)
    rs1 = lax.rsqrt(mean(center * center) + EPS)
    rs_ref[...] = jnp.broadcast_to(rs1, rs_ref.shape)
    norm1 = center * rs1
    n1_ref[...] = norm1.astype(BF)
    h1 = norm1 * col(3) + col(4)
    y2[...] = (h1 + col(5)).reshape(groups, gw, toks)
    h1x[:, :gw, :] = h1.astype(BF).reshape(groups, gw, toks)
    h1x[:, gw:, :] = jnp.ones((groups, PAD, toks), BF)

    chunks = groups * shards

    def first_dot(i, buf):
        buf[...] = dg(wf[i % shards, i // shards, :, :gw], h1x[i // shards], 0, 0)

    def second_dot(i):
        g = i // shards
        s = i % shards
        y2[g] += dg(wf[s, g, :gw, gw : 2 * gw], act[g, s], 0, 0)

    def gelu(i, buf):
        g = i // shards
        s = i % shards
        u = buf[...]
        phi = lax.erf(u * ROOT_HALF) * 0.5 + 0.5
        act[g, s] = (u * phi).astype(BF)
        slope[g, s] = phi + u * INV_ROOT_2PI * jnp.exp2(u * u * HALF_LOG2E)

    @pl.when(j == 0)
    def _():
        for copy in copies:
            copy.wait()

    first_dot(0, ua)
    first_dot(1, ub)
    gelu(0, ua)

    def forward(k, carry):
        i = 2 * k + 1
        second_dot(i - 1)
        first_dot(i + 1, ua)
        gelu(i, ub)
        second_dot(i)
        first_dot(i + 2, ub)
        gelu(i + 1, ua)
        return carry

    lax.fori_loop(0, chunks // 2 - 1, forward, 0)
    second_dot(chunks - 2)
    gelu(chunks - 1, ub)
    second_dot(chunks - 1)

    yy = y2[...].reshape(width, toks)
    center = yy - mean(yy)
    rs2 = lax.rsqrt(mean(center * center) + EPS)
    norm2 = center * rs2
    out_ref[...] = (norm2 * col(6) + col(7)).astype(BF).T
    cot = cot_ref[...].astype(F32)
    e2 = cot * col(6)
    dy2 = (e2 - mean(e2) - norm2 * mean(e2 * norm2)) * rs2
    accv[0] += lane_sum(dy2)
    accv[1] += lane_sum(cot * norm2)
    accv[2] += lane_sum(cot)
    y2[...] = dy2.reshape(groups, gw, toks)
    dyl[...] = dy2.astype(BF).reshape(groups, gw, toks)
    for g in range(groups):
        dyt[g] = dyl[g].T

    def grad_dot(i, buf):
        g = i // shards
        buf[...] = dg(wf[i % shards, g, :gw, gw : 2 * gw], dyl[g], 1, 0)

    def grads(i, buf):
        g = i // shards
        s = i % shards
        low = (buf[...] * slope[g, s]).astype(BF)
        acc2[s, g] = jnp.where(j == 0, 0.0, acc2[s, g]) + dg(act[g, s], dyt[g], 1, 0)
        y2[g] += dg(wf[s, g, :gw, :gw], low, 1, 0)
        acc1[s, g] = jnp.where(j == 0, 0.0, acc1[s, g]) + dg(h1x[g], low, 1, 1)

    grad_dot(0, ua)

    def backward(k, carry):
        grad_dot(2 * k + 1, ub)
        grads(2 * k, ua)
        grad_dot(2 * k + 2, ua)
        grads(2 * k + 1, ub)
        return carry

    lax.fori_loop(0, chunks // 2 - 1, backward, 0)
    grad_dot(chunks - 1, ub)
    grads(chunks - 2, ua)
    grads(chunks - 1, ub)
    dh_ref[...] = y2[...].reshape(width, toks)

    @pl.when(j == last)
    def _():
        for s in range(shards):

            def write(g, carry, s=s):
                grad_refs[s][g, :, :gw] = acc1[s, g].astype(BF)
                grad_refs[s][g, :gw, gw : 2 * gw] = acc2[s, g].astype(BF)
                grad_refs[s][g, gw:, gw : 2 * gw] = jnp.zeros((PAD, gw), BF)
                return carry

            lax.fori_loop(0, groups, write, 0, unroll=2)
        vg_ref[...] = spread(accv, 5)


def spread(sums, first):
    count, width, lanes = sums.shape
    lane = lax.broadcasted_iota(jnp.int32, (width, lanes), 1)
    t = jnp.zeros((width, lanes), F32)
    for i in range(count):
        t = jnp.where(lane == i + first, jnp.sum(sums[i], axis=1, keepdims=True), t)
    return t


def write_halves(full, keep_ref, send_ref, mine, rows, second=None):
    if rows % 8:
        keep_ref[...] = full[...].astype(BF)
        send_ref[...] = jnp.zeros_like(send_ref)
        return
    blocks = keep_ref.shape[0]
    for i in range(blocks):
        k = i
        if second is not None:
            k = 2 * (i % (blocks // 2)) + (second ^ (i // (blocks // 2)))
        own = pl.multiple_of((2 * k + mine) * rows, 8)
        other = pl.multiple_of((2 * k + 1 - mine) * rows, 8)
        keep_ref[i] = full[pl.ds(own, rows), :].astype(BF)
        send_ref[i] = full[pl.ds(other, rows), :].astype(BF)


def half_shapes(total, rows, cols):
    if rows % 8:
        return (total, cols), (16, 128)
    return (total // rows // 2, rows, cols), (total // rows // 2, rows, cols)


def core_step(keep, send, rows, index, count):
    if rows % 8:
        keep, send = halves(keep.reshape(-1, rows, keep.shape[-1]), 0, index)
    return keep, swap(send, 0, count)


def norm_kernel(
    me_ref, ctx, n1_ref, rs_ref, dh_ref, vec_ref, wo_ref, vga_ref,
    dy1_ref, dct_ref, keep_ref, send_ref, vg_ref, acco, accv, *, vbase, rows,
):
    j = pl.program_id(0)
    last = pl.num_programs(0) - 1
    inv_width = 1.0 / n1_ref.shape[0]

    def mean(v):
        return jnp.sum(v, axis=0, keepdims=True) * inv_width

    norm1 = n1_ref[...].astype(F32)
    dh1 = dh_ref[...]
    e1 = dh1 * vec_ref[:, vbase + 3 : vbase + 4].astype(F32)
    dy1 = (e1 - mean(e1) - norm1 * mean(e1 * norm1)) * rs_ref[0:1, :]
    dy1_ref[...] = dy1
    low1 = dy1.astype(BF)
    dct_ref[...] = dg(wo_ref[...], low1, 1, 0).astype(BF)
    sums = (lane_sum(dy1), lane_sum(dh1 * norm1), lane_sum(dh1))
    acco[...] = jnp.where(j == 0, 0.0, acco[...]) + dg(ctx[...], low1, 1, 1)
    for i in range(3):
        accv[i] = jnp.where(j == 0, 0.0, accv[i]) + sums[i]

    @pl.when(j == last)
    def _():
        write_halves(acco, keep_ref, send_ref, me_ref[1], rows, me_ref[2])
        vg_ref[...] = vga_ref[...] + spread(accv, 2)


def whole(shape):
    return pl.BlockSpec(shape, lambda j, *m: (0,) * len(shape), pipeline_mode=pl.Buffered(1))


def ffn_layer(xt, ctx, w, wo, wfs, cott, gw):
    width, toks = xt.shape
    blk = min(LONG, toks)
    shards = len(wfs)
    groups = wfs[0].shape[0]
    vec_block = (3 * gw) // 128
    col_blk = lambda rows: pl.BlockSpec((rows, blk), lambda j: (0, j))
    return pl.pallas_call(
        functools.partial(ffn_kernel, shards=shards, gw=gw, vbase=3 * gw - 128 * vec_block),
        out_shape=[
            jax.ShapeDtypeStruct((toks, width), BF),
            jax.ShapeDtypeStruct((width, toks), BF),
            jax.ShapeDtypeStruct((8, toks), F32),
            jax.ShapeDtypeStruct((width, toks), F32),
        ]
        + [jax.ShapeDtypeStruct(wfs[0].shape, BF)] * shards
        + [jax.ShapeDtypeStruct((width, 128), F32)],
        grid=(toks // blk,),
        in_specs=[
            col_blk(width),
            col_blk(width),
            pl.BlockSpec((width, 128), lambda j: (0, vec_block)),
            whole((width, width)),
            col_blk(width),
        ]
        + anywhere(shards),
        out_specs=[
            pl.BlockSpec((blk, width), lambda j: (j, 0)),
            col_blk(width),
            col_blk(8),
            col_blk(width),
        ]
        + [whole(wfs[0].shape) for _ in wfs]
        + [whole((width, 128))],
        scratch_shapes=[
            pltpu.VMEM((shards,) + wfs[0].shape, BF),
            pltpu.VMEM((groups, gw + PAD, blk), BF),
            pltpu.VMEM((gw, blk), F32),
            pltpu.VMEM((gw, blk), F32),
            pltpu.VMEM((groups, shards, gw, blk), BF),
            pltpu.VMEM((groups, shards, gw, blk), F32),
            pltpu.VMEM((groups, gw, blk), F32),
            pltpu.VMEM((groups, gw, blk), BF),
            pltpu.VMEM((groups, blk, gw), BF),
            pltpu.VMEM((shards, groups, gw + PAD, gw), F32),
            pltpu.VMEM((shards, groups, gw, gw), F32),
            pltpu.VMEM((3, width, 128), F32),
            pltpu.SemaphoreType.DMA((shards,)),
        ],
        compiler_params=params(),
        cost_estimate=cost(40),
        name="feed_forward",
    )(xt, ctx, w, wo, cott, *wfs)


def norm_layer(me, ctx, n1, rs1, dh1, w, wo, vga, gw, rows):
    width, toks = n1.shape
    blk = min(LONG, toks)
    vec_block = (3 * gw) // 128
    col_blk = lambda rows: pl.BlockSpec((rows, blk), lambda j, m: (0, j))
    keep, send = half_shapes(width, rows, width)
    return pl.pallas_call(
        functools.partial(norm_kernel, vbase=3 * gw - 128 * vec_block, rows=rows),
        out_shape=[
            jax.ShapeDtypeStruct((width, toks), F32),
            jax.ShapeDtypeStruct((width, toks), BF),
            jax.ShapeDtypeStruct(keep, BF),
            jax.ShapeDtypeStruct(send, BF),
            jax.ShapeDtypeStruct((width, 128), F32),
        ],
        grid_spec=pltpu.PrefetchScalarGridSpec(
            num_scalar_prefetch=1,
            grid=(toks // blk,),
            in_specs=[
                col_blk(width),
                col_blk(width),
                col_blk(8),
                col_blk(width),
                pl.BlockSpec((width, 128), lambda j, m: (0, vec_block)),
                whole((width, width)),
                whole((width, 128)),
            ],
            out_specs=[col_blk(width), col_blk(width), whole(keep), whole(send), whole((width, 128))],
            scratch_shapes=[
                pltpu.VMEM((width, width), F32),
                pltpu.VMEM((3, width, 128), F32),
            ],
        ),
        compiler_params=params(),
        cost_estimate=cost(7),
        name="norm_backward",
    )(me, ctx, n1, rs1, dh1, w, wo, vga)


def swap(a, bit, count):
    return lax.ppermute(a, AXES, [(i, i ^ (1 << bit)) for i in range(count)])


def gather_bit(cur, b, index, count):
    return merge(cur, swap(cur, b, count), b, index)


def merge(cur, got, b, index):
    place = lax.broadcasted_iota(jnp.int32, (1, 2) + (1,) * (cur.ndim - 1), 1)
    new = jnp.where(place == ((index >> b) & 1), cur[:, None], got[:, None])
    return new.reshape((cur.shape[0] * 2,) + cur.shape[1:])


def halves(cur, b, index):
    pair = cur.reshape((cur.shape[0] // 2, 2) + cur.shape[1:])
    mine = (index >> b) & 1
    keep = lax.dynamic_index_in_dim(pair, mine, 1, keepdims=False)
    return keep, lax.dynamic_index_in_dim(pair, 1 - mine, 1, keepdims=False)


def reduce_bit(cur, b, index, count):
    keep, send = halves(cur, b, index)
    return keep.astype(F32) + swap(send, b, count).astype(F32)


def log2(n):
    return n.bit_length() - 1


def body(
    dp, ffn, tokens, long_seq, cotangent, query_weight, key_weight, value_weight, out_weight,
    query_bias, value_bias, out_bias, attn_gain, attn_shift, ffn_in_weight, ffn_in_bias,
    ffn_out_weight, ffn_out_bias, ffn_gain, ffn_shift,
):
    count = dp * ffn
    index = lax.axis_index("dp") * ffn + lax.axis_index("ffn")
    ffn_bits = list(range(log2(ffn)))
    dp_bits = list(range(log2(ffn), log2(count)))
    all_bits = ffn_bits + dp_bits
    width = tokens.shape[1]
    groups = ffn_in_weight.shape[0]
    gw = width // groups
    hd = width // HEADS
    rows = query_weight.shape[0]

    vectors = [query_bias, value_bias, out_bias, attn_gain, attn_shift, ffn_out_bias, ffn_gain, ffn_shift]
    used = 3 * gw + len(vectors)
    cols = -(-used // 128) * 128
    columns = jnp.pad(jnp.stack(vectors), ((0, cols - used), (0, 0))).T
    both = jnp.concatenate([query_weight, key_weight, value_weight, columns, out_weight], axis=1)[None]
    top = ffn_bits[-1]
    first = jnp.concatenate([ffn_in_weight, ffn_in_bias[:, None, :], jnp.zeros((groups, PAD - 1, gw), BF)], axis=1)
    second = jnp.pad(ffn_out_weight, ((0, 0), (0, PAD), (0, 0)))
    wf = jnp.concatenate([first, second], axis=2)
    xt = tokens.T
    cott = cotangent.T
    flags = jnp.concatenate([long_seq, (index & 1).astype(jnp.int32)[None], ((index >> 1) & 1).astype(jnp.int32)[None]])
    for n, b in enumerate(reversed(dp_bits[1:])):
        both = gather_bit(both, b, index, count)
        if n == 0:
            both, flags = lax.optimization_barrier((both, flags))
        if n == 1:
            both, xt = lax.optimization_barrier((both, xt))
    both = gather_bit(both, top, index, count)
    both, wf, cott = lax.optimization_barrier((both, wf, cott))
    got_wf = swap(wf, top, count)
    both = both.reshape(both.shape[0] // 2, 2 * rows, both.shape[2])
    w = gather_bit(both[:, :, :cols], dp_bits[0], index, count).reshape(-1, rows, cols)
    wo = both[:, :, cols:]
    for b in reversed(ffn_bits[:-1]):
        w = gather_bit(w, b, index, count)
    w, wo = lax.optimization_barrier((w, wo))
    w = w.reshape(width, cols)
    got_wo = swap(wo, dp_bits[0], count)

    saved = []
    step = flags
    for i, (g0, ng) in enumerate(FORWARD):
        saved = list(attn_fwd(flags, xt, w, step, saved, g0, ng, gw, hd))
        if i == 0:
            got_wo, saved[4] = lax.optimization_barrier((got_wo, saved[4]))
            wo = merge(wo, got_wo, dp_bits[0], index)
            step = wo = wo.reshape(-1, rows, width)
            got_wo = swap(wo, 0, count)
        if i == 1:
            got_wf, got_wo, saved[4] = lax.optimization_barrier((got_wf, got_wo, saved[4]))
    wo = merge(wo, got_wo, 0, index).reshape(width, width)
    wfs = [wf, swap(wf, 0, count), got_wf, swap(got_wf, 0, count)]
    ctx = saved[4]
    outs = ffn_layer(xt, ctx, w, wo, wfs, cott, gw)
    output, n1, rs1, dh1 = outs[:4]
    gf = outs[4 : 4 + ffn]
    dyt, dct, keep_o, send_o, vg = norm_layer(flags, ctx, n1, rs1, dh1, w, wo, outs[4 + ffn], gw, rows)

    def add(keep, got):
        return (keep.astype(F32) + got.astype(F32)).astype(BF)

    got1 = swap(gf[1], 0, count)
    got3 = swap(gf[3], 0, count)
    send = add(gf[2], got3)
    got2 = swap(send, top, count)
    keep_o, got_o = core_step(keep_o, send_o, rows, index, count)

    grads = []
    step = send
    for i, (g0, ng) in enumerate(BACKWARD):
        grads = list(attn_bwd(flags, saved, dct, xt, w, dyt, vg, step, grads, g0, ng, gw, hd, rows))
        if i == 0:
            got_o, grads[0] = lax.optimization_barrier((got_o, grads[0]))
            if rows % 8:
                keep_o, send_o = halves(add(keep_o, got_o), top, index)
            else:
                cut = keep_o.shape[0] // 2
                send_o = add(keep_o[cut:], got_o[cut:])
                keep_o = add(keep_o[:cut], got_o[:cut])
            got2, send_o, grads[0] = lax.optimization_barrier((got2, send_o, grads[0]))
            got_o = swap(send_o, top, count)
            mine = (gf[0].astype(F32) + got1.astype(F32) + got2.astype(F32)).astype(BF)
            keep_f, step = halves(mine.reshape(dp, -1, mine.shape[-1]), dp_bits[0], index)
            got_f = swap(step, dp_bits[0], count)
        if i == 1:
            got_f, got_o, grads[0] = lax.optimization_barrier((got_f, got_o, grads[0]))
            keep_f, step = halves(add(keep_f, got_f), dp_bits[1], index)
            got_f = swap(step, dp_bits[1], count)
            keep_o, send_o = halves(add(keep_o, got_o), dp_bits[0], index)
            got_o = swap(send_o, dp_bits[0], count)
        if i == 2:
            got_f, got_o, grads[1] = lax.optimization_barrier((got_f, got_o, grads[1]))
    ffn_sum = add(keep_f, got_f)
    keep_f, send_f = halves(ffn_sum, dp_bits[2], index)
    got_f = swap(send_f, dp_bits[2], count)
    keep_w, got_w = core_step(grads[1], grads[2], rows, index, count)
    keep_w, send_w = halves(add(keep_w, got_w), top, index)
    keep_w, got_f = lax.optimization_barrier((keep_w, got_f))
    got_w = swap(send_w, top, count)
    ffn_sum = add(keep_f, got_f)
    for b in dp_bits[3:]:
        ffn_sum = reduce_bit(ffn_sum, b, index, count).astype(BF)
    rows_first = Layout(major_to_minor=(0, 1))
    keep_w, send_w = halves(add(keep_w, got_w), dp_bits[0], index)
    got_w = swap(send_w, dp_bits[0], count)
    keep_w, grads[0] = lax.optimization_barrier((keep_w, grads[0]))
    grad_tokens = with_layout_constraint(grads[0].T, rows_first)
    got_w, grad_tokens = lax.optimization_barrier((got_w, grad_tokens))

    for b in reversed(dp_bits):
        ffn_sum = gather_bit(ffn_sum, b, index, count)
    ffn_sum = ffn_sum.reshape(mine.shape).astype(F32)

    both = jnp.concatenate([add(keep_w, got_w), add(keep_o, got_o)], axis=2)
    for b in dp_bits[1:]:
        both = reduce_bit(both, b, index, count)
        if b != dp_bits[-1]:
            both = both.astype(BF)
    dw_sum = both[0, :, :cols]
    dwo_sum = both[0, :, cols:]
    vec = lambda i: dw_sum[:, 3 * gw + i]
    return (
        output,
        grad_tokens,
        dw_sum[:, :gw],
        dw_sum[:, gw : 2 * gw],
        dw_sum[:, 2 * gw : 3 * gw],
        dwo_sum,
        vec(0),
        vec(1),
        vec(2),
        vec(3),
        vec(4),
        ffn_sum[:, :gw, :gw],
        ffn_sum[:, gw, :gw],
        ffn_sum[:, :gw, gw:],
        vec(5),
        vec(6),
        vec(7),
    )


def solution(mesh):
    both = P(AXES)
    rows = P(AXES, None)
    return jax.shard_map(
        functools.partial(body, mesh.shape["dp"], mesh.shape["ffn"]),
        mesh=mesh,
        in_specs=(
            rows, both, rows, rows, rows, rows, rows, both, both, both, both, both,
            P(None, None, "ffn"), P(None, "ffn"), P(None, "ffn", None), both, both, both,
        ),
        out_specs=(
            rows, rows, rows, rows, rows, rows, both, both, both, both, both,
            P(None, None, "ffn"), P(None, "ffn"), P(None, "ffn", None), both, both, both,
        ),
        check_vma=False,
    )
```

```python
import functools

import jax
import jax.numpy as jnp
from jax import lax
from jax.experimental import pallas as pl
from jax.experimental.layout import Layout, with_layout_constraint
from jax.experimental.pallas import tpu as pltpu
from jax.sharding import PartitionSpec as P

F32 = jnp.float32
BF = jnp.bfloat16
HEADS = 12
LONG = 512
SHORT = 128
EPS = 1e-12
AXES = ("dp", "ffn")
PAD = 16

ROOT_HALF = 0.7071067811865476
INV_ROOT_2PI = 0.3989422804014327
HALF_LOG2E = -0.7213475204444817
FORWARD = ((0, 2), (2, 2))
BACKWARD = ((0, 2), (2, 1), (3, 1))


def dg(a, b, ca, cb):
    return lax.dot_general(a, b, (((ca,), (cb,)), ((), ())), preferred_element_type=F32)


def lane_sum(v):
    out = v[:, :128]
    for c in range(128, v.shape[1], 128):
        out = out + v[:, c : c + 128]
    return out


def params():
    return pltpu.CompilerParams(vmem_limit_bytes=63 << 20)


def cost(us):
    return pl.CostEstimate(flops=int(us * 1e9), bytes_accessed=int(us * 3e6), transcendentals=0)


def across(s, outside):
    rows = []
    for a in range(0, LONG, SHORT):
        cells = []
        for b in range(0, LONG, SHORT):
            cell = s[a : a + SHORT, b : b + SHORT]
            cells.append(cell if a == b else cell + outside)
        rows.append(jnp.concatenate(cells, axis=1))
    return jnp.concatenate(rows, axis=0)


def attn_fwd_kernel(flag_ref, x_ref, w_ref, step_ref, *refs, gw, hd):
    q_ref, k_ref, v_ref, e_ref, c_ref, inv_ref, sa, sb = refs[-8:]
    w = w_ref[...]
    p = dg(w[:, : 3 * gw], x_ref[...], 0, 0)
    bq = w[:, 3 * gw : 3 * gw + 1].astype(F32)
    bv = w[:, 3 * gw + 1 : 3 * gw + 2].astype(F32)
    q_ref[...] = (p[:gw] + bq).astype(BF)
    k_ref[...] = p[gw : 2 * gw].astype(BF)
    v_ref[...] = (p[2 * gw :] + bv).astype(BF)
    inv_ref[...] = jnp.zeros_like(inv_ref)
    outside = jnp.where(flag_ref[0] == 1, 0.0, -1e9).astype(F32)
    ones = jnp.ones((16, LONG), BF)
    heads = [slice(h * hd, (h + 1) * hd) for h in range(gw // hd)]

    def scores(h, buf):
        q = q_ref[heads[h], :] * jnp.asarray(hd**-0.5, BF)
        buf[...] = dg(k_ref[heads[h], :], q, 0, 0)

    bufs = (sa, sb)
    scores(0, sa)
    for h, r in enumerate(heads):
        if h + 1 < len(heads):
            scores(h + 1, bufs[(h + 1) % 2])
        s = across(bufs[h % 2][...], outside)
        m = jnp.max(s, axis=0, keepdims=True)
        e = jnp.exp(s - m).astype(BF)
        e_ref[h, 0] = e
        o = dg(jnp.concatenate([v_ref[r, :], ones], 0), e, 1, 0)
        inv = 1.0 / o[hd : hd + 1]
        c_ref[r, :] = (o[:hd] * inv).astype(BF)
        inv_ref[h : h + 1, :] = inv


def anywhere(count):
    return [pl.BlockSpec(memory_space=pl.ANY) for _ in range(count)]


def attn_fwd(flag, xt, w, step, before, g0, ng, gw, hd):
    width, toks = xt.shape
    groups = width // gw
    blocks = toks // LONG
    nh = gw // hd
    own = lambda: pl.BlockSpec((gw, LONG), lambda g, j, f: (g0 + g, j))
    return pl.pallas_call(
        functools.partial(attn_fwd_kernel, gw=gw, hd=hd),
        out_shape=[jax.ShapeDtypeStruct((width, toks), BF)] * 3
        + [
            jax.ShapeDtypeStruct((groups * nh, blocks, LONG, LONG), BF),
            jax.ShapeDtypeStruct((width, toks), BF),
            jax.ShapeDtypeStruct((groups * 8, toks), F32),
        ],
        grid_spec=pltpu.PrefetchScalarGridSpec(
            num_scalar_prefetch=1,
            grid=(ng, blocks),
            in_specs=[own(), pl.BlockSpec((gw, w.shape[1]), lambda g, j, f: (g0 + g, 0))] + anywhere(1 + len(before)),
            out_specs=[
                own(),
                own(),
                own(),
                pl.BlockSpec((nh, 1, LONG, LONG), lambda g, j, f: (g0 + g, j, 0, 0)),
                own(),
                pl.BlockSpec((8, LONG), lambda g, j, f: (g0 + g, j)),
            ],
            scratch_shapes=[pltpu.VMEM((LONG, LONG), F32)] * 2,
        ),
        input_output_aliases={4 + i: i for i in range(len(before))},
        compiler_params=params(),
        cost_estimate=cost(5 * ng),
        name="attention_forward",
    )(flag, xt, w, step, *before)


def attn_bwd_kernel(
    flag_ref, q_ref, k_ref, v_ref, e_ref, c_ref, inv_ref, dc_ref, x_ref, w_ref, dy_ref, vg_ref, step_ref,
    *refs, gw, hd, rows,
):
    g_ref, keep_ref, send_ref, acc, dq, bacc, pa, pb = refs[-8:]
    nh = gw // hd
    j = pl.program_id(1)
    heads = [slice(h * hd, (h + 1) * hd) for h in range(nh)]
    scaled = []

    def grad_probs(h, buf):
        dc = dc_ref[heads[h], :].astype(F32)
        inv = inv_ref[h : h + 1, :]
        total = jnp.sum(dc * c_ref[heads[h], :].astype(F32), axis=0, keepdims=True) * inv
        scaled.append(((dc * inv).astype(BF), total))
        buf[...] = dg(v_ref[heads[h], :], scaled[h][0], 0, 0)

    bufs = (pa, pb)
    grad_probs(0, pa)
    for h, r in enumerate(heads):
        if h + 1 < nh:
            grad_probs(h + 1, bufs[(h + 1) % 2])
        dci, total = scaled[h]
        e = e_ref[h, 0]
        dq[2 * gw + h * hd : 2 * gw + (h + 1) * hd, :] = dg(dci, e, 1, 1)
        ds = (e.astype(F32) * (bufs[h % 2][...] - total)).astype(BF)
        qs = q_ref[r, :] * jnp.asarray(hd**-0.5, BF)
        dq[gw + h * hd : gw + (h + 1) * hd, :] = dg(qs, ds, 1, 1)
        dq[r, :] = dg(k_ref[r, :], ds, 1, 0) * (hd**-0.5)

    d = dq[...]
    dl = d.astype(BF)
    w = w_ref[...]
    g_ref[...] = (dy_ref[...].astype(F32) + dg(w[:, : 3 * gw], dl, 1, 0)).astype(BF)
    acc[:, : 3 * gw] = jnp.where(j == 0, 0.0, acc[:, : 3 * gw]) + dg(x_ref[...], dl, 1, 1)
    bacc[0] = jnp.where(j == 0, 0.0, bacc[0]) + lane_sum(d[:gw])
    bacc[1] = jnp.where(j == 0, 0.0, bacc[1]) + lane_sum(d[2 * gw :])

    @pl.when(j == pl.num_programs(1) - 1)
    def _():
        rest = acc.shape[1] - 3 * gw
        bqc = jnp.sum(bacc[0], axis=1, keepdims=True)
        bvc = jnp.sum(bacc[1], axis=1, keepdims=True)
        lane = lax.broadcasted_iota(jnp.int32, (gw, rest), 1)
        vectors = jnp.where(lane == 0, bqc, jnp.where(lane == 1, bvc, vg_ref[...][:, :rest]))
        acc[:, 3 * gw :] = vectors
        write_halves(acc, keep_ref, send_ref, flag_ref[1], rows)


def attn_bwd(flag, saved, dct, xt, w, dyt, vg, step, before, g0, ng, gw, hd, rows):
    q, k, v, e, c, inv = saved
    width, toks = xt.shape
    groups = width // gw
    blocks = toks // LONG
    nh = gw // hd
    cols = w.shape[1]
    keep, send = half_shapes(gw, rows, cols)
    own = lambda: pl.BlockSpec((gw, LONG), lambda g, j, f: (g0 + g, j))
    return pl.pallas_call(
        functools.partial(attn_bwd_kernel, gw=gw, hd=hd, rows=rows),
        out_shape=[
            jax.ShapeDtypeStruct((width, toks), BF),
            jax.ShapeDtypeStruct((groups * keep[0],) + keep[1:], BF),
            jax.ShapeDtypeStruct((groups * send[0],) + send[1:], BF),
        ],
        grid_spec=pltpu.PrefetchScalarGridSpec(
            num_scalar_prefetch=1,
            grid=(ng, blocks),
            in_specs=[
                own(),
                own(),
                own(),
                pl.BlockSpec((nh, 1, LONG, LONG), lambda g, j, f: (g0 + g, j, 0, 0)),
                own(),
                pl.BlockSpec((8, LONG), lambda g, j, f: (g0 + g, j)),
                own(),
                own(),
                pl.BlockSpec((gw, cols), lambda g, j, f: (g0 + g, 0)),
                own(),
                pl.BlockSpec((gw, 128), lambda g, j, f: (g0 + g, 0)),
            ]
            + anywhere(1 + len(before)),
            out_specs=[
                own(),
                pl.BlockSpec(keep, lambda g, j, f: (g0 + g,) + (0,) * (len(keep) - 1)),
                pl.BlockSpec(send, lambda g, j, f: (g0 + g,) + (0,) * (len(send) - 1)),
            ],
            scratch_shapes=[
                pltpu.VMEM((gw, cols), F32),
                pltpu.VMEM((3 * gw, LONG), F32),
                pltpu.VMEM((2, gw, 128), F32),
                pltpu.VMEM((LONG, LONG), F32),
                pltpu.VMEM((LONG, LONG), F32),
            ],
        ),
        input_output_aliases={13 + i: i for i in range(len(before))},
        compiler_params=params(),
        cost_estimate=cost(7 * ng),
        name="attention_backward",
    )(flag, q, k, v, e, c, inv, dct, xt, w, dyt, vg, step, *before)


def ffn_kernel(x_ref, ctx, vec_ref, wo_ref, cot_ref, *refs, shards, gw, vbase):
    wf_refs = refs[:shards]
    rest = refs[shards:]
    out_ref, n1_ref, rs_ref, dh_ref = rest[:4]
    grad_refs = rest[4 : 4 + shards]
    vg_ref = rest[4 + shards]
    wf, h1x, ua, ub, act, slope, y2, dyl, dyt, acc1, acc2, accv, sems = rest[5 + shards :]
    j = pl.program_id(0)
    last = pl.num_programs(0) - 1
    groups = h1x.shape[0]
    toks = x_ref.shape[1]
    width = groups * gw
    inv_width = 1.0 / width

    def col(i):
        return vec_ref[:, vbase + i : vbase + i + 1].astype(F32)

    def mean(v):
        return jnp.sum(v, axis=0, keepdims=True) * inv_width

    copies = [pltpu.make_async_copy(wf_refs[s], wf.at[s], sems.at[s]) for s in range(shards)]

    @pl.when(j == 0)
    def _():
        for copy in copies:
            copy.start()
        accv[...] = jnp.zeros_like(accv)

    y1 = x_ref[...].astype(F32) + dg(wo_ref[...], ctx[...], 0, 0) + col(2)
    center = y1 - mean(y1)
    rs1 = lax.rsqrt(mean(center * center) + EPS)
    rs_ref[...] = jnp.broadcast_to(rs1, rs_ref.shape)
    norm1 = center * rs1
    n1_ref[...] = norm1.astype(BF)
    h1 = norm1 * col(3) + col(4)
    y2[...] = (h1 + col(5)).reshape(groups, gw, toks)
    h1x[:, :gw, :] = h1.astype(BF).reshape(groups, gw, toks)
    h1x[:, gw:, :] = jnp.ones((groups, PAD, toks), BF)

    chunks = groups * shards

    def first_dot(i, buf):
        buf[...] = dg(wf[i % shards, i // shards, :, :gw], h1x[i // shards], 0, 0)

    def second_dot(i):
        g = i // shards
        s = i % shards
        y2[g] += dg(wf[s, g, :gw, gw : 2 * gw], act[g, s], 0, 0)

    def gelu(i, buf):
        g = i // shards
        s = i % shards
        u = buf[...]
        phi = lax.erf(u * ROOT_HALF) * 0.5 + 0.5
        act[g, s] = (u * phi).astype(BF)
        slope[g, s] = phi + u * INV_ROOT_2PI * jnp.exp2(u * u * HALF_LOG2E)

    @pl.when(j == 0)
    def _():
        for copy in copies:
            copy.wait()

    first_dot(0, ua)
    first_dot(1, ub)
    gelu(0, ua)

    def forward(k, carry):
        i = 2 * k + 1
        second_dot(i - 1)
        first_dot(i + 1, ua)
        gelu(i, ub)
        second_dot(i)
        first_dot(i + 2, ub)
        gelu(i + 1, ua)
        return carry

    lax.fori_loop(0, chunks // 2 - 1, forward, 0)
    second_dot(chunks - 2)
    gelu(chunks - 1, ub)
    second_dot(chunks - 1)

    yy = y2[...].reshape(width, toks)
    center = yy - mean(yy)
    rs2 = lax.rsqrt(mean(center * center) + EPS)
    norm2 = center * rs2
    out_ref[...] = (norm2 * col(6) + col(7)).astype(BF).T
    cot = cot_ref[...].astype(F32)
    e2 = cot * col(6)
    dy2 = (e2 - mean(e2) - norm2 * mean(e2 * norm2)) * rs2
    accv[0] += lane_sum(dy2)
    accv[1] += lane_sum(cot * norm2)
    accv[2] += lane_sum(cot)
    y2[...] = dy2.reshape(groups, gw, toks)
    dyl[...] = dy2.astype(BF).reshape(groups, gw, toks)
    for g in range(groups):
        dyt[g] = dyl[g].T

    def grad_dot(i, buf):
        g = i // shards
        buf[...] = dg(wf[i % shards, g, :gw, gw : 2 * gw], dyl[g], 1, 0)

    def grads(i, buf):
        g = i // shards
        s = i % shards
        low = (buf[...] * slope[g, s]).astype(BF)
        acc2[s, g] = jnp.where(j == 0, 0.0, acc2[s, g]) + dg(act[g, s], dyt[g], 1, 0)
        y2[g] += dg(wf[s, g, :gw, :gw], low, 1, 0)
        acc1[s, g] = jnp.where(j == 0, 0.0, acc1[s, g]) + dg(h1x[g], low, 1, 1)

    grad_dot(0, ua)

    def backward(k, carry):
        grad_dot(2 * k + 1, ub)
        grads(2 * k, ua)
        grad_dot(2 * k + 2, ua)
        grads(2 * k + 1, ub)
        return carry

    lax.fori_loop(0, chunks // 2 - 1, backward, 0)
    grad_dot(chunks - 1, ub)
    grads(chunks - 2, ua)
    grads(chunks - 1, ub)
    dh_ref[...] = y2[...].reshape(width, toks).astype(BF)

    @pl.when(j == last)
    def _():
        for s in range(shards):

            def write(g, carry, s=s):
                grad_refs[s][g, :, :gw] = acc1[s, g].astype(BF)
                grad_refs[s][g, :gw, gw : 2 * gw] = acc2[s, g].astype(BF)
                grad_refs[s][g, gw:, gw : 2 * gw] = jnp.zeros((PAD, gw), BF)
                return carry

            lax.fori_loop(0, groups, write, 0, unroll=2)
        vg_ref[...] = spread(accv, 5)


def spread(sums, first):
    count, width, lanes = sums.shape
    lane = lax.broadcasted_iota(jnp.int32, (width, lanes), 1)
    t = jnp.zeros((width, lanes), F32)
    for i in range(count):
        t = jnp.where(lane == i + first, jnp.sum(sums[i], axis=1, keepdims=True), t)
    return t


def write_halves(full, keep_ref, send_ref, mine, rows):
    if rows % 8:
        keep_ref[...] = full[...].astype(BF)
        send_ref[...] = jnp.zeros_like(send_ref)
        return
    for k in range(keep_ref.shape[0]):
        own = pl.multiple_of((2 * k + mine) * rows, 8)
        other = pl.multiple_of((2 * k + 1 - mine) * rows, 8)
        keep_ref[k] = full[pl.ds(own, rows), :].astype(BF)
        send_ref[k] = full[pl.ds(other, rows), :].astype(BF)


def half_shapes(total, rows, cols):
    if rows % 8:
        return (total, cols), (16, 128)
    return (total // rows // 2, rows, cols), (total // rows // 2, rows, cols)


def core_step(keep, send, rows, index, count):
    if rows % 8:
        keep, send = halves(keep.reshape(-1, rows, keep.shape[-1]), 0, index)
    return keep, swap(send, 0, count)


def norm_kernel(
    me_ref, ctx, n1_ref, rs_ref, dh_ref, vec_ref, wo_ref, vga_ref,
    dy1_ref, dct_ref, keep_ref, send_ref, vg_ref, acco, accv, *, vbase, rows,
):
    j = pl.program_id(0)
    last = pl.num_programs(0) - 1
    inv_width = 1.0 / n1_ref.shape[0]

    def mean(v):
        return jnp.sum(v, axis=0, keepdims=True) * inv_width

    norm1 = n1_ref[...].astype(F32)
    dh1 = dh_ref[...].astype(F32)
    e1 = dh1 * vec_ref[:, vbase + 3 : vbase + 4].astype(F32)
    dy1 = (e1 - mean(e1) - norm1 * mean(e1 * norm1)) * rs_ref[0:1, :]
    low1 = dy1.astype(BF)
    dy1_ref[...] = low1
    dct_ref[...] = dg(wo_ref[...], low1, 1, 0).astype(BF)
    sums = (lane_sum(dy1), lane_sum(dh1 * norm1), lane_sum(dh1))
    acco[...] = jnp.where(j == 0, 0.0, acco[...]) + dg(ctx[...], low1, 1, 1)
    for i in range(3):
        accv[i] = jnp.where(j == 0, 0.0, accv[i]) + sums[i]

    @pl.when(j == last)
    def _():
        write_halves(acco, keep_ref, send_ref, me_ref[1], rows)
        vg_ref[...] = vga_ref[...] + spread(accv, 2)


def whole(shape):
    return pl.BlockSpec(shape, lambda j, *m: (0,) * len(shape), pipeline_mode=pl.Buffered(1))


def ffn_layer(xt, ctx, w, wo, wfs, cott, gw):
    width, toks = xt.shape
    blk = min(LONG, toks)
    shards = len(wfs)
    groups = wfs[0].shape[0]
    vec_block = (3 * gw) // 128
    col_blk = lambda rows: pl.BlockSpec((rows, blk), lambda j: (0, j))
    return pl.pallas_call(
        functools.partial(ffn_kernel, shards=shards, gw=gw, vbase=3 * gw - 128 * vec_block),
        out_shape=[
            jax.ShapeDtypeStruct((toks, width), BF),
            jax.ShapeDtypeStruct((width, toks), BF),
            jax.ShapeDtypeStruct((8, toks), F32),
            jax.ShapeDtypeStruct((width, toks), BF),
        ]
        + [jax.ShapeDtypeStruct(wfs[0].shape, BF)] * shards
        + [jax.ShapeDtypeStruct((width, 128), F32)],
        grid=(toks // blk,),
        in_specs=[
            col_blk(width),
            col_blk(width),
            pl.BlockSpec((width, 128), lambda j: (0, vec_block)),
            whole((width, width)),
            col_blk(width),
        ]
        + anywhere(shards),
        out_specs=[
            pl.BlockSpec((blk, width), lambda j: (j, 0)),
            col_blk(width),
            col_blk(8),
            col_blk(width),
        ]
        + [whole(wfs[0].shape) for _ in wfs]
        + [whole((width, 128))],
        scratch_shapes=[
            pltpu.VMEM((shards,) + wfs[0].shape, BF),
            pltpu.VMEM((groups, gw + PAD, blk), BF),
            pltpu.VMEM((gw, blk), F32),
            pltpu.VMEM((gw, blk), F32),
            pltpu.VMEM((groups, shards, gw, blk), BF),
            pltpu.VMEM((groups, shards, gw, blk), F32),
            pltpu.VMEM((groups, gw, blk), F32),
            pltpu.VMEM((groups, gw, blk), BF),
            pltpu.VMEM((groups, blk, gw), BF),
            pltpu.VMEM((shards, groups, gw + PAD, gw), F32),
            pltpu.VMEM((shards, groups, gw, gw), F32),
            pltpu.VMEM((3, width, 128), F32),
            pltpu.SemaphoreType.DMA((shards,)),
        ],
        compiler_params=params(),
        cost_estimate=cost(40),
        name="feed_forward",
    )(xt, ctx, w, wo, cott, *wfs)


def norm_layer(me, ctx, n1, rs1, dh1, w, wo, vga, gw, rows):
    width, toks = n1.shape
    blk = min(LONG, toks)
    vec_block = (3 * gw) // 128
    col_blk = lambda rows: pl.BlockSpec((rows, blk), lambda j, m: (0, j))
    keep, send = half_shapes(width, rows, width)
    return pl.pallas_call(
        functools.partial(norm_kernel, vbase=3 * gw - 128 * vec_block, rows=rows),
        out_shape=[
            jax.ShapeDtypeStruct((width, toks), BF),
            jax.ShapeDtypeStruct((width, toks), BF),
            jax.ShapeDtypeStruct(keep, BF),
            jax.ShapeDtypeStruct(send, BF),
            jax.ShapeDtypeStruct((width, 128), F32),
        ],
        grid_spec=pltpu.PrefetchScalarGridSpec(
            num_scalar_prefetch=1,
            grid=(toks // blk,),
            in_specs=[
                col_blk(width),
                col_blk(width),
                col_blk(8),
                col_blk(width),
                pl.BlockSpec((width, 128), lambda j, m: (0, vec_block)),
                whole((width, width)),
                whole((width, 128)),
            ],
            out_specs=[col_blk(width), col_blk(width), whole(keep), whole(send), whole((width, 128))],
            scratch_shapes=[
                pltpu.VMEM((width, width), F32),
                pltpu.VMEM((3, width, 128), F32),
            ],
        ),
        compiler_params=params(),
        cost_estimate=cost(7),
        name="norm_backward",
    )(me, ctx, n1, rs1, dh1, w, wo, vga)


def swap(a, bit, count):
    return lax.ppermute(a, AXES, [(i, i ^ (1 << bit)) for i in range(count)])


def gather_bit(cur, b, index, count):
    return merge(cur, swap(cur, b, count), b, index)


def merge(cur, got, b, index):
    place = lax.broadcasted_iota(jnp.int32, (1, 2) + (1,) * (cur.ndim - 1), 1)
    new = jnp.where(place == ((index >> b) & 1), cur[:, None], got[:, None])
    return new.reshape((cur.shape[0] * 2,) + cur.shape[1:])


def halves(cur, b, index):
    pair = cur.reshape((cur.shape[0] // 2, 2) + cur.shape[1:])
    mine = (index >> b) & 1
    keep = lax.dynamic_index_in_dim(pair, mine, 1, keepdims=False)
    return keep, lax.dynamic_index_in_dim(pair, 1 - mine, 1, keepdims=False)


def reduce_bit(cur, b, index, count):
    keep, send = halves(cur, b, index)
    return keep.astype(F32) + swap(send, b, count).astype(F32)


def log2(n):
    return n.bit_length() - 1


def body(
    dp, ffn, tokens, long_seq, cotangent, query_weight, key_weight, value_weight, out_weight,
    query_bias, value_bias, out_bias, attn_gain, attn_shift, ffn_in_weight, ffn_in_bias,
    ffn_out_weight, ffn_out_bias, ffn_gain, ffn_shift,
):
    count = dp * ffn
    index = lax.axis_index("dp") * ffn + lax.axis_index("ffn")
    ffn_bits = list(range(log2(ffn)))
    dp_bits = list(range(log2(ffn), log2(count)))
    all_bits = ffn_bits + dp_bits
    width = tokens.shape[1]
    groups = ffn_in_weight.shape[0]
    gw = width // groups
    hd = width // HEADS
    rows = query_weight.shape[0]

    vectors = [query_bias, value_bias, out_bias, attn_gain, attn_shift, ffn_out_bias, ffn_gain, ffn_shift]
    used = 3 * gw + len(vectors)
    cols = -(-used // 128) * 128
    columns = jnp.pad(jnp.stack(vectors), ((0, cols - used), (0, 0))).T
    both = jnp.concatenate([query_weight, key_weight, value_weight, columns, out_weight], axis=1)[None]
    top = ffn_bits[-1]
    first = jnp.concatenate([ffn_in_weight, ffn_in_bias[:, None, :], jnp.zeros((groups, PAD - 1, gw), BF)], axis=1)
    second = jnp.pad(ffn_out_weight, ((0, 0), (0, PAD), (0, 0)))
    wf = jnp.concatenate([first, second], axis=2)
    xt = tokens.T
    cott = cotangent.T
    flags = jnp.concatenate([long_seq, (index & 1).astype(jnp.int32)[None]])
    for n, b in enumerate(reversed(dp_bits[1:])):
        both = gather_bit(both, b, index, count)
        if n == 0:
            both, flags = lax.optimization_barrier((both, flags))
        if n == 1:
            both, xt = lax.optimization_barrier((both, xt))
    both = gather_bit(both, top, index, count)
    both, wf, cott = lax.optimization_barrier((both, wf, cott))
    got_wf = swap(wf, top, count)
    both = both.reshape(both.shape[0] // 2, 2 * rows, both.shape[2])
    w = gather_bit(both[:, :, :cols], dp_bits[0], index, count).reshape(-1, rows, cols)
    wo = both[:, :, cols:]
    for b in reversed(ffn_bits[:-1]):
        w = gather_bit(w, b, index, count)
    w, wo = lax.optimization_barrier((w, wo))
    w = w.reshape(width, cols)
    got_wo = swap(wo, dp_bits[0], count)

    saved = []
    step = flags
    for i, (g0, ng) in enumerate(FORWARD):
        saved = list(attn_fwd(flags, xt, w, step, saved, g0, ng, gw, hd))
        if i == 0:
            got_wo, saved[4] = lax.optimization_barrier((got_wo, saved[4]))
            wo = merge(wo, got_wo, dp_bits[0], index)
            step = wo = wo.reshape(-1, rows, width)
            got_wo = swap(wo, 0, count)
        if i == 1:
            got_wf, got_wo, saved[4] = lax.optimization_barrier((got_wf, got_wo, saved[4]))
    wo = merge(wo, got_wo, 0, index).reshape(width, width)
    wfs = [wf, swap(wf, 0, count), got_wf, swap(got_wf, 0, count)]
    ctx = saved[4]
    outs = ffn_layer(xt, ctx, w, wo, wfs, cott, gw)
    output, n1, rs1, dh1 = outs[:4]
    gf = outs[4 : 4 + ffn]
    dyt, dct, keep_o, send_o, vg = norm_layer(flags, ctx, n1, rs1, dh1, w, wo, outs[4 + ffn], gw, rows)

    def add(keep, got):
        return (keep.astype(F32) + got.astype(F32)).astype(BF)

    got1 = swap(gf[1], 0, count)
    got3 = swap(gf[3], 0, count)
    send = add(gf[2], got3)
    got2 = swap(send, top, count)
    keep_o, got_o = core_step(keep_o, send_o, rows, index, count)

    grads = []
    step = send
    for i, (g0, ng) in enumerate(BACKWARD):
        grads = list(attn_bwd(flags, saved, dct, xt, w, dyt, vg, step, grads, g0, ng, gw, hd, rows))
        if i == 0:
            got_o, grads[0] = lax.optimization_barrier((got_o, grads[0]))
            keep_o, send_o = halves(add(keep_o, got_o), top, index)
            got2, send_o, grads[0] = lax.optimization_barrier((got2, send_o, grads[0]))
            got_o = swap(send_o, top, count)
            mine = (gf[0].astype(F32) + got1.astype(F32) + got2.astype(F32)).astype(BF)
            keep_f, step = halves(mine.reshape(dp, -1, mine.shape[-1]), dp_bits[0], index)
            got_f = swap(step, dp_bits[0], count)
        if i == 1:
            got_f, got_o, grads[0] = lax.optimization_barrier((got_f, got_o, grads[0]))
            keep_f, step = halves(add(keep_f, got_f), dp_bits[1], index)
            got_f = swap(step, dp_bits[1], count)
            keep_o, send_o = halves(add(keep_o, got_o), dp_bits[0], index)
            got_o = swap(send_o, dp_bits[0], count)
        if i == 2:
            got_f, got_o, grads[1] = lax.optimization_barrier((got_f, got_o, grads[1]))
    ffn_sum = add(keep_f, got_f)
    keep_f, send_f = halves(ffn_sum, dp_bits[2], index)
    got_f = swap(send_f, dp_bits[2], count)
    keep_w, got_w = core_step(grads[1], grads[2], rows, index, count)
    keep_w, send_w = halves(add(keep_w, got_w), top, index)
    keep_w, got_f = lax.optimization_barrier((keep_w, got_f))
    got_w = swap(send_w, top, count)
    ffn_sum = add(keep_f, got_f)
    for b in dp_bits[3:]:
        ffn_sum = reduce_bit(ffn_sum, b, index, count).astype(BF)
    rows_first = Layout(major_to_minor=(0, 1))
    keep_w, send_w = halves(add(keep_w, got_w), dp_bits[0], index)
    got_w = swap(send_w, dp_bits[0], count)
    keep_w, grads[0] = lax.optimization_barrier((keep_w, grads[0]))
    grad_tokens = with_layout_constraint(grads[0].T, rows_first)
    got_w, grad_tokens = lax.optimization_barrier((got_w, grad_tokens))

    for b in reversed(dp_bits):
        ffn_sum = gather_bit(ffn_sum, b, index, count)
    ffn_sum = ffn_sum.reshape(mine.shape).astype(F32)

    both = jnp.concatenate([add(keep_w, got_w), add(keep_o, got_o)], axis=2)
    for b in dp_bits[1:]:
        both = reduce_bit(both, b, index, count)
        if b != dp_bits[-1]:
            both = both.astype(BF)
    dw_sum = both[0, :, :cols]
    dwo_sum = both[0, :, cols:]
    vec = lambda i: dw_sum[:, 3 * gw + i]
    return (
        output,
        grad_tokens,
        dw_sum[:, :gw],
        dw_sum[:, gw : 2 * gw],
        dw_sum[:, 2 * gw : 3 * gw],
        dwo_sum,
        vec(0),
        vec(1),
        vec(2),
        vec(3),
        vec(4),
        ffn_sum[:, :gw, :gw],
        ffn_sum[:, gw, :gw],
        ffn_sum[:, :gw, gw:],
        vec(5),
        vec(6),
        vec(7),
    )


def solution(mesh):
    both = P(AXES)
    rows = P(AXES, None)
    return jax.shard_map(
        functools.partial(body, mesh.shape["dp"], mesh.shape["ffn"]),
        mesh=mesh,
        in_specs=(
            rows, both, rows, rows, rows, rows, rows, both, both, both, both, both,
            P(None, None, "ffn"), P(None, "ffn"), P(None, "ffn", None), both, both, both,
        ),
        out_specs=(
            rows, rows, rows, rows, rows, rows, both, both, both, both, both,
            P(None, None, "ffn"), P(None, "ffn"), P(None, "ffn", None), both, both, both,
        ),
        check_vma=False,
    )
```
